32 devices in a mesh: img: 8 (over y, x, core), tile: 4 (over z).
Axes of the slice: x: 2, y: 2, z: 4, core: 2. Of those that a mesh axis runs over, the one named last changes fastest.
Arguments:
- vit_in: bfloat16 [16, 4, 144, 768], P('img', 'tile'), may hold values from -6 to 6
- map_in: bfloat16 [16, 4, 576, 1024], P('img', 'tile'), may hold values from -6 to 6
- group_images: int32 [8], P('img'), may hold values from 1 to 2, as said below
- vit_grad_out: bfloat16 [16, 4, 144, 768], P('img', 'tile'), may hold values from -6 to 6
- map_grad_out: bfloat16 [16, 4, 576, 1024], P('img', 'tile'), may hold values from -6 to 6
- w_query: bfloat16 [768, 768], replicated, may hold values from -0.21875 to 0.21875
- w_key: bfloat16 [768, 768], replicated, may hold values from -0.21875 to 0.21875
- w_value: bfloat16 [768, 768], replicated, may hold values from -0.21875 to 0.21875
- w_out: bfloat16 [768, 768], replicated, may hold values from -2.5 to 2.5
- w_up: bfloat16 [768, 3072], replicated, may hold values from -0.21875 to 0.21875
- w_down: bfloat16 [3072, 768], replicated, may hold values from -0.109375 to 0.109375
- w_expand: bfloat16 [1024, 4096], replicated, may hold values from -0.1875 to 0.1875
- w_shrink: bfloat16 [4096, 1024], replicated, may hold values from -0.09375 to 0.09375
- w_adapt: bfloat16 [1024, 768], replicated, may hold values from -0.375 to 0.375
- gain_attn: bfloat16 [768], replicated, may hold values from 0.099609375 to 1.8984375
- gain_mlp: bfloat16 [768], replicated, may hold values from 0.099609375 to 1.8984375
- gain_conv: bfloat16 [1024], replicated, may hold values from 0.099609375 to 1.8984375
- dw_large: bfloat16 [49, 1024], replicated, may hold values from -0.875 to 0.875
- dw_small: bfloat16 [9, 768], replicated, may hold values from -2 to 2
- gate_low: bfloat16 [768], replicated, may hold values from -0.21875 to 0.21875
- gate_high: bfloat16 [768], replicated, may hold values from -0.21875 to 0.21875
Outputs:
- vit_out: bfloat16 [16, 4, 144, 768], P('img', 'tile')
- map_out: bfloat16 [16, 4, 576, 1024], P('img', 'tile')
- vit_in_grad: bfloat16 [16, 4, 144, 768], P('img', 'tile')
- map_in_grad: bfloat16 [16, 4, 576, 1024], P('img', 'tile')
- w_query_grad: float32 [768, 768], P('img', 'tile')
- w_key_grad: float32 [768, 768], P('img', 'tile')
- w_value_grad: float32 [768, 768], P('img', 'tile')
- w_out_grad: float32 [768, 768], P('img', 'tile')
- w_up_grad: float32 [768, 3072], P('img', 'tile')
- w_down_grad: float32 [3072, 768], P('img', 'tile')
- w_expand_grad: float32 [1024, 4096], P('img', 'tile')
- w_shrink_grad: float32 [4096, 1024], P('img', 'tile')
- w_adapt_grad: float32 [1024, 768], P('img', 'tile')
- gain_attn_grad: float32 [768], replicated
- gain_mlp_grad: float32 [768], replicated
- gain_conv_grad: float32 [1024], replicated
- dw_large_grad: float32 [49, 1024], replicated
- dw_small_grad: float32 [9, 768], replicated
- gate_low_grad: float32 [768], replicated
- gate_high_grad: float32 [768], replicated
The draws below stay inside these ranges and needn't reach their ends.
Inputs may be any that keep to these rules, and one draw needn't show every extreme that they name: Group g holds its images in slots 0 to group_images[g] - 1 of its 2 slots; other slots hold no image. In every draw some group holds 2 images and some group holds 1.
All inputs are finite; a program needn't handle non-finite values.
Results may differ from the reference program's by a relative error of at most 0.018.
Values may be sent and summed in bfloat16 or wider, within the bound.
A program may use at most 320 MiB of HBM per device.

```python
import jax
import jax.numpy as jnp
from jax import lax

D = 768
HEADS = 12
HDIM = 64
FF = 3072
C = 1024
CF = 4096
GRID = 24
CAP = 2
TOKT = 144
PIXT = 576
SLOTS = 16


def draw_group_images(key, part):
    groups = SLOTS // CAP
    counts = jax.random.randint(key, (groups,), 1, CAP + 1, dtype=jnp.int32)
    shuffled = jax.random.permutation(jax.random.fold_in(key, 7), groups)
    counts = counts.at[shuffled[0]].set(CAP)
    counts = counts.at[shuffled[1]].set(1)
    return counts


def block_scale(stream_key, extent, pieces, least, largest):
    def one(position, parts):
        heights = jax.random.uniform(jax.random.fold_in(jax.random.fold_in(stream_key, 6), position), (parts,), jnp.float32, least / len(pieces), largest / len(pieces))
        return jnp.repeat(jnp.exp(heights), extent[position] // parts).reshape((-1,) + (1,) * (len(extent) - position - 1))

    gain = one(*pieces[0])
    for cut in pieces[1:]:
        gain = gain * one(*cut)
    return gain


def bell_draw(stream_key, shape, scale, bound, shards=(), held_as=jnp.bfloat16):
    drawn = jax.random.normal(stream_key, shape, jnp.float32) * scale
    if len(shards) > 0:
        drawn = block_scale(stream_key, shape, shards, -0.22, 0.18) * drawn
    return jnp.clip(drawn, min=-bound, max=bound).astype(held_as)


def setup_inputs(seed: int = 0) -> dict:
    streams_of = jax.random.split(jax.random.key(seed), 22)
    vit_in = bell_draw(streams_of[0], (SLOTS, 4, TOKT, D), 1.0, 6.0, ((0, 8), (1, 4)))
    map_in = bell_draw(streams_of[1], (SLOTS, 4, PIXT, C), 1.0, 6.0, ((0, 8), (1, 4)))
    group_images = draw_group_images(jax.random.fold_in(streams_of[21], 71), 0)
    vit_grad_out = bell_draw(streams_of[3], (SLOTS, 4, TOKT, D), 1.0, 6.0, ((0, 8), (1, 4)))
    map_grad_out = bell_draw(streams_of[4], (SLOTS, 4, PIXT, C), 1.0, 6.0, ((0, 8), (1, 4)))
    w_query = bell_draw(streams_of[5], (D, D), D ** -0.5, 0.21875)
    w_key = bell_draw(streams_of[6], (D, D), D ** -0.5, 0.21875)
    w_value = bell_draw(streams_of[7], (D, D), D ** -0.5, 0.21875)
    w_out = bell_draw(streams_of[8], (D, D), (max(D // 128, 1)) ** -0.5, 2.5)
    w_up = bell_draw(streams_of[9], (D, FF), D ** -0.5, 0.21875)
    w_down = bell_draw(streams_of[10], (FF, D), FF ** -0.5, 0.109375)
    w_expand = bell_draw(streams_of[11], (C, CF), C ** -0.5, 0.1875)
    w_shrink = bell_draw(streams_of[12], (CF, C), CF ** -0.5, 0.09375)
    w_adapt = bell_draw(streams_of[13], (C, D), (C // 4) ** -0.5, 0.375)
    gain_attn = jnp.clip(1.0 + 0.18 * jax.random.normal(streams_of[14], (D,), jnp.float32), 0.099609375, 1.8984375).astype(jnp.bfloat16)
    gain_mlp = jnp.clip(1.0 + 0.18 * jax.random.normal(streams_of[15], (D,), jnp.float32), 0.099609375, 1.8984375).astype(jnp.bfloat16)
    gain_conv = jnp.clip(1.0 + 0.18 * jax.random.normal(streams_of[16], (C,), jnp.float32), 0.099609375, 1.8984375).astype(jnp.bfloat16)
    dw_large = bell_draw(streams_of[17], (49, C), 49 ** -0.5, 0.875)
    dw_small = bell_draw(streams_of[18], (9, D), 9 ** -0.5, 2.0)
    gate_low = bell_draw(streams_of[19], (D,), D ** -0.5, 0.21875)
    gate_high = bell_draw(streams_of[20], (D,), D ** -0.5, 0.21875)
    return {"vit_in": vit_in, "map_in": map_in, "group_images": group_images, "vit_grad_out": vit_grad_out, "map_grad_out": map_grad_out, "w_query": w_query, "w_key": w_key, "w_value": w_value, "w_out": w_out, "w_up": w_up, "w_down": w_down, "w_expand": w_expand, "w_shrink": w_shrink, "w_adapt": w_adapt, "gain_attn": gain_attn, "gain_mlp": gain_mlp, "gain_conv": gain_conv, "dw_large": dw_large, "dw_small": dw_small, "gate_low": gate_low, "gate_high": gate_high}


highest = lax.Precision.HIGHEST

@jax.custom_vjp
def low(v):
    return lax.optimization_barrier(v.astype(jnp.bfloat16)).astype(jnp.float32)

@jax.custom_vjp
def low_back(v):
    return v

def low_keep(v):
    return (low(v), None)

def low_pass(kept, grad):
    return (grad,)

def back_keep(v):
    return (v, None)

def back_low(kept, grad):
    return (low(grad),)
low.defvjp(low_keep, low_pass)
low_back.defvjp(back_keep, back_low)

def matmul(left_side, right_side):
    return jnp.einsum('...i,ij->...j', left_side, right_side, precision=highest)

def layer_norm(values, gain_row):
    centre = values - lax.optimization_barrier(jnp.mean(values, axis=-1, keepdims=True))
    spread = lax.optimization_barrier(jnp.mean(centre * centre, axis=-1, keepdims=True))
    return centre * lax.rsqrt(spread + 1e-06) * gain_row

def gelu_exact(values):
    return 0.5 * values * (1.0 + lax.erf(values * 0.7071067811865476))

def depthwise(field_map, tap_weights, radius):
    kernel_side = 2 * radius + 1
    rows = field_map.shape[1]
    cols = field_map.shape[2]
    padded = jnp.pad(field_map, ((0, 0), (radius, radius), (radius, radius), (0, 0)))
    total = jnp.zeros(field_map.shape, field_map.dtype)
    for row_off in range(kernel_side):
        for col_off in range(kernel_side):
            window = padded[:, row_off:row_off + rows, col_off:col_off + cols, :]
            total = total + tap_weights[row_off * kernel_side + col_off] * window
    return total

def pool_pairs(field_map):
    slot_count, row_count, col_count, channels = field_map.shape
    return lax.optimization_barrier(jnp.mean(field_map.reshape(slot_count, row_count // 2, 2, col_count // 2, 2, channels), axis=(2, 4)))

def merging(residual_two, merged_tokens, gate_low, gate_high):
    gate_logit = lax.optimization_barrier(jnp.sum(residual_two * gate_low, axis=-1, keepdims=True)) + lax.optimization_barrier(jnp.sum(merged_tokens * gate_high, axis=-1, keepdims=True))
    gate_value = 1.0 / (1.0 + jnp.exp(-gate_logit))
    return residual_two + gate_value * merged_tokens

def to_image(tile_rows, half_side):
    slot_count = tile_rows.shape[0]
    channels = tile_rows.shape[-1]
    blocks = tile_rows.reshape(slot_count, 2, 2, half_side, half_side, channels)
    return blocks.transpose(0, 1, 3, 2, 4, 5).reshape(slot_count, 2 * half_side, 2 * half_side, channels)

def from_image(field_map, half_side):
    slot_count = field_map.shape[0]
    channels = field_map.shape[-1]
    blocks = field_map.reshape(slot_count, 2, half_side, 2, half_side, channels).transpose(0, 1, 3, 2, 4, 5)
    return blocks.reshape(slot_count, 4, half_side * half_side, channels)

def attend_image(packed):
    query_rows, key_rows, value_rows = packed
    token_count = query_rows.shape[0]
    query_heads = query_rows.reshape(token_count, HEADS, HDIM)
    key_heads = key_rows.reshape(token_count, HEADS, HDIM)
    value_heads = value_rows.reshape(token_count, HEADS, HDIM)
    raw_scores = jnp.einsum('qhd,khd->hqk', query_heads, key_heads, precision=highest)
    scores = low_back(raw_scores * HDIM ** (-0.5))
    row_max = lax.optimization_barrier(jnp.max(scores, axis=-1, keepdims=True))
    shifted = jnp.exp(scores - row_max)
    weights = low(shifted / lax.optimization_barrier(jnp.sum(shifted, axis=-1, keepdims=True)))
    mixed_rows = jnp.einsum('hqk,khd->qhd', weights, value_heads, precision=highest)
    return mixed_rows.reshape(token_count, HEADS * HDIM)

def forward(vit_in, map_in, w_query, w_key, w_value, w_out, w_up, w_down, w_expand, w_shrink, w_adapt, gain_attn, gain_mlp, gain_conv, dw_large, dw_small, gate_low, gate_high):
    slot_count = vit_in.shape[0]
    tokens = vit_in.reshape(slot_count, 4 * TOKT, D)
    normed_one = low(layer_norm(tokens, gain_attn))
    queries = low_back(low(matmul(normed_one, w_query)))
    key_rows = low_back(low(matmul(normed_one, w_key)))
    value_rows = low_back(low(matmul(normed_one, w_value)))
    mixed_rows = lax.map(jax.checkpoint(attend_image), (queries, key_rows, value_rows))
    mixed_rows = low_back(low(mixed_rows))
    residual_one = tokens + low_back(matmul(mixed_rows, w_out))
    normed_two = low(layer_norm(residual_one, gain_mlp))
    acted = low(gelu_exact(low_back(matmul(normed_two, w_up))))
    residual_two = residual_one + low_back(matmul(acted, w_down))
    picture = to_image(map_in, GRID)
    spread_map = depthwise(picture, dw_large, 3)
    conv_norm = low(layer_norm(spread_map, gain_conv))
    wide_act = low(gelu_exact(low_back(matmul(conv_norm, w_expand))))
    map_after = picture + low_back(matmul(wide_act, w_shrink))
    pooled = low(pool_pairs(map_after))
    adapted = low_back(low(matmul(pooled, w_adapt)))
    merged_map = depthwise(adapted, dw_small, 1)
    merged_tokens = from_image(merged_map, GRID // 2).reshape(slot_count, 4 * TOKT, D)
    vit_after = merging(residual_two, merged_tokens, gate_low, gate_high)
    return (vit_after.reshape(vit_in.shape), from_image(map_after, GRID))

def reference(vit_in, map_in, group_images, vit_grad_out, map_grad_out, w_query, w_key, w_value, w_out, w_up, w_down, w_expand, w_shrink, w_adapt, gain_attn, gain_mlp, gain_conv, dw_large, dw_small, gate_low, gate_high):
    slot_count = vit_in.shape[0]
    slot_ids = jnp.arange(slot_count, dtype=jnp.int32)
    owners = jnp.take(group_images, slot_ids // CAP)
    live_all = (slot_ids % CAP < owners).astype(jnp.float32)
    params = tuple((argument.astype(jnp.float32) for argument in (w_query, w_key, w_value, w_out, w_up, w_down, w_expand, w_shrink, w_adapt, gain_attn, gain_mlp, gain_conv, dw_large, dw_small, gate_low, gate_high)))
    zero_grads = tuple((jnp.zeros(item.shape, item.dtype) for item in params))

    def one_slot(totals, packed):
        vit_slot, map_slot, vit_cot, map_cot, live_one = packed
        vit_f = vit_slot.astype(jnp.float32)[None]
        map_f = map_slot.astype(jnp.float32)[None]
        outputs, pullback = jax.vjp(forward, vit_f, map_f, *params)
        grads = pullback((vit_cot.astype(jnp.float32)[None] * live_one, map_cot.astype(jnp.float32)[None] * live_one))
        new_totals = tuple((total + part for total, part in zip(totals, grads[2:])))
        results = ((outputs[0][0] * live_one).astype(jnp.bfloat16), (outputs[1][0] * live_one).astype(jnp.bfloat16), grads[0][0].astype(jnp.bfloat16), grads[1][0].astype(jnp.bfloat16))
        return (new_totals, results)
    totals, results = lax.scan(one_slot, zero_grads, (vit_in, map_in, vit_grad_out, map_grad_out, live_all))
    return (results[0], results[1], results[2], results[3], totals[0], totals[1], totals[2], totals[3], totals[4], totals[5], totals[6], totals[7], totals[8], totals[9], totals[10], totals[11], totals[12], totals[13], totals[14], totals[15])
```

```python
from functools import partial
import math

import jax
import jax.numpy as jnp
from jax import lax
from jax.experimental import pallas as pl
from jax.experimental.pallas import tpu as pltpu
from jax.sharding import PartitionSpec as P

HEADS = 12
HDIM = 64


highest = lax.Precision.HIGHEST


def swapped(array, axis, bit):
    return lax.ppermute(array, axis, [(i, i ^ 1 << bit) for i in range(lax.axis_size(axis))])


def layer_norm(values, gain_row):
    centre = values - jnp.mean(values, axis=-1, keepdims=True)
    spread = jnp.mean(centre * centre, axis=-1, keepdims=True)
    return centre * lax.rsqrt(spread + 1e-06) * gain_row


def gelu_exact(values):
    return 0.5 * values * (1.0 + lax.erf(values * 0.7071067811865476))


def gelu_pair(values):
    spread = 0.5 * (1.0 + lax.erf(values * 0.7071067811865476))
    bell = jnp.exp(-0.5 * values * values) * 0.3989422804014327
    return (values * spread).astype(jnp.bfloat16), (spread + values * bell).astype(jnp.bfloat16)


def depthwise(field_map, tap_weights, radius, margin):
    kernel_side = 2 * radius + 1
    channels = tap_weights.shape[1]
    kernel = tap_weights.reshape(kernel_side, kernel_side, 1, channels)
    return lax.conv_general_dilated(
        field_map,
        kernel,
        (1, 1),
        ((margin, margin), (margin, margin)),
        dimension_numbers=("NHWC", "HWIO", "NHWC"),
        feature_group_count=channels,
        precision=highest,
    )


def pool_pairs(field_map):
    slot_count, row_count, col_count, channels = field_map.shape
    return jnp.mean(
        field_map.reshape(slot_count, row_count // 2, 2, col_count // 2, 2, channels), axis=(2, 4)
    )


def merging(residual_two, merged_tokens, gate_low, gate_high):
    gate_logit = jnp.sum(residual_two * gate_low, axis=-1, keepdims=True) + jnp.sum(
        merged_tokens * gate_high, axis=-1, keepdims=True
    )
    gate_value = 1.0 / (1.0 + jnp.exp(-gate_logit))
    return residual_two + gate_value * merged_tokens


def project(left_side, right_side):
    return jnp.einsum("...i,ij->...j", left_side, right_side, preferred_element_type=jnp.float32)


def project_back(left_side, right_side):
    return jnp.einsum("...j,ij->...i", left_side, right_side, preferred_element_type=jnp.float32)


def outer_sum(left_side, right_side):
    flat_left = left_side.reshape(-1, left_side.shape[-1])
    flat_right = right_side.reshape(-1, right_side.shape[-1])
    return lax.dot_general(
        flat_left, flat_right, (((0,), (0,)), ((), ())), preferred_element_type=jnp.float32
    ).astype(jnp.bfloat16)


def split_heads(rows_low):
    return rows_low.reshape(rows_low.shape[0], rows_low.shape[1], HEADS, HDIM)


def attention_scores(query_low, key_all):
    return jnp.einsum(
        "sqhd,skhd->shqk",
        split_heads(query_low),
        split_heads(key_all),
        preferred_element_type=jnp.float32,
    ) * HDIM ** (-0.5)


def add_rims(tile_field, radius):
    tile_place = lax.axis_index("tile")
    for which_bit in range(2):
        axis_dim = 2 - which_bit
        on_low = tile_place >> which_bit & 1 == 0
        side_len = tile_field.shape[axis_dim]
        upper_rim = lax.slice_in_dim(tile_field, side_len - radius, side_len, axis=axis_dim)
        lower_rim = lax.slice_in_dim(tile_field, 0, radius, axis=axis_dim)
        outgoing = jnp.where(on_low, upper_rim, lower_rim)
        incoming = swapped(outgoing, "tile", which_bit)
        blank_rim = jnp.zeros_like(incoming)
        tile_field = jnp.where(
            on_low,
            jnp.concatenate([blank_rim, tile_field, incoming], axis_dim),
            jnp.concatenate([incoming, tile_field, blank_rim], axis_dim),
        )
    return tile_field


def return_rims(grad_field, radius):
    tile_place = lax.axis_index("tile")
    for which_bit in (1, 0):
        axis_dim = 2 - which_bit
        on_low = tile_place >> which_bit & 1 == 0
        total_len = grad_field.shape[axis_dim]
        side_len = total_len - 2 * radius
        high_rim = lax.slice_in_dim(grad_field, total_len - radius, total_len, axis=axis_dim)
        low_rim = lax.slice_in_dim(grad_field, 0, radius, axis=axis_dim)
        outgoing = jnp.where(on_low, high_rim, low_rim)
        incoming = swapped(outgoing.astype(jnp.bfloat16), "tile", which_bit).astype(outgoing.dtype)
        core_part = lax.slice_in_dim(grad_field, radius, radius + side_len, axis=axis_dim)
        filler_shape = list(incoming.shape)
        filler_shape[axis_dim] = side_len - radius
        filler = jnp.zeros(filler_shape, jnp.float32)
        grad_field = core_part + jnp.where(
            on_low,
            jnp.concatenate([filler, incoming], axis_dim),
            jnp.concatenate([incoming, filler], axis_dim),
        )
    return grad_field


def gather_pair(key_low, value_low):
    return (
        lax.all_gather(key_low, "tile", axis=1, tiled=True),
        lax.all_gather(value_low, "tile", axis=1, tiled=True),
    )


MESH = pl.DeviceIdType.MESH
VMEM_LIMIT = 60 << 20


def shift_rows(read_row, shifted, rows, side):
    def body(r, carry):
        line = read_row(r)
        for b in range(7):
            shifted[b, r] = line[b : b + side].reshape(side // 8, 8, 128)
        return carry

    lax.fori_loop(0, rows, body, 0, unroll=2)


def conv_kernel(group, flip, map_ref, tap_ref, out_ref, shifted, taps):
    rows, side = out_ref.shape[1], out_ref.shape[2]
    for k in range(49):
        tap = tap_ref[48 - k if flip else k].reshape(1, 128)
        taps[k] = jnp.broadcast_to(tap, (8, 128))
    shift_rows(lambda r: map_ref[0, r].astype(jnp.float32), shifted, rows + 6, side)

    def body(g, carry):
        first = g * group
        sums = [jnp.zeros((side // 8, 8, 128), jnp.float32) for _ in range(group)]
        for b in range(7):
            for r in range(group + 6):
                line = shifted[b, first + r]
                for k in range(group):
                    if 0 <= r - k < 7:
                        sums[k] = sums[k] + taps[(r - k) * 7 + b][None] * line
        for k in range(group):
            out_ref[0, first + k] = sums[k].reshape(side, 128)
        return carry

    lax.fori_loop(0, rows // group, body, 0)


def depthwise_seven(padded, tap_weights, flip):
    slots, rows, cols, channels = padded.shape
    side = rows - 6
    return pl.pallas_call(
        partial(conv_kernel, 4, flip),
        grid=(slots, channels // 128),
        in_specs=[
            pl.BlockSpec((1, rows, cols, 128), lambda s, c: (s, 0, 0, c)),
            pl.BlockSpec((49, 128), lambda s, c: (0, c)),
        ],
        out_specs=pl.BlockSpec((1, side, side, 128), lambda s, c: (s, 0, 0, c)),
        out_shape=jax.ShapeDtypeStruct((slots, side, side, channels), jnp.float32),
        scratch_shapes=[
            pltpu.VMEM((7, rows, side // 8, 8, 128), jnp.float32),
            pltpu.VMEM((49, 8, 128), jnp.float32),
        ],
        cost_estimate=pl.CostEstimate(
            flops=98 * slots * side * side * channels,
            bytes_accessed=8 * slots * side * side * channels,
            transcendentals=0,
        ),
        compiler_params=pltpu.CompilerParams(vmem_limit_bytes=VMEM_LIMIT),
        name="depthwise_seven",
    )(padded, tap_weights)


def tap_grad_kernel(group, map_ref, grad_ref, out_ref, shifted):
    rows, side = grad_ref.shape[1], grad_ref.shape[2]
    shift_rows(lambda r: map_ref[0, r].astype(jnp.float32), shifted, rows + 6, side)

    @pl.when(pl.program_id(1) == 0)
    def _():
        out_ref[...] = jnp.zeros_like(out_ref)

    for columns in ((0, 1, 2, 3), (4, 5, 6)):

        def body(g, sums):
            sums = [list(part) for part in sums]
            first = g * group
            lines = [
                grad_ref[0, first + k].astype(jnp.float32).reshape(side // 8, 8, 128)
                for k in range(group)
            ]
            for n, b in enumerate(columns):
                for r in range(group + 6):
                    line = shifted[b, first + r]
                    for k in range(group):
                        if 0 <= r - k < 7:
                            sums[r - k][n] = sums[r - k][n] + jnp.sum(line * lines[k], axis=0)
            return tuple(tuple(part) for part in sums)

        zero = jnp.zeros((8, 128), jnp.float32)
        sums = lax.fori_loop(
            0, rows // group, body, tuple(tuple(zero for _ in columns) for _ in range(7))
        )
        for a in range(7):
            for n, b in enumerate(columns):
                row = pl.ds(a * 7 + b, 1)
                out_ref[row, :] = out_ref[row, :] + jnp.sum(sums[a][n], axis=0, keepdims=True)


def tap_grad_seven(padded, grad):
    slots, rows, cols, channels = padded.shape
    side = rows - 6
    return pl.pallas_call(
        partial(tap_grad_kernel, 4),
        grid=(channels // 128, slots),
        in_specs=[
            pl.BlockSpec((1, rows, cols, 128), lambda c, s: (s, 0, 0, c)),
            pl.BlockSpec((1, side, side, 128), lambda c, s: (s, 0, 0, c)),
        ],
        out_specs=pl.BlockSpec((49, 128), lambda c, s: (0, c)),
        out_shape=jax.ShapeDtypeStruct((49, channels), jnp.float32),
        scratch_shapes=[pltpu.VMEM((7, rows, side // 8, 8, 128), jnp.float32)],
        cost_estimate=pl.CostEstimate(
            flops=98 * slots * side * side * channels,
            bytes_accessed=8 * slots * side * side * channels,
            transcendentals=0,
        ),
        compiler_params=pltpu.CompilerParams(vmem_limit_bytes=VMEM_LIMIT),
        name="tap_grad_seven",
    )(padded, grad)


PIECE_BYTES = 2_000_000
COPIES = 8
SMALL_ROWS = 512


def plan_pieces(shapes):
    pieces = []
    for g, (height, width) in enumerate(shapes):
        rows = height // 8
        count = max(1, round(height * width * 2 / PIECE_BYTES))
        while rows % (count * 32):
            count -= 1
        for p in range(count):
            pieces.append((g, p * (rows // count), rows // count))
    return pieces


def wide_sum(one, two):
    return one.astype(jnp.float32) + two.astype(jnp.float32)


def low_sum(one, two):
    return wide_sum(one, two).astype(jnp.bfloat16)


def row_loop(first, rows, step):
    def body(q, carry):
        step(pl.ds(pl.multiple_of(first + q * 16, 16), 16))
        return carry

    lax.fori_loop(0, rows // 16, body, 0)


def reduce_kernel(pieces, shapes, *refs):
    matrices = len(shapes)
    count = len(pieces)
    grads, small = refs[:matrices], refs[matrices]
    outs, small_out = refs[matrices + 1 : 2 * matrices + 1], refs[2 * matrices + 1]
    scratch = refs[2 * matrices + 2 :]
    own, half, quarter, eighth, pair, last = (
        scratch[k * count : (k + 1) * count] for k in range(6)
    )
    small_work, small_in, send_sem, recv_sem, own_sem, small_send, small_recv = scratch[6 * count :]
    img = lax.axis_index("img")
    tile = lax.axis_index("tile")
    core, x, y = img % 2, (img // 2) % 2, img // 4
    low, high = tile % 2, tile // 2
    to_core = (img + 1 - 2 * core, tile)
    to_x = (img + 2 - 4 * x, tile)
    to_y = (img + 4 - 8 * y, tile)
    to_low = (img, tile + 1 - 2 * low)
    to_high = (img, tile + 2 - 4 * high)
    barrier = pltpu.get_barrier_semaphore()
    for partner in (to_core, to_x, to_y, to_low, to_high):
        pl.semaphore_signal(barrier, inc=1, device_id=partner, device_id_type=MESH)
    pl.semaphore_wait(barrier, 5)
    started = []
    waiting = {}

    def send(source, target, sems, index, partner):
        copy = pltpu.make_async_remote_copy(
            src_ref=source,
            dst_ref=target,
            send_sem=sems[0].at[index],
            recv_sem=sems[1].at[index],
            device_id=partner,
            device_id_type=MESH,
        )
        copy.start()
        started.append(copy)
        return copy

    def send_piece(i, k, source, target, partner):
        return send(source, target, (send_sem, recv_sem), i * COPIES + k, partner)

    def over_core(i):
        g, first, rows = pieces[i]
        part = pl.ds(first, rows)
        copy = send_piece(i, 0, grads[g].at[:, :, 1 - core, part, :], half[i], to_core)
        local_copy = pltpu.make_async_copy(
            grads[g].at[:, :, core, part, :], own[i], own_sem.at[i]
        )
        local_copy.start()
        waiting[i] = (copy, local_copy)

    def over_first(i):
        g, first, rows = pieces[i]
        cut = rows // 2
        copy, local_copy = waiting[i]
        copy.wait_recv()
        local_copy.wait()
        for a in range(2):
            for b in range(2):

                def step(s, a=a, b=b):
                    half[i][a, b, s, :] = low_sum(half[i][a, b, s, :], own[i][a, b, s, :])

                row_loop(0, rows, step)
        top, bottom = pl.ds(0, cut), pl.ds(cut, cut)
        waiting[i] = (
            send_piece(i, 1, half[i].at[:, 1 - x, top, :], quarter[i].at[:, top, :], to_x),
            send_piece(i, 2, half[i].at[1 - y, :, bottom, :], quarter[i].at[:, bottom, :], to_y),
        )

    def over_second(i):
        g, first, rows = pieces[i]
        cut = rows // 2
        for copy in waiting[i]:
            copy.wait_recv()
        for a in range(2):

            def step_top(s, a=a):
                quarter[i][a, s, :] = low_sum(quarter[i][a, s, :], half[i][a, x, s, :])

            def step_bottom(s, a=a):
                quarter[i][a, s, :] = low_sum(quarter[i][a, s, :], half[i][y, a, s, :])

            row_loop(0, cut, step_top)
            row_loop(cut, cut, step_bottom)
        top, bottom = pl.ds(0, cut), pl.ds(cut, cut)
        waiting[i] = (
            send_piece(i, 3, quarter[i].at[1 - y, top, :], eighth[i].at[top, :], to_y),
            send_piece(i, 4, quarter[i].at[1 - x, bottom, :], eighth[i].at[bottom, :], to_x),
        )

    def lanes(start, size):
        return pl.ds(pl.multiple_of(start, 128), size)

    def over_third(i):
        g, first, rows = pieces[i]
        cut = rows // 2
        width = shapes[g][1] // 4
        for copy in waiting[i]:
            copy.wait_recv()

        def step_top(s):
            eighth[i][s, :] = low_sum(eighth[i][s, :], quarter[i][y, s, :])

        def step_bottom(s):
            eighth[i][s, :] = low_sum(eighth[i][s, :], quarter[i][x, s, :])

        row_loop(0, cut, step_top)
        row_loop(cut, cut, step_bottom)
        if width % 128 == 0:
            waiting[i] = tuple(
                send_piece(
                    i,
                    5 + q,
                    eighth[i].at[:, lanes((2 * q + 1 - low) * width, width)],
                    pair[i].at[:, pl.ds(q * width, width)],
                    to_low,
                )
                for q in range(2)
            )
        else:
            side = eighth[i].at[:, lanes((1 - high) * 2 * width, 2 * width)]
            waiting[i] = (send_piece(i, 5, side, pair[i], to_high),)

    def over_fourth(i):
        g, first, rows = pieces[i]
        width = shapes[g][1] // 4
        for copy in waiting[i]:
            copy.wait_recv()
        if width % 128 == 0:

            def step(s):
                for q in range(2):
                    at = slice(q * width, (q + 1) * width)
                    kept = eighth[i][s, lanes((2 * q + low) * width, width)]
                    pair[i][s, at] = low_sum(pair[i][s, at], kept)

            row_loop(0, rows, step)
            side = pair[i].at[:, lanes((1 - high) * width, width)]
            waiting[i] = (send_piece(i, 7, side, last[i], to_high),)
        else:

            def step(s):
                kept = eighth[i][s, lanes(high * 2 * width, 2 * width)]
                pair[i][s, :] = low_sum(pair[i][s, :], kept)

            row_loop(0, rows, step)
            waiting[i] = (send_piece(i, 7, pair[i], last[i], to_low),)

    def finish(i):
        g, first, rows = pieces[i]
        width = shapes[g][1] // 4
        for copy in waiting[i]:
            copy.wait_recv()

        def step(s):
            at = pl.ds(pl.multiple_of(s.start + first, 16), 16)
            if width % 128 == 0:
                kept = pair[i][s, lanes(high * width, width)]
                outs[g][at, :] = wide_sum(last[i][s, :], kept)
            else:
                both = wide_sum(last[i][s, :], pair[i][s, :])
                outs[g][at, :] = jnp.where(low == 0, both[:, :width], both[:, width:])

        row_loop(0, rows, step)

    halvings = ((to_core, core), (to_x, x), (to_y, y), (to_low, low), (to_high, high))
    total = small.shape[0]
    small_sems = (small_send, small_recv)
    place = {"start": 0, "size": total}

    def rows_at(start, size):
        return pl.ds(pl.multiple_of(start, 8), size)

    def small_step(k):
        if k == 0:
            small_work[...] = small[...]
        else:
            waiting["small"].wait_recv()
        if 1 <= k <= 5:
            size = place["size"]
            at = rows_at(place["start"], size)
            summed = small_work[at, :] + small_in[pl.ds(total - 2 * size, size), :]
            if k < 5:
                small_work[at, :] = summed
            else:
                small_out[at, :] = summed
        if k < 5:
            partner, bit = halvings[k]
            size = place["size"] // 2
            give = rows_at(place["start"] + (1 - bit) * size, size)
            waiting["small"] = send(
                small_work.at[give, :],
                small_in.at[pl.ds(total - 2 * size, size), :],
                small_sems,
                k,
                partner,
            )
            place["start"] = place["start"] + bit * size
            place["size"] = size
        elif k < 10:
            partner, bit = halvings[9 - k]
            if k > 5:
                before = halvings[10 - k][1]
                place["start"] = place["start"] - before * place["size"]
                place["size"] = place["size"] * 2
            mine = rows_at(place["start"], place["size"])
            waiting["small"] = send(
                small_out.at[mine, :], small_out.at[mine, :], small_sems, k, partner
            )

    stages = (over_core, over_first, over_second, over_third, over_fourth, finish)
    for step in range(count + 10):
        for k in range(len(stages) - 1, -1, -1):
            i = step - 2 * k
            if 0 <= i < count:
                stages[k](i)
        if step <= 10:
            small_step(step)
    for copy in started:
        copy.wait_send()


def reduce_matrices(grads, small):
    shapes = [grad.shape for grad in grads]
    pieces = plan_pieces(shapes)
    count = len(pieces)
    operands = [
        grad.reshape(2, 2, 2, grad.shape[0] // 8, grad.shape[1]) for grad in grads
    ]

    def buffers(shape_of):
        return [
            pltpu.VMEM(shape_of(rows, shapes[g][1]), jnp.bfloat16) for g, _, rows in pieces
        ]

    scratch = buffers(lambda rows, width: (2, 2, rows, width))
    scratch += buffers(lambda rows, width: (2, 2, rows, width))
    scratch += buffers(lambda rows, width: (2, rows, width))
    scratch += buffers(lambda rows, width: (rows, width))
    scratch += buffers(lambda rows, width: (rows, width // 2))
    scratch += buffers(
        lambda rows, width: (rows, width // 4 if width % 512 == 0 else width // 2)
    )
    scratch += [
        pltpu.VMEM(small.shape, jnp.float32),
        pltpu.VMEM(small.shape, jnp.float32),
        pltpu.SemaphoreType.DMA((count * COPIES,)),
        pltpu.SemaphoreType.DMA((count * COPIES,)),
        pltpu.SemaphoreType.DMA((count,)),
        pltpu.SemaphoreType.DMA((10,)),
        pltpu.SemaphoreType.DMA((10,)),
    ]
    in_vmem = pl.BlockSpec(memory_space=pltpu.VMEM)
    results = pl.pallas_call(
        partial(reduce_kernel, pieces, shapes),
        in_specs=[pl.BlockSpec(memory_space=pl.ANY)] * len(grads) + [in_vmem],
        out_specs=[in_vmem] * (len(grads) + 1),
        out_shape=[
            jax.ShapeDtypeStruct((height // 8, width // 4), jnp.float32)
            for height, width in shapes
        ]
        + [jax.ShapeDtypeStruct(small.shape, jnp.float32)],
        scratch_shapes=scratch,
        compiler_params=pltpu.CompilerParams(
            collective_id=0, has_side_effects=True, vmem_limit_bytes=VMEM_LIMIT
        ),
        name="reduce_matrices",
    )(*operands, small)
    return results[:-1], results[-1]


def sum_everywhere(grads, smalls):
    if lax.axis_size("img") == 8 and lax.axis_size("tile") == 4:
        flat = jnp.concatenate([part.reshape(-1) for part in smalls])
        flat = jnp.pad(flat, (0, SMALL_ROWS * 128 - flat.size)).reshape(SMALL_ROWS, 128)
        sums, small = reduce_matrices(grads, flat)
        flat = small.reshape(-1)
        parts, first = [], 0
        for part in smalls:
            parts.append(flat[first : first + part.size].reshape(part.shape))
            first += part.size
        return sums, parts
    sums = []
    for grad in grads:
        part = lax.psum_scatter(grad, "img", scatter_dimension=0, tiled=True)
        part = lax.psum_scatter(part, "tile", scatter_dimension=1, tiled=True)
        sums.append(part.astype(jnp.float32))
    return sums, lax.psum(tuple(smalls), ("img", "tile"))


def local(
    vit_in,
    map_in,
    group_images,
    vit_grad_out,
    map_grad_out,
    w_query,
    w_key,
    w_value,
    w_out,
    w_up,
    w_down,
    w_expand,
    w_shrink,
    w_adapt,
    gain_attn,
    gain_mlp,
    gain_conv,
    dw_large,
    dw_small,
    gate_low,
    gate_high,
):
    slot_count = vit_in.shape[0]
    tok_side = math.isqrt(vit_in.shape[2])
    pix_side = math.isqrt(map_in.shape[2])
    channels = map_in.shape[3]
    model_width = vit_in.shape[3]
    live_mask = (
        (jnp.arange(slot_count, dtype=jnp.int32) < group_images[0])
        .astype(jnp.float32)
        .reshape(slot_count, 1, 1)
    )
    live_cells = live_mask.reshape(slot_count, 1, 1, 1)
    tokens = vit_in[:, 0].astype(jnp.float32)
    normed_one, norm_one_pull = jax.vjp(layer_norm, tokens, gain_attn.astype(jnp.float32))
    normed_one_low = normed_one.astype(jnp.bfloat16)
    query_low = project(normed_one_low, w_query).astype(jnp.bfloat16)
    key_low = project(normed_one_low, w_key).astype(jnp.bfloat16)
    value_low = project(normed_one_low, w_value).astype(jnp.bfloat16)
    key_all, value_all = gather_pair(key_low, value_low)
    scores = attention_scores(query_low, key_all)
    row_max = jnp.max(scores, axis=-1, keepdims=True)
    shifted = jnp.exp(scores - row_max)
    row_total = jnp.sum(shifted, axis=-1, keepdims=True)
    softmax_low = (shifted / row_total).astype(jnp.bfloat16)
    log_total = row_max + jnp.log(row_total)
    mixed_low = (
        jnp.einsum(
            "shqk,skhd->sqhd",
            softmax_low,
            split_heads(value_all),
            preferred_element_type=jnp.float32,
        )
        .reshape(slot_count, -1, model_width)
        .astype(jnp.bfloat16)
    )
    residual_one = tokens + project(mixed_low, w_out)
    normed_two, norm_two_pull = jax.vjp(layer_norm, residual_one, gain_mlp.astype(jnp.float32))
    normed_two_low = normed_two.astype(jnp.bfloat16)
    acted_low, acted_slope = gelu_pair(project(normed_two_low, w_up))
    residual_two = residual_one + project(acted_low, w_down)
    map_low = map_in[:, 0].reshape(slot_count, pix_side, pix_side, channels)
    padded_map = add_rims(map_low, 3)
    large_taps = dw_large.astype(jnp.float32)
    spread_map = depthwise_seven(padded_map, large_taps, False)
    conv_norm, conv_norm_pull = jax.vjp(layer_norm, spread_map, gain_conv.astype(jnp.float32))
    conv_norm_low = conv_norm.astype(jnp.bfloat16)
    wide_low, wide_slope = gelu_pair(project(conv_norm_low, w_expand))
    map_after = map_low.astype(jnp.float32) + project(wide_low, w_shrink)
    pooled, pool_pull = jax.vjp(pool_pairs, map_after)
    pooled_low = pooled.astype(jnp.bfloat16)
    adapted_low = project(pooled_low, w_adapt).astype(jnp.bfloat16)
    padded_small = add_rims(adapted_low, 1).astype(jnp.float32)
    merged_map, merged_pull = jax.vjp(
        partial(depthwise, radius=1, margin=0), padded_small, dw_small.astype(jnp.float32)
    )
    merged_tokens = merged_map.reshape(slot_count, tok_side * tok_side, model_width)
    vit_after, merging_pull = jax.vjp(
        merging,
        residual_two,
        merged_tokens,
        gate_low.astype(jnp.float32),
        gate_high.astype(jnp.float32),
    )
    vit_cotangent = vit_grad_out[:, 0].astype(jnp.float32) * live_mask
    map_cotangent = (
        map_grad_out[:, 0].astype(jnp.float32).reshape(slot_count, pix_side, pix_side, channels)
        * live_cells
    )
    grad_residual_two, grad_merged, gate_low_grad, gate_high_grad = merging_pull(vit_cotangent)
    grad_padded_small, dw_small_grad = merged_pull(
        grad_merged.reshape(slot_count, tok_side, tok_side, model_width)
    )
    grad_adapted_low = return_rims(grad_padded_small, 1).astype(jnp.bfloat16)
    w_adapt_grad = outer_sum(pooled_low, grad_adapted_low)
    grad_map_after = map_cotangent + pool_pull(project_back(grad_adapted_low, w_adapt))[0]
    grad_conv_low = grad_map_after.astype(jnp.bfloat16)
    w_shrink_grad = outer_sum(wide_low, grad_conv_low)
    grad_wide_low = (project_back(grad_conv_low, w_shrink) * wide_slope).astype(jnp.bfloat16)
    w_expand_grad = outer_sum(conv_norm_low, grad_wide_low)
    grad_spread, gain_conv_grad = conv_norm_pull(project_back(grad_wide_low, w_expand))
    dw_large_grad = tap_grad_seven(padded_map, grad_spread)
    padded_grad = add_rims(grad_spread.astype(jnp.bfloat16), 3)
    map_in_grad = (grad_map_after + depthwise_seven(padded_grad, large_taps, True)).astype(
        jnp.bfloat16
    )
    grad_mlp_low = grad_residual_two.astype(jnp.bfloat16)
    w_down_grad = outer_sum(acted_low, grad_mlp_low)
    grad_up_low = (project_back(grad_mlp_low, w_down) * acted_slope).astype(jnp.bfloat16)
    w_up_grad = outer_sum(normed_two_low, grad_up_low)
    grad_norm_part, gain_mlp_grad = norm_two_pull(project_back(grad_up_low, w_up))
    grad_residual_one = grad_residual_two + grad_norm_part
    grad_attn_low = grad_residual_one.astype(jnp.bfloat16)
    w_out_grad = outer_sum(mixed_low, grad_attn_low)
    grad_mixed_low = project_back(grad_attn_low, w_out).astype(jnp.bfloat16)
    key_back, value_back = (key_all, value_all)
    softmax_again = jnp.exp(attention_scores(query_low, key_back) - log_total)
    softmax_again_low = softmax_again.astype(jnp.bfloat16)
    grad_mixed_heads = split_heads(grad_mixed_low)
    grad_softmax = jnp.einsum(
        "sqhd,skhd->shqk",
        grad_mixed_heads,
        split_heads(value_back),
        preferred_element_type=jnp.float32,
    )
    row_dot = jnp.sum(softmax_again * grad_softmax, axis=-1, keepdims=True)
    grad_scores_low = (softmax_again * (grad_softmax - row_dot)).astype(jnp.bfloat16)
    scale = HDIM ** (-0.5)
    grad_query_low = (
        (
            jnp.einsum(
                "shqk,skhd->sqhd",
                grad_scores_low,
                split_heads(key_back),
                preferred_element_type=jnp.float32,
            )
            * scale
        )
        .reshape(slot_count, -1, model_width)
        .astype(jnp.bfloat16)
    )
    grad_key_term = (
        jnp.einsum(
            "shqk,sqhd->skhd",
            grad_scores_low,
            split_heads(query_low),
            preferred_element_type=jnp.float32,
        )
        * scale
    ).reshape(slot_count, -1, model_width)
    grad_value_term = jnp.einsum(
        "shqk,sqhd->skhd", softmax_again_low, grad_mixed_heads, preferred_element_type=jnp.float32
    ).reshape(slot_count, -1, model_width)
    grad_key_sum, grad_value_sum = (
        lax.psum_scatter(
            grad_key_term.astype(jnp.bfloat16), "tile", scatter_dimension=1, tiled=True
        ).astype(jnp.float32),
        lax.psum_scatter(
            grad_value_term.astype(jnp.bfloat16), "tile", scatter_dimension=1, tiled=True
        ).astype(jnp.float32),
    )
    grad_key_low = grad_key_sum.astype(jnp.bfloat16)
    grad_value_low = grad_value_sum.astype(jnp.bfloat16)
    w_query_grad = outer_sum(normed_one_low, grad_query_low)
    w_key_grad = outer_sum(normed_one_low, grad_key_low)
    w_value_grad = outer_sum(normed_one_low, grad_value_low)
    grad_normed_one = (
        project_back(grad_query_low, w_query)
        + project_back(grad_key_low, w_key)
        + project_back(grad_value_low, w_value)
    )
    grad_token_part, gain_attn_grad = norm_one_pull(grad_normed_one)
    vit_in_grad = (grad_residual_one + grad_token_part).astype(jnp.bfloat16)
    matrix_sums, small_sums = sum_everywhere(
        (
            w_up_grad,
            w_down_grad,
            w_adapt_grad,
            w_expand_grad,
            w_shrink_grad,
            w_query_grad,
            w_key_grad,
            w_value_grad,
            w_out_grad,
        ),
        (
            gain_attn_grad,
            gain_mlp_grad,
            gain_conv_grad,
            dw_large_grad,
            dw_small_grad,
            gate_low_grad,
            gate_high_grad,
        ),
    )
    matrix_sums = (
        matrix_sums[5],
        matrix_sums[6],
        matrix_sums[7],
        matrix_sums[8],
        matrix_sums[0],
        matrix_sums[1],
        matrix_sums[3],
        matrix_sums[4],
        matrix_sums[2],
    )
    vit_result = (vit_after * live_mask).astype(jnp.bfloat16)[:, None]
    map_result = (
        (map_after * live_cells)
        .reshape(slot_count, pix_side * pix_side, channels)
        .astype(jnp.bfloat16)[:, None]
    )
    return (
        vit_result,
        map_result,
        vit_in_grad[:, None],
        map_in_grad.reshape(slot_count, pix_side * pix_side, channels)[:, None],
        matrix_sums[0],
        matrix_sums[1],
        matrix_sums[2],
        matrix_sums[3],
        matrix_sums[4],
        matrix_sums[5],
        matrix_sums[6],
        matrix_sums[7],
        matrix_sums[8],
        small_sums[0],
        small_sums[1],
        small_sums[2],
        small_sums[3],
        small_sums[4],
        small_sums[5],
        small_sums[6],
    )


def solution(mesh):
    in_specs = (
        P("img", "tile", None, None),
        P("img", "tile", None, None),
        P("img"),
        P("img", "tile", None, None),
        P("img", "tile", None, None),
        P(),
        P(),
        P(),
        P(),
        P(),
        P(),
        P(),
        P(),
        P(),
        P(),
        P(),
        P(),
        P(),
        P(),
        P(),
        P(),
    )
    out_specs = (
        P("img", "tile", None, None),
        P("img", "tile", None, None),
        P("img", "tile", None, None),
        P("img", "tile", None, None),
        P("img", "tile"),
        P("img", "tile"),
        P("img", "tile"),
        P("img", "tile"),
        P("img", "tile"),
        P("img", "tile"),
        P("img", "tile"),
        P("img", "tile"),
        P("img", "tile"),
        P(),
        P(),
        P(),
        P(),
        P(),
        P(),
        P(),
    )
    return jax.shard_map(local, mesh=mesh, in_specs=in_specs, out_specs=out_specs, check_vma=False)
```

```python
from functools import partial
import math

import jax
import jax.numpy as jnp
from jax import lax
from jax.experimental import pallas as pl
from jax.experimental.pallas import tpu as pltpu
from jax.sharding import PartitionSpec as P

HEADS = 12
HDIM = 64


highest = lax.Precision.HIGHEST


def swapped(array, axis, bit):
    return lax.ppermute(array, axis, [(i, i ^ 1 << bit) for i in range(lax.axis_size(axis))])


def layer_norm(values, gain_row):
    centre = values - jnp.mean(values, axis=-1, keepdims=True)
    spread = jnp.mean(centre * centre, axis=-1, keepdims=True)
    return centre * lax.rsqrt(spread + 1e-06) * gain_row


def gelu_exact(values):
    return 0.5 * values * (1.0 + lax.erf(values * 0.7071067811865476))


def gelu_pair(values):
    spread = 0.5 * (1.0 + lax.erf(values * 0.7071067811865476))
    bell = jnp.exp(-0.5 * values * values) * 0.3989422804014327
    return (values * spread).astype(jnp.bfloat16), (spread + values * bell).astype(jnp.bfloat16)


def depthwise(field_map, tap_weights, radius, margin):
    kernel_side = 2 * radius + 1
    channels = tap_weights.shape[1]
    kernel = tap_weights.reshape(kernel_side, kernel_side, 1, channels)
    return lax.conv_general_dilated(
        field_map,
        kernel,
        (1, 1),
        ((margin, margin), (margin, margin)),
        dimension_numbers=("NHWC", "HWIO", "NHWC"),
        feature_group_count=channels,
        precision=highest,
    )


def pool_pairs(field_map):
    slot_count, row_count, col_count, channels = field_map.shape
    return jnp.mean(
        field_map.reshape(slot_count, row_count // 2, 2, col_count // 2, 2, channels), axis=(2, 4)
    )


def merging(residual_two, merged_tokens, gate_low, gate_high):
    gate_logit = jnp.sum(residual_two * gate_low, axis=-1, keepdims=True) + jnp.sum(
        merged_tokens * gate_high, axis=-1, keepdims=True
    )
    gate_value = 1.0 / (1.0 + jnp.exp(-gate_logit))
    return residual_two + gate_value * merged_tokens


def project(left_side, right_side):
    return jnp.einsum("...i,ij->...j", left_side, right_side, preferred_element_type=jnp.float32)


def project_back(left_side, right_side):
    return jnp.einsum("...j,ij->...i", left_side, right_side, preferred_element_type=jnp.float32)


def outer_sum(left_side, right_side):
    flat_left = left_side.reshape(-1, left_side.shape[-1])
    flat_right = right_side.reshape(-1, right_side.shape[-1])
    return lax.dot_general(
        flat_left, flat_right, (((0,), (0,)), ((), ())), preferred_element_type=jnp.float32
    ).astype(jnp.bfloat16)


def split_heads(rows_low):
    return rows_low.reshape(rows_low.shape[0], rows_low.shape[1], HEADS, HDIM)


def attention_scores(query_low, key_all):
    return jnp.einsum(
        "sqhd,skhd->shqk",
        split_heads(query_low),
        split_heads(key_all),
        preferred_element_type=jnp.float32,
    ) * HDIM ** (-0.5)


def add_rims(tile_field, radius):
    tile_place = lax.axis_index("tile")
    for which_bit in range(2):
        axis_dim = 2 - which_bit
        on_low = tile_place >> which_bit & 1 == 0
        side_len = tile_field.shape[axis_dim]
        upper_rim = lax.slice_in_dim(tile_field, side_len - radius, side_len, axis=axis_dim)
        lower_rim = lax.slice_in_dim(tile_field, 0, radius, axis=axis_dim)
        outgoing = jnp.where(on_low, upper_rim, lower_rim)
        incoming = swapped(outgoing, "tile", which_bit)
        blank_rim = jnp.zeros_like(incoming)
        tile_field = jnp.where(
            on_low,
            jnp.concatenate([blank_rim, tile_field, incoming], axis_dim),
            jnp.concatenate([incoming, tile_field, blank_rim], axis_dim),
        )
    return tile_field


def return_rims(grad_field, radius):
    tile_place = lax.axis_index("tile")
    for which_bit in (1, 0):
        axis_dim = 2 - which_bit
        on_low = tile_place >> which_bit & 1 == 0
        total_len = grad_field.shape[axis_dim]
        side_len = total_len - 2 * radius
        high_rim = lax.slice_in_dim(grad_field, total_len - radius, total_len, axis=axis_dim)
        low_rim = lax.slice_in_dim(grad_field, 0, radius, axis=axis_dim)
        outgoing = jnp.where(on_low, high_rim, low_rim)
        incoming = swapped(outgoing.astype(jnp.bfloat16), "tile", which_bit).astype(outgoing.dtype)
        core_part = lax.slice_in_dim(grad_field, radius, radius + side_len, axis=axis_dim)
        filler_shape = list(incoming.shape)
        filler_shape[axis_dim] = side_len - radius
        filler = jnp.zeros(filler_shape, jnp.float32)
        grad_field = core_part + jnp.where(
            on_low,
            jnp.concatenate([filler, incoming], axis_dim),
            jnp.concatenate([incoming, filler], axis_dim),
        )
    return grad_field


MESH = pl.DeviceIdType.MESH
VMEM_LIMIT = 62 << 20
COPIES = 8
SMALL_ROWS = 512
RIM_ROWS = 80
CORNER_ROWS = 16


def contract(left, right, left_axis, right_axis):
    return lax.dot_general(
        left,
        right,
        (((left_axis,), (right_axis,)), ((), ())),
        preferred_element_type=jnp.float32,
    )


def wide_sum(one, two):
    return one.astype(jnp.float32) + two.astype(jnp.float32)


def low_sum(one, two):
    return wide_sum(one, two).astype(jnp.bfloat16)


def row_loop(first, rows, width, step):
    count = rows // 16
    while count > 1 and (count * 16 * width > 65536 or rows % (count * 16)):
        count -= 1
    chunk = count * 16

    def body(q, carry):
        step(pl.ds(pl.multiple_of(first + q * chunk, 16), chunk))
        return carry

    if rows == chunk:
        body(0, 0)
    else:
        lax.fori_loop(0, rows // chunk, body, 0)


def lanes(start, size):
    return pl.ds(pl.multiple_of(start, 128), size)


class Place:
    def __init__(self):
        img = lax.axis_index("img")
        tile = lax.axis_index("tile")
        self.core, self.x, self.y = img % 2, (img // 2) % 2, img // 4
        self.low, self.high = tile % 2, tile // 2
        self.to_core = (img + 1 - 2 * self.core, tile)
        self.to_x = (img + 2 - 4 * self.x, tile)
        self.to_y = (img + 4 - 8 * self.y, tile)
        self.to_low = (img, tile + 1 - 2 * self.low)
        self.to_high = (img, tile + 2 - 4 * self.high)
        self.to_across = (img, 3 - tile)


def greet(partners):
    barrier = pltpu.get_barrier_semaphore()
    for partner in partners:
        pl.semaphore_signal(barrier, inc=1, device_id=partner, device_id_type=MESH)
    pl.semaphore_wait(barrier, len(partners))


def remote(source, target, send_sem, recv_sem, partner):
    return pltpu.make_async_remote_copy(
        src_ref=source,
        dst_ref=target,
        send_sem=send_sem,
        recv_sem=recv_sem,
        device_id=partner,
        device_id_type=MESH,
    )


def plan_pieces(shapes, piece_bytes):
    pieces = []
    for g, (height, width) in enumerate(shapes):
        rows = height // 8
        count = max(1, round(height * width * 2 / piece_bytes))
        while rows % (count * 32):
            count -= 1
        for p in range(count):
            pieces.append((g, p * (rows // count), rows // count))
    return pieces


def halving_scratch(shapes, pieces):
    count = len(pieces)

    def buffers(shape_of):
        return [
            pltpu.VMEM(shape_of(rows, shapes[g][1]), jnp.bfloat16) for g, _, rows in pieces
        ]

    scratch = buffers(lambda rows, width: (2, 2, rows, width))
    scratch += buffers(lambda rows, width: (2, 2, rows, width))
    scratch += buffers(lambda rows, width: (2, rows, width))
    scratch += buffers(lambda rows, width: (rows, width))
    scratch += buffers(lambda rows, width: (rows, width // 2))
    scratch += buffers(
        lambda rows, width: (rows, width // 4 if width % 512 == 0 else width // 2)
    )
    scratch += [
        pltpu.SemaphoreType.DMA((count * COPIES,)),
        pltpu.SemaphoreType.DMA((count * COPIES,)),
        pltpu.SemaphoreType.DMA((count,)),
    ]
    return scratch


class Halving:
    def __init__(self, place, shapes, pieces, grads, outs, scratch):
        count = len(pieces)
        self.place, self.shapes, self.pieces = place, shapes, pieces
        self.grads, self.outs = grads, outs
        self.own, self.half, self.quarter, self.eighth, self.pair, self.last = (
            scratch[k * count : (k + 1) * count] for k in range(6)
        )
        self.send_sem, self.recv_sem, self.own_sem = scratch[6 * count :]
        self.stages = (
            self.over_core,
            self.over_first,
            self.over_second,
            self.over_third,
            self.over_fourth,
            self.finish,
        )

    def narrow(self, i):
        return self.shapes[self.pieces[i][0]][1] % 512 != 0

    def copy(self, i, k):
        place = self.place
        g, first, rows = self.pieces[i]
        width = self.shapes[g][1] // 4
        half, quarter, eighth = self.half[i], self.quarter[i], self.eighth[i]
        pair, last = self.pair[i], self.last[i]
        part, cut = pl.ds(first, rows), rows // 2
        top, bottom = pl.ds(0, cut), pl.ds(cut, cut)
        if k == 0:
            ends = (self.grads[g].at[:, :, 1 - place.core, part, :], half, place.to_core)
        elif k == 1:
            ends = (half.at[:, 1 - place.x, top, :], quarter.at[:, top, :], place.to_x)
        elif k == 2:
            ends = (half.at[1 - place.y, :, bottom, :], quarter.at[:, bottom, :], place.to_y)
        elif k == 3:
            ends = (quarter.at[1 - place.y, top, :], eighth.at[top, :], place.to_y)
        elif k == 4:
            ends = (quarter.at[1 - place.x, bottom, :], eighth.at[bottom, :], place.to_x)
        elif k < 7 and not self.narrow(i):
            q = k - 5
            side = eighth.at[:, lanes((2 * q + 1 - place.low) * width, width)]
            ends = (side, pair.at[:, pl.ds(q * width, width)], place.to_low)
        elif k == 5:
            side = eighth.at[:, lanes((1 - place.high) * 2 * width, 2 * width)]
            ends = (side, pair, place.to_high)
        elif not self.narrow(i):
            ends = (pair.at[:, lanes((1 - place.high) * width, width)], last, place.to_high)
        else:
            ends = (pair, last, place.to_low)
        at = i * COPIES + k
        return remote(ends[0], ends[1], self.send_sem.at[at], self.recv_sem.at[at], ends[2])

    def own_copy(self, i):
        g, first, rows = self.pieces[i]
        mine = self.grads[g].at[:, :, self.place.core, pl.ds(first, rows), :]
        return pltpu.make_async_copy(mine, self.own[i], self.own_sem.at[i])

    def copies(self, i):
        return (0, 1, 2, 3, 4, 5, 7) if self.narrow(i) else (0, 1, 2, 3, 4, 5, 6, 7)

    def over_core(self, i):
        self.copy(i, 0).start()
        self.own_copy(i).start()

    def over_first(self, i):
        rows = self.pieces[i][2]
        half, own = self.half[i], self.own[i]
        self.copy(i, 0).wait_recv()
        self.own_copy(i).wait()
        for a in range(2):
            for b in range(2):

                def step(s, a=a, b=b):
                    half[a, b, s, :] = low_sum(half[a, b, s, :], own[a, b, s, :])

                row_loop(0, rows, half.shape[-1], step)
        self.copy(i, 1).start()
        self.copy(i, 2).start()

    def over_second(self, i):
        cut = self.pieces[i][2] // 2
        place, half, quarter = self.place, self.half[i], self.quarter[i]
        self.copy(i, 1).wait_recv()
        self.copy(i, 2).wait_recv()
        for a in range(2):

            def step_top(s, a=a):
                quarter[a, s, :] = low_sum(quarter[a, s, :], half[a, place.x, s, :])

            def step_bottom(s, a=a):
                quarter[a, s, :] = low_sum(quarter[a, s, :], half[place.y, a, s, :])

            row_loop(0, cut, quarter.shape[-1], step_top)
            row_loop(cut, cut, quarter.shape[-1], step_bottom)
        self.copy(i, 3).start()
        self.copy(i, 4).start()

    def over_third(self, i):
        cut = self.pieces[i][2] // 2
        place, quarter, eighth = self.place, self.quarter[i], self.eighth[i]
        self.copy(i, 3).wait_recv()
        self.copy(i, 4).wait_recv()

        def step_top(s):
            eighth[s, :] = low_sum(eighth[s, :], quarter[place.y, s, :])

        def step_bottom(s):
            eighth[s, :] = low_sum(eighth[s, :], quarter[place.x, s, :])

        row_loop(0, cut, eighth.shape[-1], step_top)
        row_loop(cut, cut, eighth.shape[-1], step_bottom)
        self.copy(i, 5).start()
        if not self.narrow(i):
            self.copy(i, 6).start()

    def over_fourth(self, i):
        g, _, rows = self.pieces[i]
        width = self.shapes[g][1] // 4
        place, eighth, pair = self.place, self.eighth[i], self.pair[i]
        self.copy(i, 5).wait_recv()
        if self.narrow(i):

            def step(s):
                kept = eighth[s, lanes(place.high * 2 * width, 2 * width)]
                pair[s, :] = low_sum(pair[s, :], kept)

        else:
            self.copy(i, 6).wait_recv()

            def step(s):
                for q in range(2):
                    at = slice(q * width, (q + 1) * width)
                    kept = eighth[s, lanes((2 * q + place.low) * width, width)]
                    pair[s, at] = low_sum(pair[s, at], kept)

        row_loop(0, rows, pair.shape[-1], step)
        self.copy(i, 7).start()

    def finish(self, i):
        g, first, rows = self.pieces[i]
        width = self.shapes[g][1] // 4
        place, pair, last, out = self.place, self.pair[i], self.last[i], self.outs[g]
        self.copy(i, 7).wait_recv()

        def step(s):
            at = pl.ds(pl.multiple_of(s.start + first, 16), s.size)
            if self.narrow(i):
                both = wide_sum(last[s, :], pair[s, :])
                out[at, :] = jnp.where(place.low == 0, both[:, :width], both[:, width:])
            else:
                kept = pair[s, lanes(place.high * width, width)]
                out[at, :] = wide_sum(last[s, :], kept)

        row_loop(0, rows, pair.shape[-1], step)

    def wait_sends(self):
        for i in range(len(self.pieces)):
            for k in self.copies(i):
                self.copy(i, k).wait_send()


def halving_operands(grads):
    return [grad.reshape(2, 2, 2, grad.shape[0] // 8, grad.shape[1]) for grad in grads]


def halving_outputs(shapes):
    return [
        jax.ShapeDtypeStruct((height // 8, width // 4), jnp.float32) for height, width in shapes
    ]


def whole_block(shape):
    return pl.BlockSpec(shape, lambda *_: (0,) * len(shape))


def fixed_block(shape):
    return pl.BlockSpec(shape, lambda *_: (0,) * len(shape), pipeline_mode=pl.Buffered(1))


def rim_copies(place, source, rim, corner, rim_in, row_in, corner_in, sems):
    cells = source.shape[1]
    start = pl.multiple_of((1 - place.high) * (cells - RIM_ROWS), 16)
    return (
        remote(rim, rim_in, sems.at[0], sems.at[1], place.to_low),
        remote(
            source.at[:, pl.ds(start, RIM_ROWS), :], row_in, sems.at[2], sems.at[3], place.to_high
        ),
        remote(corner, corner_in, sems.at[4], sems.at[5], place.to_across),
    )


def mlp_back_kernel(shapes, pieces, plan, *refs):
    matrices = len(shapes)
    count = len(pieces)
    grad_low, norm_low, wide, slope, w_shrink, w_expand, unit, scale, gain = refs[:9]
    grads = refs[9 : 9 + matrices]
    refs = refs[9 + matrices :]
    shrink_out, expand_out, dz_out, gain_out = refs[:4]
    outs = refs[4 : 4 + matrices]
    refs = refs[4 + matrices :]
    halving_refs = refs[: 6 * count + 3]
    refs = refs[6 * count + 3 :]
    norm_turned, back, dz, out_sem = refs[:4]
    buffers, result_buffers, in_sems, result_sems = refs[4:8], refs[8:10], refs[10], refs[11]
    place = Place()
    halving = Halving(place, shapes, pieces, grads, outs, halving_refs)
    steps = plan["steps"]
    j = pl.program_id(0)

    def slot(n):
        for i, k in plan["slots"].get(n, ()):
            halving.stages[k](i)

    def slots(odd):
        for n in range(steps):
            if plan["slots"].get(2 * n + odd):
                pl.when(j == n)(partial(slot, 2 * n + odd))

    width = plan["width"]

    def fetches(n):
        slot_, at = n % 2, lanes(n * width, width)
        parts = (wide.at[:, at], slope.at[:, at], w_shrink.at[at, :], w_expand.at[:, at])
        return [
            pltpu.make_async_copy(part, buffers[k].at[slot_], in_sems.at[slot_ * 4 + k])
            for k, part in enumerate(parts)
        ]

    def stores(n):
        slot_, at = n % 2, lanes(n * width, width)
        targets = (shrink_out.at[at, :], expand_out.at[:, at])
        return [
            pltpu.make_async_copy(
                result_buffers[k].at[slot_], target, result_sems.at[slot_ * 2 + k]
            )
            for k, target in enumerate(targets)
        ]

    @pl.when(j == 0)
    def _():
        for copy in fetches(0):
            copy.start(priority=1)
        greet(
            (
                place.to_core,
                place.to_x,
                place.to_y,
                place.to_low,
                place.to_high,
            )
        )

    @pl.when(j + 1 < steps)
    def _():
        for copy in fetches(j + 1):
            copy.start(priority=1)

    slots(0)

    @pl.when(j == 0)
    def _():
        norm_turned[...] = norm_low[...].T

    for copy in fetches(j):
        copy.wait()

    @pl.when(j >= 2)
    def _():
        for copy in stores(j - 2):
            copy.wait()

    now = j % 2
    grad_wide = contract(grad_low[...], buffers[2][now], 1, 1)
    grad_wide = (grad_wide * buffers[1][now].astype(jnp.float32)).astype(jnp.bfloat16)
    turned = contract(buffers[0][now], grad_low[...], 0, 0)
    result_buffers[0][now] = turned.astype(jnp.bfloat16)
    slots(1)
    turned = contract(norm_turned[...], grad_wide, 1, 0)
    result_buffers[1][now] = turned.astype(jnp.bfloat16)
    term = contract(grad_wide, buffers[3][now], 1, 1)
    for copy in stores(j):
        copy.start(priority=1)

    @pl.when(j == 0)
    def _():
        back[...] = term

    @pl.when(j > 0)
    def _():
        back[...] = back[...] + term

    @pl.when(j == steps - 1)
    def _():
        gain_row = gain[...]
        chunk = 48

        def body(q, sums):
            at = pl.ds(pl.multiple_of(q * chunk, 16), chunk)
            grad = back[at, :]
            n = unit[at, :].astype(jnp.float32)
            t = grad * gain_row
            mean_t = jnp.mean(t, axis=-1, keepdims=True)
            mean_tn = jnp.mean(t * n, axis=-1, keepdims=True)
            dz[at, :] = (scale[at, :] * (t - mean_t - n * mean_tn)).astype(jnp.bfloat16)
            return sums + jnp.sum((grad * n).reshape(chunk // 8, 8, -1), axis=0)

        sums = jnp.zeros((8, dz.shape[1]), jnp.float32)
        sums = lax.fori_loop(0, dz.shape[0] // chunk, body, sums)
        gain_out[...] = jnp.sum(sums, axis=0, keepdims=True)
        back_copy = pltpu.make_async_copy(dz, dz_out, out_sem)
        back_copy.start()
        for n in range(2 * steps, plan["last"] + 1):
            slot(n)
        back_copy.wait()
        for n in (steps - 2, steps - 1):
            for copy in stores(n):
                copy.wait()
        halving.wait_sends()


def spread_plan(count, steps, first, second, rest):
    slots = {0: [(i, 0) for i in range(count)]}
    last = 0
    for i in range(count):
        at = [int(first[0] + first[1] * i), int(second[0] + second[1] * i)]
        at += [at[1] + r for r in rest]
        for k, n in enumerate(at):
            slots.setdefault(n, []).append((i, k + 1))
        last = max(last, at[-1])
    for n in slots:
        slots[n].sort(key=lambda item: (-item[1], item[0]))
    return {"slots": slots, "last": last, "steps": steps}


def map_mlp_back(
    grad_low, norm_low, wide, slope, w_shrink, w_expand, unit, scale, gain, grads
):
    tokens, channels = grad_low.shape
    hidden = w_shrink.shape[0]
    width = 512
    steps = hidden // width
    shapes = [grad.shape for grad in grads]
    pieces = plan_pieces(shapes, 1_600_000)
    plan = spread_plan(len(pieces), steps, (1, 1.0), (4, 1.0), (2, 4, 6))
    plan["width"] = width
    low = jnp.bfloat16
    any_space = pl.BlockSpec(memory_space=pl.ANY)
    results = pl.pallas_call(
        partial(mlp_back_kernel, shapes, pieces, plan),
        grid=(steps,),
        in_specs=[
            fixed_block((tokens, channels)),
            fixed_block((tokens, channels)),
            any_space,
            any_space,
            any_space,
            any_space,
            fixed_block((tokens, channels)),
            fixed_block((tokens, 1)),
            fixed_block((1, channels)),
        ]
        + [any_space] * len(grads),
        out_specs=[
            any_space,
            any_space,
            any_space,
            whole_block((1, channels)),
        ]
        + [whole_block(item.shape) for item in halving_outputs(shapes)],
        out_shape=[
            jax.ShapeDtypeStruct((hidden, channels), low),
            jax.ShapeDtypeStruct((channels, hidden), low),
            jax.ShapeDtypeStruct((tokens, channels), low),
            jax.ShapeDtypeStruct((1, channels), jnp.float32),
        ]
        + halving_outputs(shapes),
        scratch_shapes=halving_scratch(shapes, pieces)
        + [
            pltpu.VMEM((channels, tokens), low),
            pltpu.VMEM((tokens, channels), jnp.float32),
            pltpu.VMEM((tokens, channels), low),
            pltpu.SemaphoreType.DMA,
            pltpu.VMEM((2, tokens, width), low),
            pltpu.VMEM((2, tokens, width), low),
            pltpu.VMEM((2, width, channels), low),
            pltpu.VMEM((2, channels, width), low),
            pltpu.VMEM((2, width, channels), low),
            pltpu.VMEM((2, channels, width), low),
            pltpu.SemaphoreType.DMA((8,)),
            pltpu.SemaphoreType.DMA((4,)),
        ],
        compiler_params=pltpu.CompilerParams(
            collective_id=0, has_side_effects=True, vmem_limit_bytes=VMEM_LIMIT
        ),
        name="map_mlp_back",
    )(
        grad_low,
        norm_low,
        wide,
        slope,
        w_shrink,
        w_expand,
        unit,
        scale,
        gain,
        *halving_operands(grads),
    )
    return results[:4], results[4:]


def shift_rows(read_row, shifted, rows, side):
    def body(r, carry):
        line = read_row(r)
        for b in range(7):
            shifted[b, r] = line[b : b + side].reshape(side // 8, 8, 128)
        return carry

    lax.fori_loop(0, rows, body, 0, unroll=2)


def fill_taps(tap_ref, taps, flip):
    for k in range(49):
        tap = tap_ref[48 - k if flip else k].reshape(1, 128)
        taps[k] = jnp.broadcast_to(tap, (8, 128))


def seven_rows(shifted, taps, first, group, side):
    sums = [jnp.zeros((side // 8, 8, 128), jnp.float32) for _ in range(group)]
    for b in range(7):
        for r in range(group + 6):
            line = shifted[b, first + r]
            for k in range(group):
                if 0 <= r - k < 7:
                    sums[k] = sums[k] + taps[(r - k) * 7 + b][None] * line
    return sums


def tap_sums(shifted, read_line, rows, side, group, keep):
    for columns in ((0, 1, 2, 3), (4, 5, 6)):

        def body(g, sums):
            sums = [list(part) for part in sums]
            first = g * group
            lines = [read_line(first + k).reshape(side // 8, 8, 128) for k in range(group)]
            for n, b in enumerate(columns):
                for r in range(group + 6):
                    line = shifted[b, first + r]
                    for k in range(group):
                        if 0 <= r - k < 7:
                            sums[r - k][n] = sums[r - k][n] + jnp.sum(line * lines[k], axis=0)
            return tuple(tuple(part) for part in sums)

        zero = jnp.zeros((8, 128), jnp.float32)
        sums = lax.fori_loop(
            0, rows // group, body, tuple(tuple(zero for _ in columns) for _ in range(7))
        )
        for a in range(7):
            for n, b in enumerate(columns):
                keep(a * 7 + b, jnp.sum(sums[a][n], axis=0, keepdims=True))


def conv_kernel(map_ref, tap_ref, out_ref, shifted, taps):
    rows, side = out_ref.shape[1], out_ref.shape[2]
    fill_taps(tap_ref, taps, False)
    shift_rows(lambda r: map_ref[0, r].astype(jnp.float32), shifted, rows + 6, side)

    def body(g, carry):
        for k, line in enumerate(seven_rows(shifted, taps, g * 4, 4, side)):
            out_ref[0, g * 4 + k] = line.reshape(side, 128)
        return carry

    lax.fori_loop(0, rows // 4, body, 0)


def depthwise_seven(padded, tap_weights):
    slots, rows, cols, channels = padded.shape
    side = rows - 6
    return pl.pallas_call(
        conv_kernel,
        grid=(slots, channels // 128),
        in_specs=[
            pl.BlockSpec((1, rows, cols, 128), lambda s, c: (s, 0, 0, c)),
            pl.BlockSpec((49, 128), lambda s, c: (0, c)),
        ],
        out_specs=pl.BlockSpec((1, side, side, 128), lambda s, c: (s, 0, 0, c)),
        out_shape=jax.ShapeDtypeStruct((slots, side, side, channels), jnp.float32),
        scratch_shapes=[
            pltpu.VMEM((7, rows, side // 8, 8, 128), jnp.float32),
            pltpu.VMEM((49, 8, 128), jnp.float32),
        ],
        cost_estimate=pl.CostEstimate(
            flops=98 * slots * side * side * channels,
            bytes_accessed=8 * slots * side * side * channels,
            transcendentals=0,
        ),
        compiler_params=pltpu.CompilerParams(vmem_limit_bytes=VMEM_LIMIT),
        name="depthwise_seven",
    )(padded, tap_weights)


class SmallSum:
    def __init__(self, place, out, work, inbox, send_sem, recv_sem):
        self.out, self.work, self.inbox = out, work, inbox
        self.send_sem, self.recv_sem = send_sem, recv_sem
        self.total = out.shape[0]
        self.halvings = (
            (place.to_core, place.core),
            (place.to_x, place.x),
            (place.to_y, place.y),
            (place.to_low, place.low),
            (place.to_high, place.high),
        )
        starts, size = [0], self.total
        for _, bit in self.halvings:
            size //= 2
            starts.append(starts[-1] + bit * size)
        self.starts = starts

    def rows(self, start, size):
        return pl.ds(pl.multiple_of(start, 8), size)

    def copy(self, k):
        if k < 5:
            partner, bit = self.halvings[k]
            size = self.total >> (k + 1)
            give = self.rows(self.starts[k] + (1 - bit) * size, size)
            source = self.work.at[give, :]
            target = self.inbox.at[pl.ds(self.total - 2 * size, size), :]
        else:
            partner, _ = self.halvings[9 - k]
            mine = self.rows(self.starts[10 - k], self.total >> (10 - k))
            source = target = self.out.at[mine, :]
        return remote(source, target, self.send_sem.at[k], self.recv_sem.at[k], partner)

    def step(self, k):
        if k > 0:
            self.copy(k - 1).wait_recv()
        if 1 <= k <= 5:
            size = self.total >> k
            at = self.rows(self.starts[k], size)
            summed = self.work[at, :] + self.inbox[pl.ds(self.total - 2 * size, size), :]
            if k < 5:
                self.work[at, :] = summed
            else:
                self.out[at, :] = summed
        if k < 10:
            self.copy(k).start()

    def wait_sends(self):
        for k in range(10):
            self.copy(k).wait_send()


def conv_back_kernel(shapes, pieces, plan, *refs):
    matrices = len(shapes)
    count = len(pieces)
    (dz, pick, place_map, padded, grad_low, tap_ref, small) = refs[:7]
    grads = refs[7 : 7 + matrices]
    refs = refs[7 + matrices :]
    map_out, small_out = refs[:2]
    outs = refs[2 : 2 + matrices]
    refs = refs[2 + matrices :]
    halving_refs = refs[: 6 * count + 3]
    refs = refs[6 * count + 3 :]
    field, shifted, taps, tap_out, work, inbox, gathered, small_send, small_recv = refs[:9]
    rim, corner, rim_in, row_in, corner_in, rim_sems = refs[9:]
    place = Place()
    halving = Halving(place, shapes, pieces, grads, outs, halving_refs)
    smalls = SmallSum(place, gathered, work, inbox, small_send, small_recv)
    slots_, cells, channels = dz.shape
    side = padded.shape[1] - 6
    blocks = channels // 128
    j = pl.program_id(0)
    s = j % 2
    c = (j // 2) % blocks
    columns = lanes(c * 128, 128)

    def slot(n):
        for i, k in plan["slots"].get(n, ()):
            if i == "small":
                smalls.step(k)
            else:
                halving.stages[k](i)

    @pl.when(j == 0)
    def _():
        greet(
            (
                place.to_core,
                place.to_x,
                place.to_y,
                place.to_low,
                place.to_high,
                place.to_across,
            )
        )

    rims = rim_copies(place, dz, rim, corner, rim_in, row_in, corner_in, rim_sems)

    for n in range(plan["steps"]):
        if n in plan["slots"] and n != 2 * blocks:
            pl.when(j == n)(partial(slot, n))

    @pl.when(j == 0)
    def _():
        for s in range(slots_):
            both = contract(pick[...], dz[s], 1, 0).astype(jnp.bfloat16)
            rim[s] = both[:RIM_ROWS]
            corner[s] = both[RIM_ROWS:]
        for copy in rims:
            copy.start()

    @pl.when(j < 2 * blocks)
    def _():
        shift_rows(lambda r: padded[0, r].astype(jnp.float32), shifted, side + 6, side)

        @pl.when(s == 0)
        def _():
            tap_out[c] = jnp.zeros(tap_out.shape[1:], jnp.float32)

        def read_line(i):
            line = dz[s, pl.ds(pl.multiple_of(i * side, 8), side), columns]
            return line.astype(jnp.float32)

        def keep(k, value):
            tap_out[c, k : k + 1, :] = tap_out[c, k : k + 1, :] + value

        tap_sums(shifted, read_line, side, side, 4, keep)

    @pl.when(j == 2 * blocks)
    def _():
        for q in range(blocks):
            work[q * 49 : (q + 1) * 49, :] = tap_out[q, :49, :]
        work[blocks * 49 :, :] = small[...]
        slot(2 * blocks)
        for copy in rims:
            copy.wait()
        for q in range(slots_):
            parts = jnp.concatenate([dz[q], rim_in[q], row_in[q], corner_in[q]], axis=0)
            whole = contract(place_map[...], parts, 1, 0).astype(jnp.bfloat16)
            field[q] = whole.reshape(field.shape[1:])

    @pl.when(j >= 2 * blocks)
    def _():
        fill_taps(tap_ref, taps, True)
        shift_rows(
            lambda r: field[s, r, :, columns].astype(jnp.float32), shifted, side + 6, side
        )

        def body(g, carry):
            for k, line in enumerate(seven_rows(shifted, taps, g * 4, 4, side)):
                at = pl.ds(pl.multiple_of((g * 4 + k) * side, 8), side)
                total = line.reshape(side, 128) + grad_low[0, at, :].astype(jnp.float32)
                map_out[0, at, :] = total.astype(jnp.bfloat16)
            return carry

        lax.fori_loop(0, side // 4, body, 0)

    @pl.when(j == plan["steps"] - 1)
    def _():
        for n in range(plan["steps"], plan["last"] + 1):
            slot(n)
        small_out[...] = gathered[...]
        halving.wait_sends()
        smalls.wait_sends()


def conv_back(
    dz, pick, place_map, padded, grad_low, tap_weights, small, grads
):
    slots, cells, channels = grad_low.shape
    rows, cols = padded.shape[1:3]
    side = rows - 6
    blocks = channels // 128
    steps = 4 * blocks
    shapes = [grad.shape for grad in grads]
    pieces = plan_pieces(shapes, 2_100_000)
    plan = spread_plan(len(pieces), steps, (1, 3), (7, 3), (4, 8, 12))
    for k in range(11):
        at = 2 * blocks + 2 * k
        plan["slots"].setdefault(at, []).append(("small", k))
        plan["last"] = max(plan["last"], at)
    any_space = pl.BlockSpec(memory_space=pl.ANY)

    def first_half(j):
        k = jnp.minimum(j, 2 * blocks - 1)
        return (k % 2, 0, 0, k // 2)

    def second_half(j):
        k = jnp.maximum(j - 2 * blocks, 0)
        return (k % 2, 0, k // 2)

    results = pl.pallas_call(
        partial(conv_back_kernel, shapes, pieces, plan),
        grid=(steps,),
        in_specs=[
            fixed_block(dz.shape),
            fixed_block(pick.shape),
            fixed_block(place_map.shape),
            pl.BlockSpec((1, rows, cols, 128), first_half),
            pl.BlockSpec((1, cells, 128), second_half),
            pl.BlockSpec((49, 128), lambda j: (0, jnp.maximum(j - 2 * blocks, 0) // 2)),
            fixed_block(small.shape),
        ]
        + [any_space] * len(grads),
        out_specs=[
            pl.BlockSpec((1, cells, 128), second_half),
            whole_block((SMALL_ROWS, 128)),
        ]
        + [whole_block(item.shape) for item in halving_outputs(shapes)],
        out_shape=[
            jax.ShapeDtypeStruct((slots, cells, channels), jnp.bfloat16),
            jax.ShapeDtypeStruct((SMALL_ROWS, 128), jnp.float32),
        ]
        + halving_outputs(shapes),
        scratch_shapes=halving_scratch(shapes, pieces)
        + [
            pltpu.VMEM((slots, rows, 32, channels), jnp.bfloat16),
            pltpu.VMEM((7, rows, side // 8, 8, 128), jnp.float32),
            pltpu.VMEM((49, 8, 128), jnp.float32),
            pltpu.VMEM((blocks, 56, 128), jnp.float32),
            pltpu.VMEM((SMALL_ROWS, 128), jnp.float32),
            pltpu.VMEM((SMALL_ROWS, 128), jnp.float32),
            pltpu.VMEM((SMALL_ROWS, 128), jnp.float32),
            pltpu.SemaphoreType.DMA((10,)),
            pltpu.SemaphoreType.DMA((10,)),
            pltpu.VMEM((slots, RIM_ROWS, channels), jnp.bfloat16),
            pltpu.VMEM((slots, CORNER_ROWS, channels), jnp.bfloat16),
            pltpu.VMEM((slots, RIM_ROWS, channels), jnp.bfloat16),
            pltpu.VMEM((slots, RIM_ROWS, channels), jnp.bfloat16),
            pltpu.VMEM((slots, CORNER_ROWS, channels), jnp.bfloat16),
            pltpu.SemaphoreType.DMA((6,)),
        ],
        compiler_params=pltpu.CompilerParams(
            collective_id=1, has_side_effects=True, vmem_limit_bytes=VMEM_LIMIT
        ),
        name="conv_back",
    )(
        dz,
        pick,
        place_map,
        padded,
        grad_low,
        tap_weights,
        small,
        *halving_operands(grads),
    )
    return results[0], results[1], results[2:]


def rim_maps(side):
    tile = lax.axis_index("tile")
    low, high = tile % 2, tile // 2
    cells = side * side
    row = jnp.arange(RIM_ROWS + CORNER_ROWS, dtype=jnp.int32)
    edge_col = jnp.where(low == 0, side - 3, 0)
    edge_row = jnp.where(high == 0, side - 3, 0)
    rim_from = (row % side) * side + edge_col + row // side
    k = row - RIM_ROWS
    corner_from = (edge_row + k // 3) * side + edge_col + k % 3
    source = jnp.where(
        row < 3 * side, rim_from, jnp.where((k >= 0) & (k < 9), corner_from, -1)
    )
    pick = (source[:, None] == jnp.arange(cells, dtype=jnp.int32)[None, :]).astype(jnp.bfloat16)
    at = jnp.arange((side + 6) * 32, dtype=jnp.int32)
    i, j = at // 32 - 3, at % 32 - 3
    inside_i, inside_j = (i >= 0) & (i < side), (j >= 0) & (j < side)
    beside_j = ((j < 0) & (low == 1)) | ((j >= side) & (j < side + 3) & (low == 0))
    beside_i = ((i < 0) & (high == 1)) | ((i >= side) & (high == 0))
    q = jnp.where(j < 0, j + 3, j - side)
    p = jnp.where(i < 0, i + 3, i - side)
    skip = jnp.where(high == 1, RIM_ROWS - 3 * side, 0)
    source = jnp.where(
        inside_i & inside_j,
        i * side + j,
        jnp.where(
            inside_i & beside_j,
            cells + q * side + i,
            jnp.where(
                beside_i & inside_j,
                cells + RIM_ROWS + skip + p * side + j,
                jnp.where(beside_i & beside_j, cells + 2 * RIM_ROWS + p * 3 + q, -1),
            ),
        ),
    )
    parts = cells + 2 * RIM_ROWS + CORNER_ROWS
    place_map = (source[:, None] == jnp.arange(parts, dtype=jnp.int32)[None, :]).astype(
        jnp.bfloat16
    )
    return pick, place_map


def chip_layout():
    return lax.axis_size("img") == 8 and lax.axis_size("tile") == 4


def sum_plain(grads, smalls):
    sums = []
    for grad in grads:
        part = lax.psum_scatter(grad, "img", scatter_dimension=0, tiled=True)
        part = lax.psum_scatter(part, "tile", scatter_dimension=1, tiled=True)
        sums.append(part.astype(jnp.float32))
    return sums, lax.psum(tuple(smalls), ("img", "tile"))


def map_back(
    grad_low,
    norm_low,
    wide_low,
    wide_slope,
    w_shrink,
    w_expand,
    unit_low,
    scale,
    gain,
    padded_map,
    taps,
    grads,
    smalls,
):
    slots, cells, channels = grad_low.shape
    side = math.isqrt(cells)
    flat = (slots * cells, -1)
    if not chip_layout():
        w_shrink_grad = outer_sum(wide_low, grad_low)
        grad_wide_low = (project_back(grad_low, w_shrink) * wide_slope).astype(jnp.bfloat16)
        w_expand_grad = outer_sum(norm_low, grad_wide_low)
        back = project_back(grad_wide_low, w_expand)
        unit = unit_low.astype(jnp.float32)
        turned = back * gain
        gain_conv_grad = jnp.sum(back * unit, axis=(0, 1))
        grad_spread = scale * (
            turned
            - jnp.mean(turned, axis=-1, keepdims=True)
            - unit * jnp.mean(turned * unit, axis=-1, keepdims=True)
        )
        grad_spread = grad_spread.reshape(slots, side, side, channels)
        field = padded_map[:, :, : side + 6].astype(jnp.float32)
        taps_grad = jnp.stack(
            [
                jnp.sum(field[:, a : a + side, b : b + side] * grad_spread, axis=(0, 1, 2))
                for a in range(7)
                for b in range(7)
            ]
        )
        padded_grad = add_rims(grad_spread.astype(jnp.bfloat16), 3).astype(jnp.float32)
        moved = depthwise(padded_grad, taps[::-1], 3, 0).reshape(slots, cells, channels)
        map_grad = (grad_low.astype(jnp.float32) + moved).astype(jnp.bfloat16)
        sums, small_sums = sum_plain(
            tuple(grads) + (w_expand_grad, w_shrink_grad),
            tuple(smalls) + (gain_conv_grad, taps_grad),
        )
        return map_grad, sums, small_sums
    pick, place_map = rim_maps(side)
    first, first_sums = map_mlp_back(
        grad_low.reshape(flat),
        norm_low.reshape(flat),
        wide_low.reshape(flat),
        wide_slope.reshape(flat),
        w_shrink,
        w_expand,
        unit_low.reshape(flat),
        scale.reshape(flat),
        gain.reshape(1, channels),
        grads,
    )
    w_shrink_grad, w_expand_grad, dz, gain_conv_grad = first
    smalls = tuple(smalls) + (gain_conv_grad.reshape(channels),)
    tap_rows = channels // 128 * 49
    packed = jnp.concatenate([part.reshape(-1, 128) for part in smalls])
    packed = jnp.pad(packed, ((0, SMALL_ROWS - tap_rows - packed.shape[0]), (0, 0)))
    map_grad, small, last_sums = conv_back(
        dz.reshape(grad_low.shape),
        pick,
        place_map,
        padded_map,
        grad_low,
        taps,
        packed,
        (w_expand_grad, w_shrink_grad),
    )
    small_sums, first_row = [], tap_rows
    for part in smalls:
        rows = part.size // 128
        small_sums.append(small[first_row : first_row + rows].reshape(part.shape))
        first_row += rows
    taps_grad = small[:tap_rows].reshape(-1, 49, 128).transpose(1, 0, 2).reshape(49, channels)
    small_sums.append(taps_grad)
    return map_grad, tuple(first_sums) + tuple(last_sums), small_sums


def local(
    vit_in,
    map_in,
    group_images,
    vit_grad_out,
    map_grad_out,
    w_query,
    w_key,
    w_value,
    w_out,
    w_up,
    w_down,
    w_expand,
    w_shrink,
    w_adapt,
    gain_attn,
    gain_mlp,
    gain_conv,
    dw_large,
    dw_small,
    gate_low,
    gate_high,
):
    slot_count = vit_in.shape[0]
    tok_side = math.isqrt(vit_in.shape[2])
    pix_side = math.isqrt(map_in.shape[2])
    channels = map_in.shape[3]
    model_width = vit_in.shape[3]
    live_mask = (
        (jnp.arange(slot_count, dtype=jnp.int32) < group_images[0])
        .astype(jnp.float32)
        .reshape(slot_count, 1, 1)
    )
    live_cells = live_mask.reshape(slot_count, 1, 1, 1)
    tokens = vit_in[:, 0].astype(jnp.float32)
    normed_one, norm_one_pull = jax.vjp(layer_norm, tokens, gain_attn.astype(jnp.float32))
    normed_one_low = normed_one.astype(jnp.bfloat16)
    query_low = project(normed_one_low, w_query).astype(jnp.bfloat16)
    tokens_all = lax.all_gather(vit_in[:, 0], "tile", axis=1, tiled=True)
    normed_all_low = layer_norm(
        tokens_all.astype(jnp.float32), gain_attn.astype(jnp.float32)
    ).astype(jnp.bfloat16)
    key_all = project(normed_all_low, w_key).astype(jnp.bfloat16)
    value_all = project(normed_all_low, w_value).astype(jnp.bfloat16)
    scores = attention_scores(query_low, key_all)
    row_max = jnp.max(scores, axis=-1, keepdims=True)
    shifted = jnp.exp(scores - row_max)
    row_total = jnp.sum(shifted, axis=-1, keepdims=True)
    softmax_low = (shifted / row_total).astype(jnp.bfloat16)
    log_total = row_max + jnp.log(row_total)
    mixed_low = (
        jnp.einsum(
            "shqk,skhd->sqhd",
            softmax_low,
            split_heads(value_all),
            preferred_element_type=jnp.float32,
        )
        .reshape(slot_count, -1, model_width)
        .astype(jnp.bfloat16)
    )
    residual_one = tokens + project(mixed_low, w_out)
    normed_two, norm_two_pull = jax.vjp(layer_norm, residual_one, gain_mlp.astype(jnp.float32))
    normed_two_low = normed_two.astype(jnp.bfloat16)
    acted_low, acted_slope = gelu_pair(project(normed_two_low, w_up))
    residual_two = residual_one + project(acted_low, w_down)
    map_low = map_in[:, 0].reshape(slot_count, pix_side, pix_side, channels)
    padded_map = jnp.pad(add_rims(map_low, 3), ((0, 0), (0, 0), (0, 2), (0, 0)))
    large_taps = dw_large.astype(jnp.float32)
    cells = pix_side * pix_side
    spread_map = depthwise_seven(padded_map, large_taps).reshape(slot_count, cells, channels)
    centre = spread_map - jnp.mean(spread_map, axis=-1, keepdims=True)
    conv_scale = lax.rsqrt(jnp.mean(centre * centre, axis=-1, keepdims=True) + 1e-06)
    conv_unit = centre * conv_scale
    conv_gain = gain_conv.astype(jnp.float32)
    conv_norm_low = (conv_unit * conv_gain).astype(jnp.bfloat16)
    conv_unit_low = conv_unit.astype(jnp.bfloat16)
    wide_low, wide_slope = gelu_pair(project(conv_norm_low, w_expand))
    map_after = map_low.astype(jnp.float32) + project(wide_low, w_shrink).reshape(map_low.shape)
    pooled, pool_pull = jax.vjp(pool_pairs, map_after)
    pooled_low = pooled.astype(jnp.bfloat16)
    adapted_low = project(pooled_low, w_adapt).astype(jnp.bfloat16)
    padded_small = add_rims(adapted_low, 1).astype(jnp.float32)
    merged_map, merged_pull = jax.vjp(
        partial(depthwise, radius=1, margin=0), padded_small, dw_small.astype(jnp.float32)
    )
    merged_tokens = merged_map.reshape(slot_count, tok_side * tok_side, model_width)
    vit_after, merging_pull = jax.vjp(
        merging,
        residual_two,
        merged_tokens,
        gate_low.astype(jnp.float32),
        gate_high.astype(jnp.float32),
    )
    vit_cotangent = vit_grad_out[:, 0].astype(jnp.float32) * live_mask
    map_cotangent = (
        map_grad_out[:, 0].astype(jnp.float32).reshape(slot_count, pix_side, pix_side, channels)
        * live_cells
    )
    grad_residual_two, grad_merged, gate_low_grad, gate_high_grad = merging_pull(vit_cotangent)
    grad_padded_small, dw_small_grad = merged_pull(
        grad_merged.reshape(slot_count, tok_side, tok_side, model_width)
    )
    grad_adapted_low = return_rims(grad_padded_small, 1).astype(jnp.bfloat16)
    w_adapt_grad = outer_sum(pooled_low, grad_adapted_low)
    grad_map_after = map_cotangent + pool_pull(project_back(grad_adapted_low, w_adapt))[0]
    grad_conv_low = grad_map_after.astype(jnp.bfloat16)
    grad_mlp_low = grad_residual_two.astype(jnp.bfloat16)
    w_down_grad = outer_sum(acted_low, grad_mlp_low)
    grad_up_low = (project_back(grad_mlp_low, w_down) * acted_slope).astype(jnp.bfloat16)
    w_up_grad = outer_sum(normed_two_low, grad_up_low)
    grad_norm_part, gain_mlp_grad = norm_two_pull(project_back(grad_up_low, w_up))
    grad_residual_one = grad_residual_two + grad_norm_part
    grad_attn_low = grad_residual_one.astype(jnp.bfloat16)
    w_out_grad = outer_sum(mixed_low, grad_attn_low)
    grad_mixed_low = project_back(grad_attn_low, w_out).astype(jnp.bfloat16)
    key_back, value_back = (key_all, value_all)
    softmax_again = jnp.exp(attention_scores(query_low, key_back) - log_total)
    softmax_again_low = softmax_again.astype(jnp.bfloat16)
    grad_mixed_heads = split_heads(grad_mixed_low)
    grad_softmax = jnp.einsum(
        "sqhd,skhd->shqk",
        grad_mixed_heads,
        split_heads(value_back),
        preferred_element_type=jnp.float32,
    )
    row_dot = jnp.sum(softmax_again * grad_softmax, axis=-1, keepdims=True)
    grad_scores_low = (softmax_again * (grad_softmax - row_dot)).astype(jnp.bfloat16)
    scale = HDIM ** (-0.5)
    grad_query_low = (
        (
            jnp.einsum(
                "shqk,skhd->sqhd",
                grad_scores_low,
                split_heads(key_back),
                preferred_element_type=jnp.float32,
            )
            * scale
        )
        .reshape(slot_count, -1, model_width)
        .astype(jnp.bfloat16)
    )
    grad_key_term = (
        jnp.einsum(
            "shqk,sqhd->skhd",
            grad_scores_low,
            split_heads(query_low),
            preferred_element_type=jnp.float32,
        )
        * scale
    ).reshape(slot_count, -1, model_width)
    grad_value_term = jnp.einsum(
        "shqk,sqhd->skhd", softmax_again_low, grad_mixed_heads, preferred_element_type=jnp.float32
    ).reshape(slot_count, -1, model_width)
    grad_key_low = grad_key_term.astype(jnp.bfloat16)
    grad_value_low = grad_value_term.astype(jnp.bfloat16)
    w_query_grad = outer_sum(normed_one_low, grad_query_low)
    w_key_grad = outer_sum(normed_all_low, grad_key_low)
    w_value_grad = outer_sum(normed_all_low, grad_value_low)
    grad_normed_all = project_back(grad_key_low, w_key) + project_back(grad_value_low, w_value)
    grad_normed_one = project_back(grad_query_low, w_query) + lax.psum_scatter(
        grad_normed_all.astype(jnp.bfloat16), "tile", scatter_dimension=1, tiled=True
    ).astype(jnp.float32)
    grad_token_part, gain_attn_grad = norm_one_pull(grad_normed_one)
    vit_in_grad = (grad_residual_one + grad_token_part).astype(jnp.bfloat16)
    map_in_grad, matrix_sums, small_sums = map_back(
        grad_conv_low.reshape(slot_count, cells, channels),
        conv_norm_low,
        wide_low,
        wide_slope,
        w_shrink,
        w_expand,
        conv_unit_low,
        conv_scale,
        conv_gain,
        padded_map,
        large_taps,
        (
            w_up_grad,
            w_down_grad,
            w_adapt_grad,
            w_query_grad,
            w_key_grad,
            w_value_grad,
            w_out_grad,
        ),
        (gain_attn_grad, gain_mlp_grad, dw_small_grad, gate_low_grad, gate_high_grad),
    )
    vit_result = (vit_after * live_mask).astype(jnp.bfloat16)[:, None]
    map_result = (
        (map_after * live_cells)
        .reshape(slot_count, pix_side * pix_side, channels)
        .astype(jnp.bfloat16)[:, None]
    )
    return (
        vit_result,
        map_result,
        vit_in_grad[:, None],
        map_in_grad[:, None],
        matrix_sums[3],
        matrix_sums[4],
        matrix_sums[5],
        matrix_sums[6],
        matrix_sums[0],
        matrix_sums[1],
        matrix_sums[7],
        matrix_sums[8],
        matrix_sums[2],
        small_sums[0],
        small_sums[1],
        small_sums[5],
        small_sums[6],
        small_sums[2],
        small_sums[3],
        small_sums[4],
    )


def solution(mesh):
    in_specs = (
        P("img", "tile", None, None),
        P("img", "tile", None, None),
        P("img"),
        P("img", "tile", None, None),
        P("img", "tile", None, None),
        P(),
        P(),
        P(),
        P(),
        P(),
        P(),
        P(),
        P(),
        P(),
        P(),
        P(),
        P(),
        P(),
        P(),
        P(),
        P(),
    )
    out_specs = (
        P("img", "tile", None, None),
        P("img", "tile", None, None),
        P("img", "tile", None, None),
        P("img", "tile", None, None),
        P("img", "tile"),
        P("img", "tile"),
        P("img", "tile"),
        P("img", "tile"),
        P("img", "tile"),
        P("img", "tile"),
        P("img", "tile"),
        P("img", "tile"),
        P("img", "tile"),
        P(),
        P(),
        P(),
        P(),
        P(),
        P(),
        P(),
    )
    return jax.shard_map(local, mesh=mesh, in_specs=in_specs, out_specs=out_specs, check_vma=False)
```

```python
from functools import partial
import math

import jax
import jax.numpy as jnp
from jax import lax
from jax.experimental import pallas as pl
from jax.experimental.pallas import tpu as pltpu
from jax.sharding import PartitionSpec as P

HEADS = 12
HDIM = 64


highest = lax.Precision.HIGHEST


def swapped(array, axis, bit):
    return lax.ppermute(array, axis, [(i, i ^ 1 << bit) for i in range(lax.axis_size(axis))])


def gelu_pair(values):
    spread = 0.5 * (1.0 + lax.erf(values * 0.7071067811865476))
    bell = jnp.exp(-0.5 * values * values) * 0.3989422804014327
    return (values * spread).astype(jnp.bfloat16), (spread + values * bell).astype(jnp.bfloat16)


def depthwise(field_map, tap_weights, radius, margin):
    kernel_side = 2 * radius + 1
    channels = tap_weights.shape[1]
    kernel = tap_weights.reshape(kernel_side, kernel_side, 1, channels)
    return lax.conv_general_dilated(
        field_map,
        kernel,
        (1, 1),
        ((margin, margin), (margin, margin)),
        dimension_numbers=("NHWC", "HWIO", "NHWC"),
        feature_group_count=channels,
        precision=highest,
    )


def merging(residual_two, merged_tokens, gate_low, gate_high):
    gate_logit = jnp.sum(residual_two * gate_low, axis=-1, keepdims=True) + jnp.sum(
        merged_tokens * gate_high, axis=-1, keepdims=True
    )
    gate_value = 1.0 / (1.0 + jnp.exp(-gate_logit))
    return residual_two + gate_value * merged_tokens


def project_back(left_side, right_side):
    return jnp.einsum("...j,ij->...i", left_side, right_side, preferred_element_type=jnp.float32)


def outer_sum(left_side, right_side):
    flat_left = left_side.reshape(-1, left_side.shape[-1])
    flat_right = right_side.reshape(-1, right_side.shape[-1])
    return lax.dot_general(
        flat_left, flat_right, (((0,), (0,)), ((), ())), preferred_element_type=jnp.float32
    ).astype(jnp.bfloat16)


def add_rims(tile_field, radius):
    tile_place = lax.axis_index("tile")
    for which_bit in range(2):
        axis_dim = 2 - which_bit
        on_low = tile_place >> which_bit & 1 == 0
        side_len = tile_field.shape[axis_dim]
        upper_rim = lax.slice_in_dim(tile_field, side_len - radius, side_len, axis=axis_dim)
        lower_rim = lax.slice_in_dim(tile_field, 0, radius, axis=axis_dim)
        outgoing = jnp.where(on_low, upper_rim, lower_rim)
        incoming = swapped(outgoing, "tile", which_bit)
        blank_rim = jnp.zeros_like(incoming)
        tile_field = jnp.where(
            on_low,
            jnp.concatenate([blank_rim, tile_field, incoming], axis_dim),
            jnp.concatenate([incoming, tile_field, blank_rim], axis_dim),
        )
    return tile_field


def return_rims(grad_field, radius):
    tile_place = lax.axis_index("tile")
    for which_bit in (1, 0):
        axis_dim = 2 - which_bit
        on_low = tile_place >> which_bit & 1 == 0
        total_len = grad_field.shape[axis_dim]
        side_len = total_len - 2 * radius
        high_rim = lax.slice_in_dim(grad_field, total_len - radius, total_len, axis=axis_dim)
        low_rim = lax.slice_in_dim(grad_field, 0, radius, axis=axis_dim)
        outgoing = jnp.where(on_low, high_rim, low_rim)
        incoming = swapped(outgoing.astype(jnp.bfloat16), "tile", which_bit).astype(outgoing.dtype)
        core_part = lax.slice_in_dim(grad_field, radius, radius + side_len, axis=axis_dim)
        filler_shape = list(incoming.shape)
        filler_shape[axis_dim] = side_len - radius
        filler = jnp.zeros(filler_shape, jnp.float32)
        grad_field = core_part + jnp.where(
            on_low,
            jnp.concatenate([filler, incoming], axis_dim),
            jnp.concatenate([incoming, filler], axis_dim),
        )
    return grad_field


MESH = pl.DeviceIdType.MESH
VMEM_LIMIT = 62 << 20
COPIES = 8
SMALL_ROWS = 512
RIM_ROWS = 80
CORNER_ROWS = 16


def contract(left, right, left_axis, right_axis):
    return lax.dot_general(
        left,
        right,
        (((left_axis,), (right_axis,)), ((), ())),
        preferred_element_type=jnp.float32,
    )


def wide_sum(one, two):
    return one.astype(jnp.float32) + two.astype(jnp.float32)


def low_sum(one, two):
    return wide_sum(one, two).astype(jnp.bfloat16)


def row_loop(first, rows, width, step):
    count = rows // 16
    while count > 1 and (count * 16 * width > 65536 or rows % (count * 16)):
        count -= 1
    chunk = count * 16

    def body(q, carry):
        step(pl.ds(pl.multiple_of(first + q * chunk, 16), chunk))
        return carry

    if rows == chunk:
        body(0, 0)
    else:
        lax.fori_loop(0, rows // chunk, body, 0)


def lanes(start, size):
    return pl.ds(pl.multiple_of(start, 128), size)


class Place:
    def __init__(self):
        img = lax.axis_index("img")
        tile = lax.axis_index("tile")
        self.core, self.x, self.y = img % 2, (img // 2) % 2, img // 4
        self.low, self.high = tile % 2, tile // 2
        self.to_core = (img + 1 - 2 * self.core, tile)
        self.to_x = (img + 2 - 4 * self.x, tile)
        self.to_y = (img + 4 - 8 * self.y, tile)
        self.to_low = (img, tile + 1 - 2 * self.low)
        self.to_high = (img, tile + 2 - 4 * self.high)
        self.to_across = (img, 3 - tile)


def greet(partners):
    barrier = pltpu.get_barrier_semaphore()
    for partner in partners:
        pl.semaphore_signal(barrier, inc=1, device_id=partner, device_id_type=MESH)
    pl.semaphore_wait(barrier, len(partners))


def remote(source, target, send_sem, recv_sem, partner):
    return pltpu.make_async_remote_copy(
        src_ref=source,
        dst_ref=target,
        send_sem=send_sem,
        recv_sem=recv_sem,
        device_id=partner,
        device_id_type=MESH,
    )


def plan_pieces(shapes, piece_bytes):
    pieces = []
    for g, (height, width) in enumerate(shapes):
        rows = height // 8
        count = max(1, round(height * width * 2 / piece_bytes))
        while rows % (count * 32):
            count -= 1
        for p in range(count):
            pieces.append((g, p * (rows // count), rows // count))
    return pieces


def halving_scratch(shapes, pieces):
    count = len(pieces)

    def buffers(shape_of):
        return [
            pltpu.VMEM(shape_of(rows, shapes[g][1]), jnp.bfloat16) for g, _, rows in pieces
        ]

    scratch = buffers(lambda rows, width: (2, 2, rows, width))
    scratch += buffers(lambda rows, width: (2, 2, rows, width))
    scratch += buffers(lambda rows, width: (2, rows, width))
    scratch += buffers(lambda rows, width: (rows, width))
    scratch += buffers(lambda rows, width: (rows, width // 2))
    scratch += buffers(
        lambda rows, width: (rows, width // 4 if width % 512 == 0 else width // 2)
    )
    scratch += [
        pltpu.SemaphoreType.DMA((count * COPIES,)),
        pltpu.SemaphoreType.DMA((count * COPIES,)),
        pltpu.SemaphoreType.DMA((count,)),
    ]
    return scratch


class Halving:
    def __init__(self, place, shapes, pieces, grads, outs, scratch):
        count = len(pieces)
        self.place, self.shapes, self.pieces = place, shapes, pieces
        self.grads, self.outs = grads, outs
        self.own, self.half, self.quarter, self.eighth, self.pair, self.last = (
            scratch[k * count : (k + 1) * count] for k in range(6)
        )
        self.send_sem, self.recv_sem, self.own_sem = scratch[6 * count :]
        self.stages = (
            self.over_core,
            self.over_first,
            self.over_second,
            self.over_third,
            self.over_fourth,
            self.finish,
        )

    def narrow(self, i):
        return self.shapes[self.pieces[i][0]][1] % 512 != 0

    def copy(self, i, k):
        place = self.place
        g, first, rows = self.pieces[i]
        width = self.shapes[g][1] // 4
        half, quarter, eighth = self.half[i], self.quarter[i], self.eighth[i]
        pair, last = self.pair[i], self.last[i]
        part, cut = pl.ds(first, rows), rows // 2
        top, bottom = pl.ds(0, cut), pl.ds(cut, cut)
        if k == 0:
            ends = (self.grads[g].at[:, :, 1 - place.core, part, :], half, place.to_core)
        elif k == 1:
            ends = (half.at[:, 1 - place.x, top, :], quarter.at[:, top, :], place.to_x)
        elif k == 2:
            ends = (half.at[1 - place.y, :, bottom, :], quarter.at[:, bottom, :], place.to_y)
        elif k == 3:
            ends = (quarter.at[1 - place.y, top, :], eighth.at[top, :], place.to_y)
        elif k == 4:
            ends = (quarter.at[1 - place.x, bottom, :], eighth.at[bottom, :], place.to_x)
        elif k < 7 and not self.narrow(i):
            q = k - 5
            side = eighth.at[:, lanes((2 * q + 1 - place.low) * width, width)]
            ends = (side, pair.at[:, pl.ds(q * width, width)], place.to_low)
        elif k == 5:
            side = eighth.at[:, lanes((1 - place.high) * 2 * width, 2 * width)]
            ends = (side, pair, place.to_high)
        elif not self.narrow(i):
            ends = (pair.at[:, lanes((1 - place.high) * width, width)], last, place.to_high)
        else:
            ends = (pair, last, place.to_low)
        at = i * COPIES + k
        return remote(ends[0], ends[1], self.send_sem.at[at], self.recv_sem.at[at], ends[2])

    def own_copy(self, i):
        g, first, rows = self.pieces[i]
        mine = self.grads[g].at[:, :, self.place.core, pl.ds(first, rows), :]
        return pltpu.make_async_copy(mine, self.own[i], self.own_sem.at[i])

    def copies(self, i):
        return (0, 1, 2, 3, 4, 5, 7) if self.narrow(i) else (0, 1, 2, 3, 4, 5, 6, 7)

    def over_core(self, i):
        self.copy(i, 0).start()
        self.own_copy(i).start()

    def over_first(self, i):
        rows = self.pieces[i][2]
        half, own = self.half[i], self.own[i]
        self.copy(i, 0).wait_recv()
        self.own_copy(i).wait()
        for a in range(2):
            for b in range(2):

                def step(s, a=a, b=b):
                    half[a, b, s, :] = low_sum(half[a, b, s, :], own[a, b, s, :])

                row_loop(0, rows, half.shape[-1], step)
        self.copy(i, 1).start()
        self.copy(i, 2).start()

    def over_second(self, i):
        cut = self.pieces[i][2] // 2
        place, half, quarter = self.place, self.half[i], self.quarter[i]
        self.copy(i, 1).wait_recv()
        self.copy(i, 2).wait_recv()
        for a in range(2):

            def step_top(s, a=a):
                quarter[a, s, :] = low_sum(quarter[a, s, :], half[a, place.x, s, :])

            def step_bottom(s, a=a):
                quarter[a, s, :] = low_sum(quarter[a, s, :], half[place.y, a, s, :])

            row_loop(0, cut, quarter.shape[-1], step_top)
            row_loop(cut, cut, quarter.shape[-1], step_bottom)
        self.copy(i, 3).start()
        self.copy(i, 4).start()

    def over_third(self, i):
        cut = self.pieces[i][2] // 2
        place, quarter, eighth = self.place, self.quarter[i], self.eighth[i]
        self.copy(i, 3).wait_recv()
        self.copy(i, 4).wait_recv()

        def step_top(s):
            eighth[s, :] = low_sum(eighth[s, :], quarter[place.y, s, :])

        def step_bottom(s):
            eighth[s, :] = low_sum(eighth[s, :], quarter[place.x, s, :])

        row_loop(0, cut, eighth.shape[-1], step_top)
        row_loop(cut, cut, eighth.shape[-1], step_bottom)
        self.copy(i, 5).start()
        if not self.narrow(i):
            self.copy(i, 6).start()

    def over_fourth(self, i):
        g, _, rows = self.pieces[i]
        width = self.shapes[g][1] // 4
        place, eighth, pair = self.place, self.eighth[i], self.pair[i]
        self.copy(i, 5).wait_recv()
        if self.narrow(i):

            def step(s):
                kept = eighth[s, lanes(place.high * 2 * width, 2 * width)]
                pair[s, :] = low_sum(pair[s, :], kept)

        else:
            self.copy(i, 6).wait_recv()

            def step(s):
                for q in range(2):
                    at = slice(q * width, (q + 1) * width)
                    kept = eighth[s, lanes((2 * q + place.low) * width, width)]
                    pair[s, at] = low_sum(pair[s, at], kept)

        row_loop(0, rows, pair.shape[-1], step)
        self.copy(i, 7).start()

    def finish(self, i):
        g, first, rows = self.pieces[i]
        width = self.shapes[g][1] // 4
        place, pair, last, out = self.place, self.pair[i], self.last[i], self.outs[g]
        self.copy(i, 7).wait_recv()

        def step(s):
            at = pl.ds(pl.multiple_of(s.start + first, 16), s.size)
            if self.narrow(i):
                both = wide_sum(last[s, :], pair[s, :])
                out[at, :] = jnp.where(place.low == 0, both[:, :width], both[:, width:])
            else:
                kept = pair[s, lanes(place.high * width, width)]
                out[at, :] = wide_sum(last[s, :], kept)

        row_loop(0, rows, pair.shape[-1], step)

    def wait_sends(self):
        for i in range(len(self.pieces)):
            for k in self.copies(i):
                self.copy(i, k).wait_send()


def halving_operands(grads):
    return [grad.reshape(2, 2, 2, grad.shape[0] // 8, grad.shape[1]) for grad in grads]


def halving_outputs(shapes):
    return [
        jax.ShapeDtypeStruct((height // 8, width // 4), jnp.float32) for height, width in shapes
    ]


def whole_block(shape):
    return pl.BlockSpec(shape, lambda *_: (0,) * len(shape))


def fixed_block(shape):
    return pl.BlockSpec(shape, lambda *_: (0,) * len(shape), pipeline_mode=pl.Buffered(1))


def rim_copies(place, source, rim, corner, rim_in, row_in, corner_in, sems):
    cells = source.shape[1]
    start = pl.multiple_of((1 - place.high) * (cells - RIM_ROWS), 16)
    return (
        remote(rim, rim_in, sems.at[0], sems.at[1], place.to_low),
        remote(
            source.at[:, pl.ds(start, RIM_ROWS), :], row_in, sems.at[2], sems.at[3], place.to_high
        ),
        remote(corner, corner_in, sems.at[4], sems.at[5], place.to_across),
    )


def mlp_back_kernel(shapes, pieces, plan, *refs):
    matrices = len(shapes)
    count = len(pieces)
    grad_low, norm_low, wide, slope, w_shrink, w_expand, unit, scale, gain = refs[:9]
    grads = refs[9 : 9 + matrices]
    refs = refs[9 + matrices :]
    shrink_out, expand_out, dz_out, gain_out = refs[:4]
    outs = refs[4 : 4 + matrices]
    refs = refs[4 + matrices :]
    halving_refs = refs[: 6 * count + 3]
    refs = refs[6 * count + 3 :]
    norm_turned, back, dz, out_sem = refs[:4]
    buffers, result_buffers, in_sems, result_sems = refs[4:8], refs[8:10], refs[10], refs[11]
    place = Place()
    halving = Halving(place, shapes, pieces, grads, outs, halving_refs)
    steps = plan["steps"]
    j = pl.program_id(0)

    def slot(n):
        for i, k in plan["slots"].get(n, ()):
            halving.stages[k](i)

    def slots(odd):
        for n in range(steps):
            if plan["slots"].get(2 * n + odd):
                pl.when(j == n)(partial(slot, 2 * n + odd))

    width = plan["width"]

    def fetches(n):
        slot_, at = n % 2, lanes(n * width, width)
        parts = (wide.at[:, at], slope.at[:, at], w_shrink.at[at, :], w_expand.at[:, at])
        return [
            pltpu.make_async_copy(part, buffers[k].at[slot_], in_sems.at[slot_ * 4 + k])
            for k, part in enumerate(parts)
        ]

    def stores(n):
        slot_, at = n % 2, lanes(n * width, width)
        targets = (shrink_out.at[at, :], expand_out.at[:, at])
        return [
            pltpu.make_async_copy(
                result_buffers[k].at[slot_], target, result_sems.at[slot_ * 2 + k]
            )
            for k, target in enumerate(targets)
        ]

    @pl.when(j == 0)
    def _():
        for copy in fetches(0):
            copy.start(priority=1)
        greet(
            (
                place.to_core,
                place.to_x,
                place.to_y,
                place.to_low,
                place.to_high,
            )
        )

    @pl.when(j + 1 < steps)
    def _():
        for copy in fetches(j + 1):
            copy.start(priority=1)

    slots(0)

    @pl.when(j == 0)
    def _():
        norm_turned[...] = norm_low[...].T

    for copy in fetches(j):
        copy.wait()

    @pl.when(j >= 2)
    def _():
        for copy in stores(j - 2):
            copy.wait()

    now = j % 2
    grad_wide = contract(grad_low[...], buffers[2][now], 1, 1)
    grad_wide = (grad_wide * buffers[1][now].astype(jnp.float32)).astype(jnp.bfloat16)
    turned = contract(buffers[0][now], grad_low[...], 0, 0)
    result_buffers[0][now] = turned.astype(jnp.bfloat16)
    slots(1)
    turned = contract(norm_turned[...], grad_wide, 1, 0)
    result_buffers[1][now] = turned.astype(jnp.bfloat16)
    term = contract(grad_wide, buffers[3][now], 1, 1)
    for copy in stores(j):
        copy.start(priority=1)

    @pl.when(j == 0)
    def _():
        back[...] = term

    @pl.when(j > 0)
    def _():
        back[...] = back[...] + term

    @pl.when(j == steps - 1)
    def _():
        gain_row = gain[...]
        chunk = 48

        def body(q, sums):
            at = pl.ds(pl.multiple_of(q * chunk, 16), chunk)
            grad = back[at, :]
            n = unit[at, :].astype(jnp.float32)
            t = grad * gain_row
            mean_t = jnp.mean(t, axis=-1, keepdims=True)
            mean_tn = jnp.mean(t * n, axis=-1, keepdims=True)
            dz[at, :] = (scale[at, :] * (t - mean_t - n * mean_tn)).astype(jnp.bfloat16)
            return sums + jnp.sum((grad * n).reshape(chunk // 8, 8, -1), axis=0)

        sums = jnp.zeros((8, dz.shape[1]), jnp.float32)
        sums = lax.fori_loop(0, dz.shape[0] // chunk, body, sums)
        gain_out[...] = jnp.sum(sums, axis=0, keepdims=True)
        back_copy = pltpu.make_async_copy(dz, dz_out, out_sem)
        back_copy.start()
        for n in range(2 * steps, plan["last"] + 1):
            slot(n)
        back_copy.wait()
        for n in (steps - 2, steps - 1):
            for copy in stores(n):
                copy.wait()
        halving.wait_sends()


def spread_plan(count, steps, first, second, rest):
    slots = {0: [(i, 0) for i in range(count)]}
    last = 0
    for i in range(count):
        at = [int(first[0] + first[1] * i), int(second[0] + second[1] * i)]
        at += [at[1] + r for r in rest]
        for k, n in enumerate(at):
            slots.setdefault(n, []).append((i, k + 1))
        last = max(last, at[-1])
    for n in slots:
        slots[n].sort(key=lambda item: (-item[1], item[0]))
    return {"slots": slots, "last": last, "steps": steps}


def map_mlp_back(
    grad_low, norm_low, wide, slope, w_shrink, w_expand, unit, scale, gain, grads
):
    tokens, channels = grad_low.shape
    hidden = w_shrink.shape[0]
    width = 512
    steps = hidden // width
    shapes = [grad.shape for grad in grads]
    pieces = plan_pieces(shapes, 1_600_000)
    plan = spread_plan(len(pieces), steps, (1, 1.0), (4, 1.0), (2, 4, 6))
    plan["width"] = width
    low = jnp.bfloat16
    any_space = pl.BlockSpec(memory_space=pl.ANY)
    results = pl.pallas_call(
        partial(mlp_back_kernel, shapes, pieces, plan),
        grid=(steps,),
        in_specs=[
            fixed_block((tokens, channels)),
            fixed_block((tokens, channels)),
            any_space,
            any_space,
            any_space,
            any_space,
            fixed_block((tokens, channels)),
            fixed_block((tokens, 1)),
            fixed_block((1, channels)),
        ]
        + [any_space] * len(grads),
        out_specs=[
            any_space,
            any_space,
            any_space,
            whole_block((1, channels)),
        ]
        + [whole_block(item.shape) for item in halving_outputs(shapes)],
        out_shape=[
            jax.ShapeDtypeStruct((hidden, channels), low),
            jax.ShapeDtypeStruct((channels, hidden), low),
            jax.ShapeDtypeStruct((tokens, channels), low),
            jax.ShapeDtypeStruct((1, channels), jnp.float32),
        ]
        + halving_outputs(shapes),
        scratch_shapes=halving_scratch(shapes, pieces)
        + [
            pltpu.VMEM((channels, tokens), low),
            pltpu.VMEM((tokens, channels), jnp.float32),
            pltpu.VMEM((tokens, channels), low),
            pltpu.SemaphoreType.DMA,
            pltpu.VMEM((2, tokens, width), low),
            pltpu.VMEM((2, tokens, width), low),
            pltpu.VMEM((2, width, channels), low),
            pltpu.VMEM((2, channels, width), low),
            pltpu.VMEM((2, width, channels), low),
            pltpu.VMEM((2, channels, width), low),
            pltpu.SemaphoreType.DMA((8,)),
            pltpu.SemaphoreType.DMA((4,)),
        ],
        compiler_params=pltpu.CompilerParams(
            collective_id=0, has_side_effects=True, vmem_limit_bytes=VMEM_LIMIT
        ),
        name="map_mlp_back",
    )(
        grad_low,
        norm_low,
        wide,
        slope,
        w_shrink,
        w_expand,
        unit,
        scale,
        gain,
        *halving_operands(grads),
    )
    return results[:4], results[4:]


def shift_rows(read_row, shifted, rows, side):
    def body(r, carry):
        line = read_row(r)
        for b in range(7):
            shifted[b, r] = line[b : b + side].reshape(side // 8, 8, 128)
        return carry

    lax.fori_loop(0, rows, body, 0, unroll=2)


def fill_taps(tap_ref, taps, flip):
    for k in range(49):
        tap = tap_ref[48 - k if flip else k].reshape(1, 128)
        taps[k] = jnp.broadcast_to(tap, (8, 128))


def seven_rows(shifted, taps, first, group, side):
    sums = [jnp.zeros((side // 8, 8, 128), jnp.float32) for _ in range(group)]
    for b in range(7):
        for r in range(group + 6):
            line = shifted[b, first + r]
            for k in range(group):
                if 0 <= r - k < 7:
                    sums[k] = sums[k] + taps[(r - k) * 7 + b][None] * line
    return sums


def tap_sums(shifted, read_line, rows, side, group, keep):
    for columns in ((0, 1, 2, 3), (4, 5, 6)):

        def body(g, sums):
            sums = [list(part) for part in sums]
            first = g * group
            lines = [read_line(first + k).reshape(side // 8, 8, 128) for k in range(group)]
            for n, b in enumerate(columns):
                for r in range(group + 6):
                    line = shifted[b, first + r]
                    for k in range(group):
                        if 0 <= r - k < 7:
                            sums[r - k][n] = sums[r - k][n] + jnp.sum(line * lines[k], axis=0)
            return tuple(tuple(part) for part in sums)

        zero = jnp.zeros((8, 128), jnp.float32)
        sums = lax.fori_loop(
            0, rows // group, body, tuple(tuple(zero for _ in columns) for _ in range(7))
        )
        for a in range(7):
            for n, b in enumerate(columns):
                keep(a * 7 + b, jnp.sum(sums[a][n], axis=0, keepdims=True))


class SmallSum:
    def __init__(self, place, out, work, inbox, send_sem, recv_sem):
        self.out, self.work, self.inbox = out, work, inbox
        self.send_sem, self.recv_sem = send_sem, recv_sem
        self.total = out.shape[0]
        self.halvings = (
            (place.to_core, place.core),
            (place.to_x, place.x),
            (place.to_y, place.y),
            (place.to_low, place.low),
            (place.to_high, place.high),
        )
        starts, size = [0], self.total
        for _, bit in self.halvings:
            size //= 2
            starts.append(starts[-1] + bit * size)
        self.starts = starts

    def rows(self, start, size):
        return pl.ds(pl.multiple_of(start, 8), size)

    def copy(self, k):
        if k < 5:
            partner, bit = self.halvings[k]
            size = self.total >> (k + 1)
            give = self.rows(self.starts[k] + (1 - bit) * size, size)
            source = self.work.at[give, :]
            target = self.inbox.at[pl.ds(self.total - 2 * size, size), :]
        else:
            partner, _ = self.halvings[9 - k]
            mine = self.rows(self.starts[10 - k], self.total >> (10 - k))
            source = target = self.out.at[mine, :]
        return remote(source, target, self.send_sem.at[k], self.recv_sem.at[k], partner)

    def step(self, k):
        if k > 0:
            self.copy(k - 1).wait_recv()
        if 1 <= k <= 5:
            size = self.total >> k
            at = self.rows(self.starts[k], size)
            summed = self.work[at, :] + self.inbox[pl.ds(self.total - 2 * size, size), :]
            if k < 5:
                self.work[at, :] = summed
            else:
                self.out[at, :] = summed
        if k < 10:
            self.copy(k).start()

    def wait_sends(self):
        for k in range(10):
            self.copy(k).wait_send()


def conv_back_kernel(shapes, pieces, plan, *refs):
    matrices = len(shapes)
    count = len(pieces)
    (dz, pick, place_map, padded, grad_low, tap_ref, small) = refs[:7]
    grads = refs[7 : 7 + matrices]
    refs = refs[7 + matrices :]
    map_out, small_out = refs[:2]
    outs = refs[2 : 2 + matrices]
    refs = refs[2 + matrices :]
    halving_refs = refs[: 6 * count + 3]
    refs = refs[6 * count + 3 :]
    field, shifted, taps, tap_out, work, inbox, gathered, small_send, small_recv = refs[:9]
    rim, corner, rim_in, row_in, corner_in, rim_sems = refs[9:]
    place = Place()
    halving = Halving(place, shapes, pieces, grads, outs, halving_refs)
    smalls = SmallSum(place, gathered, work, inbox, small_send, small_recv)
    slots_, cells, channels = dz.shape
    side = padded.shape[1] - 6
    blocks = channels // 128
    j = pl.program_id(0)
    s = j % 2
    c = (j // 2) % blocks
    columns = lanes(c * 128, 128)

    def slot(n):
        for i, k in plan["slots"].get(n, ()):
            if i == "small":
                smalls.step(k)
            else:
                halving.stages[k](i)

    @pl.when(j == 0)
    def _():
        greet(
            (
                place.to_core,
                place.to_x,
                place.to_y,
                place.to_low,
                place.to_high,
                place.to_across,
            )
        )

    rims = rim_copies(place, dz, rim, corner, rim_in, row_in, corner_in, rim_sems)

    for n in range(plan["steps"]):
        if n in plan["slots"] and n != 2 * blocks:
            pl.when(j == n)(partial(slot, n))

    @pl.when(j == 0)
    def _():
        for s in range(slots_):
            both = contract(pick[...], dz[s], 1, 0).astype(jnp.bfloat16)
            rim[s] = both[:RIM_ROWS]
            corner[s] = both[RIM_ROWS:]
        for copy in rims:
            copy.start()

    @pl.when(j < 2 * blocks)
    def _():
        shift_rows(lambda r: padded[0, r].astype(jnp.float32), shifted, side + 6, side)

        @pl.when(s == 0)
        def _():
            tap_out[c] = jnp.zeros(tap_out.shape[1:], jnp.float32)

        def read_line(i):
            line = dz[s, pl.ds(pl.multiple_of(i * side, 8), side), columns]
            return line.astype(jnp.float32)

        def keep(k, value):
            tap_out[c, k : k + 1, :] = tap_out[c, k : k + 1, :] + value

        tap_sums(shifted, read_line, side, side, 4, keep)

    @pl.when(j == 2 * blocks)
    def _():
        for q in range(blocks):
            work[q * 49 : (q + 1) * 49, :] = tap_out[q, :49, :]
        work[blocks * 49 :, :] = small[...]
        slot(2 * blocks)
        for copy in rims:
            copy.wait()
        for q in range(slots_):
            parts = jnp.concatenate([dz[q], rim_in[q], row_in[q], corner_in[q]], axis=0)
            whole = contract(place_map[...], parts, 1, 0).astype(jnp.bfloat16)
            field[q] = whole.reshape(field.shape[1:])

    @pl.when(j >= 2 * blocks)
    def _():
        fill_taps(tap_ref, taps, True)
        shift_rows(
            lambda r: field[s, r, :, columns].astype(jnp.float32), shifted, side + 6, side
        )

        def body(g, carry):
            for k, line in enumerate(seven_rows(shifted, taps, g * 4, 4, side)):
                at = pl.ds(pl.multiple_of((g * 4 + k) * side, 8), side)
                total = line.reshape(side, 128) + grad_low[0, at, :].astype(jnp.float32)
                map_out[0, at, :] = total.astype(jnp.bfloat16)
            return carry

        lax.fori_loop(0, side // 4, body, 0)

    @pl.when(j == plan["steps"] - 1)
    def _():
        for n in range(plan["steps"], plan["last"] + 1):
            slot(n)
        small_out[...] = gathered[...]
        halving.wait_sends()
        smalls.wait_sends()


def conv_back(
    dz, pick, place_map, padded, grad_low, tap_weights, small, grads
):
    slots, cells, channels = grad_low.shape
    rows, cols = padded.shape[1:3]
    side = rows - 6
    blocks = channels // 128
    steps = 4 * blocks
    shapes = [grad.shape for grad in grads]
    pieces = plan_pieces(shapes, 2_100_000)
    plan = spread_plan(len(pieces), steps, (1, 3), (7, 3), (4, 8, 12))
    for k in range(11):
        at = 2 * blocks + 2 * k
        plan["slots"].setdefault(at, []).append(("small", k))
        plan["last"] = max(plan["last"], at)
    any_space = pl.BlockSpec(memory_space=pl.ANY)

    def first_half(j):
        k = jnp.minimum(j, 2 * blocks - 1)
        return (k % 2, 0, 0, k // 2)

    def second_half(j):
        k = jnp.maximum(j - 2 * blocks, 0)
        return (k % 2, 0, k // 2)

    results = pl.pallas_call(
        partial(conv_back_kernel, shapes, pieces, plan),
        grid=(steps,),
        in_specs=[
            fixed_block(dz.shape),
            fixed_block(pick.shape),
            fixed_block(place_map.shape),
            pl.BlockSpec((1, rows, cols, 128), first_half),
            pl.BlockSpec((1, cells, 128), second_half),
            pl.BlockSpec((49, 128), lambda j: (0, jnp.maximum(j - 2 * blocks, 0) // 2)),
            fixed_block(small.shape),
        ]
        + [any_space] * len(grads),
        out_specs=[
            pl.BlockSpec((1, cells, 128), second_half),
            whole_block((SMALL_ROWS, 128)),
        ]
        + [whole_block(item.shape) for item in halving_outputs(shapes)],
        out_shape=[
            jax.ShapeDtypeStruct((slots, cells, channels), jnp.bfloat16),
            jax.ShapeDtypeStruct((SMALL_ROWS, 128), jnp.float32),
        ]
        + halving_outputs(shapes),
        scratch_shapes=halving_scratch(shapes, pieces)
        + [
            pltpu.VMEM((slots, rows, 32, channels), jnp.bfloat16),
            pltpu.VMEM((7, rows, side // 8, 8, 128), jnp.float32),
            pltpu.VMEM((49, 8, 128), jnp.float32),
            pltpu.VMEM((blocks, 56, 128), jnp.float32),
            pltpu.VMEM((SMALL_ROWS, 128), jnp.float32),
            pltpu.VMEM((SMALL_ROWS, 128), jnp.float32),
            pltpu.VMEM((SMALL_ROWS, 128), jnp.float32),
            pltpu.SemaphoreType.DMA((10,)),
            pltpu.SemaphoreType.DMA((10,)),
            pltpu.VMEM((slots, RIM_ROWS, channels), jnp.bfloat16),
            pltpu.VMEM((slots, CORNER_ROWS, channels), jnp.bfloat16),
            pltpu.VMEM((slots, RIM_ROWS, channels), jnp.bfloat16),
            pltpu.VMEM((slots, RIM_ROWS, channels), jnp.bfloat16),
            pltpu.VMEM((slots, CORNER_ROWS, channels), jnp.bfloat16),
            pltpu.SemaphoreType.DMA((6,)),
        ],
        compiler_params=pltpu.CompilerParams(
            collective_id=1, has_side_effects=True, vmem_limit_bytes=VMEM_LIMIT
        ),
        name="conv_back",
    )(
        dz,
        pick,
        place_map,
        padded,
        grad_low,
        tap_weights,
        small,
        *halving_operands(grads),
    )
    return results[0], results[1], results[2:]


def rim_maps(side):
    tile = lax.axis_index("tile")
    low, high = tile % 2, tile // 2
    cells = side * side
    row = jnp.arange(RIM_ROWS + CORNER_ROWS, dtype=jnp.int32)
    edge_col = jnp.where(low == 0, side - 3, 0)
    edge_row = jnp.where(high == 0, side - 3, 0)
    rim_from = (row % side) * side + edge_col + row // side
    k = row - RIM_ROWS
    corner_from = (edge_row + k // 3) * side + edge_col + k % 3
    source = jnp.where(
        row < 3 * side, rim_from, jnp.where((k >= 0) & (k < 9), corner_from, -1)
    )
    pick = (source[:, None] == jnp.arange(cells, dtype=jnp.int32)[None, :]).astype(jnp.bfloat16)
    at = jnp.arange((side + 6) * 32, dtype=jnp.int32)
    i, j = at // 32 - 3, at % 32 - 3
    inside_i, inside_j = (i >= 0) & (i < side), (j >= 0) & (j < side)
    beside_j = ((j < 0) & (low == 1)) | ((j >= side) & (j < side + 3) & (low == 0))
    beside_i = ((i < 0) & (high == 1)) | ((i >= side) & (high == 0))
    q = jnp.where(j < 0, j + 3, j - side)
    p = jnp.where(i < 0, i + 3, i - side)
    skip = jnp.where(high == 1, RIM_ROWS - 3 * side, 0)
    source = jnp.where(
        inside_i & inside_j,
        i * side + j,
        jnp.where(
            inside_i & beside_j,
            cells + q * side + i,
            jnp.where(
                beside_i & inside_j,
                cells + RIM_ROWS + skip + p * side + j,
                jnp.where(beside_i & beside_j, cells + 2 * RIM_ROWS + p * 3 + q, -1),
            ),
        ),
    )
    parts = cells + 2 * RIM_ROWS + CORNER_ROWS
    place_map = (source[:, None] == jnp.arange(parts, dtype=jnp.int32)[None, :]).astype(
        jnp.bfloat16
    )
    return pick, place_map


def slot_rims(place, s, source, rim, corner, rim_in, row_in, corner_in, sems):
    cells = source.shape[1]
    start = pl.multiple_of((1 - place.high) * (cells - RIM_ROWS), 16)
    row = source.at[s, pl.ds(start, RIM_ROWS), :]
    return (
        remote(rim.at[s], rim_in.at[s], sems.at[6 * s], sems.at[6 * s + 1], place.to_low),
        remote(row, row_in.at[s], sems.at[6 * s + 2], sems.at[6 * s + 3], place.to_high),
        remote(
            corner.at[s], corner_in.at[s], sems.at[6 * s + 4], sems.at[6 * s + 5], place.to_across
        ),
    )


def conv_front_kernel(
    source,
    pick,
    place_map,
    tap_ref,
    gain,
    norm_out,
    unit_out,
    scale_out,
    field_out,
    cells_ref,
    field,
    spread,
    shifted,
    taps,
    rim,
    corner,
    rim_in,
    row_in,
    corner_in,
    sems,
    load_sem,
    store_sem,
):
    place = Place()
    slots, cells, channels = cells_ref.shape
    blocks = channels // 128
    side = field.shape[1] - 6
    j = pl.program_id(0)
    s, c = j // blocks, j % blocks
    columns = lanes(c * 128, 128)
    low = jnp.bfloat16

    def rims(q):
        return slot_rims(place, q, cells_ref, rim, corner, rim_in, row_in, corner_in, sems)

    def select(q):
        both = contract(pick[...], cells_ref[q], 1, 0).astype(low)
        rim[q] = both[:RIM_ROWS]
        corner[q] = both[RIM_ROWS:]
        for copy in rims(q):
            copy.start()

    def store(q):
        return pltpu.make_async_copy(field.at[q], field_out.at[q], store_sem.at[q])

    def build(q):
        for copy in rims(q):
            copy.wait()
        parts = jnp.concatenate([cells_ref[q], rim_in[q], row_in[q], corner_in[q]], axis=0)
        whole = contract(place_map[...], parts, 1, 0).astype(low)
        field[q] = whole.reshape(field.shape[1:])
        store(q).start()

    @pl.when(j == 0)
    def _():
        load = pltpu.make_async_copy(source, cells_ref, load_sem)
        load.start()
        greet((place.to_low, place.to_high, place.to_across))
        load.wait()
        select(0)
        build(0)
        for q in range(1, slots):
            select(q)

    for q in range(1, slots):
        pl.when(j == q * blocks)(partial(build, q))

    fill_taps(tap_ref, taps, False)
    shift_rows(lambda r: field[s, r, :, columns].astype(jnp.float32), shifted, side + 6, side)

    def body(g, carry):
        for k, line in enumerate(seven_rows(shifted, taps, g * 4, 4, side)):
            at = pl.ds(pl.multiple_of((g * 4 + k) * side, 8), side)
            spread[c, at, :] = line.reshape(side, 128)
        return carry

    lax.fori_loop(0, side // 4, body, 0)

    @pl.when(c == blocks - 1)
    def _():
        gain_row = gain[...]
        chunk = 48

        def norm(n, carry):
            at = pl.ds(pl.multiple_of(n * chunk, 16), chunk)
            values = jnp.concatenate([spread[b, at, :] for b in range(blocks)], axis=1)
            unit, scale = norm_parts(values)
            unit_out[0, at, :] = unit.astype(low)
            norm_out[0, at, :] = (unit * gain_row).astype(low)
            scale_out[0, at, :] = scale
            return carry

        lax.fori_loop(0, cells // chunk, norm, 0)

    @pl.when(j == slots * blocks - 1)
    def _():
        for q in range(slots):
            store(q).wait()


def conv_front(source, pick, place_map, tap_weights, gain):
    slots, cells, channels = source.shape
    side = math.isqrt(cells)
    blocks = channels // 128
    low = jnp.bfloat16
    field_shape = (slots, side + 6, 32, channels)
    any_space = pl.BlockSpec(memory_space=pl.ANY)
    by_slot = lambda j: (j // blocks, 0, 0)
    return pl.pallas_call(
        conv_front_kernel,
        grid=(slots * blocks,),
        in_specs=[
            any_space,
            fixed_block(pick.shape),
            fixed_block(place_map.shape),
            pl.BlockSpec((49, 128), lambda j: (0, j % blocks)),
            fixed_block(gain.shape),
        ],
        out_specs=[
            pl.BlockSpec((1, cells, channels), by_slot),
            pl.BlockSpec((1, cells, channels), by_slot),
            pl.BlockSpec((1, cells, 1), by_slot),
            any_space,
        ],
        out_shape=[
            jax.ShapeDtypeStruct((slots, cells, channels), low),
            jax.ShapeDtypeStruct((slots, cells, channels), low),
            jax.ShapeDtypeStruct((slots, cells, 1), jnp.float32),
            jax.ShapeDtypeStruct(field_shape, low),
        ],
        scratch_shapes=[
            pltpu.VMEM((slots, cells, channels), low),
            pltpu.VMEM(field_shape, low),
            pltpu.VMEM((blocks, cells, 128), jnp.float32),
            pltpu.VMEM((7, side + 6, side // 8, 8, 128), jnp.float32),
            pltpu.VMEM((49, 8, 128), jnp.float32),
            pltpu.VMEM((slots, RIM_ROWS, channels), low),
            pltpu.VMEM((slots, CORNER_ROWS, channels), low),
            pltpu.VMEM((slots, RIM_ROWS, channels), low),
            pltpu.VMEM((slots, RIM_ROWS, channels), low),
            pltpu.VMEM((slots, CORNER_ROWS, channels), low),
            pltpu.SemaphoreType.DMA((6 * slots,)),
            pltpu.SemaphoreType.DMA,
            pltpu.SemaphoreType.DMA((slots,)),
        ],
        compiler_params=pltpu.CompilerParams(
            collective_id=2, has_side_effects=True, vmem_limit_bytes=VMEM_LIMIT
        ),
        name="conv_front",
    )(source, pick, place_map, tap_weights, gain)


def map_mlp_kernel(
    norm_low,
    source,
    w_expand,
    w_shrink,
    w_adapt,
    pool,
    live,
    wide_out,
    slope_out,
    map_out,
    pooled_out,
    adapted_out,
    total,
):
    j = pl.program_id(0)
    low = jnp.bfloat16
    rows, width = norm_low.shape[0], w_expand.shape[1]
    half = rows // 2
    for part in (pl.ds(0, half), pl.ds(half, half)):
        wide, slope = gelu_pair(contract(norm_low[part, :], w_expand[...], 1, 0))
        wide_out[part, :] = wide
        slope_out[part, :] = slope
        term = contract(wide, w_shrink[...], 1, 0)

        @pl.when(j == 0)
        def _():
            total[part, :] = source[part, :].astype(jnp.float32) + term

        @pl.when(j > 0)
        def _():
            total[part, :] = total[part, :] + term

    @pl.when(j == pl.num_programs(0) - 1)
    def _():
        slots, cells, _ = map_out.shape
        for s in range(slots):
            after = total[pl.ds(s * cells, cells), :].astype(low)
            keep = jnp.broadcast_to(live[s], after.shape) > 0
            map_out[s] = jnp.where(keep, after, jnp.zeros_like(after))
            pooled = contract(pool[...], after, 1, 0).astype(low)
            pooled_out[s] = pooled
            adapted_out[s] = contract(pooled, w_adapt[...], 1, 0).astype(low)


def map_mlp(norm_low, source, w_expand, w_shrink, w_adapt, pool, live):
    slots, cells, channels = source.shape
    hidden, width = w_expand.shape[1], 1024
    few, model = pool.shape[0], w_adapt.shape[1]
    low = jnp.bfloat16
    rows = slots * cells
    return pl.pallas_call(
        map_mlp_kernel,
        grid=(hidden // width,),
        in_specs=[
            fixed_block((rows, channels)),
            fixed_block((rows, channels)),
            pl.BlockSpec((channels, width), lambda j: (0, j)),
            pl.BlockSpec((width, channels), lambda j: (j, 0)),
            fixed_block(w_adapt.shape),
            fixed_block(pool.shape),
            fixed_block(live.shape),
        ],
        out_specs=[
            pl.BlockSpec((rows, width), lambda j: (0, j)),
            pl.BlockSpec((rows, width), lambda j: (0, j)),
            whole_block((slots, cells, channels)),
            whole_block((slots, few, channels)),
            whole_block((slots, few, model)),
        ],
        out_shape=[
            jax.ShapeDtypeStruct((rows, hidden), low),
            jax.ShapeDtypeStruct((rows, hidden), low),
            jax.ShapeDtypeStruct((slots, cells, channels), low),
            jax.ShapeDtypeStruct((slots, few, channels), low),
            jax.ShapeDtypeStruct((slots, few, model), low),
        ],
        scratch_shapes=[pltpu.VMEM((rows, channels), jnp.float32)],
        cost_estimate=pl.CostEstimate(
            flops=4 * rows * channels * hidden,
            bytes_accessed=45 * 10**6,
            transcendentals=2 * rows * hidden,
        ),
        compiler_params=pltpu.CompilerParams(vmem_limit_bytes=VMEM_LIMIT),
        name="map_mlp",
    )(norm_low.reshape(rows, channels), source.reshape(rows, channels), w_expand, w_shrink, w_adapt, pool, live)


def norm_parts(values):
    centre = values - jnp.mean(values, axis=-1, keepdims=True)
    scale = lax.rsqrt(jnp.mean(centre * centre, axis=-1, keepdims=True) + 1e-06)
    return centre * scale, scale


def norm_back(grad, unit, scale, gain):
    turned = grad * gain
    mean = jnp.mean(turned, axis=-1, keepdims=True)
    mean_unit = jnp.mean(turned * unit, axis=-1, keepdims=True)
    return scale * (turned - mean - unit * mean_unit)


def head_lanes(rows, odd):
    lane = lax.broadcasted_iota(jnp.int32, (rows, 2 * HDIM), 1)
    return (lane >= HDIM) if odd else (lane < HDIM)


def token_front_kernel(*refs):
    (own, everyone, gain_a, gain_m), refs = refs[:4], refs[4:]
    weights, refs = refs[:6], refs[6:]
    outs, refs = refs[:11], refs[11:]
    (own_out, all_out, q_out, k_out, v_out, p_out, o_out, x1_out, h_out, g_out, slope_out) = outs
    x2_out, refs = refs[0], refs[1:]
    buffers, sems = refs[:6], refs[6]
    copies = [
        pltpu.make_async_copy(weights[n], buffers[n], sems.at[n]) for n in range(6)
    ]
    for copy in copies:
        copy.start()
    low = jnp.bfloat16
    slots, count, width = own.shape
    total = everyone.shape[1]
    gain = gain_a[...]

    def norm_chunks(source, target, rows):
        def body(n, carry):
            at = pl.ds(pl.multiple_of(n * 48, 16), 48)
            unit, _ = norm_parts(source[at, :].astype(jnp.float32))
            target[at, :] = (unit * gain).astype(low)
            return carry

        lax.fori_loop(0, rows // 48, body, 0)

    for s in range(slots):
        norm_chunks(own.at[s], own_out.at[s], count)
        norm_chunks(everyone.at[s], all_out.at[s], total)
    copies[0].wait()
    for s in range(slots):
        q_out[s] = contract(own_out[s], buffers[0][...], 1, 0).astype(low)
    copies[1].wait()
    copies[2].wait()
    for s in range(slots):
        k_out[s] = contract(all_out[s], buffers[1][...], 1, 0).astype(low)
        v_out[s] = contract(all_out[s], buffers[2][...], 1, 0).astype(low)

    for s in range(slots):
        for pair in range(HEADS // 2):
            at = pl.ds(pair * 2 * HDIM, 2 * HDIM)
            q, k, v = q_out[s, :, at], k_out[s, :, at], v_out[s, :, at]
            mixed = []
            for odd in range(2):
                part = jnp.where(head_lanes(count, odd), q, jnp.zeros_like(q))
                scores = contract(part, k, 1, 1) * HDIM ** (-0.5)
                shifted = jnp.exp(scores - jnp.max(scores, axis=-1, keepdims=True))
                share = 1.0 / jnp.sum(shifted, axis=-1, keepdims=True)
                p = (shifted * share).astype(low)
                p_out[s * HEADS + 2 * pair + odd] = p
                mixed.append(contract(p, v, 1, 0))
            o_out[s, :, at] = jnp.where(head_lanes(count, 0), mixed[0], mixed[1]).astype(low)
    copies[3].wait()
    gain_two = gain_m[...]
    for s in range(slots):
        x1 = own[s].astype(jnp.float32) + contract(o_out[s], buffers[3][...], 1, 0)
        x1_out[s] = x1
        unit, _ = norm_parts(x1)
        h_out[s] = (unit * gain_two).astype(low)
    copies[4].wait()
    hidden = g_out.shape[2]
    for s in range(slots):
        for c in range(0, hidden, 768):
            at = pl.ds(c, 768)
            g_out[s, :, at], slope_out[s, :, at] = gelu_pair(
                contract(h_out[s], buffers[4][:, at], 1, 0)
            )
    copies[5].wait()
    for s in range(slots):
        x2_out[s] = x1_out[s] + contract(g_out[s], buffers[5][...], 1, 0)


def token_front(own, everyone, gain_attn, gain_mlp, weights):
    slots, count, width = own.shape
    total, hidden = everyone.shape[1], weights[4].shape[1]
    low, wide = jnp.bfloat16, jnp.float32
    shapes = [
        ((slots, count, width), low),
        ((slots, total, width), low),
        ((slots, count, width), low),
        ((slots, total, width), low),
        ((slots, total, width), low),
        ((slots * HEADS, count, total), low),
        ((slots, count, width), low),
        ((slots, count, width), wide),
        ((slots, count, width), low),
        ((slots, count, hidden), low),
        ((slots, count, hidden), low),
        ((slots, count, width), wide),
    ]
    in_vmem = pl.BlockSpec(memory_space=pltpu.VMEM)
    return pl.pallas_call(
        token_front_kernel,
        in_specs=[in_vmem] * 4 + [pl.BlockSpec(memory_space=pl.ANY)] * 6,
        out_specs=[in_vmem] * len(shapes),
        out_shape=[jax.ShapeDtypeStruct(shape, dtype) for shape, dtype in shapes],
        scratch_shapes=[pltpu.VMEM(weight.shape, low) for weight in weights]
        + [pltpu.SemaphoreType.DMA((6,))],
        cost_estimate=pl.CostEstimate(
            flops=9 * 10**9, bytes_accessed=30 * 10**6, transcendentals=3 * 10**6
        ),
        compiler_params=pltpu.CompilerParams(vmem_limit_bytes=VMEM_LIMIT),
        name="token_front",
    )(own, everyone, gain_attn, gain_mlp, *weights)


def token_back_kernel(*refs):
    (dx2, x1_ref, gain_m), refs = refs[:3], refs[3:]
    saved, refs = refs[:10], refs[10:]
    weights, refs = refs[:6], refs[6:]
    (up_out, down_out, q_out, k_out, v_out, o_out), refs = refs[:6], refs[6:]
    (dx1_out, da_own_out, da_all_out, gain_out), refs = refs[:4], refs[4:]
    kept, refs = refs[:10], refs[10:]
    buffers, refs = refs[:6], refs[6:]
    du, do, dq, dk, dv, sems, weight_sems = refs
    (own, everyone, q_all, k_all, v_all, p_all, o_all, h_all, g_all, slope_all) = kept
    order = (8, 9, 7, 6, 4, 5, 3, 2, 0, 1)
    saved_copies = [
        pltpu.make_async_copy(saved[n], kept[n], sems.at[n]) for n in range(10)
    ]
    weight_copies = [
        pltpu.make_async_copy(weights[n], buffers[n], weight_sems.at[n]) for n in range(6)
    ]
    weight_copies[5].start()
    for n in order[:3]:
        saved_copies[n].start()
    weight_copies[4].start()
    weight_copies[3].start()
    for n in order[3:]:
        saved_copies[n].start()
    for n in range(3):
        weight_copies[n].start()
    low = jnp.bfloat16
    slots, count, width = dx2.shape
    hidden = g_all.shape[2]
    gain = gain_m[...]
    flat = lambda ref: ref[...].reshape(-1, ref.shape[-1])
    grad_low = flat(dx2).astype(low)
    weight_copies[5].wait()
    for n in order[:3]:
        saved_copies[n].wait()
    for c in range(0, hidden, 768):
        at = pl.ds(c, 768)
        grad = contract(grad_low, buffers[5][at, :], 1, 1)
        slope = slope_all[:, :, at].reshape(-1, 768).astype(jnp.float32)
        du[:, at] = (grad * slope).astype(low)
        g = g_all[:, :, at].reshape(-1, 768)
        down_out[at, :] = contract(g, grad_low, 0, 0).astype(low)
        h = flat(h_all)
        up_out[:, at] = contract(h, du[:, at], 0, 0).astype(low)
    weight_copies[4].wait()
    dh = contract(du[...], buffers[4][...], 1, 1)
    unit, scale = norm_parts(flat(x1_ref))
    gain_out[...] = jnp.sum(dh * unit, axis=0, keepdims=True)
    dx1 = flat(dx2) + norm_back(dh, unit, scale, gain)
    dx1_out[...] = dx1.reshape(dx1_out.shape)
    dar = dx1.astype(low)
    weight_copies[3].wait()
    for n in order[3:]:
        saved_copies[n].wait()
    o_out[...] = contract(flat(o_all), dar, 0, 0).astype(low)
    do[...] = contract(dar, buffers[3][...], 1, 1).astype(low).reshape(do.shape)
    for s in range(slots):
        for pair in range(HEADS // 2):
            at = pl.ds(pair * 2 * HDIM, 2 * HDIM)
            q, k, v, grad = q_all[s, :, at], k_all[s, :, at], v_all[s, :, at], do[s, :, at]
            parts = []
            for odd in range(2):
                p = p_all[s * HEADS + 2 * pair + odd]
                mine = jnp.where(head_lanes(count, odd), grad, jnp.zeros_like(grad))
                dp = contract(mine, v, 1, 1)
                wide_p = p.astype(jnp.float32)
                row = jnp.sum(wide_p * dp, axis=-1, keepdims=True)
                ds = (wide_p * (dp - row)).astype(low)
                parts.append(
                    (contract(ds, k, 1, 0), contract(ds, q, 0, 0), contract(p, grad, 0, 0))
                )
            few, many = head_lanes(count, 0), head_lanes(k.shape[0], 0)
            root = HDIM ** (-0.5)
            dq[s, :, at] = (jnp.where(few, parts[0][0], parts[1][0]) * root).astype(low)
            dk[s, :, at] = (jnp.where(many, parts[0][1], parts[1][1]) * root).astype(low)
            dv[s, :, at] = jnp.where(many, parts[0][2], parts[1][2]).astype(low)
    for n in range(3):
        weight_copies[n].wait()
    q_out[...] = contract(flat(own), flat(dq), 0, 0).astype(low)
    k_out[...] = contract(flat(everyone), flat(dk), 0, 0).astype(low)
    v_out[...] = contract(flat(everyone), flat(dv), 0, 0).astype(low)
    for s in range(slots):
        da_own_out[s] = contract(dq[s], buffers[0][...], 1, 1)
        both = contract(dk[s], buffers[1][...], 1, 1) + contract(dv[s], buffers[2][...], 1, 1)
        da_all_out[s] = both.astype(low)


def token_back(dx2, x1, gain_mlp, saved, weights):
    slots, count, width = dx2.shape
    total, hidden = saved[1].shape[1], weights[4].shape[1]
    low, wide = jnp.bfloat16, jnp.float32
    shapes = [
        ((width, hidden), low),
        ((hidden, width), low),
        ((width, width), low),
        ((width, width), low),
        ((width, width), low),
        ((width, width), low),
        ((slots, count, width), wide),
        ((slots, count, width), wide),
        ((slots, total, width), low),
        ((1, width), wide),
    ]
    in_vmem = pl.BlockSpec(memory_space=pltpu.VMEM)
    any_space = pl.BlockSpec(memory_space=pl.ANY)
    return pl.pallas_call(
        token_back_kernel,
        in_specs=[in_vmem] * 3 + [any_space] * 16,
        out_specs=[in_vmem] * len(shapes),
        out_shape=[jax.ShapeDtypeStruct(shape, dtype) for shape, dtype in shapes],
        scratch_shapes=[pltpu.VMEM(item.shape, low) for item in saved]
        + [pltpu.VMEM(weight.shape, low) for weight in weights]
        + [
            pltpu.VMEM((slots * count, hidden), low),
            pltpu.VMEM((slots, count, width), low),
            pltpu.VMEM((slots, count, width), low),
            pltpu.VMEM((slots, total, width), low),
            pltpu.VMEM((slots, total, width), low),
            pltpu.SemaphoreType.DMA((10,)),
            pltpu.SemaphoreType.DMA((6,)),
        ],
        cost_estimate=pl.CostEstimate(
            flops=18 * 10**9, bytes_accessed=50 * 10**6, transcendentals=10**6
        ),
        compiler_params=pltpu.CompilerParams(vmem_limit_bytes=VMEM_LIMIT),
        name="token_back",
    )(dx2, x1, gain_mlp, *saved, *weights)


def chip_layout():
    return lax.axis_size("img") == 8 and lax.axis_size("tile") == 4


def sum_plain(grads, smalls):
    sums = []
    for grad in grads:
        part = lax.psum_scatter(grad, "img", scatter_dimension=0, tiled=True)
        part = lax.psum_scatter(part, "tile", scatter_dimension=1, tiled=True)
        sums.append(part.astype(jnp.float32))
    return sums, lax.psum(tuple(smalls), ("img", "tile"))


def map_back(
    grad_low,
    norm_low,
    wide_low,
    wide_slope,
    w_shrink,
    w_expand,
    unit_low,
    scale,
    gain,
    padded_map,
    taps,
    pick,
    place_map,
    grads,
    smalls,
):
    slots, cells, channels = grad_low.shape
    side = math.isqrt(cells)
    flat = (slots * cells, -1)
    if not chip_layout():
        wide_low = wide_low.reshape(slots, cells, -1)
        wide_slope = wide_slope.reshape(slots, cells, -1)
        w_shrink_grad = outer_sum(wide_low, grad_low)
        grad_wide_low = (project_back(grad_low, w_shrink) * wide_slope).astype(jnp.bfloat16)
        w_expand_grad = outer_sum(norm_low, grad_wide_low)
        back = project_back(grad_wide_low, w_expand)
        unit = unit_low.astype(jnp.float32)
        turned = back * gain
        gain_conv_grad = jnp.sum(back * unit, axis=(0, 1))
        grad_spread = scale * (
            turned
            - jnp.mean(turned, axis=-1, keepdims=True)
            - unit * jnp.mean(turned * unit, axis=-1, keepdims=True)
        )
        grad_spread = grad_spread.reshape(slots, side, side, channels)
        field = padded_map[:, :, : side + 6].astype(jnp.float32)
        taps_grad = jnp.stack(
            [
                jnp.sum(field[:, a : a + side, b : b + side] * grad_spread, axis=(0, 1, 2))
                for a in range(7)
                for b in range(7)
            ]
        )
        padded_grad = add_rims(grad_spread.astype(jnp.bfloat16), 3).astype(jnp.float32)
        moved = depthwise(padded_grad, taps[::-1], 3, 0).reshape(slots, cells, channels)
        map_grad = (grad_low.astype(jnp.float32) + moved).astype(jnp.bfloat16)
        sums, small_sums = sum_plain(
            tuple(grads) + (w_expand_grad, w_shrink_grad),
            tuple(smalls) + (gain_conv_grad, taps_grad),
        )
        return map_grad, sums, small_sums
    first, first_sums = map_mlp_back(
        grad_low.reshape(flat),
        norm_low.reshape(flat),
        wide_low.reshape(flat),
        wide_slope.reshape(flat),
        w_shrink,
        w_expand,
        unit_low.reshape(flat),
        scale.reshape(flat),
        gain.reshape(1, channels),
        grads,
    )
    w_shrink_grad, w_expand_grad, dz, gain_conv_grad = first
    smalls = tuple(smalls) + (gain_conv_grad.reshape(channels),)
    tap_rows = channels // 128 * 49
    packed = jnp.concatenate([part.reshape(-1, 128) for part in smalls])
    packed = jnp.pad(packed, ((0, SMALL_ROWS - tap_rows - packed.shape[0]), (0, 0)))
    map_grad, small, last_sums = conv_back(
        dz.reshape(grad_low.shape),
        pick,
        place_map,
        padded_map,
        grad_low,
        taps,
        packed,
        (w_expand_grad, w_shrink_grad),
    )
    small_sums, first_row = [], tap_rows
    for part in smalls:
        rows = part.size // 128
        small_sums.append(small[first_row : first_row + rows].reshape(part.shape))
        first_row += rows
    taps_grad = small[:tap_rows].reshape(-1, 49, 128).transpose(1, 0, 2).reshape(49, channels)
    small_sums.append(taps_grad)
    return map_grad, tuple(first_sums) + tuple(last_sums), small_sums


def local(
    vit_in,
    map_in,
    group_images,
    vit_grad_out,
    map_grad_out,
    w_query,
    w_key,
    w_value,
    w_out,
    w_up,
    w_down,
    w_expand,
    w_shrink,
    w_adapt,
    gain_attn,
    gain_mlp,
    gain_conv,
    dw_large,
    dw_small,
    gate_low,
    gate_high,
):
    slot_count = vit_in.shape[0]
    tok_side = math.isqrt(vit_in.shape[2])
    pix_side = math.isqrt(map_in.shape[2])
    channels = map_in.shape[3]
    model_width = vit_in.shape[3]
    live_mask = (
        (jnp.arange(slot_count, dtype=jnp.int32) < group_images[0])
        .astype(jnp.float32)
        .reshape(slot_count, 1, 1)
    )
    live_cells = live_mask.reshape(slot_count, 1, 1, 1)
    cells = pix_side * pix_side
    on_chips = chip_layout()
    own = vit_in[:, 0]
    tokens = own.astype(jnp.float32)
    gain_one = gain_attn.astype(jnp.float32)
    gain_two = gain_mlp.astype(jnp.float32)
    conv_gain = gain_conv.astype(jnp.float32)
    large_taps = dw_large.astype(jnp.float32)
    few = jnp.arange(tok_side * tok_side, dtype=jnp.int32)[:, None]
    cell = jnp.arange(cells, dtype=jnp.int32)[None, :]
    holder = cell // pix_side // 2 * tok_side + cell % pix_side // 2
    pool = jnp.where(holder == few, 0.25, 0.0).astype(jnp.bfloat16)
    if on_chips:
        pick, place_map = rim_maps(pix_side)
        conv_norm_low, conv_unit_low, conv_scale, padded_map = conv_front(
            map_in[:, 0], pick, place_map, large_taps, conv_gain.reshape(1, channels)
        )
        own_later, conv_norm_low = lax.optimization_barrier((own, conv_norm_low))
    else:
        pick, place_map = None, None
        own_later = own
        map_low = map_in[:, 0].reshape(slot_count, pix_side, pix_side, channels)
        padded_map = add_rims(map_low, 3)
        spread_map = depthwise(padded_map.astype(jnp.float32), large_taps, 3, 0)
        conv_unit, conv_scale = norm_parts(spread_map.reshape(slot_count, cells, channels))
        conv_norm_low = (conv_unit * conv_gain).astype(jnp.bfloat16)
        conv_unit_low = conv_unit.astype(jnp.bfloat16)
    own_all = lax.all_gather(own_later, "tile", axis=1, tiled=True)
    wide_low, wide_slope, map_result, pooled_low, adapted_low = map_mlp(
        conv_norm_low, map_in[:, 0], w_expand, w_shrink, w_adapt, pool, live_mask
    )
    token_weights = (w_query, w_key, w_value, w_out, w_up, w_down)
    front = token_front(
        own, own_all, gain_one.reshape(1, -1), gain_two.reshape(1, -1), token_weights
    )
    residual_one, residual_two = front[7], front[11]
    saved = front[:7] + front[8:11]
    adapted_low = adapted_low.reshape(slot_count, tok_side, tok_side, model_width)
    padded_small = add_rims(adapted_low, 1).astype(jnp.float32)
    merged_map, merged_pull = jax.vjp(
        partial(depthwise, radius=1, margin=0), padded_small, dw_small.astype(jnp.float32)
    )
    merged_tokens = merged_map.reshape(slot_count, tok_side * tok_side, model_width)
    vit_after, merging_pull = jax.vjp(
        merging,
        residual_two,
        merged_tokens,
        gate_low.astype(jnp.float32),
        gate_high.astype(jnp.float32),
    )
    vit_cotangent = vit_grad_out[:, 0].astype(jnp.float32) * live_mask
    map_cotangent = map_grad_out[:, 0].astype(jnp.float32) * live_mask
    grad_residual_two, grad_merged, gate_low_grad, gate_high_grad = merging_pull(vit_cotangent)
    grad_padded_small, dw_small_grad = merged_pull(
        grad_merged.reshape(slot_count, tok_side, tok_side, model_width)
    )
    grad_adapted_low = return_rims(grad_padded_small, 1).astype(jnp.bfloat16)
    grad_adapted_low = grad_adapted_low.reshape(slot_count, tok_side * tok_side, model_width)
    w_adapt_grad = outer_sum(pooled_low, grad_adapted_low)
    grad_pooled = project_back(grad_adapted_low, w_adapt).astype(jnp.bfloat16)
    grad_conv_low = (
        map_cotangent
        + jnp.einsum("pc,spk->sck", pool, grad_pooled, preferred_element_type=jnp.float32)
    ).astype(jnp.bfloat16)
    (
        w_up_grad,
        w_down_grad,
        w_query_grad,
        w_key_grad,
        w_value_grad,
        w_out_grad,
        grad_residual_one,
        grad_own,
        grad_everyone,
        gain_mlp_grad,
    ) = token_back(
        grad_residual_two, residual_one, gain_two.reshape(1, -1), saved, token_weights
    )
    gain_mlp_grad = gain_mlp_grad.reshape(model_width)
    grad_normed_one = grad_own + lax.psum_scatter(
        grad_everyone, "tile", scatter_dimension=1, tiled=True
    ).astype(jnp.float32)
    unit_one, scale_one = norm_parts(tokens)
    gain_attn_grad = jnp.sum(grad_normed_one * unit_one, axis=(0, 1))
    vit_in_grad = (
        grad_residual_one + norm_back(grad_normed_one, unit_one, scale_one, gain_one)
    ).astype(jnp.bfloat16)
    map_in_grad, matrix_sums, small_sums = map_back(
        grad_conv_low,
        conv_norm_low,
        wide_low,
        wide_slope,
        w_shrink,
        w_expand,
        conv_unit_low,
        conv_scale,
        conv_gain,
        padded_map,
        large_taps,
        pick,
        place_map,
        (
            w_up_grad,
            w_down_grad,
            w_adapt_grad,
            w_query_grad,
            w_key_grad,
            w_value_grad,
            w_out_grad,
        ),
        (gain_attn_grad, gain_mlp_grad, dw_small_grad, gate_low_grad, gate_high_grad),
    )
    vit_result = (vit_after * live_mask).astype(jnp.bfloat16)[:, None]
    return (
        vit_result,
        map_result[:, None],
        vit_in_grad[:, None],
        map_in_grad[:, None],
        matrix_sums[3],
        matrix_sums[4],
        matrix_sums[5],
        matrix_sums[6],
        matrix_sums[0],
        matrix_sums[1],
        matrix_sums[7],
        matrix_sums[8],
        matrix_sums[2],
        small_sums[0],
        small_sums[1],
        small_sums[5],
        small_sums[6],
        small_sums[2],
        small_sums[3],
        small_sums[4],
    )


def solution(mesh):
    in_specs = (
        P("img", "tile", None, None),
        P("img", "tile", None, None),
        P("img"),
        P("img", "tile", None, None),
        P("img", "tile", None, None),
        P(),
        P(),
        P(),
        P(),
        P(),
        P(),
        P(),
        P(),
        P(),
        P(),
        P(),
        P(),
        P(),
        P(),
        P(),
        P(),
    )
    out_specs = (
        P("img", "tile", None, None),
        P("img", "tile", None, None),
        P("img", "tile", None, None),
        P("img", "tile", None, None),
        P("img", "tile"),
        P("img", "tile"),
        P("img", "tile"),
        P("img", "tile"),
        P("img", "tile"),
        P("img", "tile"),
        P("img", "tile"),
        P("img", "tile"),
        P("img", "tile"),
        P(),
        P(),
        P(),
        P(),
        P(),
        P(),
        P(),
    )
    return jax.shard_map(local, mesh=mesh, in_specs=in_specs, out_specs=out_specs, check_vma=False)
```

```python
from functools import partial
import math

import jax
import jax.numpy as jnp
from jax import lax
from jax.experimental import pallas as pl
from jax.experimental.pallas import tpu as pltpu
from jax.sharding import PartitionSpec as P

HEADS = 12
HDIM = 64


highest = lax.Precision.HIGHEST


def swapped(array, axis, bit):
    return lax.ppermute(array, axis, [(i, i ^ 1 << bit) for i in range(lax.axis_size(axis))])


def gelu_pair(values):
    spread = 0.5 * (1.0 + lax.erf(values * 0.7071067811865476))
    bell = jnp.exp(-0.5 * values * values) * 0.3989422804014327
    return (values * spread).astype(jnp.bfloat16), (spread + values * bell).astype(jnp.bfloat16)


def depthwise(field_map, tap_weights, radius, margin):
    kernel_side = 2 * radius + 1
    channels = tap_weights.shape[1]
    kernel = tap_weights.reshape(kernel_side, kernel_side, 1, channels)
    return lax.conv_general_dilated(
        field_map,
        kernel,
        (1, 1),
        ((margin, margin), (margin, margin)),
        dimension_numbers=("NHWC", "HWIO", "NHWC"),
        feature_group_count=channels,
        precision=highest,
    )


def merging(residual_two, merged_tokens, gate_low, gate_high):
    gate_logit = jnp.sum(residual_two * gate_low, axis=-1, keepdims=True) + jnp.sum(
        merged_tokens * gate_high, axis=-1, keepdims=True
    )
    gate_value = 1.0 / (1.0 + jnp.exp(-gate_logit))
    return residual_two + gate_value * merged_tokens


def project_back(left_side, right_side):
    return jnp.einsum("...j,ij->...i", left_side, right_side, preferred_element_type=jnp.float32)


def outer_sum(left_side, right_side):
    flat_left = left_side.reshape(-1, left_side.shape[-1])
    flat_right = right_side.reshape(-1, right_side.shape[-1])
    return lax.dot_general(
        flat_left, flat_right, (((0,), (0,)), ((), ())), preferred_element_type=jnp.float32
    ).astype(jnp.bfloat16)


def add_rims(tile_field, radius):
    tile_place = lax.axis_index("tile")
    for which_bit in range(2):
        axis_dim = 2 - which_bit
        on_low = tile_place >> which_bit & 1 == 0
        side_len = tile_field.shape[axis_dim]
        upper_rim = lax.slice_in_dim(tile_field, side_len - radius, side_len, axis=axis_dim)
        lower_rim = lax.slice_in_dim(tile_field, 0, radius, axis=axis_dim)
        outgoing = jnp.where(on_low, upper_rim, lower_rim)
        incoming = swapped(outgoing, "tile", which_bit)
        blank_rim = jnp.zeros_like(incoming)
        tile_field = jnp.where(
            on_low,
            jnp.concatenate([blank_rim, tile_field, incoming], axis_dim),
            jnp.concatenate([incoming, tile_field, blank_rim], axis_dim),
        )
    return tile_field


def return_rims(grad_field, radius):
    tile_place = lax.axis_index("tile")
    for which_bit in (1, 0):
        axis_dim = 2 - which_bit
        on_low = tile_place >> which_bit & 1 == 0
        total_len = grad_field.shape[axis_dim]
        side_len = total_len - 2 * radius
        high_rim = lax.slice_in_dim(grad_field, total_len - radius, total_len, axis=axis_dim)
        low_rim = lax.slice_in_dim(grad_field, 0, radius, axis=axis_dim)
        outgoing = jnp.where(on_low, high_rim, low_rim)
        incoming = swapped(outgoing.astype(jnp.bfloat16), "tile", which_bit).astype(outgoing.dtype)
        core_part = lax.slice_in_dim(grad_field, radius, radius + side_len, axis=axis_dim)
        filler_shape = list(incoming.shape)
        filler_shape[axis_dim] = side_len - radius
        filler = jnp.zeros(filler_shape, jnp.float32)
        grad_field = core_part + jnp.where(
            on_low,
            jnp.concatenate([filler, incoming], axis_dim),
            jnp.concatenate([incoming, filler], axis_dim),
        )
    return grad_field


MESH = pl.DeviceIdType.MESH
VMEM_LIMIT = 62 << 20
COPIES = 8
SMALL_ROWS = 512
RIM_ROWS = 80
CORNER_ROWS = 16


def contract(left, right, left_axis, right_axis):
    return lax.dot_general(
        left,
        right,
        (((left_axis,), (right_axis,)), ((), ())),
        preferred_element_type=jnp.float32,
    )


def wide_sum(one, two):
    return one.astype(jnp.float32) + two.astype(jnp.float32)


def low_sum(one, two):
    return wide_sum(one, two).astype(jnp.bfloat16)


def row_loop(first, rows, width, step):
    count = rows // 16
    while count > 1 and (count * 16 * width > 65536 or rows % (count * 16)):
        count -= 1
    chunk = count * 16

    def body(q, carry):
        step(pl.ds(pl.multiple_of(first + q * chunk, 16), chunk))
        return carry

    if rows == chunk:
        body(0, 0)
    else:
        lax.fori_loop(0, rows // chunk, body, 0)


def lanes(start, size):
    return pl.ds(pl.multiple_of(start, 128), size)


class Place:
    def __init__(self):
        img = lax.axis_index("img")
        tile = lax.axis_index("tile")
        self.core, self.x, self.y = img % 2, (img // 2) % 2, img // 4
        self.low, self.high = tile % 2, tile // 2
        self.to_core = (img + 1 - 2 * self.core, tile)
        self.to_x = (img + 2 - 4 * self.x, tile)
        self.to_y = (img + 4 - 8 * self.y, tile)
        self.to_low = (img, tile + 1 - 2 * self.low)
        self.to_high = (img, tile + 2 - 4 * self.high)
        self.to_across = (img, 3 - tile)


def greet(partners):
    barrier = pltpu.get_barrier_semaphore()
    for partner in partners:
        pl.semaphore_signal(barrier, inc=1, device_id=partner, device_id_type=MESH)
    pl.semaphore_wait(barrier, len(partners))


def remote(source, target, send_sem, recv_sem, partner):
    return pltpu.make_async_remote_copy(
        src_ref=source,
        dst_ref=target,
        send_sem=send_sem,
        recv_sem=recv_sem,
        device_id=partner,
        device_id_type=MESH,
    )


def plan_pieces(shapes, piece_bytes):
    pieces = []
    for g, (height, width) in enumerate(shapes):
        rows = height // 8
        count = max(1, round(height * width * 2 / piece_bytes))
        while rows % (count * 32):
            count -= 1
        for p in range(count):
            pieces.append((g, p * (rows // count), rows // count))
    return pieces


def halving_scratch(shapes, pieces):
    count = len(pieces)

    def buffers(shape_of):
        return [
            pltpu.VMEM(shape_of(rows, shapes[g][1]), jnp.bfloat16) for g, _, rows in pieces
        ]

    scratch = buffers(lambda rows, width: (2, 2, rows, width))
    scratch += buffers(lambda rows, width: (2, 2, rows, width))
    scratch += buffers(lambda rows, width: (2, rows, width))
    scratch += buffers(lambda rows, width: (rows, width))
    scratch += buffers(lambda rows, width: (rows, width // 2))
    scratch += buffers(
        lambda rows, width: (rows, width // 4 if width % 512 == 0 else width // 2)
    )
    scratch += [
        pltpu.SemaphoreType.DMA((count * COPIES,)),
        pltpu.SemaphoreType.DMA((count * COPIES,)),
        pltpu.SemaphoreType.DMA((count,)),
    ]
    return scratch


class Halving:
    def __init__(self, place, shapes, pieces, grads, outs, scratch):
        count = len(pieces)
        self.place, self.shapes, self.pieces = place, shapes, pieces
        self.grads, self.outs = grads, outs
        self.own, self.half, self.quarter, self.eighth, self.pair, self.last = (
            scratch[k * count : (k + 1) * count] for k in range(6)
        )
        self.send_sem, self.recv_sem, self.own_sem = scratch[6 * count :]
        self.stages = (
            self.over_core,
            self.over_first,
            self.over_second,
            self.over_third,
            self.over_fourth,
            self.finish,
        )

    def narrow(self, i):
        return self.shapes[self.pieces[i][0]][1] % 512 != 0

    def copy(self, i, k):
        place = self.place
        g, first, rows = self.pieces[i]
        width = self.shapes[g][1] // 4
        half, quarter, eighth = self.half[i], self.quarter[i], self.eighth[i]
        pair, last = self.pair[i], self.last[i]
        part, cut = pl.ds(first, rows), rows // 2
        top, bottom = pl.ds(0, cut), pl.ds(cut, cut)
        if k == 0:
            ends = (self.grads[g].at[:, :, 1 - place.core, part, :], half, place.to_core)
        elif k == 1:
            ends = (half.at[:, 1 - place.x, top, :], quarter.at[:, top, :], place.to_x)
        elif k == 2:
            ends = (half.at[1 - place.y, :, bottom, :], quarter.at[:, bottom, :], place.to_y)
        elif k == 3:
            ends = (quarter.at[1 - place.y, top, :], eighth.at[top, :], place.to_y)
        elif k == 4:
            ends = (quarter.at[1 - place.x, bottom, :], eighth.at[bottom, :], place.to_x)
        elif k < 7 and not self.narrow(i):
            q = k - 5
            side = eighth.at[:, lanes((2 * q + 1 - place.low) * width, width)]
            ends = (side, pair.at[:, pl.ds(q * width, width)], place.to_low)
        elif k == 5:
            side = eighth.at[:, lanes((1 - place.high) * 2 * width, 2 * width)]
            ends = (side, pair, place.to_high)
        elif not self.narrow(i):
            ends = (pair.at[:, lanes((1 - place.high) * width, width)], last, place.to_high)
        else:
            ends = (pair, last, place.to_low)
        at = i * COPIES + k
        return remote(ends[0], ends[1], self.send_sem.at[at], self.recv_sem.at[at], ends[2])

    def own_copy(self, i):
        g, first, rows = self.pieces[i]
        mine = self.grads[g].at[:, :, self.place.core, pl.ds(first, rows), :]
        return pltpu.make_async_copy(mine, self.own[i], self.own_sem.at[i])

    def copies(self, i):
        return (0, 1, 2, 3, 4, 5, 7) if self.narrow(i) else (0, 1, 2, 3, 4, 5, 6, 7)

    def over_core(self, i):
        self.copy(i, 0).start()
        self.own_copy(i).start()

    def over_first(self, i):
        rows = self.pieces[i][2]
        half, own = self.half[i], self.own[i]
        self.copy(i, 0).wait_recv()
        self.own_copy(i).wait()
        for a in range(2):
            for b in range(2):

                def step(s, a=a, b=b):
                    half[a, b, s, :] = low_sum(half[a, b, s, :], own[a, b, s, :])

                row_loop(0, rows, half.shape[-1], step)
        self.copy(i, 1).start()
        self.copy(i, 2).start()

    def over_second(self, i):
        cut = self.pieces[i][2] // 2
        place, half, quarter = self.place, self.half[i], self.quarter[i]
        self.copy(i, 1).wait_recv()
        self.copy(i, 2).wait_recv()
        for a in range(2):

            def step_top(s, a=a):
                quarter[a, s, :] = low_sum(quarter[a, s, :], half[a, place.x, s, :])

            def step_bottom(s, a=a):
                quarter[a, s, :] = low_sum(quarter[a, s, :], half[place.y, a, s, :])

            row_loop(0, cut, quarter.shape[-1], step_top)
            row_loop(cut, cut, quarter.shape[-1], step_bottom)
        self.copy(i, 3).start()
        self.copy(i, 4).start()

    def over_third(self, i):
        cut = self.pieces[i][2] // 2
        place, quarter, eighth = self.place, self.quarter[i], self.eighth[i]
        self.copy(i, 3).wait_recv()
        self.copy(i, 4).wait_recv()

        def step_top(s):
            eighth[s, :] = low_sum(eighth[s, :], quarter[place.y, s, :])

        def step_bottom(s):
            eighth[s, :] = low_sum(eighth[s, :], quarter[place.x, s, :])

        row_loop(0, cut, eighth.shape[-1], step_top)
        row_loop(cut, cut, eighth.shape[-1], step_bottom)
        self.copy(i, 5).start()
        if not self.narrow(i):
            self.copy(i, 6).start()

    def over_fourth(self, i):
        g, _, rows = self.pieces[i]
        width = self.shapes[g][1] // 4
        place, eighth, pair = self.place, self.eighth[i], self.pair[i]
        self.copy(i, 5).wait_recv()
        if self.narrow(i):

            def step(s):
                kept = eighth[s, lanes(place.high * 2 * width, 2 * width)]
                pair[s, :] = low_sum(pair[s, :], kept)

        else:
            self.copy(i, 6).wait_recv()

            def step(s):
                for q in range(2):
                    at = slice(q * width, (q + 1) * width)
                    kept = eighth[s, lanes((2 * q + place.low) * width, width)]
                    pair[s, at] = low_sum(pair[s, at], kept)

        row_loop(0, rows, pair.shape[-1], step)
        self.copy(i, 7).start()

    def finish(self, i):
        g, first, rows = self.pieces[i]
        width = self.shapes[g][1] // 4
        place, pair, last, out = self.place, self.pair[i], self.last[i], self.outs[g]
        self.copy(i, 7).wait_recv()

        def step(s):
            at = pl.ds(pl.multiple_of(s.start + first, 16), s.size)
            if self.narrow(i):
                both = wide_sum(last[s, :], pair[s, :])
                out[at, :] = jnp.where(place.low == 0, both[:, :width], both[:, width:])
            else:
                kept = pair[s, lanes(place.high * width, width)]
                out[at, :] = wide_sum(last[s, :], kept)

        row_loop(0, rows, pair.shape[-1], step)

    def wait_sends(self):
        for i in range(len(self.pieces)):
            for k in self.copies(i):
                self.copy(i, k).wait_send()


def halving_operands(grads):
    return [grad.reshape(2, 2, 2, grad.shape[0] // 8, grad.shape[1]) for grad in grads]


def halving_outputs(shapes):
    return [
        jax.ShapeDtypeStruct((height // 8, width // 4), jnp.float32) for height, width in shapes
    ]


def whole_block(shape):
    return pl.BlockSpec(shape, lambda *_: (0,) * len(shape))


def fixed_block(shape):
    return pl.BlockSpec(shape, lambda *_: (0,) * len(shape), pipeline_mode=pl.Buffered(1))


def rim_copies(place, source, rim, corner, rim_in, row_in, corner_in, sems):
    cells = source.shape[1]
    start = pl.multiple_of((1 - place.high) * (cells - RIM_ROWS), 16)
    return (
        remote(rim, rim_in, sems.at[0], sems.at[1], place.to_low),
        remote(
            source.at[:, pl.ds(start, RIM_ROWS), :], row_in, sems.at[2], sems.at[3], place.to_high
        ),
        remote(corner, corner_in, sems.at[4], sems.at[5], place.to_across),
    )


def mlp_back_kernel(shapes, pieces, plan, *refs):
    matrices = len(shapes)
    count = len(pieces)
    grad_low, norm_low, wide, slope, w_shrink, w_expand, unit, scale, gain = refs[:9]
    grads = refs[9 : 9 + matrices]
    refs = refs[9 + matrices :]
    shrink_out, expand_out, dz_out, gain_out = refs[:4]
    outs = refs[4 : 4 + matrices]
    refs = refs[4 + matrices :]
    halving_refs = refs[: 6 * count + 3]
    refs = refs[6 * count + 3 :]
    norm_turned, back, dz, out_sem = refs[:4]
    buffers, result_buffers, in_sems, result_sems = refs[4:8], refs[8:10], refs[10], refs[11]
    place = Place()
    halving = Halving(place, shapes, pieces, grads, outs, halving_refs)
    steps = plan["steps"]
    j = pl.program_id(0)

    def slot(n):
        for i, k in plan["slots"].get(n, ()):
            halving.stages[k](i)

    def slots(odd):
        for n in range(steps):
            if plan["slots"].get(2 * n + odd):
                pl.when(j == n)(partial(slot, 2 * n + odd))

    width = plan["width"]

    def fetches(n):
        slot_, at = n % 2, lanes(n * width, width)
        parts = (wide.at[:, at], slope.at[:, at], w_shrink.at[at, :], w_expand.at[:, at])
        return [
            pltpu.make_async_copy(part, buffers[k].at[slot_], in_sems.at[slot_ * 4 + k])
            for k, part in enumerate(parts)
        ]

    def stores(n):
        slot_, at = n % 2, lanes(n * width, width)
        targets = (shrink_out.at[at, :], expand_out.at[:, at])
        return [
            pltpu.make_async_copy(
                result_buffers[k].at[slot_], target, result_sems.at[slot_ * 2 + k]
            )
            for k, target in enumerate(targets)
        ]

    @pl.when(j == 0)
    def _():
        for copy in fetches(0):
            copy.start(priority=1)
        greet(
            (
                place.to_core,
                place.to_x,
                place.to_y,
                place.to_low,
                place.to_high,
            )
        )

    @pl.when(j + 1 < steps)
    def _():
        for copy in fetches(j + 1):
            copy.start(priority=1)

    slots(0)

    @pl.when(j == 0)
    def _():
        norm_turned[...] = norm_low[...].T

    for copy in fetches(j):
        copy.wait()

    @pl.when(j >= 2)
    def _():
        for copy in stores(j - 2):
            copy.wait()

    now = j % 2
    grad_wide = contract(grad_low[...], buffers[2][now], 1, 1)
    grad_wide = (grad_wide * buffers[1][now].astype(jnp.float32)).astype(jnp.bfloat16)
    turned = contract(buffers[0][now], grad_low[...], 0, 0)
    result_buffers[0][now] = turned.astype(jnp.bfloat16)
    slots(1)
    turned = contract(norm_turned[...], grad_wide, 1, 0)
    result_buffers[1][now] = turned.astype(jnp.bfloat16)
    term = contract(grad_wide, buffers[3][now], 1, 1)
    for copy in stores(j):
        copy.start(priority=1)

    @pl.when(j == 0)
    def _():
        back[...] = term

    @pl.when(j > 0)
    def _():
        back[...] = back[...] + term

    @pl.when(j == steps - 1)
    def _():
        gain_row = gain[...]
        chunk = 48

        def body(q, sums):
            at = pl.ds(pl.multiple_of(q * chunk, 16), chunk)
            grad = back[at, :]
            n = unit[at, :].astype(jnp.float32)
            t = grad * gain_row
            mean_t = jnp.mean(t, axis=-1, keepdims=True)
            mean_tn = jnp.mean(t * n, axis=-1, keepdims=True)
            dz[at, :] = (scale[at, :] * (t - mean_t - n * mean_tn)).astype(jnp.bfloat16)
            return sums + jnp.sum((grad * n).reshape(chunk // 8, 8, -1), axis=0)

        sums = jnp.zeros((8, dz.shape[1]), jnp.float32)
        sums = lax.fori_loop(0, dz.shape[0] // chunk, body, sums)
        gain_out[...] = jnp.sum(sums, axis=0, keepdims=True)
        back_copy = pltpu.make_async_copy(dz, dz_out, out_sem)
        back_copy.start()
        for n in range(2 * steps, plan["last"] + 1):
            slot(n)
        back_copy.wait()
        for n in (steps - 2, steps - 1):
            for copy in stores(n):
                copy.wait()
        halving.wait_sends()


def spread_plan(count, steps, first, second, rest):
    slots = {0: [(i, 0) for i in range(count)]}
    last = 0
    for i in range(count):
        at = [int(first[0] + first[1] * i), int(second[0] + second[1] * i)]
        at += [at[1] + r for r in rest]
        for k, n in enumerate(at):
            slots.setdefault(n, []).append((i, k + 1))
        last = max(last, at[-1])
    for n in slots:
        slots[n].sort(key=lambda item: (-item[1], item[0]))
    return {"slots": slots, "last": last, "steps": steps}


def map_mlp_back(
    grad_low, norm_low, wide, slope, w_shrink, w_expand, unit, scale, gain, grads
):
    tokens, channels = grad_low.shape
    hidden = w_shrink.shape[0]
    width = 512
    steps = hidden // width
    shapes = [grad.shape for grad in grads]
    pieces = plan_pieces(shapes, 1_600_000)
    plan = spread_plan(len(pieces), steps, (1, 1.0), (4, 1.0), (2, 4, 6))
    plan["width"] = width
    low = jnp.bfloat16
    any_space = pl.BlockSpec(memory_space=pl.ANY)
    results = pl.pallas_call(
        partial(mlp_back_kernel, shapes, pieces, plan),
        grid=(steps,),
        in_specs=[
            fixed_block((tokens, channels)),
            fixed_block((tokens, channels)),
            any_space,
            any_space,
            any_space,
            any_space,
            fixed_block((tokens, channels)),
            fixed_block((tokens, 1)),
            fixed_block((1, channels)),
        ]
        + [any_space] * len(grads),
        out_specs=[
            any_space,
            any_space,
            any_space,
            whole_block((1, channels)),
        ]
        + [whole_block(item.shape) for item in halving_outputs(shapes)],
        out_shape=[
            jax.ShapeDtypeStruct((hidden, channels), low),
            jax.ShapeDtypeStruct((channels, hidden), low),
            jax.ShapeDtypeStruct((tokens, channels), low),
            jax.ShapeDtypeStruct((1, channels), jnp.float32),
        ]
        + halving_outputs(shapes),
        scratch_shapes=halving_scratch(shapes, pieces)
        + [
            pltpu.VMEM((channels, tokens), low),
            pltpu.VMEM((tokens, channels), jnp.float32),
            pltpu.VMEM((tokens, channels), low),
            pltpu.SemaphoreType.DMA,
            pltpu.VMEM((2, tokens, width), low),
            pltpu.VMEM((2, tokens, width), low),
            pltpu.VMEM((2, width, channels), low),
            pltpu.VMEM((2, channels, width), low),
            pltpu.VMEM((2, width, channels), low),
            pltpu.VMEM((2, channels, width), low),
            pltpu.SemaphoreType.DMA((8,)),
            pltpu.SemaphoreType.DMA((4,)),
        ],
        compiler_params=pltpu.CompilerParams(
            collective_id=0, has_side_effects=True, vmem_limit_bytes=VMEM_LIMIT
        ),
        name="map_mlp_back",
    )(
        grad_low,
        norm_low,
        wide,
        slope,
        w_shrink,
        w_expand,
        unit,
        scale,
        gain,
        *halving_operands(grads),
    )
    return results[:4], results[4:]


def shift_rows(read_row, shifted, rows, side):
    def body(r, carry):
        line = read_row(r)
        for b in range(7):
            shifted[b, r] = line[b : b + side].reshape(side // 8, 8, 128)
        return carry

    lax.fori_loop(0, rows, body, 0, unroll=2)


def fill_taps(tap_ref, taps, flip):
    for k in range(49):
        tap = tap_ref[48 - k if flip else k].reshape(1, 128)
        taps[k] = jnp.broadcast_to(tap, (8, 128))


def seven_rows(shifted, taps, first, group, side):
    sums = [jnp.zeros((side // 8, 8, 128), jnp.float32) for _ in range(group)]
    for b in range(7):
        for r in range(group + 6):
            line = shifted[b, first + r]
            for k in range(group):
                if 0 <= r - k < 7:
                    sums[k] = sums[k] + taps[(r - k) * 7 + b][None] * line
    return sums


def tap_sums(shifted, read_line, rows, side, group, keep):
    for columns in ((0, 1, 2, 3), (4, 5, 6)):

        def body(g, sums):
            sums = [list(part) for part in sums]
            first = g * group
            lines = [read_line(first + k).reshape(side // 8, 8, 128) for k in range(group)]
            for n, b in enumerate(columns):
                for r in range(group + 6):
                    line = shifted[b, first + r]
                    for k in range(group):
                        if 0 <= r - k < 7:
                            sums[r - k][n] = sums[r - k][n] + jnp.sum(line * lines[k], axis=0)
            return tuple(tuple(part) for part in sums)

        zero = jnp.zeros((8, 128), jnp.float32)
        sums = lax.fori_loop(
            0, rows // group, body, tuple(tuple(zero for _ in columns) for _ in range(7))
        )
        for a in range(7):
            for n, b in enumerate(columns):
                keep(a * 7 + b, jnp.sum(sums[a][n], axis=0, keepdims=True))


class SmallSum:
    def __init__(self, place, out, work, inbox, send_sem, recv_sem):
        self.out, self.work, self.inbox = out, work, inbox
        self.send_sem, self.recv_sem = send_sem, recv_sem
        self.total = out.shape[0]
        self.halvings = (
            (place.to_core, place.core),
            (place.to_x, place.x),
            (place.to_y, place.y),
            (place.to_low, place.low),
            (place.to_high, place.high),
        )
        starts, size = [0], self.total
        for _, bit in self.halvings:
            size //= 2
            starts.append(starts[-1] + bit * size)
        self.starts = starts

    def rows(self, start, size):
        return pl.ds(pl.multiple_of(start, 8), size)

    def copy(self, k):
        if k < 5:
            partner, bit = self.halvings[k]
            size = self.total >> (k + 1)
            give = self.rows(self.starts[k] + (1 - bit) * size, size)
            source = self.work.at[give, :]
            target = self.inbox.at[pl.ds(self.total - 2 * size, size), :]
        else:
            partner, _ = self.halvings[9 - k]
            mine = self.rows(self.starts[10 - k], self.total >> (10 - k))
            source = target = self.out.at[mine, :]
        return remote(source, target, self.send_sem.at[k], self.recv_sem.at[k], partner)

    def step(self, k):
        if k > 0:
            self.copy(k - 1).wait_recv()
        if 1 <= k <= 5:
            size = self.total >> k
            at = self.rows(self.starts[k], size)
            summed = self.work[at, :] + self.inbox[pl.ds(self.total - 2 * size, size), :]
            if k < 5:
                self.work[at, :] = summed
            else:
                self.out[at, :] = summed
        if k < 10:
            self.copy(k).start()

    def wait_sends(self):
        for k in range(10):
            self.copy(k).wait_send()


def conv_back_kernel(shapes, pieces, plan, *refs):
    matrices = len(shapes)
    count = len(pieces)
    (dz, pick, place_map, padded, grad_low, tap_ref, sides, one, two, gain) = refs[:10]
    grads = refs[10 : 10 + matrices]
    refs = refs[10 + matrices :]
    map_out, small_out = refs[:2]
    outs = refs[2 : 2 + matrices]
    refs = refs[2 + matrices :]
    halving_refs = refs[: 6 * count + 3]
    refs = refs[6 * count + 3 :]
    field, shifted, taps, tap_out, work, inbox, gathered, small_send, small_recv = refs[:9]
    rim, corner, rim_in, row_in, corner_in, rim_sems = refs[9:]
    place = Place()
    halving = Halving(place, shapes, pieces, grads, outs, halving_refs)
    smalls = SmallSum(place, gathered, work, inbox, small_send, small_recv)
    slots_, cells, channels = dz.shape
    side = padded.shape[1] - 6
    blocks = channels // 128
    j = pl.program_id(0)
    s = j % 2
    c = (j // 2) % blocks
    columns = lanes(c * 128, 128)

    def slot(n):
        for i, k in plan["slots"].get(n, ()):
            if i == "small":
                smalls.step(k)
            else:
                halving.stages[k](i)

    @pl.when(j == 0)
    def _():
        greet(
            (
                place.to_core,
                place.to_x,
                place.to_y,
                place.to_low,
                place.to_high,
                place.to_across,
            )
        )

    rims = rim_copies(place, dz, rim, corner, rim_in, row_in, corner_in, rim_sems)

    for n in range(plan["steps"]):
        if n in plan["slots"] and n != 2 * blocks:
            pl.when(j == n)(partial(slot, n))

    @pl.when(j == 0)
    def _():
        for s in range(slots_):
            both = contract(pick[...], dz[s], 1, 0).astype(jnp.bfloat16)
            rim[s] = both[:RIM_ROWS]
            corner[s] = both[RIM_ROWS:]
        for copy in rims:
            copy.start()

    @pl.when(j < 2 * blocks)
    def _():
        shift_rows(lambda r: padded[0, r].astype(jnp.float32), shifted, side + 6, side)

        @pl.when(s == 0)
        def _():
            tap_out[c] = jnp.zeros(tap_out.shape[1:], jnp.float32)

        def read_line(i):
            line = dz[s, pl.ds(pl.multiple_of(i * side, 8), side), columns]
            return line.astype(jnp.float32)

        def keep(k, value):
            tap_out[c, k : k + 1, :] = tap_out[c, k : k + 1, :] + value

        tap_sums(shifted, read_line, side, side, 4, keep)

    @pl.when(j == 2 * blocks)
    def _():
        for q in range(blocks):
            work[q * 49 : (q + 1) * 49, :] = tap_out[q, :49, :]
        base = blocks * 49
        work[base:, :] = jnp.zeros((SMALL_ROWS - base, 128), jnp.float32)
        for q in range(sides.shape[1] // 128):
            at = slice(q * 128, (q + 1) * 128)
            row = base + q * 16
            work[row : row + 11, :] = sides[:11, at]
            work[row + 11 : row + 12, :] = one[:, at]
            work[row + 12 : row + 13, :] = two[:, at]
        for q in range(blocks):
            row = base + sides.shape[1] // 8 + q
            work[row : row + 1, :] = gain[:, q * 128 : (q + 1) * 128]
        slot(2 * blocks)
        for copy in rims:
            copy.wait()
        for q in range(slots_):
            parts = jnp.concatenate([dz[q], rim_in[q], row_in[q], corner_in[q]], axis=0)
            whole = contract(place_map[...], parts, 1, 0).astype(jnp.bfloat16)
            field[q] = whole.reshape(field.shape[1:])

    @pl.when(j >= 2 * blocks)
    def _():
        fill_taps(tap_ref, taps, True)
        shift_rows(
            lambda r: field[s, r, :, columns].astype(jnp.float32), shifted, side + 6, side
        )

        def body(g, carry):
            for k, line in enumerate(seven_rows(shifted, taps, g * 4, 4, side)):
                at = pl.ds(pl.multiple_of((g * 4 + k) * side, 8), side)
                total = line.reshape(side, 128) + grad_low[0, at, :].astype(jnp.float32)
                map_out[0, at, :] = total.astype(jnp.bfloat16)
            return carry

        lax.fori_loop(0, side // 4, body, 0)

    @pl.when(j == plan["steps"] - 1)
    def _():
        for n in range(plan["steps"], plan["last"] + 1):
            slot(n)
        small_out[...] = gathered[...]
        halving.wait_sends()
        smalls.wait_sends()


def conv_back(
    dz, pick, place_map, padded, grad_low, tap_weights, smalls, grads
):
    slots, cells, channels = grad_low.shape
    rows, cols = padded.shape[1:3]
    side = rows - 6
    blocks = channels // 128
    steps = 4 * blocks
    shapes = [grad.shape for grad in grads]
    pieces = plan_pieces(shapes, 2_100_000)
    plan = spread_plan(len(pieces), steps, (1, 3), (7, 3), (4, 8, 12))
    for k in range(11):
        at = 2 * blocks + 2 * k
        plan["slots"].setdefault(at, []).append(("small", k))
        plan["last"] = max(plan["last"], at)
    any_space = pl.BlockSpec(memory_space=pl.ANY)

    def first_half(j):
        k = jnp.minimum(j, 2 * blocks - 1)
        return (k % 2, 0, 0, k // 2)

    def second_half(j):
        k = jnp.maximum(j - 2 * blocks, 0)
        return (k % 2, 0, k // 2)

    results = pl.pallas_call(
        partial(conv_back_kernel, shapes, pieces, plan),
        grid=(steps,),
        in_specs=[
            fixed_block(dz.shape),
            fixed_block(pick.shape),
            fixed_block(place_map.shape),
            pl.BlockSpec((1, rows, cols, 128), first_half),
            pl.BlockSpec((1, cells, 128), second_half),
            pl.BlockSpec((49, 128), lambda j: (0, jnp.maximum(j - 2 * blocks, 0) // 2)),
        ]
        + [fixed_block(item.shape) for item in smalls]
        + [any_space] * len(grads),
        out_specs=[
            pl.BlockSpec((1, cells, 128), second_half),
            whole_block((SMALL_ROWS, 128)),
        ]
        + [whole_block(item.shape) for item in halving_outputs(shapes)],
        out_shape=[
            jax.ShapeDtypeStruct((slots, cells, channels), jnp.bfloat16),
            jax.ShapeDtypeStruct((SMALL_ROWS, 128), jnp.float32),
        ]
        + halving_outputs(shapes),
        scratch_shapes=halving_scratch(shapes, pieces)
        + [
            pltpu.VMEM((slots, rows, 32, channels), jnp.bfloat16),
            pltpu.VMEM((7, rows, side // 8, 8, 128), jnp.float32),
            pltpu.VMEM((49, 8, 128), jnp.float32),
            pltpu.VMEM((blocks, 56, 128), jnp.float32),
            pltpu.VMEM((SMALL_ROWS, 128), jnp.float32),
            pltpu.VMEM((SMALL_ROWS, 128), jnp.float32),
            pltpu.VMEM((SMALL_ROWS, 128), jnp.float32),
            pltpu.SemaphoreType.DMA((10,)),
            pltpu.SemaphoreType.DMA((10,)),
            pltpu.VMEM((slots, RIM_ROWS, channels), jnp.bfloat16),
            pltpu.VMEM((slots, CORNER_ROWS, channels), jnp.bfloat16),
            pltpu.VMEM((slots, RIM_ROWS, channels), jnp.bfloat16),
            pltpu.VMEM((slots, RIM_ROWS, channels), jnp.bfloat16),
            pltpu.VMEM((slots, CORNER_ROWS, channels), jnp.bfloat16),
            pltpu.SemaphoreType.DMA((6,)),
        ],
        compiler_params=pltpu.CompilerParams(
            collective_id=1, has_side_effects=True, vmem_limit_bytes=VMEM_LIMIT
        ),
        name="conv_back",
    )(
        dz,
        pick,
        place_map,
        padded,
        grad_low,
        tap_weights,
        *smalls,
        *halving_operands(grads),
    )
    return results[0], results[1], results[2:]


def rim_maps(side):
    tile = lax.axis_index("tile")
    low, high = tile % 2, tile // 2
    cells = side * side
    row = jnp.arange(RIM_ROWS + CORNER_ROWS, dtype=jnp.int32)
    edge_col = jnp.where(low == 0, side - 3, 0)
    edge_row = jnp.where(high == 0, side - 3, 0)
    rim_from = (row % side) * side + edge_col + row // side
    k = row - RIM_ROWS
    corner_from = (edge_row + k // 3) * side + edge_col + k % 3
    source = jnp.where(
        row < 3 * side, rim_from, jnp.where((k >= 0) & (k < 9), corner_from, -1)
    )
    pick = (source[:, None] == jnp.arange(cells, dtype=jnp.int32)[None, :]).astype(jnp.bfloat16)
    at = jnp.arange((side + 6) * 32, dtype=jnp.int32)
    i, j = at // 32 - 3, at % 32 - 3
    inside_i, inside_j = (i >= 0) & (i < side), (j >= 0) & (j < side)
    beside_j = ((j < 0) & (low == 1)) | ((j >= side) & (j < side + 3) & (low == 0))
    beside_i = ((i < 0) & (high == 1)) | ((i >= side) & (high == 0))
    q = jnp.where(j < 0, j + 3, j - side)
    p = jnp.where(i < 0, i + 3, i - side)
    skip = jnp.where(high == 1, RIM_ROWS - 3 * side, 0)
    source = jnp.where(
        inside_i & inside_j,
        i * side + j,
        jnp.where(
            inside_i & beside_j,
            cells + q * side + i,
            jnp.where(
                beside_i & inside_j,
                cells + RIM_ROWS + skip + p * side + j,
                jnp.where(beside_i & beside_j, cells + 2 * RIM_ROWS + p * 3 + q, -1),
            ),
        ),
    )
    parts = cells + 2 * RIM_ROWS + CORNER_ROWS
    place_map = (source[:, None] == jnp.arange(parts, dtype=jnp.int32)[None, :]).astype(
        jnp.bfloat16
    )
    return pick, place_map


def slot_rims(place, s, source, rim, corner, rim_in, row_in, corner_in, sems):
    cells = source.shape[1]
    start = pl.multiple_of((1 - place.high) * (cells - RIM_ROWS), 16)
    row = source.at[s, pl.ds(start, RIM_ROWS), :]
    return (
        remote(rim.at[s], rim_in.at[s], sems.at[6 * s], sems.at[6 * s + 1], place.to_low),
        remote(row, row_in.at[s], sems.at[6 * s + 2], sems.at[6 * s + 3], place.to_high),
        remote(
            corner.at[s], corner_in.at[s], sems.at[6 * s + 4], sems.at[6 * s + 5], place.to_across
        ),
    )


def conv_front_kernel(
    source,
    pick,
    place_map,
    tap_ref,
    gain,
    norm_out,
    unit_out,
    scale_out,
    field_out,
    cells_ref,
    field,
    spread,
    shifted,
    taps,
    rim,
    corner,
    rim_in,
    row_in,
    corner_in,
    sems,
    load_sem,
    store_sem,
):
    place = Place()
    slots, cells, channels = cells_ref.shape
    blocks = channels // 128
    side = field.shape[1] - 6
    j = pl.program_id(0)
    s, c = j // blocks, j % blocks
    columns = lanes(c * 128, 128)
    low = jnp.bfloat16

    def rims(q):
        return slot_rims(place, q, cells_ref, rim, corner, rim_in, row_in, corner_in, sems)

    def select(q):
        both = contract(pick[...], cells_ref[q], 1, 0).astype(low)
        rim[q] = both[:RIM_ROWS]
        corner[q] = both[RIM_ROWS:]
        for copy in rims(q):
            copy.start()

    def store(q):
        return pltpu.make_async_copy(field.at[q], field_out.at[q], store_sem.at[q])

    def build(q):
        for copy in rims(q):
            copy.wait()
        parts = jnp.concatenate([cells_ref[q], rim_in[q], row_in[q], corner_in[q]], axis=0)
        whole = contract(place_map[...], parts, 1, 0).astype(low)
        field[q] = whole.reshape(field.shape[1:])
        store(q).start()

    @pl.when(j == 0)
    def _():
        load = pltpu.make_async_copy(source, cells_ref, load_sem)
        load.start()
        greet((place.to_low, place.to_high, place.to_across))
        load.wait()
        select(0)
        build(0)
        for q in range(1, slots):
            select(q)

    for q in range(1, slots):
        pl.when(j == q * blocks)(partial(build, q))

    fill_taps(tap_ref, taps, False)
    shift_rows(lambda r: field[s, r, :, columns].astype(jnp.float32), shifted, side + 6, side)

    def body(g, carry):
        for k, line in enumerate(seven_rows(shifted, taps, g * 4, 4, side)):
            at = pl.ds(pl.multiple_of((g * 4 + k) * side, 8), side)
            spread[c, at, :] = line.reshape(side, 128)
        return carry

    lax.fori_loop(0, side // 4, body, 0)

    @pl.when(c == blocks - 1)
    def _():
        gain_row = gain[...]
        chunk = 48

        def norm(n, carry):
            at = pl.ds(pl.multiple_of(n * chunk, 16), chunk)
            values = jnp.concatenate([spread[b, at, :] for b in range(blocks)], axis=1)
            unit, scale = norm_parts(values)
            unit_out[0, at, :] = unit.astype(low)
            norm_out[0, at, :] = (unit * gain_row).astype(low)
            scale_out[0, at, :] = scale
            return carry

        lax.fori_loop(0, cells // chunk, norm, 0)

    @pl.when(j == slots * blocks - 1)
    def _():
        for q in range(slots):
            store(q).wait()


def conv_front(source, pick, place_map, tap_weights, gain):
    slots, cells, channels = source.shape
    side = math.isqrt(cells)
    blocks = channels // 128
    low = jnp.bfloat16
    field_shape = (slots, side + 6, 32, channels)
    any_space = pl.BlockSpec(memory_space=pl.ANY)
    by_slot = lambda j: (j // blocks, 0, 0)
    return pl.pallas_call(
        conv_front_kernel,
        grid=(slots * blocks,),
        in_specs=[
            any_space,
            fixed_block(pick.shape),
            fixed_block(place_map.shape),
            pl.BlockSpec((49, 128), lambda j: (0, j % blocks)),
            fixed_block(gain.shape),
        ],
        out_specs=[
            pl.BlockSpec((1, cells, channels), by_slot),
            pl.BlockSpec((1, cells, channels), by_slot),
            pl.BlockSpec((1, cells, 1), by_slot),
            any_space,
        ],
        out_shape=[
            jax.ShapeDtypeStruct((slots, cells, channels), low),
            jax.ShapeDtypeStruct((slots, cells, channels), low),
            jax.ShapeDtypeStruct((slots, cells, 1), jnp.float32),
            jax.ShapeDtypeStruct(field_shape, low),
        ],
        scratch_shapes=[
            pltpu.VMEM((slots, cells, channels), low),
            pltpu.VMEM(field_shape, low),
            pltpu.VMEM((blocks, cells, 128), jnp.float32),
            pltpu.VMEM((7, side + 6, side // 8, 8, 128), jnp.float32),
            pltpu.VMEM((49, 8, 128), jnp.float32),
            pltpu.VMEM((slots, RIM_ROWS, channels), low),
            pltpu.VMEM((slots, CORNER_ROWS, channels), low),
            pltpu.VMEM((slots, RIM_ROWS, channels), low),
            pltpu.VMEM((slots, RIM_ROWS, channels), low),
            pltpu.VMEM((slots, CORNER_ROWS, channels), low),
            pltpu.SemaphoreType.DMA((6 * slots,)),
            pltpu.SemaphoreType.DMA,
            pltpu.SemaphoreType.DMA((slots,)),
        ],
        compiler_params=pltpu.CompilerParams(
            collective_id=2, has_side_effects=True, vmem_limit_bytes=VMEM_LIMIT
        ),
        name="conv_front",
    )(source, pick, place_map, tap_weights, gain)


def map_mlp_kernel(
    norm_low,
    source,
    w_expand,
    w_shrink,
    w_adapt,
    pool,
    live,
    wide_out,
    slope_out,
    map_out,
    pooled_out,
    adapted_out,
    total,
):
    j = pl.program_id(0)
    low = jnp.bfloat16
    rows, width = norm_low.shape[0], w_expand.shape[1]
    half = rows // 2
    for part in (pl.ds(0, half), pl.ds(half, half)):
        wide, slope = gelu_pair(contract(norm_low[part, :], w_expand[...], 1, 0))
        wide_out[part, :] = wide
        slope_out[part, :] = slope
        term = contract(wide, w_shrink[...], 1, 0)

        @pl.when(j == 0)
        def _():
            total[part, :] = source[part, :].astype(jnp.float32) + term

        @pl.when(j > 0)
        def _():
            total[part, :] = total[part, :] + term

    @pl.when(j == pl.num_programs(0) - 1)
    def _():
        slots, cells, _ = map_out.shape
        for s in range(slots):
            after = total[pl.ds(s * cells, cells), :].astype(low)
            keep = jnp.broadcast_to(live[s], after.shape) > 0
            map_out[s] = jnp.where(keep, after, jnp.zeros_like(after))
            pooled = contract(pool[...], after, 1, 0).astype(low)
            pooled_out[s] = pooled
            adapted_out[s] = contract(pooled, w_adapt[...], 1, 0).astype(low)


def map_mlp(norm_low, source, w_expand, w_shrink, w_adapt, pool, live):
    slots, cells, channels = source.shape
    hidden, width = w_expand.shape[1], 1024
    few, model = pool.shape[0], w_adapt.shape[1]
    low = jnp.bfloat16
    rows = slots * cells
    return pl.pallas_call(
        map_mlp_kernel,
        grid=(hidden // width,),
        in_specs=[
            fixed_block((rows, channels)),
            fixed_block((rows, channels)),
            pl.BlockSpec((channels, width), lambda j: (0, j)),
            pl.BlockSpec((width, channels), lambda j: (j, 0)),
            fixed_block(w_adapt.shape),
            fixed_block(pool.shape),
            fixed_block(live.shape),
        ],
        out_specs=[
            pl.BlockSpec((rows, width), lambda j: (0, j)),
            pl.BlockSpec((rows, width), lambda j: (0, j)),
            whole_block((slots, cells, channels)),
            whole_block((slots, few, channels)),
            whole_block((slots, few, model)),
        ],
        out_shape=[
            jax.ShapeDtypeStruct((rows, hidden), low),
            jax.ShapeDtypeStruct((rows, hidden), low),
            jax.ShapeDtypeStruct((slots, cells, channels), low),
            jax.ShapeDtypeStruct((slots, few, channels), low),
            jax.ShapeDtypeStruct((slots, few, model), low),
        ],
        scratch_shapes=[pltpu.VMEM((rows, channels), jnp.float32)],
        cost_estimate=pl.CostEstimate(
            flops=4 * rows * channels * hidden,
            bytes_accessed=45 * 10**6,
            transcendentals=2 * rows * hidden,
        ),
        compiler_params=pltpu.CompilerParams(vmem_limit_bytes=VMEM_LIMIT),
        name="map_mlp",
    )(norm_low.reshape(rows, channels), source.reshape(rows, channels), w_expand, w_shrink, w_adapt, pool, live)


def norm_parts(values):
    centre = values - jnp.mean(values, axis=-1, keepdims=True)
    scale = lax.rsqrt(jnp.mean(centre * centre, axis=-1, keepdims=True) + 1e-06)
    return centre * scale, scale


def norm_back(grad, unit, scale, gain):
    turned = grad * gain
    mean = jnp.mean(turned, axis=-1, keepdims=True)
    mean_unit = jnp.mean(turned * unit, axis=-1, keepdims=True)
    return scale * (turned - mean - unit * mean_unit)


def head_lanes(rows, odd):
    lane = lax.broadcasted_iota(jnp.int32, (rows, 2 * HDIM), 1)
    return (lane >= HDIM) if odd else (lane < HDIM)


def token_front_kernel(*refs):
    (own, everyone, gain_a, gain_m), refs = refs[:4], refs[4:]
    weights, refs = refs[:6], refs[6:]
    outs, refs = refs[:11], refs[11:]
    (own_out, all_out, q_out, k_out, v_out, p_out, o_out, x1_out, h_out, g_out, slope_out) = outs
    x2_out, refs = refs[0], refs[1:]
    buffers, sems = refs[:6], refs[6]
    copies = [
        pltpu.make_async_copy(weights[n], buffers[n], sems.at[n]) for n in range(6)
    ]
    for copy in copies:
        copy.start()
    low = jnp.bfloat16
    slots, count, width = own.shape
    total = everyone.shape[1]
    gain = gain_a[...]

    def norm_chunks(source, target, rows):
        def body(n, carry):
            at = pl.ds(pl.multiple_of(n * 48, 16), 48)
            unit, _ = norm_parts(source[at, :].astype(jnp.float32))
            target[at, :] = (unit * gain).astype(low)
            return carry

        lax.fori_loop(0, rows // 48, body, 0)

    for s in range(slots):
        norm_chunks(own.at[s], own_out.at[s], count)
        norm_chunks(everyone.at[s], all_out.at[s], total)
    copies[0].wait()
    for s in range(slots):
        q_out[s] = contract(own_out[s], buffers[0][...], 1, 0).astype(low)
    copies[1].wait()
    copies[2].wait()
    for s in range(slots):
        k_out[s] = contract(all_out[s], buffers[1][...], 1, 0).astype(low)
        v_out[s] = contract(all_out[s], buffers[2][...], 1, 0).astype(low)

    for s in range(slots):
        for pair in range(HEADS // 2):
            at = pl.ds(pair * 2 * HDIM, 2 * HDIM)
            q, k, v = q_out[s, :, at], k_out[s, :, at], v_out[s, :, at]
            mixed = []
            for odd in range(2):
                part = jnp.where(head_lanes(count, odd), q, jnp.zeros_like(q))
                scores = contract(part, k, 1, 1) * HDIM ** (-0.5)
                shifted = jnp.exp(scores - jnp.max(scores, axis=-1, keepdims=True))
                share = 1.0 / jnp.sum(shifted, axis=-1, keepdims=True)
                p = (shifted * share).astype(low)
                p_out[s * HEADS + 2 * pair + odd] = p
                mixed.append(contract(p, v, 1, 0))
            o_out[s, :, at] = jnp.where(head_lanes(count, 0), mixed[0], mixed[1]).astype(low)
    copies[3].wait()
    gain_two = gain_m[...]
    for s in range(slots):
        x1 = own[s].astype(jnp.float32) + contract(o_out[s], buffers[3][...], 1, 0)
        x1_out[s] = x1
        unit, _ = norm_parts(x1)
        h_out[s] = (unit * gain_two).astype(low)
    copies[4].wait()
    hidden = g_out.shape[2]
    for s in range(slots):
        for c in range(0, hidden, 768):
            at = pl.ds(c, 768)
            g_out[s, :, at], slope_out[s, :, at] = gelu_pair(
                contract(h_out[s], buffers[4][:, at], 1, 0)
            )
    copies[5].wait()
    for s in range(slots):
        x2_out[s] = x1_out[s] + contract(g_out[s], buffers[5][...], 1, 0)


def token_front(own, everyone, gain_attn, gain_mlp, weights):
    slots, count, width = own.shape
    total, hidden = everyone.shape[1], weights[4].shape[1]
    low, wide = jnp.bfloat16, jnp.float32
    shapes = [
        ((slots, count, width), low),
        ((slots, total, width), low),
        ((slots, count, width), low),
        ((slots, total, width), low),
        ((slots, total, width), low),
        ((slots * HEADS, count, total), low),
        ((slots, count, width), low),
        ((slots, count, width), wide),
        ((slots, count, width), low),
        ((slots, count, hidden), low),
        ((slots, count, hidden), low),
        ((slots, count, width), wide),
    ]
    in_vmem = pl.BlockSpec(memory_space=pltpu.VMEM)
    return pl.pallas_call(
        token_front_kernel,
        in_specs=[in_vmem] * 4 + [pl.BlockSpec(memory_space=pl.ANY)] * 6,
        out_specs=[in_vmem] * len(shapes),
        out_shape=[jax.ShapeDtypeStruct(shape, dtype) for shape, dtype in shapes],
        scratch_shapes=[pltpu.VMEM(weight.shape, low) for weight in weights]
        + [pltpu.SemaphoreType.DMA((6,))],
        cost_estimate=pl.CostEstimate(
            flops=9 * 10**9, bytes_accessed=30 * 10**6, transcendentals=3 * 10**6
        ),
        compiler_params=pltpu.CompilerParams(vmem_limit_bytes=VMEM_LIMIT),
        name="token_front",
    )(own, everyone, gain_attn, gain_mlp, *weights)


def token_back_kernel(*refs):
    (dx2, x1_ref, gain_m), refs = refs[:3], refs[3:]
    saved, refs = refs[:10], refs[10:]
    weights, refs = refs[:6], refs[6:]
    (up_out, down_out, q_out, k_out, v_out, o_out), refs = refs[:6], refs[6:]
    (dx1_out, da_own_out, da_all_out, gain_out), refs = refs[:4], refs[4:]
    kept, refs = refs[:10], refs[10:]
    buffers, refs = refs[:6], refs[6:]
    du, do, dq, dk, dv, sems, weight_sems = refs
    (own, everyone, q_all, k_all, v_all, p_all, o_all, h_all, g_all, slope_all) = kept
    order = (8, 9, 7, 6, 4, 5, 3, 2, 0, 1)
    saved_copies = [
        pltpu.make_async_copy(saved[n], kept[n], sems.at[n]) for n in range(10)
    ]
    weight_copies = [
        pltpu.make_async_copy(weights[n], buffers[n], weight_sems.at[n]) for n in range(6)
    ]
    weight_copies[5].start()
    for n in order[:3]:
        saved_copies[n].start()
    weight_copies[4].start()
    weight_copies[3].start()
    for n in order[3:]:
        saved_copies[n].start()
    for n in range(3):
        weight_copies[n].start()
    low = jnp.bfloat16
    slots, count, width = dx2.shape
    hidden = g_all.shape[2]
    gain = gain_m[...]
    flat = lambda ref: ref[...].reshape(-1, ref.shape[-1])
    grad_low = flat(dx2).astype(low)
    weight_copies[5].wait()
    for n in order[:3]:
        saved_copies[n].wait()
    for c in range(0, hidden, 768):
        at = pl.ds(c, 768)
        grad = contract(grad_low, buffers[5][at, :], 1, 1)
        slope = slope_all[:, :, at].reshape(-1, 768).astype(jnp.float32)
        du[:, at] = (grad * slope).astype(low)
        g = g_all[:, :, at].reshape(-1, 768)
        down_out[at, :] = contract(g, grad_low, 0, 0).astype(low)
        h = flat(h_all)
        up_out[:, at] = contract(h, du[:, at], 0, 0).astype(low)
    weight_copies[4].wait()
    dh = contract(du[...], buffers[4][...], 1, 1)
    unit, scale = norm_parts(flat(x1_ref))
    gain_out[...] = jnp.sum(dh * unit, axis=0, keepdims=True)
    dx1 = flat(dx2) + norm_back(dh, unit, scale, gain)
    dx1_out[...] = dx1.reshape(dx1_out.shape)
    dar = dx1.astype(low)
    weight_copies[3].wait()
    for n in order[3:]:
        saved_copies[n].wait()
    o_out[...] = contract(flat(o_all), dar, 0, 0).astype(low)
    do[...] = contract(dar, buffers[3][...], 1, 1).astype(low).reshape(do.shape)
    for s in range(slots):
        for pair in range(HEADS // 2):
            at = pl.ds(pair * 2 * HDIM, 2 * HDIM)
            q, k, v, grad = q_all[s, :, at], k_all[s, :, at], v_all[s, :, at], do[s, :, at]
            parts = []
            for odd in range(2):
                p = p_all[s * HEADS + 2 * pair + odd]
                mine = jnp.where(head_lanes(count, odd), grad, jnp.zeros_like(grad))
                dp = contract(mine, v, 1, 1)
                wide_p = p.astype(jnp.float32)
                row = jnp.sum(wide_p * dp, axis=-1, keepdims=True)
                ds = (wide_p * (dp - row)).astype(low)
                parts.append(
                    (contract(ds, k, 1, 0), contract(ds, q, 0, 0), contract(p, grad, 0, 0))
                )
            few, many = head_lanes(count, 0), head_lanes(k.shape[0], 0)
            root = HDIM ** (-0.5)
            dq[s, :, at] = (jnp.where(few, parts[0][0], parts[1][0]) * root).astype(low)
            dk[s, :, at] = (jnp.where(many, parts[0][1], parts[1][1]) * root).astype(low)
            dv[s, :, at] = jnp.where(many, parts[0][2], parts[1][2]).astype(low)
    for n in range(3):
        weight_copies[n].wait()
    q_out[...] = contract(flat(own), flat(dq), 0, 0).astype(low)
    k_out[...] = contract(flat(everyone), flat(dk), 0, 0).astype(low)
    v_out[...] = contract(flat(everyone), flat(dv), 0, 0).astype(low)
    for s in range(slots):
        da_own_out[s] = contract(dq[s], buffers[0][...], 1, 1)
        both = contract(dk[s], buffers[1][...], 1, 1) + contract(dv[s], buffers[2][...], 1, 1)
        da_all_out[s] = both.astype(low)


def token_back(dx2, x1, gain_mlp, saved, weights):
    slots, count, width = dx2.shape
    total, hidden = saved[1].shape[1], weights[4].shape[1]
    low, wide = jnp.bfloat16, jnp.float32
    shapes = [
        ((width, hidden), low),
        ((hidden, width), low),
        ((width, width), low),
        ((width, width), low),
        ((width, width), low),
        ((width, width), low),
        ((slots, count, width), wide),
        ((slots, count, width), wide),
        ((slots, total, width), low),
        ((1, width), wide),
    ]
    in_vmem = pl.BlockSpec(memory_space=pltpu.VMEM)
    any_space = pl.BlockSpec(memory_space=pl.ANY)
    return pl.pallas_call(
        token_back_kernel,
        in_specs=[in_vmem] * 3 + [any_space] * 16,
        out_specs=[in_vmem] * len(shapes),
        out_shape=[jax.ShapeDtypeStruct(shape, dtype) for shape, dtype in shapes],
        scratch_shapes=[pltpu.VMEM(item.shape, low) for item in saved]
        + [pltpu.VMEM(weight.shape, low) for weight in weights]
        + [
            pltpu.VMEM((slots * count, hidden), low),
            pltpu.VMEM((slots, count, width), low),
            pltpu.VMEM((slots, count, width), low),
            pltpu.VMEM((slots, total, width), low),
            pltpu.VMEM((slots, total, width), low),
            pltpu.SemaphoreType.DMA((10,)),
            pltpu.SemaphoreType.DMA((6,)),
        ],
        cost_estimate=pl.CostEstimate(
            flops=18 * 10**9, bytes_accessed=50 * 10**6, transcendentals=10**6
        ),
        compiler_params=pltpu.CompilerParams(vmem_limit_bytes=VMEM_LIMIT),
        name="token_back",
    )(dx2, x1, gain_mlp, *saved, *weights)


SMALL_SIDE = 16


def merge_maps(side):
    tile = lax.axis_index("tile")
    low, high = tile % 2, tile // 2
    cells = side * side
    row = jnp.arange(3 * SMALL_SIDE, dtype=jnp.int32)
    edge_col = jnp.where(low == 0, side - 1, 0)
    edge_row = jnp.where(high == 0, side - 1, 0)
    k = row % SMALL_SIDE
    source = jnp.where(
        (row < SMALL_SIDE) & (k < side),
        k * side + edge_col,
        jnp.where(
            (row >= SMALL_SIDE) & (row < 2 * SMALL_SIDE) & (k < side),
            edge_row * side + k,
            jnp.where(row == 2 * SMALL_SIDE, edge_row * side + edge_col, -1),
        ),
    )
    pick = source[:, None] == jnp.arange(cells, dtype=jnp.int32)[None, :]
    at = jnp.arange(9 * cells, dtype=jnp.int32)
    tap, cell = at // cells, at % cells
    i, j = cell // side + tap // 3 - 1, cell % side + tap % 3 - 1
    inside_i, inside_j = (i >= 0) & (i < side), (j >= 0) & (j < side)
    beside_j = ((j < 0) & (low == 1)) | ((j >= side) & (low == 0))
    beside_i = ((i < 0) & (high == 1)) | ((i >= side) & (high == 0))
    source = jnp.where(
        inside_i & inside_j,
        i * side + j,
        jnp.where(
            inside_i & beside_j,
            cells + i,
            jnp.where(
                beside_i & inside_j,
                cells + SMALL_SIDE + j,
                jnp.where(beside_i & beside_j, cells + 2 * SMALL_SIDE, -1),
            ),
        ),
    )
    parts = cells + 3 * SMALL_SIDE
    shifts = source[:, None] == jnp.arange(parts, dtype=jnp.int32)[None, :]
    return pick.astype(jnp.bfloat16), shifts.astype(jnp.bfloat16)


def merge_kernel(
    adapted,
    pooled,
    tokens,
    vit_grad,
    map_grad,
    live,
    taps,
    gate_low,
    gate_high,
    w_adapt,
    pool,
    pick,
    shifts,
    vit_out,
    dx2_out,
    grad_out,
    adapt_out,
    small_out,
    rims,
    inbox,
    moved,
    grads,
    back,
    send_sem,
    recv_sem,
):
    place = Place()
    partners = (place.to_low, place.to_high, place.to_across)
    low = jnp.bfloat16
    slots, cells, width = adapted.shape

    def copies(phase, s):
        made = []
        for n, partner in enumerate(partners):
            at = (phase * slots + s) * 3 + n
            made.append(
                remote(
                    rims.at[phase, s, pl.ds(n * SMALL_SIDE, SMALL_SIDE), :],
                    inbox.at[phase, s, pl.ds(n * SMALL_SIDE, SMALL_SIDE), :],
                    send_sem.at[at],
                    recv_sem.at[at],
                    partner,
                )
            )
        return made

    def give(phase, s, source):
        rims[phase, s] = contract(pick[...], source[s], 1, 0).astype(low)
        for copy in copies(phase, s):
            copy.start()

    def shift(phase, s, source):
        for copy in copies(phase, s):
            copy.wait()
        parts = jnp.concatenate([source[s], inbox[phase, s]], axis=0)
        for k in range(9):
            rows = shifts[pl.ds(k * cells, cells), :]
            moved[s, k] = contract(rows, parts, 1, 0).astype(low)

    greet(partners)
    for s in range(slots):
        give(0, s, adapted)
    small_out[...] = jnp.zeros_like(small_out)
    for s in range(slots):
        shift(0, s, adapted)
        f = jnp.zeros((cells, width), jnp.float32)
        for k in range(9):
            f = f + taps[k : k + 1, :] * moved[s, k].astype(jnp.float32)
        x2 = tokens[s]
        alive = live[s]
        logit = jnp.sum(x2 * gate_low[...], axis=-1, keepdims=True) + jnp.sum(
            f * gate_high[...], axis=-1, keepdims=True
        )
        gate = 1.0 / (1.0 + jnp.exp(-logit))
        vit_out[s] = ((x2 + gate * f) * alive).astype(low)
        dvo = vit_grad[s].astype(jnp.float32) * alive
        dl = jnp.sum(dvo * f, axis=-1, keepdims=True) * gate * (1.0 - gate)
        dx2_out[s] = dvo + dl * gate_low[...]
        df = gate * dvo + dl * gate_high[...]
        grads[s] = df.astype(low)
        give(1, s, grads)
        for k in range(9):
            part = jnp.sum(df * moved[s, k].astype(jnp.float32), axis=0, keepdims=True)
            small_out[k : k + 1, :] = small_out[k : k + 1, :] + part
        small_out[9:10, :] = small_out[9:10, :] + jnp.sum(dl * x2, axis=0, keepdims=True)
        small_out[10:11, :] = small_out[10:11, :] + jnp.sum(dl * f, axis=0, keepdims=True)
    for s in range(slots):
        shift(1, s, grads)
        total = jnp.zeros((cells, width), jnp.float32)
        for k in range(9):
            total = total + taps[8 - k : 9 - k, :] * moved[s, k].astype(jnp.float32)
        back[pl.ds(s * cells, cells), :] = total.astype(low)
    flat = pooled[...].reshape(slots * cells, -1)
    adapt_out[...] = contract(flat, back[...], 0, 0).astype(low)
    for s in range(slots):
        part = contract(back[pl.ds(s * cells, cells), :], w_adapt[...], 1, 1).astype(low)
        spread = contract(pool[...], part, 0, 0)
        grad_out[s] = (map_grad[s].astype(jnp.float32) * live[s] + spread).astype(low)


def merge_step(
    adapted, pooled, tokens, vit_grad, map_grad, live, taps, gate_low, gate_high, w_adapt, pool
):
    slots, cells, width = adapted.shape
    low = jnp.bfloat16
    pick, shifts = merge_maps(math.isqrt(cells))
    in_vmem = pl.BlockSpec(memory_space=pltpu.VMEM)
    return pl.pallas_call(
        merge_kernel,
        in_specs=[in_vmem] * 13,
        out_specs=[in_vmem] * 5,
        out_shape=[
            jax.ShapeDtypeStruct(adapted.shape, low),
            jax.ShapeDtypeStruct(adapted.shape, jnp.float32),
            jax.ShapeDtypeStruct(map_grad.shape, low),
            jax.ShapeDtypeStruct(w_adapt.shape, low),
            jax.ShapeDtypeStruct((16, width), jnp.float32),
        ],
        scratch_shapes=[
            pltpu.VMEM((2, slots, 3 * SMALL_SIDE, width), low),
            pltpu.VMEM((2, slots, 3 * SMALL_SIDE, width), low),
            pltpu.VMEM((slots, 9, cells, width), low),
            pltpu.VMEM((slots, cells, width), low),
            pltpu.VMEM((slots * cells, width), low),
            pltpu.SemaphoreType.DMA((6 * slots,)),
            pltpu.SemaphoreType.DMA((6 * slots,)),
        ],
        compiler_params=pltpu.CompilerParams(
            collective_id=3, has_side_effects=True, vmem_limit_bytes=VMEM_LIMIT
        ),
        name="merge_step",
    )(
        adapted,
        pooled,
        tokens,
        vit_grad,
        map_grad,
        live,
        taps,
        gate_low,
        gate_high,
        w_adapt,
        pool,
        pick,
        shifts,
    )


def turned(shape):
    return shape[1] % 128 != 0 and shape[0] % 128 == 0


def hand_out_kernel(count, *refs):
    small, refs = refs[0], refs[1:]
    matrices, refs = refs[:count], refs[count:]
    outs, refs = refs[:count], refs[count:]
    large_out, conv_out, side_out = refs
    for n in range(count):
        value = matrices[n][...]
        outs[n][...] = value.T if turned(value.shape) else value
    blocks = large_out.shape[1] // 128
    for b in range(blocks):
        large_out[:, b * 128 : (b + 1) * 128] = small[b * 49 : (b + 1) * 49, :]
        row = 49 * blocks + 6 * 16 + b
        conv_out[:, b * 128 : (b + 1) * 128] = small[row : row + 1, :]
    for b in range(side_out.shape[1] // 128):
        row = 49 * blocks + b * 16
        side_out[:, b * 128 : (b + 1) * 128] = small[row : row + 16, :]


def hand_out(small, matrices, channels, width):
    in_vmem = pl.BlockSpec(memory_space=pltpu.VMEM)
    count = len(matrices)
    results = pl.pallas_call(
        partial(hand_out_kernel, count),
        in_specs=[in_vmem] * (count + 1),
        out_specs=[in_vmem] * (count + 3),
        out_shape=[
            jax.ShapeDtypeStruct(
                item.shape[::-1] if turned(item.shape) else item.shape, item.dtype
            )
            for item in matrices
        ]
        + [
            jax.ShapeDtypeStruct((49, channels), jnp.float32),
            jax.ShapeDtypeStruct((1, channels), jnp.float32),
            jax.ShapeDtypeStruct((16, width), jnp.float32),
        ],
        name="hand_out",
    )(small, *matrices)
    return [
        result.T if turned(item.shape) else result for result, item in zip(results, matrices)
    ] + list(results[count:])


def chip_layout():
    return lax.axis_size("img") == 8 and lax.axis_size("tile") == 4


def sum_plain(grads, smalls):
    sums = []
    for grad in grads:
        part = lax.psum_scatter(grad, "img", scatter_dimension=0, tiled=True)
        part = lax.psum_scatter(part, "tile", scatter_dimension=1, tiled=True)
        sums.append(part.astype(jnp.float32))
    return sums, lax.psum(tuple(smalls), ("img", "tile"))


def map_back(
    grad_low,
    norm_low,
    wide_low,
    wide_slope,
    w_shrink,
    w_expand,
    unit_low,
    scale,
    gain,
    padded_map,
    taps,
    pick,
    place_map,
    grads,
    smalls,
):
    slots, cells, channels = grad_low.shape
    side = math.isqrt(cells)
    flat = (slots * cells, -1)
    if not chip_layout():
        wide_low = wide_low.reshape(slots, cells, -1)
        wide_slope = wide_slope.reshape(slots, cells, -1)
        w_shrink_grad = outer_sum(wide_low, grad_low)
        grad_wide_low = (project_back(grad_low, w_shrink) * wide_slope).astype(jnp.bfloat16)
        w_expand_grad = outer_sum(norm_low, grad_wide_low)
        back = project_back(grad_wide_low, w_expand)
        unit = unit_low.astype(jnp.float32)
        turned = back * gain
        gain_conv_grad = jnp.sum(back * unit, axis=(0, 1))
        grad_spread = scale * (
            turned
            - jnp.mean(turned, axis=-1, keepdims=True)
            - unit * jnp.mean(turned * unit, axis=-1, keepdims=True)
        )
        grad_spread = grad_spread.reshape(slots, side, side, channels)
        field = padded_map[:, :, : side + 6].astype(jnp.float32)
        taps_grad = jnp.stack(
            [
                jnp.sum(field[:, a : a + side, b : b + side] * grad_spread, axis=(0, 1, 2))
                for a in range(7)
                for b in range(7)
            ]
        )
        padded_grad = add_rims(grad_spread.astype(jnp.bfloat16), 3).astype(jnp.float32)
        moved = depthwise(padded_grad, taps[::-1], 3, 0).reshape(slots, cells, channels)
        map_grad = (grad_low.astype(jnp.float32) + moved).astype(jnp.bfloat16)
        sums, small_sums = sum_plain(
            tuple(grads) + (w_expand_grad, w_shrink_grad),
            tuple(smalls) + (gain_conv_grad, taps_grad),
        )
        return map_grad, sums, small_sums
    first, first_sums = map_mlp_back(
        grad_low.reshape(flat),
        norm_low.reshape(flat),
        wide_low.reshape(flat),
        wide_slope.reshape(flat),
        w_shrink,
        w_expand,
        unit_low.reshape(flat),
        scale.reshape(flat),
        gain.reshape(1, channels),
        grads,
    )
    w_shrink_grad, w_expand_grad, dz, gain_conv_grad = first
    gain_one_grad, gain_two_grad, sides = smalls
    map_grad, small, last_sums = conv_back(
        dz.reshape(grad_low.shape),
        pick,
        place_map,
        padded_map,
        grad_low,
        taps,
        (sides, gain_one_grad, gain_two_grad, gain_conv_grad),
        (w_expand_grad, w_shrink_grad),
    )
    width = sides.shape[1]
    final = hand_out(small, tuple(first_sums) + tuple(last_sums), channels, width)
    taps_grad, gain_conv_grad, sides = final[-3:]
    small_sums = (
        sides[11],
        sides[12],
        sides[:9],
        sides[9],
        sides[10],
        gain_conv_grad.reshape(channels),
        taps_grad,
    )
    return map_grad, final[:-3], small_sums


def local(
    vit_in,
    map_in,
    group_images,
    vit_grad_out,
    map_grad_out,
    w_query,
    w_key,
    w_value,
    w_out,
    w_up,
    w_down,
    w_expand,
    w_shrink,
    w_adapt,
    gain_attn,
    gain_mlp,
    gain_conv,
    dw_large,
    dw_small,
    gate_low,
    gate_high,
):
    slot_count = vit_in.shape[0]
    tok_side = math.isqrt(vit_in.shape[2])
    pix_side = math.isqrt(map_in.shape[2])
    channels = map_in.shape[3]
    model_width = vit_in.shape[3]
    live_mask = (
        (jnp.arange(slot_count, dtype=jnp.int32) < group_images[0])
        .astype(jnp.float32)
        .reshape(slot_count, 1, 1)
    )
    cells = pix_side * pix_side
    on_chips = chip_layout()
    own = vit_in[:, 0]
    tokens = own.astype(jnp.float32)
    gain_one = gain_attn.astype(jnp.float32)
    gain_two = gain_mlp.astype(jnp.float32)
    conv_gain = gain_conv.astype(jnp.float32)
    large_taps = dw_large.astype(jnp.float32)
    few = jnp.arange(tok_side * tok_side, dtype=jnp.int32)[:, None]
    cell = jnp.arange(cells, dtype=jnp.int32)[None, :]
    holder = cell // pix_side // 2 * tok_side + cell % pix_side // 2
    pool = jnp.where(holder == few, 0.25, 0.0).astype(jnp.bfloat16)
    if on_chips:
        pick, place_map = rim_maps(pix_side)
        conv_norm_low, conv_unit_low, conv_scale, padded_map = conv_front(
            map_in[:, 0], pick, place_map, large_taps, conv_gain.reshape(1, channels)
        )
        own_later, conv_norm_low = lax.optimization_barrier((own, conv_norm_low))
    else:
        pick, place_map = None, None
        own_later = own
        map_low = map_in[:, 0].reshape(slot_count, pix_side, pix_side, channels)
        padded_map = add_rims(map_low, 3)
        spread_map = depthwise(padded_map.astype(jnp.float32), large_taps, 3, 0)
        conv_unit, conv_scale = norm_parts(spread_map.reshape(slot_count, cells, channels))
        conv_norm_low = (conv_unit * conv_gain).astype(jnp.bfloat16)
        conv_unit_low = conv_unit.astype(jnp.bfloat16)
    own_all = lax.all_gather(own_later, "tile", axis=1, tiled=True)
    wide_low, wide_slope, map_result, pooled_low, adapted_low = map_mlp(
        conv_norm_low, map_in[:, 0], w_expand, w_shrink, w_adapt, pool, live_mask
    )
    token_weights = (w_query, w_key, w_value, w_out, w_up, w_down)
    front = token_front(
        own, own_all, gain_one.reshape(1, -1), gain_two.reshape(1, -1), token_weights
    )
    residual_one, residual_two = front[7], front[11]
    saved = front[:7] + front[8:11]
    low_gate = gate_low.astype(jnp.float32)
    high_gate = gate_high.astype(jnp.float32)
    small_taps = dw_small.astype(jnp.float32)
    if on_chips:
        vit_result, grad_residual_two, grad_conv_low, w_adapt_grad, sides = merge_step(
            adapted_low,
            pooled_low,
            residual_two,
            vit_grad_out[:, 0],
            map_grad_out[:, 0],
            live_mask,
            small_taps,
            low_gate.reshape(1, -1),
            high_gate.reshape(1, -1),
            w_adapt,
            pool,
        )
    else:
        adapted_low = adapted_low.reshape(slot_count, tok_side, tok_side, model_width)
        padded_small = add_rims(adapted_low, 1).astype(jnp.float32)
        merged_map, merged_pull = jax.vjp(
            partial(depthwise, radius=1, margin=0), padded_small, small_taps
        )
        merged_tokens = merged_map.reshape(slot_count, tok_side * tok_side, model_width)
        vit_after, merging_pull = jax.vjp(
            merging,
            residual_two,
            merged_tokens,
            low_gate,
            high_gate,
        )
        vit_result = (vit_after * live_mask).astype(jnp.bfloat16)
        vit_cotangent = vit_grad_out[:, 0].astype(jnp.float32) * live_mask
        map_cotangent = map_grad_out[:, 0].astype(jnp.float32) * live_mask
        grad_residual_two, grad_merged, gate_low_grad, gate_high_grad = merging_pull(vit_cotangent)
        grad_padded_small, dw_small_grad = merged_pull(
            grad_merged.reshape(slot_count, tok_side, tok_side, model_width)
        )
        grad_adapted_low = return_rims(grad_padded_small, 1).astype(jnp.bfloat16)
        grad_adapted_low = grad_adapted_low.reshape(slot_count, tok_side * tok_side, model_width)
        w_adapt_grad = outer_sum(pooled_low, grad_adapted_low)
        grad_pooled = project_back(grad_adapted_low, w_adapt).astype(jnp.bfloat16)
        grad_conv_low = (
            map_cotangent
            + jnp.einsum("pc,spk->sck", pool, grad_pooled, preferred_element_type=jnp.float32)
        ).astype(jnp.bfloat16)
    (
        w_up_grad,
        w_down_grad,
        w_query_grad,
        w_key_grad,
        w_value_grad,
        w_out_grad,
        grad_residual_one,
        grad_own,
        grad_everyone,
        gain_mlp_grad,
    ) = token_back(
        grad_residual_two, residual_one, gain_two.reshape(1, -1), saved, token_weights
    )
    grad_normed_one = grad_own + lax.psum_scatter(
        grad_everyone, "tile", scatter_dimension=1, tiled=True
    ).astype(jnp.float32)
    unit_one, scale_one = norm_parts(tokens)
    gain_attn_grad = jnp.sum(grad_normed_one * unit_one, axis=(0, 1)).reshape(1, model_width)
    if on_chips:
        smalls = (gain_attn_grad, gain_mlp_grad, sides)
    else:
        smalls = (
            gain_attn_grad.reshape(model_width),
            gain_mlp_grad.reshape(model_width),
            dw_small_grad,
            gate_low_grad,
            gate_high_grad,
        )
    vit_in_grad = (
        grad_residual_one + norm_back(grad_normed_one, unit_one, scale_one, gain_one)
    ).astype(jnp.bfloat16)
    map_in_grad, matrix_sums, small_sums = map_back(
        grad_conv_low,
        conv_norm_low,
        wide_low,
        wide_slope,
        w_shrink,
        w_expand,
        conv_unit_low,
        conv_scale,
        conv_gain,
        padded_map,
        large_taps,
        pick,
        place_map,
        (
            w_up_grad,
            w_down_grad,
            w_adapt_grad,
            w_query_grad,
            w_key_grad,
            w_value_grad,
            w_out_grad,
        ),
        smalls,
    )
    return (
        vit_result[:, None],
        map_result[:, None],
        vit_in_grad[:, None],
        map_in_grad[:, None],
        matrix_sums[3],
        matrix_sums[4],
        matrix_sums[5],
        matrix_sums[6],
        matrix_sums[0],
        matrix_sums[1],
        matrix_sums[7],
        matrix_sums[8],
        matrix_sums[2],
        small_sums[0],
        small_sums[1],
        small_sums[5],
        small_sums[6],
        small_sums[2],
        small_sums[3],
        small_sums[4],
    )


def solution(mesh):
    in_specs = (
        P("img", "tile", None, None),
        P("img", "tile", None, None),
        P("img"),
        P("img", "tile", None, None),
        P("img", "tile", None, None),
        P(),
        P(),
        P(),
        P(),
        P(),
        P(),
        P(),
        P(),
        P(),
        P(),
        P(),
        P(),
        P(),
        P(),
        P(),
        P(),
    )
    out_specs = (
        P("img", "tile", None, None),
        P("img", "tile", None, None),
        P("img", "tile", None, None),
        P("img", "tile", None, None),
        P("img", "tile"),
        P("img", "tile"),
        P("img", "tile"),
        P("img", "tile"),
        P("img", "tile"),
        P("img", "tile"),
        P("img", "tile"),
        P("img", "tile"),
        P("img", "tile"),
        P(),
        P(),
        P(),
        P(),
        P(),
        P(),
        P(),
    )
    return jax.shard_map(local, mesh=mesh, in_specs=in_specs, out_specs=out_specs, check_vma=False)
```

```python
from functools import partial
import math

import jax
import jax.numpy as jnp
from jax import lax
from jax.experimental import pallas as pl
from jax.experimental.pallas import tpu as pltpu
from jax.sharding import PartitionSpec as P

HEADS = 12
HDIM = 64


highest = lax.Precision.HIGHEST


def swapped(array, axis, bit):
    return lax.ppermute(array, axis, [(i, i ^ 1 << bit) for i in range(lax.axis_size(axis))])


def gelu_pair(values):
    spread = 0.5 * (1.0 + lax.erf(values * 0.7071067811865476))
    bell = jnp.exp(-0.5 * values * values) * 0.3989422804014327
    return (values * spread).astype(jnp.bfloat16), (spread + values * bell).astype(jnp.bfloat16)


def depthwise(field_map, tap_weights, radius, margin):
    kernel_side = 2 * radius + 1
    channels = tap_weights.shape[1]
    kernel = tap_weights.reshape(kernel_side, kernel_side, 1, channels)
    return lax.conv_general_dilated(
        field_map,
        kernel,
        (1, 1),
        ((margin, margin), (margin, margin)),
        dimension_numbers=("NHWC", "HWIO", "NHWC"),
        feature_group_count=channels,
        precision=highest,
    )


def merging(residual_two, merged_tokens, gate_low, gate_high):
    gate_logit = jnp.sum(residual_two * gate_low, axis=-1, keepdims=True) + jnp.sum(
        merged_tokens * gate_high, axis=-1, keepdims=True
    )
    gate_value = 1.0 / (1.0 + jnp.exp(-gate_logit))
    return residual_two + gate_value * merged_tokens


def project_back(left_side, right_side):
    return jnp.einsum("...j,ij->...i", left_side, right_side, preferred_element_type=jnp.float32)


def outer_sum(left_side, right_side):
    flat_left = left_side.reshape(-1, left_side.shape[-1])
    flat_right = right_side.reshape(-1, right_side.shape[-1])
    return lax.dot_general(
        flat_left, flat_right, (((0,), (0,)), ((), ())), preferred_element_type=jnp.float32
    ).astype(jnp.bfloat16)


def add_rims(tile_field, radius):
    tile_place = lax.axis_index("tile")
    for which_bit in range(2):
        axis_dim = 2 - which_bit
        on_low = tile_place >> which_bit & 1 == 0
        side_len = tile_field.shape[axis_dim]
        upper_rim = lax.slice_in_dim(tile_field, side_len - radius, side_len, axis=axis_dim)
        lower_rim = lax.slice_in_dim(tile_field, 0, radius, axis=axis_dim)
        outgoing = jnp.where(on_low, upper_rim, lower_rim)
        incoming = swapped(outgoing, "tile", which_bit)
        blank_rim = jnp.zeros_like(incoming)
        tile_field = jnp.where(
            on_low,
            jnp.concatenate([blank_rim, tile_field, incoming], axis_dim),
            jnp.concatenate([incoming, tile_field, blank_rim], axis_dim),
        )
    return tile_field


def return_rims(grad_field, radius):
    tile_place = lax.axis_index("tile")
    for which_bit in (1, 0):
        axis_dim = 2 - which_bit
        on_low = tile_place >> which_bit & 1 == 0
        total_len = grad_field.shape[axis_dim]
        side_len = total_len - 2 * radius
        high_rim = lax.slice_in_dim(grad_field, total_len - radius, total_len, axis=axis_dim)
        low_rim = lax.slice_in_dim(grad_field, 0, radius, axis=axis_dim)
        outgoing = jnp.where(on_low, high_rim, low_rim)
        incoming = swapped(outgoing.astype(jnp.bfloat16), "tile", which_bit).astype(outgoing.dtype)
        core_part = lax.slice_in_dim(grad_field, radius, radius + side_len, axis=axis_dim)
        filler_shape = list(incoming.shape)
        filler_shape[axis_dim] = side_len - radius
        filler = jnp.zeros(filler_shape, jnp.float32)
        grad_field = core_part + jnp.where(
            on_low,
            jnp.concatenate([filler, incoming], axis_dim),
            jnp.concatenate([incoming, filler], axis_dim),
        )
    return grad_field


MESH = pl.DeviceIdType.MESH
VMEM_LIMIT = 62 << 20
COPIES = 8
SMALL_ROWS = 512
RIM_ROWS = 80
CORNER_ROWS = 16


def contract(left, right, left_axis, right_axis):
    return lax.dot_general(
        left,
        right,
        (((left_axis,), (right_axis,)), ((), ())),
        preferred_element_type=jnp.float32,
    )


def wide_sum(one, two):
    return one.astype(jnp.float32) + two.astype(jnp.float32)


def low_sum(one, two):
    return wide_sum(one, two).astype(jnp.bfloat16)


def row_loop(first, rows, width, step):
    count = rows // 16
    while count > 1 and (count * 16 * width > 65536 or rows % (count * 16)):
        count -= 1
    chunk = count * 16

    def body(q, carry):
        step(pl.ds(pl.multiple_of(first + q * chunk, 16), chunk))
        return carry

    if rows == chunk:
        body(0, 0)
    else:
        lax.fori_loop(0, rows // chunk, body, 0)


def lanes(start, size):
    return pl.ds(pl.multiple_of(start, 128), size)


class Place:
    def __init__(self):
        img = lax.axis_index("img")
        tile = lax.axis_index("tile")
        self.core, self.x, self.y = img % 2, (img // 2) % 2, img // 4
        self.low, self.high = tile % 2, tile // 2
        self.to_core = (img + 1 - 2 * self.core, tile)
        self.to_x = (img + 2 - 4 * self.x, tile)
        self.to_y = (img + 4 - 8 * self.y, tile)
        self.to_low = (img, tile + 1 - 2 * self.low)
        self.to_high = (img, tile + 2 - 4 * self.high)
        self.to_across = (img, 3 - tile)


def greet(partners):
    barrier = pltpu.get_barrier_semaphore()
    for partner in partners:
        pl.semaphore_signal(barrier, inc=1, device_id=partner, device_id_type=MESH)
    pl.semaphore_wait(barrier, len(partners))


def remote(source, target, send_sem, recv_sem, partner):
    return pltpu.make_async_remote_copy(
        src_ref=source,
        dst_ref=target,
        send_sem=send_sem,
        recv_sem=recv_sem,
        device_id=partner,
        device_id_type=MESH,
    )


def plan_pieces(shapes, piece_bytes):
    pieces = []
    for g, (height, width) in enumerate(shapes):
        rows = height // 8
        count = max(1, round(height * width * 2 / piece_bytes))
        while rows % (count * 32):
            count -= 1
        for p in range(count):
            pieces.append((g, p * (rows // count), rows // count))
    return pieces


def halving_scratch(shapes, pieces):
    count = len(pieces)

    def buffers(shape_of):
        return [
            pltpu.VMEM(shape_of(rows, shapes[g][1]), jnp.bfloat16) for g, _, rows in pieces
        ]

    scratch = buffers(lambda rows, width: (2, 2, rows, width))
    scratch += buffers(lambda rows, width: (2, 2, rows, width))
    scratch += buffers(lambda rows, width: (2, rows, width))
    scratch += buffers(lambda rows, width: (rows, width))
    scratch += buffers(lambda rows, width: (rows, width // 2))
    scratch += buffers(
        lambda rows, width: (rows, width // 4 if width % 512 == 0 else width // 2)
    )
    scratch += [
        pltpu.SemaphoreType.DMA((count * COPIES,)),
        pltpu.SemaphoreType.DMA((count * COPIES,)),
        pltpu.SemaphoreType.DMA((count,)),
    ]
    return scratch


class Halving:
    def __init__(self, place, shapes, pieces, grads, outs, scratch):
        count = len(pieces)
        self.place, self.shapes, self.pieces = place, shapes, pieces
        self.grads, self.outs = grads, outs
        self.own, self.half, self.quarter, self.eighth, self.pair, self.last = (
            scratch[k * count : (k + 1) * count] for k in range(6)
        )
        self.send_sem, self.recv_sem, self.own_sem = scratch[6 * count :]
        self.stages = (
            self.over_core,
            self.over_first,
            self.over_second,
            self.over_third,
            self.over_fourth,
            self.finish,
        )

    def narrow(self, i):
        return self.shapes[self.pieces[i][0]][1] % 512 != 0

    def copy(self, i, k):
        place = self.place
        g, first, rows = self.pieces[i]
        width = self.shapes[g][1] // 4
        half, quarter, eighth = self.half[i], self.quarter[i], self.eighth[i]
        pair, last = self.pair[i], self.last[i]
        part, cut = pl.ds(first, rows), rows // 2
        top, bottom = pl.ds(0, cut), pl.ds(cut, cut)
        if k == 0:
            ends = (self.grads[g].at[:, :, 1 - place.core, part, :], half, place.to_core)
        elif k == 1:
            ends = (half.at[:, 1 - place.x, top, :], quarter.at[:, top, :], place.to_x)
        elif k == 2:
            ends = (half.at[1 - place.y, :, bottom, :], quarter.at[:, bottom, :], place.to_y)
        elif k == 3:
            ends = (quarter.at[1 - place.y, top, :], eighth.at[top, :], place.to_y)
        elif k == 4:
            ends = (quarter.at[1 - place.x, bottom, :], eighth.at[bottom, :], place.to_x)
        elif k < 7 and not self.narrow(i):
            q = k - 5
            side = eighth.at[:, lanes((2 * q + 1 - place.low) * width, width)]
            ends = (side, pair.at[:, pl.ds(q * width, width)], place.to_low)
        elif k == 5:
            side = eighth.at[:, lanes((1 - place.high) * 2 * width, 2 * width)]
            ends = (side, pair, place.to_high)
        elif not self.narrow(i):
            ends = (pair.at[:, lanes((1 - place.high) * width, width)], last, place.to_high)
        else:
            ends = (pair, last, place.to_low)
        at = i * COPIES + k
        return remote(ends[0], ends[1], self.send_sem.at[at], self.recv_sem.at[at], ends[2])

    def own_copy(self, i):
        g, first, rows = self.pieces[i]
        mine = self.grads[g].at[:, :, self.place.core, pl.ds(first, rows), :]
        return pltpu.make_async_copy(mine, self.own[i], self.own_sem.at[i])

    def copies(self, i):
        return (0, 1, 2, 3, 4, 5, 7) if self.narrow(i) else (0, 1, 2, 3, 4, 5, 6, 7)

    def over_core(self, i):
        self.copy(i, 0).start()
        self.own_copy(i).start()

    def over_first(self, i):
        rows = self.pieces[i][2]
        half, own = self.half[i], self.own[i]
        self.copy(i, 0).wait_recv()
        self.own_copy(i).wait()
        for a in range(2):
            for b in range(2):

                def step(s, a=a, b=b):
                    half[a, b, s, :] = low_sum(half[a, b, s, :], own[a, b, s, :])

                row_loop(0, rows, half.shape[-1], step)
        self.copy(i, 1).start()
        self.copy(i, 2).start()

    def over_second(self, i):
        cut = self.pieces[i][2] // 2
        place, half, quarter = self.place, self.half[i], self.quarter[i]
        self.copy(i, 1).wait_recv()
        self.copy(i, 2).wait_recv()
        for a in range(2):

            def step_top(s, a=a):
                quarter[a, s, :] = low_sum(quarter[a, s, :], half[a, place.x, s, :])

            def step_bottom(s, a=a):
                quarter[a, s, :] = low_sum(quarter[a, s, :], half[place.y, a, s, :])

            row_loop(0, cut, quarter.shape[-1], step_top)
            row_loop(cut, cut, quarter.shape[-1], step_bottom)
        self.copy(i, 3).start()
        self.copy(i, 4).start()

    def over_third(self, i):
        cut = self.pieces[i][2] // 2
        place, quarter, eighth = self.place, self.quarter[i], self.eighth[i]
        self.copy(i, 3).wait_recv()
        self.copy(i, 4).wait_recv()

        def step_top(s):
            eighth[s, :] = low_sum(eighth[s, :], quarter[place.y, s, :])

        def step_bottom(s):
            eighth[s, :] = low_sum(eighth[s, :], quarter[place.x, s, :])

        row_loop(0, cut, eighth.shape[-1], step_top)
        row_loop(cut, cut, eighth.shape[-1], step_bottom)
        self.copy(i, 5).start()
        if not self.narrow(i):
            self.copy(i, 6).start()

    def over_fourth(self, i):
        g, _, rows = self.pieces[i]
        width = self.shapes[g][1] // 4
        place, eighth, pair = self.place, self.eighth[i], self.pair[i]
        self.copy(i, 5).wait_recv()
        if self.narrow(i):

            def step(s):
                kept = eighth[s, lanes(place.high * 2 * width, 2 * width)]
                pair[s, :] = low_sum(pair[s, :], kept)

        else:
            self.copy(i, 6).wait_recv()

            def step(s):
                for q in range(2):
                    at = slice(q * width, (q + 1) * width)
                    kept = eighth[s, lanes((2 * q + place.low) * width, width)]
                    pair[s, at] = low_sum(pair[s, at], kept)

        row_loop(0, rows, pair.shape[-1], step)
        self.copy(i, 7).start()

    def finish(self, i):
        g, first, rows = self.pieces[i]
        width = self.shapes[g][1] // 4
        place, pair, last, out = self.place, self.pair[i], self.last[i], self.outs[g]
        self.copy(i, 7).wait_recv()

        def step(s):
            at = pl.ds(pl.multiple_of(s.start + first, 16), s.size)
            if self.narrow(i):
                both = wide_sum(last[s, :], pair[s, :])
                out[at, :] = jnp.where(place.low == 0, both[:, :width], both[:, width:])
            else:
                kept = pair[s, lanes(place.high * width, width)]
                out[at, :] = wide_sum(last[s, :], kept)

        row_loop(0, rows, pair.shape[-1], step)

    def wait_sends(self):
        for i in range(len(self.pieces)):
            for k in self.copies(i):
                self.copy(i, k).wait_send()


def halving_operands(grads):
    return [grad.reshape(2, 2, 2, grad.shape[0] // 8, grad.shape[1]) for grad in grads]


def halving_outputs(shapes):
    return [
        jax.ShapeDtypeStruct((height // 8, width // 4), jnp.float32) for height, width in shapes
    ]


def whole_block(shape):
    return pl.BlockSpec(shape, lambda *_: (0,) * len(shape))


def fixed_block(shape):
    return pl.BlockSpec(shape, lambda *_: (0,) * len(shape), pipeline_mode=pl.Buffered(1))


def rim_copies(place, source, rim, corner, rim_in, row_in, corner_in, sems):
    cells = source.shape[1]
    start = pl.multiple_of((1 - place.high) * (cells - RIM_ROWS), 16)
    return (
        remote(rim, rim_in, sems.at[0], sems.at[1], place.to_low),
        remote(
            source.at[:, pl.ds(start, RIM_ROWS), :], row_in, sems.at[2], sems.at[3], place.to_high
        ),
        remote(corner, corner_in, sems.at[4], sems.at[5], place.to_across),
    )


def mlp_back_kernel(shapes, pieces, plan, *refs):
    matrices = len(shapes)
    count = len(pieces)
    grad_low, norm_low, wide, slope, w_shrink, w_expand, unit, scale, table, parts = refs[:10]
    grads = refs[10 : 10 + matrices]
    refs = refs[10 + matrices :]
    shrink_out, expand_out, dz_out, gain_out, token_out = refs[:5]
    outs = refs[5 : 5 + matrices]
    refs = refs[5 + matrices :]
    halving_refs = refs[: 6 * count + 3]
    refs = refs[6 * count + 3 :]
    norm_turned, back, dz, out_sem, unit_sem = refs[:5]
    buffers, result_buffers, in_sems, result_sems = refs[5:9], refs[9:11], refs[11], refs[12]
    token_refs = refs[13:]
    place = Place()
    halving = Halving(place, shapes, pieces, grads, outs, halving_refs)
    token_sum = TokenSum(place, parts, token_out, token_refs)
    steps = plan["steps"]
    j = pl.program_id(0)

    def slot(n):
        for i, k in plan["slots"].get(n, ()):
            if i == "tokens":
                token_sum.step(k)
            else:
                halving.stages[k](i)

    def slots(odd):
        for n in range(steps):
            if plan["slots"].get(2 * n + odd):
                pl.when(j == n)(partial(slot, 2 * n + odd))

    width = plan["width"]

    unit_load = pltpu.make_async_copy(unit, dz, unit_sem)

    def fetches(n):
        slot_, at = n % 2, lanes(n * width, width)
        parts = (wide.at[:, at], slope.at[:, at], w_shrink.at[at, :], w_expand.at[:, at])
        return [
            pltpu.make_async_copy(part, buffers[k].at[slot_], in_sems.at[slot_ * 4 + k])
            for k, part in enumerate(parts)
        ]

    def stores(n):
        slot_, at = n % 2, lanes(n * width, width)
        targets = (shrink_out.at[at, :], expand_out.at[:, at])
        return [
            pltpu.make_async_copy(
                result_buffers[k].at[slot_], target, result_sems.at[slot_ * 2 + k]
            )
            for k, target in enumerate(targets)
        ]

    @pl.when(j == 0)
    def _():
        for copy in fetches(0):
            copy.start(priority=1)
        unit_load.start()
        greet(
            (
                place.to_core,
                place.to_x,
                place.to_y,
                place.to_low,
                place.to_high,
            )
        )

    @pl.when(j + 1 < steps)
    def _():
        for copy in fetches(j + 1):
            copy.start(priority=1)

    slots(0)

    @pl.when(j == 0)
    def _():
        norm_turned[...] = norm_low[...].T

    for copy in fetches(j):
        copy.wait()

    @pl.when(j >= 2)
    def _():
        for copy in stores(j - 2):
            copy.wait()

    now = j % 2
    grad_wide = contract(grad_low[...], buffers[2][now], 1, 1)
    grad_wide = (grad_wide * buffers[1][now].astype(jnp.float32)).astype(jnp.bfloat16)
    turned = contract(buffers[0][now], grad_low[...], 0, 0)
    result_buffers[0][now] = turned.astype(jnp.bfloat16)
    slots(1)
    turned = contract(norm_turned[...], grad_wide, 1, 0)
    result_buffers[1][now] = turned.astype(jnp.bfloat16)
    term = contract(grad_wide, buffers[3][now], 1, 1)
    for copy in stores(j):
        copy.start(priority=1)

    @pl.when(j == 0)
    def _():
        back[...] = term

    @pl.when(j > 0)
    def _():
        back[...] = back[...] + term

    @pl.when(j == steps - 1)
    def _():
        unit_load.wait()
        gain_row = table[49:50, :]
        chunk = 48

        def body(q, sums):
            at = pl.ds(pl.multiple_of(q * chunk, 16), chunk)
            grad = back[at, :]
            n = dz[at, :].astype(jnp.float32)
            t = grad * gain_row
            mean_t = jnp.mean(t, axis=-1, keepdims=True)
            mean_tn = jnp.mean(t * n, axis=-1, keepdims=True)
            dz[at, :] = (scale[at, :] * (t - mean_t - n * mean_tn)).astype(jnp.bfloat16)
            return sums + jnp.sum((grad * n).reshape(chunk // 8, 8, -1), axis=0)

        sums = jnp.zeros((8, dz.shape[1]), jnp.float32)
        sums = lax.fori_loop(0, dz.shape[0] // chunk, body, sums)
        gain_out[...] = jnp.sum(sums, axis=0, keepdims=True)
        back_copy = pltpu.make_async_copy(dz, dz_out, out_sem)
        back_copy.start()
        for n in range(2 * steps, plan["last"] + 1):
            slot(n)
        back_copy.wait()
        for n in (steps - 2, steps - 1):
            for copy in stores(n):
                copy.wait()
        token_sum.wait_sends()
        halving.wait_sends()


def spread_plan(count, steps, first, second, rest):
    slots = {0: [(i, 0) for i in range(count)]}
    last = 0
    for i in range(count):
        at = [int(first[0] + first[1] * i), int(second[0] + second[1] * i)]
        at += [at[1] + r for r in rest]
        for k, n in enumerate(at):
            slots.setdefault(n, []).append((i, k + 1))
        last = max(last, at[-1])
    for n in slots:
        slots[n].sort(key=lambda item: (-item[1], item[0]))
    return {"slots": slots, "last": last, "steps": steps}


def map_mlp_back(
    grad_low, norm_low, wide, slope, w_shrink, w_expand, unit, scale, table, parts, grads
):
    tokens, channels = grad_low.shape
    hidden = w_shrink.shape[0]
    width = 512
    steps = hidden // width
    shapes = [grad.shape for grad in grads]
    pieces = plan_pieces(shapes, 1_600_000)
    plan = spread_plan(len(pieces), steps, (1, 1.0), (4, 1.0), (2, 4, 6))
    plan["width"] = width
    for k, n in enumerate((0, 5, 11)):
        plan["slots"].setdefault(n, []).append(("tokens", k))
    token_shape = parts.shape[1:]
    low = jnp.bfloat16
    any_space = pl.BlockSpec(memory_space=pl.ANY)
    results = pl.pallas_call(
        partial(mlp_back_kernel, shapes, pieces, plan),
        grid=(steps,),
        in_specs=[
            fixed_block((tokens, channels)),
            fixed_block((tokens, channels)),
            any_space,
            any_space,
            any_space,
            any_space,
            any_space,
            fixed_block((tokens, 1)),
            fixed_block(table.shape),
            any_space,
        ]
        + [any_space] * len(grads),
        out_specs=[
            any_space,
            any_space,
            any_space,
            whole_block((1, channels)),
            whole_block(token_shape),
        ]
        + [whole_block(item.shape) for item in halving_outputs(shapes)],
        out_shape=[
            jax.ShapeDtypeStruct((hidden, channels), low),
            jax.ShapeDtypeStruct((channels, hidden), low),
            jax.ShapeDtypeStruct((tokens, channels), low),
            jax.ShapeDtypeStruct((1, channels), jnp.float32),
            jax.ShapeDtypeStruct(token_shape, jnp.float32),
        ]
        + halving_outputs(shapes),
        scratch_shapes=halving_scratch(shapes, pieces)
        + [
            pltpu.VMEM((channels, tokens), low),
            pltpu.VMEM((tokens, channels), jnp.float32),
            pltpu.VMEM((tokens, channels), low),
            pltpu.SemaphoreType.DMA,
            pltpu.SemaphoreType.DMA,
            pltpu.VMEM((2, tokens, width), low),
            pltpu.VMEM((2, tokens, width), low),
            pltpu.VMEM((2, width, channels), low),
            pltpu.VMEM((2, channels, width), low),
            pltpu.VMEM((2, width, channels), low),
            pltpu.VMEM((2, channels, width), low),
            pltpu.SemaphoreType.DMA((8,)),
            pltpu.SemaphoreType.DMA((4,)),
            pltpu.VMEM((2,) + token_shape, low),
            pltpu.VMEM((2,) + token_shape, low),
            pltpu.VMEM(token_shape, low),
            pltpu.SemaphoreType.DMA((8,)),
        ],
        compiler_params=pltpu.CompilerParams(
            collective_id=0, has_side_effects=True, vmem_limit_bytes=VMEM_LIMIT
        ),
        name="map_mlp_back",
    )(
        grad_low,
        norm_low,
        wide,
        slope,
        w_shrink,
        w_expand,
        unit,
        scale,
        table,
        parts,
        *halving_operands(grads),
    )
    return results[:5], results[5:]


def shift_rows(read_row, shifted, rows, side):
    def body(r, carry):
        line = read_row(r)
        for b in range(7):
            shifted[b, r] = line[b : b + side].reshape(side // 8, 8, 128)
        return carry

    lax.fori_loop(0, rows, body, 0, unroll=2)


def fill_taps(tap_ref, taps, flip):
    for k in range(49):
        tap = tap_ref[48 - k if flip else k].reshape(1, 128)
        taps[k] = jnp.broadcast_to(tap, (8, 128))


def seven_rows(shifted, taps, first, group, side):
    sums = [jnp.zeros((side // 8, 8, 128), jnp.float32) for _ in range(group)]
    for b in range(7):
        for r in range(group + 6):
            line = shifted[b, first + r]
            for k in range(group):
                if 0 <= r - k < 7:
                    sums[k] = sums[k] + taps[(r - k) * 7 + b][None] * line
    return sums


def tap_sums(shifted, read_line, rows, side, group, keep):
    for columns in ((0, 1, 2, 3), (4, 5, 6)):

        def body(g, sums):
            sums = [list(part) for part in sums]
            first = g * group
            lines = [read_line(first + k).reshape(side // 8, 8, 128) for k in range(group)]
            for n, b in enumerate(columns):
                for r in range(group + 6):
                    line = shifted[b, first + r]
                    for k in range(group):
                        if 0 <= r - k < 7:
                            sums[r - k][n] = sums[r - k][n] + jnp.sum(line * lines[k], axis=0)
            return tuple(tuple(part) for part in sums)

        zero = jnp.zeros((8, 128), jnp.float32)
        sums = lax.fori_loop(
            0, rows // group, body, tuple(tuple(zero for _ in columns) for _ in range(7))
        )
        for a in range(7):
            for n, b in enumerate(columns):
                keep(a * 7 + b, jnp.sum(sums[a][n], axis=0, keepdims=True))


class TokenGather:
    def __init__(self, own, everyone, held, own_sems, sems):
        self.img = lax.axis_index("img")
        self.tile = lax.axis_index("tile")
        self.own, self.everyone, self.held = own, everyone, held
        self.own_sems, self.sems = own_sems, sems

    def copy(self, k, up, origin, source):
        at = 4 * k + 2 * up
        partner = (self.img, self.tile + 1 if up else self.tile - 1)
        target = self.everyone.at[origin]
        return remote(source, target, self.sems.at[at], self.sems.at[at + 1], partner)

    def given(self, k, up):
        origin = self.tile - k if up else self.tile + k
        source = self.held if k == 0 else self.everyone.at[origin]
        return self.copy(k, up, origin, source)

    def gives(self, k, up):
        if up:
            return (self.tile >= k) & (self.tile < 3)
        return (self.tile + k <= 3) & (self.tile > 0)

    def load(self):
        return pltpu.make_async_copy(self.own, self.held, self.own_sems.at[0])

    def store(self):
        return pltpu.make_async_copy(self.held, self.everyone.at[self.tile], self.own_sems.at[1])

    def hand_on(self, k):
        for up in (0, 1):

            @pl.when(self.gives(k, up))
            def _():
                self.given(k, up).start()

    def take(self, k):
        for up in (0, 1):

            @pl.when(self.tile > k if up else self.tile + k < 3)
            def _():
                origin = self.tile - 1 - k if up else self.tile + 1 + k
                self.copy(k, up, origin, self.held).wait_recv()

    def wait_sends(self):
        for k in range(3):
            for up in (0, 1):

                @pl.when(self.gives(k, up))
                def _():
                    self.given(k, up).wait_send()


class TokenSum:
    def __init__(self, place, parts, out, scratch):
        self.place, self.parts, self.out = place, parts, out
        self.mine, self.first, self.second, self.sems = scratch

    def copy(self, k):
        place, sems = self.place, self.sems
        if k < 2:
            source, target = self.parts.at[2 * k + 1 - place.low], self.first.at[k]
            partner = place.to_low
        else:
            source, target = self.mine.at[1 - place.high], self.second
            partner = place.to_high
        return remote(source, target, sems.at[2 * k], sems.at[2 * k + 1], partner)

    def load(self, k):
        part = self.parts.at[2 * k + self.place.low]
        return pltpu.make_async_copy(part, self.mine.at[k], self.sems.at[6 + k])

    def step(self, k):
        if k == 0:
            for n in range(2):
                self.copy(n).start()
                self.load(n).start()
        elif k == 1:
            for n in range(2):
                self.copy(n).wait_recv()
                self.load(n).wait()
                for q in range(self.mine.shape[1]):
                    self.mine[n, q] = low_sum(self.mine[n, q], self.first[n, q])
            self.copy(2).start()
        else:
            self.copy(2).wait_recv()
            for q in range(self.out.shape[0]):
                self.out[q] = wide_sum(self.mine[self.place.high, q], self.second[q])

    def wait_sends(self):
        for k in range(3):
            self.copy(k).wait_send()


class SmallSum:
    def __init__(self, place, out, work, inbox, send_sem, recv_sem):
        self.out, self.work, self.inbox = out, work, inbox
        self.send_sem, self.recv_sem = send_sem, recv_sem
        self.total = out.shape[0]
        self.halvings = (
            (place.to_core, place.core),
            (place.to_x, place.x),
            (place.to_y, place.y),
            (place.to_low, place.low),
            (place.to_high, place.high),
        )
        starts, size = [0], self.total
        for _, bit in self.halvings:
            size //= 2
            starts.append(starts[-1] + bit * size)
        self.starts = starts

    def rows(self, start, size):
        return pl.ds(pl.multiple_of(start, 8), size)

    def copy(self, k):
        if k < 5:
            partner, bit = self.halvings[k]
            size = self.total >> (k + 1)
            give = self.rows(self.starts[k] + (1 - bit) * size, size)
            source = self.work.at[give, :]
            target = self.inbox.at[pl.ds(self.total - 2 * size, size), :]
        else:
            partner, _ = self.halvings[9 - k]
            mine = self.rows(self.starts[10 - k], self.total >> (10 - k))
            source = target = self.out.at[mine, :]
        return remote(source, target, self.send_sem.at[k], self.recv_sem.at[k], partner)

    def step(self, k):
        if k > 0:
            self.copy(k - 1).wait_recv()
        if 1 <= k <= 5:
            size = self.total >> k
            at = self.rows(self.starts[k], size)
            summed = self.work[at, :] + self.inbox[pl.ds(self.total - 2 * size, size), :]
            if k < 5:
                self.work[at, :] = summed
            else:
                self.out[at, :] = summed
        if k < 10:
            self.copy(k).start()

    def wait_sends(self):
        for k in range(10):
            self.copy(k).wait_send()


def conv_back_kernel(shapes, pieces, plan, *refs):
    matrices = len(shapes)
    count = len(pieces)
    (dz, pick, place_map, padded, grad_low, tap_ref, sides, one, two, gain) = refs[:10]
    grads = refs[10 : 10 + matrices]
    refs = refs[10 + matrices :]
    map_out, small_out = refs[:2]
    outs = refs[2 : 2 + matrices]
    refs = refs[2 + matrices :]
    halving_refs = refs[: 6 * count + 3]
    refs = refs[6 * count + 3 :]
    field, shifted, taps, tap_out, work, inbox, gathered, small_send, small_recv = refs[:9]
    rim, corner, rim_in, row_in, corner_in, rim_sems = refs[9:]
    place = Place()
    halving = Halving(place, shapes, pieces, grads, outs, halving_refs)
    smalls = SmallSum(place, gathered, work, inbox, small_send, small_recv)
    slots_, cells, channels = dz.shape
    side = padded.shape[1] - 6
    blocks = channels // 128
    j = pl.program_id(0)
    s = j % 2
    c = (j // 2) % blocks
    columns = lanes(c * 128, 128)

    def slot(n):
        for i, k in plan["slots"].get(n, ()):
            if i == "small":
                smalls.step(k)
            else:
                halving.stages[k](i)

    @pl.when(j == 0)
    def _():
        greet(
            (
                place.to_core,
                place.to_x,
                place.to_y,
                place.to_low,
                place.to_high,
                place.to_across,
            )
        )

    rims = rim_copies(place, dz, rim, corner, rim_in, row_in, corner_in, rim_sems)

    for n in range(plan["steps"]):
        if n in plan["slots"] and n != 2 * blocks:
            pl.when(j == n)(partial(slot, n))

    @pl.when(j == 0)
    def _():
        for s in range(slots_):
            both = contract(pick[...], dz[s], 1, 0).astype(jnp.bfloat16)
            rim[s] = both[:RIM_ROWS]
            corner[s] = both[RIM_ROWS:]
        for copy in rims:
            copy.start()

    @pl.when(j < 2 * blocks)
    def _():
        shift_rows(lambda r: padded[0, r].astype(jnp.float32), shifted, side + 6, side)

        @pl.when(s == 0)
        def _():
            tap_out[c] = jnp.zeros(tap_out.shape[1:], jnp.float32)

        def read_line(i):
            line = dz[s, pl.ds(pl.multiple_of(i * side, 8), side), columns]
            return line.astype(jnp.float32)

        def keep(k, value):
            tap_out[c, k : k + 1, :] = tap_out[c, k : k + 1, :] + value

        tap_sums(shifted, read_line, side, side, 4, keep)

    @pl.when(j == 2 * blocks)
    def _():
        for q in range(blocks):
            work[q * 49 : (q + 1) * 49, :] = tap_out[q, :49, :]
        base = blocks * 49
        work[base:, :] = jnp.zeros((SMALL_ROWS - base, 128), jnp.float32)
        for q in range(sides.shape[1] // 128):
            at = slice(q * 128, (q + 1) * 128)
            row = base + q * 16
            work[row : row + 11, :] = sides[:11, at]
            work[row + 11 : row + 12, :] = one[:, at]
            work[row + 12 : row + 13, :] = two[:, at]
        for q in range(blocks):
            row = base + sides.shape[1] // 8 + q
            work[row : row + 1, :] = gain[:, q * 128 : (q + 1) * 128]
        slot(2 * blocks)
        for copy in rims:
            copy.wait()
        for q in range(slots_):
            parts = jnp.concatenate([dz[q], rim_in[q], row_in[q], corner_in[q]], axis=0)
            whole = contract(place_map[...], parts, 1, 0).astype(jnp.bfloat16)
            field[q] = whole.reshape(field.shape[1:])

    @pl.when(j >= 2 * blocks)
    def _():
        fill_taps(tap_ref, taps, True)
        shift_rows(
            lambda r: field[s, r, :, columns].astype(jnp.float32), shifted, side + 6, side
        )

        def body(g, carry):
            for k, line in enumerate(seven_rows(shifted, taps, g * 4, 4, side)):
                at = pl.ds(pl.multiple_of((g * 4 + k) * side, 8), side)
                total = line.reshape(side, 128) + grad_low[0, at, :].astype(jnp.float32)
                map_out[0, at, :] = total.astype(jnp.bfloat16)
            return carry

        lax.fori_loop(0, side // 4, body, 0)

    @pl.when(j == plan["steps"] - 1)
    def _():
        for n in range(plan["steps"], plan["last"] + 1):
            slot(n)
        small_out[...] = gathered[...]
        halving.wait_sends()
        smalls.wait_sends()


def conv_back(
    dz, pick, place_map, padded, grad_low, tap_weights, smalls, grads
):
    slots, cells, channels = grad_low.shape
    rows, cols = padded.shape[1:3]
    side = rows - 6
    blocks = channels // 128
    steps = 4 * blocks
    shapes = [grad.shape for grad in grads]
    pieces = plan_pieces(shapes, 2_100_000)
    plan = spread_plan(len(pieces), steps, (1, 3), (7, 3), (4, 8, 12))
    for k in range(11):
        at = 2 * blocks + 2 * k
        plan["slots"].setdefault(at, []).append(("small", k))
        plan["last"] = max(plan["last"], at)
    any_space = pl.BlockSpec(memory_space=pl.ANY)

    def first_half(j):
        k = jnp.minimum(j, 2 * blocks - 1)
        return (k % 2, 0, 0, k // 2)

    def second_half(j):
        k = jnp.maximum(j - 2 * blocks, 0)
        return (k % 2, 0, k // 2)

    results = pl.pallas_call(
        partial(conv_back_kernel, shapes, pieces, plan),
        grid=(steps,),
        in_specs=[
            fixed_block(dz.shape),
            fixed_block(pick.shape),
            fixed_block(place_map.shape),
            pl.BlockSpec((1, rows, cols, 128), first_half),
            pl.BlockSpec((1, cells, 128), second_half),
            pl.BlockSpec(
                (tap_weights.shape[0], 128), lambda j: (0, jnp.maximum(j - 2 * blocks, 0) // 2)
            ),
        ]
        + [fixed_block(item.shape) for item in smalls]
        + [any_space] * len(grads),
        out_specs=[
            pl.BlockSpec((1, cells, 128), second_half),
            whole_block((SMALL_ROWS, 128)),
        ]
        + [whole_block(item.shape) for item in halving_outputs(shapes)],
        out_shape=[
            jax.ShapeDtypeStruct((slots, cells, channels), jnp.bfloat16),
            jax.ShapeDtypeStruct((SMALL_ROWS, 128), jnp.float32),
        ]
        + halving_outputs(shapes),
        scratch_shapes=halving_scratch(shapes, pieces)
        + [
            pltpu.VMEM((slots, rows, 32, channels), jnp.bfloat16),
            pltpu.VMEM((7, rows, side // 8, 8, 128), jnp.float32),
            pltpu.VMEM((49, 8, 128), jnp.float32),
            pltpu.VMEM((blocks, 56, 128), jnp.float32),
            pltpu.VMEM((SMALL_ROWS, 128), jnp.float32),
            pltpu.VMEM((SMALL_ROWS, 128), jnp.float32),
            pltpu.VMEM((SMALL_ROWS, 128), jnp.float32),
            pltpu.SemaphoreType.DMA((10,)),
            pltpu.SemaphoreType.DMA((10,)),
            pltpu.VMEM((slots, RIM_ROWS, channels), jnp.bfloat16),
            pltpu.VMEM((slots, CORNER_ROWS, channels), jnp.bfloat16),
            pltpu.VMEM((slots, RIM_ROWS, channels), jnp.bfloat16),
            pltpu.VMEM((slots, RIM_ROWS, channels), jnp.bfloat16),
            pltpu.VMEM((slots, CORNER_ROWS, channels), jnp.bfloat16),
            pltpu.SemaphoreType.DMA((6,)),
        ],
        compiler_params=pltpu.CompilerParams(
            collective_id=1, has_side_effects=True, vmem_limit_bytes=VMEM_LIMIT
        ),
        name="conv_back",
    )(
        dz,
        pick,
        place_map,
        padded,
        grad_low,
        tap_weights,
        *smalls,
        *halving_operands(grads),
    )
    return results[0], results[1], results[2:]


def rim_maps(side):
    tile = lax.axis_index("tile")
    low, high = tile % 2, tile // 2
    cells = side * side
    row = jnp.arange(RIM_ROWS + CORNER_ROWS, dtype=jnp.int32)
    edge_col = jnp.where(low == 0, side - 3, 0)
    edge_row = jnp.where(high == 0, side - 3, 0)
    rim_from = (row % side) * side + edge_col + row // side
    k = row - RIM_ROWS
    corner_from = (edge_row + k // 3) * side + edge_col + k % 3
    source = jnp.where(
        row < 3 * side, rim_from, jnp.where((k >= 0) & (k < 9), corner_from, -1)
    )
    pick = (source[:, None] == jnp.arange(cells, dtype=jnp.int32)[None, :]).astype(jnp.bfloat16)
    at = jnp.arange((side + 6) * 32, dtype=jnp.int32)
    i, j = at // 32 - 3, at % 32 - 3
    inside_i, inside_j = (i >= 0) & (i < side), (j >= 0) & (j < side)
    beside_j = ((j < 0) & (low == 1)) | ((j >= side) & (j < side + 3) & (low == 0))
    beside_i = ((i < 0) & (high == 1)) | ((i >= side) & (high == 0))
    q = jnp.where(j < 0, j + 3, j - side)
    p = jnp.where(i < 0, i + 3, i - side)
    skip = jnp.where(high == 1, RIM_ROWS - 3 * side, 0)
    source = jnp.where(
        inside_i & inside_j,
        i * side + j,
        jnp.where(
            inside_i & beside_j,
            cells + q * side + i,
            jnp.where(
                beside_i & inside_j,
                cells + RIM_ROWS + skip + p * side + j,
                jnp.where(beside_i & beside_j, cells + 2 * RIM_ROWS + p * 3 + q, -1),
            ),
        ),
    )
    parts = cells + 2 * RIM_ROWS + CORNER_ROWS
    place_map = (source[:, None] == jnp.arange(parts, dtype=jnp.int32)[None, :]).astype(
        jnp.bfloat16
    )
    return pick, place_map


def slot_rims(place, s, source, rim, corner, rim_in, row_in, corner_in, sems):
    cells = source.shape[1]
    start = pl.multiple_of((1 - place.high) * (cells - RIM_ROWS), 16)
    row = source.at[s, pl.ds(start, RIM_ROWS), :]
    return (
        remote(rim.at[s], rim_in.at[s], sems.at[6 * s], sems.at[6 * s + 1], place.to_low),
        remote(row, row_in.at[s], sems.at[6 * s + 2], sems.at[6 * s + 3], place.to_high),
        remote(
            corner.at[s], corner_in.at[s], sems.at[6 * s + 4], sems.at[6 * s + 5], place.to_across
        ),
    )


def conv_front_kernel(
    source,
    pick,
    place_map,
    tap_ref,
    table,
    norm_out,
    unit_out,
    scale_out,
    field_out,
    cells_ref,
    field,
    spread,
    shifted,
    taps,
    rim,
    corner,
    rim_in,
    row_in,
    corner_in,
    sems,
    load_sem,
    store_sem,
):
    place = Place()
    slots, cells, channels = cells_ref.shape
    blocks = channels // 128
    side = field.shape[1] - 6
    j = pl.program_id(0)
    s, c = j // blocks, j % blocks
    columns = lanes(c * 128, 128)
    low = jnp.bfloat16

    def rims(q):
        return slot_rims(place, q, cells_ref, rim, corner, rim_in, row_in, corner_in, sems)

    def select(q):
        both = contract(pick[...], cells_ref[q], 1, 0).astype(low)
        rim[q] = both[:RIM_ROWS]
        corner[q] = both[RIM_ROWS:]
        for copy in rims(q):
            copy.start()

    def store(q):
        return pltpu.make_async_copy(field.at[q], field_out.at[q], store_sem.at[q])

    def build(q):
        for copy in rims(q):
            copy.wait()
        parts = jnp.concatenate([cells_ref[q], rim_in[q], row_in[q], corner_in[q]], axis=0)
        whole = contract(place_map[...], parts, 1, 0).astype(low)
        field[q] = whole.reshape(field.shape[1:])
        store(q).start()

    @pl.when(j == 0)
    def _():
        load = pltpu.make_async_copy(source, cells_ref, load_sem)
        load.start()
        greet((place.to_low, place.to_high, place.to_across))
        load.wait()
        select(0)
        build(0)
        for q in range(1, slots):
            select(q)

    for q in range(1, slots):
        pl.when(j == q * blocks)(partial(build, q))

    fill_taps(tap_ref, taps, False)
    shift_rows(lambda r: field[s, r, :, columns].astype(jnp.float32), shifted, side + 6, side)

    def body(g, carry):
        for k, line in enumerate(seven_rows(shifted, taps, g * 4, 4, side)):
            at = pl.ds(pl.multiple_of((g * 4 + k) * side, 8), side)
            spread[c, at, :] = line.reshape(side, 128)
        return carry

    lax.fori_loop(0, side // 4, body, 0)

    @pl.when(c == blocks - 1)
    def _():
        gain_row = table[49:50, :]
        chunk = 48

        def norm(n, carry):
            at = pl.ds(pl.multiple_of(n * chunk, 16), chunk)
            values = jnp.concatenate([spread[b, at, :] for b in range(blocks)], axis=1)
            unit, scale = norm_parts(values)
            unit_out[at, :] = unit.astype(low)
            norm_out[at, :] = (unit * gain_row).astype(low)
            scale_out[at, :] = scale
            return carry

        lax.fori_loop(0, cells // chunk, norm, 0)

    @pl.when(j == slots * blocks - 1)
    def _():
        for q in range(slots):
            store(q).wait()


def conv_front(source, pick, place_map, table):
    slots, cells, channels = source.shape
    side = math.isqrt(cells)
    blocks = channels // 128
    low = jnp.bfloat16
    field_shape = (slots, side + 6, 32, channels)
    any_space = pl.BlockSpec(memory_space=pl.ANY)
    by_slot = lambda j: (j // blocks, 0)
    rows = slots * cells
    return pl.pallas_call(
        conv_front_kernel,
        grid=(slots * blocks,),
        in_specs=[
            any_space,
            fixed_block(pick.shape),
            fixed_block(place_map.shape),
            pl.BlockSpec((table.shape[0], 128), lambda j: (0, j % blocks)),
            fixed_block(table.shape),
        ],
        out_specs=[
            pl.BlockSpec((cells, channels), by_slot),
            pl.BlockSpec((cells, channels), by_slot),
            pl.BlockSpec((cells, 1), by_slot),
            any_space,
        ],
        out_shape=[
            jax.ShapeDtypeStruct((rows, channels), low),
            jax.ShapeDtypeStruct((rows, channels), low),
            jax.ShapeDtypeStruct((rows, 1), jnp.float32),
            jax.ShapeDtypeStruct(field_shape, low),
        ],
        scratch_shapes=[
            pltpu.VMEM((slots, cells, channels), low),
            pltpu.VMEM(field_shape, low),
            pltpu.VMEM((blocks, cells, 128), jnp.float32),
            pltpu.VMEM((7, side + 6, side // 8, 8, 128), jnp.float32),
            pltpu.VMEM((49, 8, 128), jnp.float32),
            pltpu.VMEM((slots, RIM_ROWS, channels), low),
            pltpu.VMEM((slots, CORNER_ROWS, channels), low),
            pltpu.VMEM((slots, RIM_ROWS, channels), low),
            pltpu.VMEM((slots, RIM_ROWS, channels), low),
            pltpu.VMEM((slots, CORNER_ROWS, channels), low),
            pltpu.SemaphoreType.DMA((6 * slots,)),
            pltpu.SemaphoreType.DMA,
            pltpu.SemaphoreType.DMA((slots,)),
        ],
        compiler_params=pltpu.CompilerParams(
            collective_id=2, has_side_effects=True, vmem_limit_bytes=VMEM_LIMIT
        ),
        name="conv_front",
    )(source, pick, place_map, table, table)


def map_mlp_kernel(
    norm_low,
    source,
    w_expand,
    w_shrink,
    w_adapt,
    pool,
    live,
    *refs,
):
    gathers = len(refs) > 6
    if gathers:
        own, everyone = refs[0], refs[6]
        refs, rest = refs[1:6] + refs[7:8], refs[8:]
    wide_out, slope_out, map_out, pooled_out, adapted_out, total = refs
    j = pl.program_id(0)
    low = jnp.bfloat16
    if gathers:
        place = Place()
        gather = TokenGather(own, everyone, *rest)

        @pl.when(j == 0)
        def _():
            gather.load().start()
            greet((place.to_low, place.to_high, place.to_across))
            gather.load().wait()
            gather.store().start()
            gather.hand_on(0)

        for k in (1, 2):

            @pl.when(j == k)
            def _():
                gather.take(k - 1)
                gather.hand_on(k)

    rows, width = norm_low.shape[0], w_expand.shape[1]
    half = rows // 2
    for part in (pl.ds(0, half), pl.ds(half, half)):
        wide, slope = gelu_pair(contract(norm_low[part, :], w_expand[...], 1, 0))
        wide_out[part, :] = wide
        slope_out[part, :] = slope
        term = contract(wide, w_shrink[...], 1, 0)

        @pl.when(j == 0)
        def _():
            total[part, :] = source[part, :].astype(jnp.float32) + term

        @pl.when(j > 0)
        def _():
            total[part, :] = total[part, :] + term

    @pl.when(j == pl.num_programs(0) - 1)
    def _():
        slots, cells, _ = map_out.shape
        for s in range(slots):
            after = total[pl.ds(s * cells, cells), :].astype(low)
            keep = jnp.broadcast_to(live[s], after.shape) > 0
            map_out[s] = jnp.where(keep, after, jnp.zeros_like(after))
            pooled = contract(pool[...], after, 1, 0).astype(low)
            pooled_out[s] = pooled
            adapted_out[s] = contract(pooled, w_adapt[...], 1, 0).astype(low)
        if gathers:
            gather.take(2)
            gather.store().wait()
            gather.wait_sends()


def map_mlp(norm_low, source, w_expand, w_shrink, w_adapt, pool, live, own=None):
    slots, cells, channels = source.shape
    hidden, width = w_expand.shape[1], 1024
    few, model = pool.shape[0], w_adapt.shape[1]
    low = jnp.bfloat16
    extra, extra_space, extra_shape, extra_scratch = [], [], [], []
    params = pltpu.CompilerParams(vmem_limit_bytes=VMEM_LIMIT)
    if own is not None:
        extra, extra_space = [own], [pl.BlockSpec(memory_space=pl.ANY)]
        extra_shape = [jax.ShapeDtypeStruct((4,) + own.shape, low)]
        extra_scratch = [
            pltpu.VMEM(own.shape, low),
            pltpu.SemaphoreType.DMA((2,)),
            pltpu.SemaphoreType.DMA((12,)),
        ]
        params = pltpu.CompilerParams(
            collective_id=4, has_side_effects=True, vmem_limit_bytes=VMEM_LIMIT
        )
    rows = slots * cells
    return pl.pallas_call(
        map_mlp_kernel,
        grid=(hidden // width,),
        in_specs=[
            fixed_block((rows, channels)),
            fixed_block((rows, channels)),
            pl.BlockSpec((channels, width), lambda j: (0, j)),
            pl.BlockSpec((width, channels), lambda j: (j, 0)),
            fixed_block(w_adapt.shape),
            fixed_block(pool.shape),
            fixed_block(live.shape),
        ]
        + extra_space,
        out_specs=[
            pl.BlockSpec((rows, width), lambda j: (0, j)),
            pl.BlockSpec((rows, width), lambda j: (0, j)),
            whole_block((slots, cells, channels)),
            whole_block((slots, few, channels)),
            whole_block((slots, few, model)),
        ]
        + extra_space,
        out_shape=[
            jax.ShapeDtypeStruct((rows, hidden), low),
            jax.ShapeDtypeStruct((rows, hidden), low),
            jax.ShapeDtypeStruct((slots, cells, channels), low),
            jax.ShapeDtypeStruct((slots, few, channels), low),
            jax.ShapeDtypeStruct((slots, few, model), low),
        ]
        + extra_shape,
        scratch_shapes=[pltpu.VMEM((rows, channels), jnp.float32)] + extra_scratch,
        cost_estimate=pl.CostEstimate(
            flops=4 * rows * channels * hidden,
            bytes_accessed=45 * 10**6,
            transcendentals=2 * rows * hidden,
        ),
        compiler_params=params,
        name="map_mlp",
    )(
        norm_low,
        source.reshape(rows, channels),
        w_expand,
        w_shrink,
        w_adapt,
        pool,
        live,
        *extra,
    )


def norm_parts(values):
    centre = values - jnp.mean(values, axis=-1, keepdims=True)
    scale = lax.rsqrt(jnp.mean(centre * centre, axis=-1, keepdims=True) + 1e-06)
    return centre * scale, scale


def norm_back(grad, unit, scale, gain):
    turned = grad * gain
    mean = jnp.mean(turned, axis=-1, keepdims=True)
    mean_unit = jnp.mean(turned * unit, axis=-1, keepdims=True)
    return scale * (turned - mean - unit * mean_unit)


def head_lanes(rows, odd):
    lane = lax.broadcasted_iota(jnp.int32, (rows, 2 * HDIM), 1)
    return (lane >= HDIM) if odd else (lane < HDIM)


def token_front_kernel(*refs):
    (own, everyone, table), refs = refs[:3], refs[3:]
    weights, refs = refs[:6], refs[6:]
    outs, refs = refs[:12], refs[12:]
    buffers, sems, refs = refs[:6], refs[6], refs[7:]
    held, out_sems = refs[:12], refs[12]
    (own_out, all_out, q_out, k_out, v_out, p_out) = held[:6]
    (o_out, x1_out, h_out, g_out, slope_out, x2_out) = held[6:]
    stores = [pltpu.make_async_copy(held[n], outs[n], out_sems.at[n]) for n in range(12)]
    copies = [
        pltpu.make_async_copy(weights[n], buffers[n], sems.at[n]) for n in range(6)
    ]
    for copy in copies:
        copy.start()
    low = jnp.bfloat16
    slots, count, width = own.shape
    gain = table[0:1, :]

    def norm_chunks(source, target, rows):
        def body(n, carry):
            at = pl.ds(pl.multiple_of(n * 48, 16), 48)
            unit, _ = norm_parts(source[at, :].astype(jnp.float32))
            target[at, :] = (unit * gain).astype(low)
            return carry

        lax.fori_loop(0, rows // 48, body, 0)

    for s in range(slots):
        norm_chunks(own.at[s], own_out.at[s], count)
        for t in range(everyone.shape[0]):
            norm_chunks(everyone.at[t, s], all_out.at[s, pl.ds(t * count, count), :], count)
    stores[0].start()
    stores[1].start()
    copies[0].wait()
    for s in range(slots):
        q_out[s] = contract(own_out[s], buffers[0][...], 1, 0).astype(low)
    stores[2].start()
    copies[1].wait()
    copies[2].wait()
    for s in range(slots):
        k_out[s] = contract(all_out[s], buffers[1][...], 1, 0).astype(low)
        v_out[s] = contract(all_out[s], buffers[2][...], 1, 0).astype(low)
    stores[3].start()
    stores[4].start()
    for s in range(slots):
        for pair in range(HEADS // 2):
            at = pl.ds(pair * 2 * HDIM, 2 * HDIM)
            q, k, v = q_out[s, :, at], k_out[s, :, at], v_out[s, :, at]
            q = q * jnp.asarray(HDIM ** (-0.5), low)
            mixed = []
            for odd in range(2):
                part = jnp.where(head_lanes(count, odd), q, jnp.zeros_like(q))
                scores = contract(part, k, 1, 1)
                shifted = jnp.exp(scores - jnp.max(scores, axis=-1, keepdims=True))
                share = 1.0 / jnp.sum(shifted, axis=-1, keepdims=True)
                p = (shifted * share).astype(low)
                p_out[s * HEADS + 2 * pair + odd] = p
                mixed.append(contract(p, v, 1, 0))
            o_out[s, :, at] = jnp.where(head_lanes(count, 0), mixed[0], mixed[1]).astype(low)
    stores[5].start()
    stores[6].start()
    copies[3].wait()
    gain_two = table[1:2, :]
    for s in range(slots):
        x1 = own[s].astype(jnp.float32) + contract(o_out[s], buffers[3][...], 1, 0)
        x1_out[s] = x1
        unit, _ = norm_parts(x1)
        h_out[s] = (unit * gain_two).astype(low)
    stores[7].start()
    stores[8].start()
    copies[4].wait()
    hidden = g_out.shape[2]
    for s in range(slots):
        for c in range(0, hidden, 768):
            at = pl.ds(c, 768)
            g_out[s, :, at], slope_out[s, :, at] = gelu_pair(
                contract(h_out[s], buffers[4][:, at], 1, 0)
            )
    stores[9].start()
    stores[10].start()
    copies[5].wait()
    for s in range(slots):
        x2_out[s] = x1_out[s] + contract(g_out[s], buffers[5][...], 1, 0)
    stores[11].start()
    for copy in stores:
        copy.wait()


def token_front(own, everyone, table, weights):
    slots, count, width = own.shape
    total, hidden = everyone.shape[0] * count, weights[4].shape[1]
    low, wide = jnp.bfloat16, jnp.float32
    shapes = [
        ((slots, count, width), low),
        ((slots, total, width), low),
        ((slots, count, width), low),
        ((slots, total, width), low),
        ((slots, total, width), low),
        ((slots * HEADS, count, total), low),
        ((slots, count, width), low),
        ((slots, count, width), wide),
        ((slots, count, width), low),
        ((slots, count, hidden), low),
        ((slots, count, hidden), low),
        ((slots, count, width), wide),
    ]
    in_vmem = pl.BlockSpec(memory_space=pltpu.VMEM)
    return pl.pallas_call(
        token_front_kernel,
        in_specs=[in_vmem] * 3 + [pl.BlockSpec(memory_space=pl.ANY)] * 6,
        out_specs=[pl.BlockSpec(memory_space=pl.ANY)] * len(shapes),
        out_shape=[jax.ShapeDtypeStruct(shape, dtype) for shape, dtype in shapes],
        scratch_shapes=[pltpu.VMEM(weight.shape, low) for weight in weights]
        + [pltpu.SemaphoreType.DMA((6,))]
        + [pltpu.VMEM(shape, dtype) for shape, dtype in shapes]
        + [pltpu.SemaphoreType.DMA((12,))],
        cost_estimate=pl.CostEstimate(
            flops=9 * 10**9, bytes_accessed=30 * 10**6, transcendentals=3 * 10**6
        ),
        compiler_params=pltpu.CompilerParams(vmem_limit_bytes=VMEM_LIMIT),
        name="token_front",
    )(own, everyone, table, *weights)


def token_back_kernel(*refs):
    (dx2, x1_ref, table), refs = refs[:3], refs[3:]
    saved, refs = refs[:10], refs[10:]
    weights, refs = refs[:6], refs[6:]
    outs, refs = refs[:9], refs[9:]
    gain_out, refs = refs[0], refs[1:]
    kept, refs = refs[:10], refs[10:]
    buffers, refs = refs[:6], refs[6:]
    held, refs = refs[:9], refs[9:]
    du, do, dq, dk, dv, sems, weight_sems, out_sems = refs
    (up_out, down_out, q_out, k_out, v_out, o_out, dx1_out, da_own_out, da_all_out) = held
    stores = [pltpu.make_async_copy(held[n], outs[n], out_sems.at[n]) for n in range(9)]
    (own, everyone, q_all, k_all, v_all, p_all, o_all, h_all, g_all, slope_all) = kept
    order = (8, 9, 7, 6, 4, 5, 3, 2, 0, 1)
    saved_copies = [
        pltpu.make_async_copy(saved[n], kept[n], sems.at[n]) for n in range(10)
    ]
    weight_copies = [
        pltpu.make_async_copy(weights[n], buffers[n], weight_sems.at[n]) for n in range(6)
    ]
    weight_copies[5].start()
    for n in order[:3]:
        saved_copies[n].start()
    weight_copies[4].start()
    weight_copies[3].start()
    for n in order[3:]:
        saved_copies[n].start()
    for n in range(3):
        weight_copies[n].start()
    low = jnp.bfloat16
    slots, count, width = dx2.shape
    hidden = g_all.shape[2]
    gain = table[1:2, :]
    flat = lambda ref: ref[...].reshape(-1, ref.shape[-1])
    grad_low = flat(dx2).astype(low)
    weight_copies[5].wait()
    for n in order[:3]:
        saved_copies[n].wait()
    for c in range(0, hidden, 768):
        at = pl.ds(c, 768)
        grad = contract(grad_low, buffers[5][at, :], 1, 1)
        slope = slope_all[:, :, at].reshape(-1, 768).astype(jnp.float32)
        du[:, at] = (grad * slope).astype(low)
        g = g_all[:, :, at].reshape(-1, 768)
        down_out[at, :] = contract(g, grad_low, 0, 0).astype(low)
        h = flat(h_all)
        up_out[:, at] = contract(h, du[:, at], 0, 0).astype(low)
    stores[0].start()
    stores[1].start()
    weight_copies[4].wait()
    dh = contract(du[...], buffers[4][...], 1, 1)
    unit, scale = norm_parts(flat(x1_ref))
    gain_out[...] = jnp.sum(dh * unit, axis=0, keepdims=True)
    dx1 = flat(dx2) + norm_back(dh, unit, scale, gain)
    dx1_out[...] = dx1.reshape(dx1_out.shape)
    stores[6].start()
    dar = dx1.astype(low)
    weight_copies[3].wait()
    for n in order[3:]:
        saved_copies[n].wait()
    o_out[...] = contract(flat(o_all), dar, 0, 0).astype(low)
    stores[5].start()
    do[...] = contract(dar, buffers[3][...], 1, 1).astype(low).reshape(do.shape)
    for s in range(slots):
        for pair in range(HEADS // 2):
            at = pl.ds(pair * 2 * HDIM, 2 * HDIM)
            q, k, v, grad = q_all[s, :, at], k_all[s, :, at], v_all[s, :, at], do[s, :, at]
            parts = []
            for odd in range(2):
                p = p_all[s * HEADS + 2 * pair + odd]
                mine = jnp.where(head_lanes(count, odd), grad, jnp.zeros_like(grad))
                dp = contract(mine, v, 1, 1)
                wide_p = p.astype(jnp.float32)
                row = jnp.sum(wide_p * dp, axis=-1, keepdims=True)
                ds = (wide_p * (dp - row)).astype(low)
                parts.append(
                    (contract(ds, k, 1, 0), contract(ds, q, 0, 0), contract(p, grad, 0, 0))
                )
            few, many = head_lanes(count, 0), head_lanes(k.shape[0], 0)
            root = HDIM ** (-0.5)
            dq[s, :, at] = (jnp.where(few, parts[0][0], parts[1][0]) * root).astype(low)
            dk[s, :, at] = (jnp.where(many, parts[0][1], parts[1][1]) * root).astype(low)
            dv[s, :, at] = jnp.where(many, parts[0][2], parts[1][2]).astype(low)
    for n in range(3):
        weight_copies[n].wait()
    for s in range(slots):
        da_own_out[s] = contract(dq[s], buffers[0][...], 1, 1)
        both = contract(dk[s], buffers[1][...], 1, 1) + contract(dv[s], buffers[2][...], 1, 1)
        for t in range(da_all_out.shape[0]):
            da_all_out[t, s] = both[t * count : (t + 1) * count].astype(low)
    stores[7].start()
    stores[8].start()
    q_out[...] = contract(flat(own), flat(dq), 0, 0).astype(low)
    stores[2].start()
    k_out[...] = contract(flat(everyone), flat(dk), 0, 0).astype(low)
    stores[3].start()
    v_out[...] = contract(flat(everyone), flat(dv), 0, 0).astype(low)
    stores[4].start()
    for copy in stores:
        copy.wait()


def token_back(dx2, x1, table, saved, weights):
    slots, count, width = dx2.shape
    total, hidden = saved[1].shape[1], weights[4].shape[1]
    low, wide = jnp.bfloat16, jnp.float32
    shapes = [
        ((width, hidden), low),
        ((hidden, width), low),
        ((width, width), low),
        ((width, width), low),
        ((width, width), low),
        ((width, width), low),
        ((slots, count, width), wide),
        ((slots, count, width), wide),
        ((total // count, slots, count, width), low),
        ((1, width), wide),
    ]
    in_vmem = pl.BlockSpec(memory_space=pltpu.VMEM)
    any_space = pl.BlockSpec(memory_space=pl.ANY)
    return pl.pallas_call(
        token_back_kernel,
        in_specs=[in_vmem] * 3 + [any_space] * 16,
        out_specs=[any_space] * 9 + [in_vmem],
        out_shape=[jax.ShapeDtypeStruct(shape, dtype) for shape, dtype in shapes],
        scratch_shapes=[pltpu.VMEM(item.shape, low) for item in saved]
        + [pltpu.VMEM(weight.shape, low) for weight in weights]
        + [pltpu.VMEM(shape, dtype) for shape, dtype in shapes[:9]]
        + [
            pltpu.VMEM((slots * count, hidden), low),
            pltpu.VMEM((slots, count, width), low),
            pltpu.VMEM((slots, count, width), low),
            pltpu.VMEM((slots, total, width), low),
            pltpu.VMEM((slots, total, width), low),
            pltpu.SemaphoreType.DMA((10,)),
            pltpu.SemaphoreType.DMA((6,)),
            pltpu.SemaphoreType.DMA((9,)),
        ],
        cost_estimate=pl.CostEstimate(
            flops=18 * 10**9, bytes_accessed=50 * 10**6, transcendentals=10**6
        ),
        compiler_params=pltpu.CompilerParams(vmem_limit_bytes=VMEM_LIMIT),
        name="token_back",
    )(dx2, x1, table, *saved, *weights)


SMALL_SIDE = 16


def merge_maps(side):
    tile = lax.axis_index("tile")
    low, high = tile % 2, tile // 2
    cells = side * side
    row = jnp.arange(3 * SMALL_SIDE, dtype=jnp.int32)
    edge_col = jnp.where(low == 0, side - 1, 0)
    edge_row = jnp.where(high == 0, side - 1, 0)
    k = row % SMALL_SIDE
    source = jnp.where(
        (row < SMALL_SIDE) & (k < side),
        k * side + edge_col,
        jnp.where(
            (row >= SMALL_SIDE) & (row < 2 * SMALL_SIDE) & (k < side),
            edge_row * side + k,
            jnp.where(row == 2 * SMALL_SIDE, edge_row * side + edge_col, -1),
        ),
    )
    pick = source[:, None] == jnp.arange(cells, dtype=jnp.int32)[None, :]
    at = jnp.arange(9 * cells, dtype=jnp.int32)
    tap, cell = at // cells, at % cells
    i, j = cell // side + tap // 3 - 1, cell % side + tap % 3 - 1
    inside_i, inside_j = (i >= 0) & (i < side), (j >= 0) & (j < side)
    beside_j = ((j < 0) & (low == 1)) | ((j >= side) & (low == 0))
    beside_i = ((i < 0) & (high == 1)) | ((i >= side) & (high == 0))
    source = jnp.where(
        inside_i & inside_j,
        i * side + j,
        jnp.where(
            inside_i & beside_j,
            cells + i,
            jnp.where(
                beside_i & inside_j,
                cells + SMALL_SIDE + j,
                jnp.where(beside_i & beside_j, cells + 2 * SMALL_SIDE, -1),
            ),
        ),
    )
    parts = cells + 3 * SMALL_SIDE
    shifts = source[:, None] == jnp.arange(parts, dtype=jnp.int32)[None, :]
    return pick.astype(jnp.bfloat16), shifts.astype(jnp.bfloat16)


def merge_kernel(
    adapted,
    pooled,
    tokens,
    vit_grad,
    map_grad,
    live,
    table,
    w_adapt,
    pool,
    pick,
    shifts,
    vit_out,
    dx2_out,
    grad_out,
    adapt_out,
    small_out,
    rims,
    inbox,
    moved,
    grads,
    back,
    send_sem,
    recv_sem,
):
    place = Place()
    partners = (place.to_low, place.to_high, place.to_across)
    low = jnp.bfloat16
    slots, cells, width = adapted.shape

    def copies(phase, s):
        made = []
        for n, partner in enumerate(partners):
            at = (phase * slots + s) * 3 + n
            made.append(
                remote(
                    rims.at[phase, s, pl.ds(n * SMALL_SIDE, SMALL_SIDE), :],
                    inbox.at[phase, s, pl.ds(n * SMALL_SIDE, SMALL_SIDE), :],
                    send_sem.at[at],
                    recv_sem.at[at],
                    partner,
                )
            )
        return made

    def give(phase, s, source):
        rims[phase, s] = contract(pick[...], source[s], 1, 0).astype(low)
        for copy in copies(phase, s):
            copy.start()

    def shift(phase, s, source):
        for copy in copies(phase, s):
            copy.wait()
        parts = jnp.concatenate([source[s], inbox[phase, s]], axis=0)
        for k in range(9):
            rows = shifts[pl.ds(k * cells, cells), :]
            moved[s, k] = contract(rows, parts, 1, 0).astype(low)

    gate_low, gate_high = table[2:3, :], table[3:4, :]
    greet(partners)
    for s in range(slots):
        give(0, s, adapted)
    small_out[...] = jnp.zeros_like(small_out)
    for s in range(slots):
        shift(0, s, adapted)
        f = jnp.zeros((cells, width), jnp.float32)
        for k in range(9):
            f = f + table[4 + k : 5 + k, :] * moved[s, k].astype(jnp.float32)
        x2 = tokens[s]
        alive = live[s]
        logit = jnp.sum(x2 * gate_low, axis=-1, keepdims=True) + jnp.sum(
            f * gate_high, axis=-1, keepdims=True
        )
        gate = 1.0 / (1.0 + jnp.exp(-logit))
        vit_out[s] = ((x2 + gate * f) * alive).astype(low)
        dvo = vit_grad[s].astype(jnp.float32) * alive
        dl = jnp.sum(dvo * f, axis=-1, keepdims=True) * gate * (1.0 - gate)
        dx2_out[s] = dvo + dl * gate_low
        df = gate * dvo + dl * gate_high
        grads[s] = df.astype(low)
        give(1, s, grads)
        for k in range(9):
            part = jnp.sum(df * moved[s, k].astype(jnp.float32), axis=0, keepdims=True)
            small_out[k : k + 1, :] = small_out[k : k + 1, :] + part
        small_out[9:10, :] = small_out[9:10, :] + jnp.sum(dl * x2, axis=0, keepdims=True)
        small_out[10:11, :] = small_out[10:11, :] + jnp.sum(dl * f, axis=0, keepdims=True)
    for s in range(slots):
        shift(1, s, grads)
        total = jnp.zeros((cells, width), jnp.float32)
        for k in range(9):
            total = total + table[12 - k : 13 - k, :] * moved[s, k].astype(jnp.float32)
        back[pl.ds(s * cells, cells), :] = total.astype(low)
    flat = pooled[...].reshape(slots * cells, -1)
    adapt_out[...] = contract(flat, back[...], 0, 0).astype(low)
    for s in range(slots):
        part = contract(back[pl.ds(s * cells, cells), :], w_adapt[...], 1, 1).astype(low)
        spread = contract(pool[...], part, 0, 0)
        grad_out[s] = (map_grad[s].astype(jnp.float32) * live[s] + spread).astype(low)


def merge_step(adapted, pooled, tokens, vit_grad, map_grad, live, table, w_adapt, pool):
    slots, cells, width = adapted.shape
    low = jnp.bfloat16
    pick, shifts = merge_maps(math.isqrt(cells))
    in_vmem = pl.BlockSpec(memory_space=pltpu.VMEM)
    return pl.pallas_call(
        merge_kernel,
        in_specs=[in_vmem] * 11,
        out_specs=[in_vmem] * 5,
        out_shape=[
            jax.ShapeDtypeStruct(adapted.shape, low),
            jax.ShapeDtypeStruct(adapted.shape, jnp.float32),
            jax.ShapeDtypeStruct(map_grad.shape, low),
            jax.ShapeDtypeStruct(w_adapt.shape, low),
            jax.ShapeDtypeStruct((16, width), jnp.float32),
        ],
        scratch_shapes=[
            pltpu.VMEM((2, slots, 3 * SMALL_SIDE, width), low),
            pltpu.VMEM((2, slots, 3 * SMALL_SIDE, width), low),
            pltpu.VMEM((slots, 9, cells, width), low),
            pltpu.VMEM((slots, cells, width), low),
            pltpu.VMEM((slots * cells, width), low),
            pltpu.SemaphoreType.DMA((6 * slots,)),
            pltpu.SemaphoreType.DMA((6 * slots,)),
        ],
        compiler_params=pltpu.CompilerParams(
            collective_id=3, has_side_effects=True, vmem_limit_bytes=VMEM_LIMIT
        ),
        name="merge_step",
    )(
        adapted,
        pooled,
        tokens,
        vit_grad,
        map_grad,
        live,
        table,
        w_adapt,
        pool,
        pick,
        shifts,
    )


def turned(shape):
    return shape[1] % 128 != 0 and shape[0] % 128 == 0


def hand_out_kernel(count, *refs):
    small, refs = refs[0], refs[1:]
    matrices, refs = refs[:count], refs[count:]
    outs, refs = refs[:count], refs[count:]
    large_out, conv_out, small_out, *rows_out = refs
    for n in range(count):
        value = matrices[n][...]
        outs[n][...] = value.T if turned(value.shape) else value
    blocks = large_out.shape[1] // 128
    for b in range(blocks):
        large_out[:, b * 128 : (b + 1) * 128] = small[b * 49 : (b + 1) * 49, :]
        row = 49 * blocks + small_out.shape[1] // 8 + b
        conv_out[pl.ds(b * 128, 128)] = small[row]
    for b in range(small_out.shape[1] // 128):
        row = 49 * blocks + b * 16
        small_out[:, b * 128 : (b + 1) * 128] = small[row : row + 9, :]
        for n, out in enumerate(rows_out):
            out[pl.ds(b * 128, 128)] = small[row + 9 + n]


def hand_out(small, matrices, channels, width):
    in_vmem = pl.BlockSpec(memory_space=pltpu.VMEM)
    count = len(matrices)
    results = pl.pallas_call(
        partial(hand_out_kernel, count),
        in_specs=[in_vmem] * (count + 1),
        out_specs=[in_vmem] * (count + 7),
        out_shape=[
            jax.ShapeDtypeStruct(
                item.shape[::-1] if turned(item.shape) else item.shape, item.dtype
            )
            for item in matrices
        ]
        + [
            jax.ShapeDtypeStruct((49, channels), jnp.float32),
            jax.ShapeDtypeStruct((channels,), jnp.float32),
            jax.ShapeDtypeStruct((9, width), jnp.float32),
        ]
        + [jax.ShapeDtypeStruct((width,), jnp.float32)] * 4,
        name="hand_out",
    )(small, *matrices)
    taps_grad, gain_conv_grad, small_grad, low_grad, high_grad, one_grad, two_grad = results[count:]
    return [
        result.T if turned(item.shape) else result for result, item in zip(results, matrices)
    ] + [one_grad, two_grad, small_grad, low_grad, high_grad, gain_conv_grad, taps_grad]


def chip_layout():
    return lax.axis_size("img") == 8 and lax.axis_size("tile") == 4


def sum_plain(grads, smalls):
    sums = []
    for grad in grads:
        part = lax.psum_scatter(grad, "img", scatter_dimension=0, tiled=True)
        part = lax.psum_scatter(part, "tile", scatter_dimension=1, tiled=True)
        sums.append(part.astype(jnp.float32))
    return sums, lax.psum(tuple(smalls), ("img", "tile"))


def map_back_plain(
    grad_low, norm_low, wide_low, wide_slope, w_shrink, w_expand, unit, scale, gain, padded, taps
):
    slots, cells, channels = grad_low.shape
    side = math.isqrt(cells)
    wide_low = wide_low.reshape(slots, cells, -1)
    wide_slope = wide_slope.reshape(slots, cells, -1)
    w_shrink_grad = outer_sum(wide_low, grad_low)
    grad_wide_low = (project_back(grad_low, w_shrink) * wide_slope).astype(jnp.bfloat16)
    w_expand_grad = outer_sum(norm_low, grad_wide_low)
    back = project_back(grad_wide_low, w_expand)
    gain_conv_grad = jnp.sum(back * unit, axis=(0, 1))
    grad_spread = norm_back(back, unit, scale, gain).reshape(slots, side, side, channels)
    field = padded.astype(jnp.float32)
    taps_grad = jnp.stack(
        [
            jnp.sum(field[:, a : a + side, b : b + side] * grad_spread, axis=(0, 1, 2))
            for a in range(7)
            for b in range(7)
        ]
    )
    padded_grad = add_rims(grad_spread.astype(jnp.bfloat16), 3).astype(jnp.float32)
    moved = depthwise(padded_grad, taps[::-1], 3, 0).reshape(slots, cells, channels)
    map_grad = (grad_low.astype(jnp.float32) + moved).astype(jnp.bfloat16)
    return map_grad, w_expand_grad, w_shrink_grad, gain_conv_grad, taps_grad


def local(
    vit_in,
    map_in,
    group_images,
    vit_grad_out,
    map_grad_out,
    w_query,
    w_key,
    w_value,
    w_out,
    w_up,
    w_down,
    w_expand,
    w_shrink,
    w_adapt,
    gain_attn,
    gain_mlp,
    gain_conv,
    dw_large,
    dw_small,
    gate_low,
    gate_high,
):
    slot_count = vit_in.shape[0]
    tok_side = math.isqrt(vit_in.shape[2])
    pix_side = math.isqrt(map_in.shape[2])
    channels = map_in.shape[3]
    model_width = vit_in.shape[3]
    live_mask = (
        (jnp.arange(slot_count, dtype=jnp.int32) < group_images[0])
        .astype(jnp.float32)
        .reshape(slot_count, 1, 1)
    )
    cells = pix_side * pix_side
    on_chips = chip_layout()
    own = vit_in[:, 0]
    tokens = own.astype(jnp.float32)
    gain_one = gain_attn.astype(jnp.float32)
    conv_gain = gain_conv.astype(jnp.float32)
    large_taps = dw_large.astype(jnp.float32)
    map_table = jnp.concatenate([dw_large, gain_conv[None]]).astype(jnp.float32)
    token_table = jnp.concatenate(
        [gain_attn[None], gain_mlp[None], gate_low[None], gate_high[None], dw_small]
    ).astype(jnp.float32)
    few = jnp.arange(tok_side * tok_side, dtype=jnp.int32)[:, None]
    cell = jnp.arange(cells, dtype=jnp.int32)[None, :]
    holder = cell // pix_side // 2 * tok_side + cell % pix_side // 2
    pool = jnp.where(holder == few, 0.25, 0.0).astype(jnp.bfloat16)
    if on_chips:
        pick, place_map = rim_maps(pix_side)
        conv_norm_low, conv_unit_low, conv_scale, padded_map = conv_front(
            map_in[:, 0], pick, place_map, map_table
        )
    else:
        map_low = map_in[:, 0].reshape(slot_count, pix_side, pix_side, channels)
        padded_map = add_rims(map_low, 3)
        spread_map = depthwise(padded_map.astype(jnp.float32), large_taps, 3, 0)
        conv_unit, conv_scale = norm_parts(spread_map.reshape(slot_count, cells, channels))
        conv_norm_low = (conv_unit * conv_gain).astype(jnp.bfloat16).reshape(-1, channels)
    wide_low, wide_slope, map_result, pooled_low, adapted_low, *gathered = map_mlp(
        conv_norm_low,
        map_in[:, 0],
        w_expand,
        w_shrink,
        w_adapt,
        pool,
        live_mask,
        own if on_chips else None,
    )
    own_all = gathered[0] if on_chips else lax.all_gather(own, "tile", axis=0, tiled=False)
    token_weights = (w_query, w_key, w_value, w_out, w_up, w_down)
    front = token_front(own, own_all, token_table, token_weights)
    residual_one, residual_two = front[7], front[11]
    saved = front[:7] + front[8:11]
    if on_chips:
        vit_result, grad_residual_two, grad_conv_low, w_adapt_grad, sides = merge_step(
            adapted_low,
            pooled_low,
            residual_two,
            vit_grad_out[:, 0],
            map_grad_out[:, 0],
            live_mask,
            token_table,
            w_adapt,
            pool,
        )
    else:
        adapted_low = adapted_low.reshape(slot_count, tok_side, tok_side, model_width)
        padded_small = add_rims(adapted_low, 1).astype(jnp.float32)
        merged_map, merged_pull = jax.vjp(
            partial(depthwise, radius=1, margin=0), padded_small, dw_small.astype(jnp.float32)
        )
        merged_tokens = merged_map.reshape(slot_count, tok_side * tok_side, model_width)
        vit_after, merging_pull = jax.vjp(
            merging,
            residual_two,
            merged_tokens,
            gate_low.astype(jnp.float32),
            gate_high.astype(jnp.float32),
        )
        vit_result = (vit_after * live_mask).astype(jnp.bfloat16)
        vit_cotangent = vit_grad_out[:, 0].astype(jnp.float32) * live_mask
        map_cotangent = map_grad_out[:, 0].astype(jnp.float32) * live_mask
        grad_residual_two, grad_merged, gate_low_grad, gate_high_grad = merging_pull(vit_cotangent)
        grad_padded_small, dw_small_grad = merged_pull(
            grad_merged.reshape(slot_count, tok_side, tok_side, model_width)
        )
        grad_adapted_low = return_rims(grad_padded_small, 1).astype(jnp.bfloat16)
        grad_adapted_low = grad_adapted_low.reshape(slot_count, tok_side * tok_side, model_width)
        w_adapt_grad = outer_sum(pooled_low, grad_adapted_low)
        grad_pooled = project_back(grad_adapted_low, w_adapt).astype(jnp.bfloat16)
        grad_conv_low = (
            map_cotangent
            + jnp.einsum("pc,spk->sck", pool, grad_pooled, preferred_element_type=jnp.float32)
        ).astype(jnp.bfloat16)
    (
        w_up_grad,
        w_down_grad,
        w_query_grad,
        w_key_grad,
        w_value_grad,
        w_out_grad,
        grad_residual_one,
        grad_own,
        grad_everyone,
        gain_mlp_grad,
    ) = token_back(grad_residual_two, residual_one, token_table, saved, token_weights)
    token_grads = (
        w_up_grad,
        w_down_grad,
        w_adapt_grad,
        w_query_grad,
        w_key_grad,
        w_value_grad,
        w_out_grad,
    )
    if on_chips:
        first, first_sums = map_mlp_back(
            grad_conv_low.reshape(-1, channels),
            conv_norm_low,
            wide_low,
            wide_slope,
            w_shrink,
            w_expand,
            conv_unit_low,
            conv_scale,
            map_table,
            grad_everyone,
            token_grads,
        )
        w_shrink_grad, w_expand_grad, dz, gain_conv_grad, grad_shared = first
    else:
        grad_shared = lax.psum_scatter(
            grad_everyone, "tile", scatter_dimension=0, tiled=False
        ).astype(jnp.float32)
    grad_normed_one = grad_own + grad_shared
    unit_one, scale_one = norm_parts(tokens)
    gain_attn_grad = jnp.sum(grad_normed_one * unit_one, axis=(0, 1)).reshape(1, model_width)
    vit_in_grad = (
        grad_residual_one + norm_back(grad_normed_one, unit_one, scale_one, gain_one)
    ).astype(jnp.bfloat16)
    if on_chips:
        map_in_grad, small, last_sums = conv_back(
            dz.reshape(grad_conv_low.shape),
            pick,
            place_map,
            padded_map,
            grad_conv_low,
            map_table,
            (sides, gain_attn_grad, gain_mlp_grad, gain_conv_grad),
            (w_expand_grad, w_shrink_grad),
        )
        final = hand_out(small, tuple(first_sums) + tuple(last_sums), channels, model_width)
        matrix_sums, small_sums = final[:9], final[9:]
    else:
        map_in_grad, w_expand_grad, w_shrink_grad, gain_conv_grad, taps_grad = map_back_plain(
            grad_conv_low,
            conv_norm_low,
            wide_low,
            wide_slope,
            w_shrink,
            w_expand,
            conv_unit,
            conv_scale,
            conv_gain,
            padded_map,
            large_taps,
        )
        matrix_sums, small_sums = sum_plain(
            token_grads + (w_expand_grad, w_shrink_grad),
            (
                gain_attn_grad.reshape(model_width),
                gain_mlp_grad.reshape(model_width),
                dw_small_grad,
                gate_low_grad,
                gate_high_grad,
                gain_conv_grad,
                taps_grad,
            ),
        )
    return (
        vit_result[:, None],
        map_result[:, None],
        vit_in_grad[:, None],
        map_in_grad[:, None],
        matrix_sums[3],
        matrix_sums[4],
        matrix_sums[5],
        matrix_sums[6],
        matrix_sums[0],
        matrix_sums[1],
        matrix_sums[7],
        matrix_sums[8],
        matrix_sums[2],
        small_sums[0],
        small_sums[1],
        small_sums[5],
        small_sums[6],
        small_sums[2],
        small_sums[3],
        small_sums[4],
    )


def solution(mesh):
    in_specs = (
        P("img", "tile", None, None),
        P("img", "tile", None, None),
        P("img"),
        P("img", "tile", None, None),
        P("img", "tile", None, None),
        P(),
        P(),
        P(),
        P(),
        P(),
        P(),
        P(),
        P(),
        P(),
        P(),
        P(),
        P(),
        P(),
        P(),
        P(),
        P(),
    )
    out_specs = (
        P("img", "tile", None, None),
        P("img", "tile", None, None),
        P("img", "tile", None, None),
        P("img", "tile", None, None),
        P("img", "tile"),
        P("img", "tile"),
        P("img", "tile"),
        P("img", "tile"),
        P("img", "tile"),
        P("img", "tile"),
        P("img", "tile"),
        P("img", "tile"),
        P("img", "tile"),
        P(),
        P(),
        P(),
        P(),
        P(),
        P(),
        P(),
    )
    return jax.shard_map(local, mesh=mesh, in_specs=in_specs, out_specs=out_specs, check_vma=False)
```

```python
from functools import partial
import math

import jax
import jax.numpy as jnp
from jax import lax
from jax.experimental import pallas as pl
from jax.experimental.pallas import tpu as pltpu
from jax.sharding import PartitionSpec as P

HEADS = 12
HDIM = 64


highest = lax.Precision.HIGHEST


def swapped(array, axis, bit):
    return lax.ppermute(array, axis, [(i, i ^ 1 << bit) for i in range(lax.axis_size(axis))])


def gelu_pair(values):
    spread = 0.5 * (1.0 + lax.erf(values * 0.7071067811865476))
    bell = jnp.exp(-0.5 * values * values) * 0.3989422804014327
    return (values * spread).astype(jnp.bfloat16), (spread + values * bell).astype(jnp.bfloat16)


def depthwise(field_map, tap_weights, radius, margin):
    kernel_side = 2 * radius + 1
    channels = tap_weights.shape[1]
    kernel = tap_weights.reshape(kernel_side, kernel_side, 1, channels)
    return lax.conv_general_dilated(
        field_map,
        kernel,
        (1, 1),
        ((margin, margin), (margin, margin)),
        dimension_numbers=("NHWC", "HWIO", "NHWC"),
        feature_group_count=channels,
        precision=highest,
    )


def merging(residual_two, merged_tokens, gate_low, gate_high):
    gate_logit = jnp.sum(residual_two * gate_low, axis=-1, keepdims=True) + jnp.sum(
        merged_tokens * gate_high, axis=-1, keepdims=True
    )
    gate_value = 1.0 / (1.0 + jnp.exp(-gate_logit))
    return residual_two + gate_value * merged_tokens


def project_back(left_side, right_side):
    return jnp.einsum("...j,ij->...i", left_side, right_side, preferred_element_type=jnp.float32)


def outer_sum(left_side, right_side):
    flat_left = left_side.reshape(-1, left_side.shape[-1])
    flat_right = right_side.reshape(-1, right_side.shape[-1])
    return lax.dot_general(
        flat_left, flat_right, (((0,), (0,)), ((), ())), preferred_element_type=jnp.float32
    ).astype(jnp.bfloat16)


def add_rims(tile_field, radius):
    tile_place = lax.axis_index("tile")
    for which_bit in range(2):
        axis_dim = 2 - which_bit
        on_low = tile_place >> which_bit & 1 == 0
        side_len = tile_field.shape[axis_dim]
        upper_rim = lax.slice_in_dim(tile_field, side_len - radius, side_len, axis=axis_dim)
        lower_rim = lax.slice_in_dim(tile_field, 0, radius, axis=axis_dim)
        outgoing = jnp.where(on_low, upper_rim, lower_rim)
        incoming = swapped(outgoing, "tile", which_bit)
        blank_rim = jnp.zeros_like(incoming)
        tile_field = jnp.where(
            on_low,
            jnp.concatenate([blank_rim, tile_field, incoming], axis_dim),
            jnp.concatenate([incoming, tile_field, blank_rim], axis_dim),
        )
    return tile_field


def return_rims(grad_field, radius):
    tile_place = lax.axis_index("tile")
    for which_bit in (1, 0):
        axis_dim = 2 - which_bit
        on_low = tile_place >> which_bit & 1 == 0
        total_len = grad_field.shape[axis_dim]
        side_len = total_len - 2 * radius
        high_rim = lax.slice_in_dim(grad_field, total_len - radius, total_len, axis=axis_dim)
        low_rim = lax.slice_in_dim(grad_field, 0, radius, axis=axis_dim)
        outgoing = jnp.where(on_low, high_rim, low_rim)
        incoming = swapped(outgoing.astype(jnp.bfloat16), "tile", which_bit).astype(outgoing.dtype)
        core_part = lax.slice_in_dim(grad_field, radius, radius + side_len, axis=axis_dim)
        filler_shape = list(incoming.shape)
        filler_shape[axis_dim] = side_len - radius
        filler = jnp.zeros(filler_shape, jnp.float32)
        grad_field = core_part + jnp.where(
            on_low,
            jnp.concatenate([filler, incoming], axis_dim),
            jnp.concatenate([incoming, filler], axis_dim),
        )
    return grad_field


MESH = pl.DeviceIdType.MESH
VMEM_LIMIT = 62 << 20
COPIES = 8
SMALL_ROWS = 512
RIM_ROWS = 80
CORNER_ROWS = 16


def contract(left, right, left_axis, right_axis):
    return lax.dot_general(
        left,
        right,
        (((left_axis,), (right_axis,)), ((), ())),
        preferred_element_type=jnp.float32,
    )


def wide_sum(one, two):
    return one.astype(jnp.float32) + two.astype(jnp.float32)


def low_sum(one, two):
    return wide_sum(one, two).astype(jnp.bfloat16)


def row_loop(first, rows, width, step):
    count = rows // 16
    while count > 1 and (count * 16 * width > 65536 or rows % (count * 16)):
        count -= 1
    chunk = count * 16

    def body(q, carry):
        step(pl.ds(pl.multiple_of(first + q * chunk, 16), chunk))
        return carry

    if rows == chunk:
        body(0, 0)
    else:
        lax.fori_loop(0, rows // chunk, body, 0)


def lanes(start, size):
    return pl.ds(pl.multiple_of(start, 128), size)


class Place:
    def __init__(self):
        img = lax.axis_index("img")
        tile = lax.axis_index("tile")
        self.core, self.x, self.y = img % 2, (img // 2) % 2, img // 4
        self.low, self.high = tile % 2, tile // 2
        self.to_core = (img + 1 - 2 * self.core, tile)
        self.to_x = (img + 2 - 4 * self.x, tile)
        self.to_y = (img + 4 - 8 * self.y, tile)
        self.to_low = (img, tile + 1 - 2 * self.low)
        self.to_high = (img, tile + 2 - 4 * self.high)
        self.to_across = (img, 3 - tile)


def greet(partners):
    barrier = pltpu.get_barrier_semaphore()
    for partner in partners:
        pl.semaphore_signal(barrier, inc=1, device_id=partner, device_id_type=MESH)
    pl.semaphore_wait(barrier, len(partners))


def remote(source, target, send_sem, recv_sem, partner):
    return pltpu.make_async_remote_copy(
        src_ref=source,
        dst_ref=target,
        send_sem=send_sem,
        recv_sem=recv_sem,
        device_id=partner,
        device_id_type=MESH,
    )


def plan_pieces(shapes, piece_bytes):
    pieces = []
    for g, (height, width) in enumerate(shapes):
        rows = height // 8
        count = max(1, round(height * width * 2 / piece_bytes))
        while rows % (count * 32):
            count -= 1
        for p in range(count):
            pieces.append((g, p * (rows // count), rows // count))
    return pieces


def halving_scratch(shapes, pieces):
    count = len(pieces)

    def buffers(shape_of):
        return [
            pltpu.VMEM(shape_of(rows, shapes[g][1]), jnp.bfloat16) for g, _, rows in pieces
        ]

    scratch = buffers(lambda rows, width: (2, 2, rows, width))
    scratch += buffers(lambda rows, width: (2, 2, rows, width))
    scratch += buffers(lambda rows, width: (2, rows, width))
    scratch += buffers(lambda rows, width: (rows, width))
    scratch += buffers(lambda rows, width: (rows, width // 2))
    scratch += buffers(
        lambda rows, width: (rows, width // 4 if width % 512 == 0 else width // 2)
    )
    scratch += [
        pltpu.SemaphoreType.DMA((count * COPIES,)),
        pltpu.SemaphoreType.DMA((count * COPIES,)),
        pltpu.SemaphoreType.DMA((count,)),
    ]
    return scratch


class Halving:
    def __init__(self, place, shapes, pieces, grads, outs, scratch):
        count = len(pieces)
        self.place, self.shapes, self.pieces = place, shapes, pieces
        self.grads, self.outs = grads, outs
        self.own, self.half, self.quarter, self.eighth, self.pair, self.last = (
            scratch[k * count : (k + 1) * count] for k in range(6)
        )
        self.send_sem, self.recv_sem, self.own_sem = scratch[6 * count :]
        self.stages = (
            self.over_core,
            self.over_first,
            self.over_second,
            self.over_third,
            self.over_fourth,
            self.finish,
        )

    def narrow(self, i):
        return self.shapes[self.pieces[i][0]][1] % 512 != 0

    def copy(self, i, k):
        place = self.place
        g, first, rows = self.pieces[i]
        width = self.shapes[g][1] // 4
        half, quarter, eighth = self.half[i], self.quarter[i], self.eighth[i]
        pair, last = self.pair[i], self.last[i]
        part, cut = pl.ds(first, rows), rows // 2
        top, bottom = pl.ds(0, cut), pl.ds(cut, cut)
        if k == 0:
            ends = (self.grads[g].at[:, :, 1 - place.core, part, :], half, place.to_core)
        elif k == 1:
            ends = (half.at[:, 1 - place.x, top, :], quarter.at[:, top, :], place.to_x)
        elif k == 2:
            ends = (half.at[1 - place.y, :, bottom, :], quarter.at[:, bottom, :], place.to_y)
        elif k == 3:
            ends = (quarter.at[1 - place.y, top, :], eighth.at[top, :], place.to_y)
        elif k == 4:
            ends = (quarter.at[1 - place.x, bottom, :], eighth.at[bottom, :], place.to_x)
        elif k < 7 and not self.narrow(i):
            q = k - 5
            side = eighth.at[:, lanes((2 * q + 1 - place.low) * width, width)]
            ends = (side, pair.at[:, pl.ds(q * width, width)], place.to_low)
        elif k == 5:
            side = eighth.at[:, lanes((1 - place.high) * 2 * width, 2 * width)]
            ends = (side, pair, place.to_high)
        elif not self.narrow(i):
            ends = (pair.at[:, lanes((1 - place.high) * width, width)], last, place.to_high)
        else:
            ends = (pair, last, place.to_low)
        at = i * COPIES + k
        return remote(ends[0], ends[1], self.send_sem.at[at], self.recv_sem.at[at], ends[2])

    def own_copy(self, i):
        g, first, rows = self.pieces[i]
        mine = self.grads[g].at[:, :, self.place.core, pl.ds(first, rows), :]
        return pltpu.make_async_copy(mine, self.own[i], self.own_sem.at[i])

    def copies(self, i):
        return (0, 1, 2, 3, 4, 5, 7) if self.narrow(i) else (0, 1, 2, 3, 4, 5, 6, 7)

    def over_core(self, i):
        self.copy(i, 0).start()
        self.own_copy(i).start()

    def over_first(self, i):
        rows = self.pieces[i][2]
        half, own = self.half[i], self.own[i]
        self.copy(i, 0).wait_recv()
        self.own_copy(i).wait()
        for a in range(2):
            for b in range(2):

                def step(s, a=a, b=b):
                    half[a, b, s, :] = low_sum(half[a, b, s, :], own[a, b, s, :])

                row_loop(0, rows, half.shape[-1], step)
        self.copy(i, 1).start()
        self.copy(i, 2).start()

    def over_second(self, i):
        cut = self.pieces[i][2] // 2
        place, half, quarter = self.place, self.half[i], self.quarter[i]
        self.copy(i, 1).wait_recv()
        self.copy(i, 2).wait_recv()
        for a in range(2):

            def step_top(s, a=a):
                quarter[a, s, :] = low_sum(quarter[a, s, :], half[a, place.x, s, :])

            def step_bottom(s, a=a):
                quarter[a, s, :] = low_sum(quarter[a, s, :], half[place.y, a, s, :])

            row_loop(0, cut, quarter.shape[-1], step_top)
            row_loop(cut, cut, quarter.shape[-1], step_bottom)
        self.copy(i, 3).start()
        self.copy(i, 4).start()

    def over_third(self, i):
        cut = self.pieces[i][2] // 2
        place, quarter, eighth = self.place, self.quarter[i], self.eighth[i]
        self.copy(i, 3).wait_recv()
        self.copy(i, 4).wait_recv()

        def step_top(s):
            eighth[s, :] = low_sum(eighth[s, :], quarter[place.y, s, :])

        def step_bottom(s):
            eighth[s, :] = low_sum(eighth[s, :], quarter[place.x, s, :])

        row_loop(0, cut, eighth.shape[-1], step_top)
        row_loop(cut, cut, eighth.shape[-1], step_bottom)
        self.copy(i, 5).start()
        if not self.narrow(i):
            self.copy(i, 6).start()

    def over_fourth(self, i):
        g, _, rows = self.pieces[i]
        width = self.shapes[g][1] // 4
        place, eighth, pair = self.place, self.eighth[i], self.pair[i]
        self.copy(i, 5).wait_recv()
        if self.narrow(i):

            def step(s):
                kept = eighth[s, lanes(place.high * 2 * width, 2 * width)]
                pair[s, :] = low_sum(pair[s, :], kept)

        else:
            self.copy(i, 6).wait_recv()

            def step(s):
                for q in range(2):
                    at = slice(q * width, (q + 1) * width)
                    kept = eighth[s, lanes((2 * q + place.low) * width, width)]
                    pair[s, at] = low_sum(pair[s, at], kept)

        row_loop(0, rows, pair.shape[-1], step)
        self.copy(i, 7).start()

    def finish(self, i):
        g, first, rows = self.pieces[i]
        width = self.shapes[g][1] // 4
        place, pair, last, out = self.place, self.pair[i], self.last[i], self.outs[g]
        self.copy(i, 7).wait_recv()

        def step(s):
            at = pl.ds(pl.multiple_of(s.start + first, 16), s.size)
            if self.narrow(i):
                both = wide_sum(last[s, :], pair[s, :])
                out[at, :] = jnp.where(place.low == 0, both[:, :width], both[:, width:])
            else:
                kept = pair[s, lanes(place.high * width, width)]
                out[at, :] = wide_sum(last[s, :], kept)

        row_loop(0, rows, pair.shape[-1], step)

    def wait_sends(self):
        for i in range(len(self.pieces)):
            for k in self.copies(i):
                self.copy(i, k).wait_send()


def halving_operands(grads):
    return [grad.reshape(2, 2, 2, grad.shape[0] // 8, grad.shape[1]) for grad in grads]


def halving_outputs(shapes):
    return [
        jax.ShapeDtypeStruct((height // 8, width // 4), jnp.float32) for height, width in shapes
    ]


def whole_block(shape):
    return pl.BlockSpec(shape, lambda *_: (0,) * len(shape))


def fixed_block(shape):
    return pl.BlockSpec(shape, lambda *_: (0,) * len(shape), pipeline_mode=pl.Buffered(1))


def rim_copies(place, source, rim, corner, rim_in, row_in, corner_in, sems):
    cells = source.shape[1]
    start = pl.multiple_of((1 - place.high) * (cells - RIM_ROWS), 16)
    return (
        remote(rim, rim_in, sems.at[0], sems.at[1], place.to_low),
        remote(
            source.at[:, pl.ds(start, RIM_ROWS), :], row_in, sems.at[2], sems.at[3], place.to_high
        ),
        remote(corner, corner_in, sems.at[4], sems.at[5], place.to_across),
    )


def mlp_back_kernel(shapes, pieces, plan, *refs):
    matrices = len(shapes)
    count = len(pieces)
    grad_low, norm_low, wide, slope, w_shrink, w_expand, unit, scale, table, parts = refs[:10]
    grads = refs[10 : 10 + matrices]
    refs = refs[10 + matrices :]
    shrink_out, expand_out, dz_out, gain_out, token_out = refs[:5]
    outs = refs[5 : 5 + matrices]
    refs = refs[5 + matrices :]
    halving_refs = refs[: 6 * count + 3]
    refs = refs[6 * count + 3 :]
    norm_turned, back, dz, out_sem, unit_sem = refs[:5]
    buffers, result_buffers, in_sems, result_sems = refs[5:9], refs[9:11], refs[11], refs[12]
    token_refs = refs[13:]
    place = Place()
    halving = Halving(place, shapes, pieces, grads, outs, halving_refs)
    token_sum = TokenSum(place, parts, token_out, token_refs)
    steps = plan["steps"]
    j = pl.program_id(0)

    def slot(n):
        for i, k in plan["slots"].get(n, ()):
            if i == "tokens":
                token_sum.step(k)
            else:
                halving.stages[k](i)

    def slots(odd):
        for n in range(steps):
            if plan["slots"].get(2 * n + odd):
                pl.when(j == n)(partial(slot, 2 * n + odd))

    width = plan["width"]

    unit_load = pltpu.make_async_copy(unit, dz, unit_sem)

    def fetches(n):
        slot_, at = n % 2, lanes(n * width, width)
        parts = (wide.at[:, at], slope.at[:, at], w_shrink.at[at, :], w_expand.at[:, at])
        return [
            pltpu.make_async_copy(part, buffers[k].at[slot_], in_sems.at[slot_ * 4 + k])
            for k, part in enumerate(parts)
        ]

    def stores(n):
        slot_, at = n % 2, lanes(n * width, width)
        targets = (shrink_out.at[at, :], expand_out.at[:, at])
        return [
            pltpu.make_async_copy(
                result_buffers[k].at[slot_], target, result_sems.at[slot_ * 2 + k]
            )
            for k, target in enumerate(targets)
        ]

    @pl.when(j == 0)
    def _():
        for copy in fetches(0):
            copy.start(priority=1)
        unit_load.start()
        greet(
            (
                place.to_core,
                place.to_x,
                place.to_y,
                place.to_low,
                place.to_high,
            )
        )

    @pl.when(j + 1 < steps)
    def _():
        for copy in fetches(j + 1):
            copy.start(priority=1)

    slots(0)

    @pl.when(j == 0)
    def _():
        norm_turned[...] = norm_low[...].T

    for copy in fetches(j):
        copy.wait()

    @pl.when(j >= 2)
    def _():
        for copy in stores(j - 2):
            copy.wait()

    now = j % 2
    grad_wide = contract(grad_low[...], buffers[2][now], 1, 1)
    grad_wide = (grad_wide * buffers[1][now].astype(jnp.float32)).astype(jnp.bfloat16)
    turned = contract(buffers[0][now], grad_low[...], 0, 0)
    result_buffers[0][now] = turned.astype(jnp.bfloat16)
    slots(1)
    turned = contract(norm_turned[...], grad_wide, 1, 0)
    result_buffers[1][now] = turned.astype(jnp.bfloat16)
    term = contract(grad_wide, buffers[3][now], 1, 1)
    for copy in stores(j):
        copy.start(priority=1)

    @pl.when(j == 0)
    def _():
        back[...] = term

    @pl.when(j > 0)
    def _():
        back[...] = back[...] + term

    @pl.when(j == steps - 1)
    def _():
        unit_load.wait()
        gain_row = table[49:50, :]
        chunk = 48

        def body(q, sums):
            at = pl.ds(pl.multiple_of(q * chunk, 16), chunk)
            grad = back[at, :]
            n = dz[at, :].astype(jnp.float32)
            t = grad * gain_row
            mean_t = jnp.mean(t, axis=-1, keepdims=True)
            mean_tn = jnp.mean(t * n, axis=-1, keepdims=True)
            dz[at, :] = (scale[at, :] * (t - mean_t - n * mean_tn)).astype(jnp.bfloat16)
            return sums + jnp.sum((grad * n).reshape(chunk // 8, 8, -1), axis=0)

        sums = jnp.zeros((8, dz.shape[1]), jnp.float32)
        sums = lax.fori_loop(0, dz.shape[0] // chunk, body, sums)
        gain_out[...] = jnp.sum(sums, axis=0, keepdims=True)
        back_copy = pltpu.make_async_copy(dz, dz_out, out_sem)
        back_copy.start()
        for n in range(2 * steps, plan["last"] + 1):
            slot(n)
        back_copy.wait()
        for n in (steps - 2, steps - 1):
            for copy in stores(n):
                copy.wait()
        token_sum.wait_sends()
        halving.wait_sends()


def spread_plan(count, steps, first, second, rest):
    slots = {0: [(i, 0) for i in range(count)]}
    last = 0
    for i in range(count):
        at = [int(first[0] + first[1] * i), int(second[0] + second[1] * i)]
        at += [at[1] + r for r in rest]
        for k, n in enumerate(at):
            slots.setdefault(n, []).append((i, k + 1))
        last = max(last, at[-1])
    for n in slots:
        slots[n].sort(key=lambda item: (-item[1], item[0]))
    return {"slots": slots, "last": last, "steps": steps}


def map_mlp_back(
    grad_low, norm_low, wide, slope, w_shrink, w_expand, unit, scale, table, parts, grads
):
    tokens, channels = grad_low.shape
    hidden = w_shrink.shape[0]
    width = 512
    steps = hidden // width
    shapes = [grad.shape for grad in grads]
    pieces = plan_pieces(shapes, 1_600_000)
    plan = spread_plan(len(pieces), steps, (1, 1.0), (4, 1.0), (2, 4, 6))
    plan["width"] = width
    for k, n in enumerate((0, 5, 11)):
        plan["slots"].setdefault(n, []).append(("tokens", k))
    token_shape = parts.shape[1:]
    low = jnp.bfloat16
    any_space = pl.BlockSpec(memory_space=pl.ANY)
    results = pl.pallas_call(
        partial(mlp_back_kernel, shapes, pieces, plan),
        grid=(steps,),
        in_specs=[
            fixed_block((tokens, channels)),
            fixed_block((tokens, channels)),
            any_space,
            any_space,
            any_space,
            any_space,
            any_space,
            fixed_block((tokens, 1)),
            fixed_block(table.shape),
            any_space,
        ]
        + [any_space] * len(grads),
        out_specs=[
            any_space,
            any_space,
            any_space,
            whole_block((1, channels)),
            whole_block(token_shape),
        ]
        + [whole_block(item.shape) for item in halving_outputs(shapes)],
        out_shape=[
            jax.ShapeDtypeStruct((hidden, channels), low),
            jax.ShapeDtypeStruct((channels, hidden), low),
            jax.ShapeDtypeStruct((tokens, channels), low),
            jax.ShapeDtypeStruct((1, channels), jnp.float32),
            jax.ShapeDtypeStruct(token_shape, jnp.float32),
        ]
        + halving_outputs(shapes),
        scratch_shapes=halving_scratch(shapes, pieces)
        + [
            pltpu.VMEM((channels, tokens), low),
            pltpu.VMEM((tokens, channels), jnp.float32),
            pltpu.VMEM((tokens, channels), low),
            pltpu.SemaphoreType.DMA,
            pltpu.SemaphoreType.DMA,
            pltpu.VMEM((2, tokens, width), low),
            pltpu.VMEM((2, tokens, width), low),
            pltpu.VMEM((2, width, channels), low),
            pltpu.VMEM((2, channels, width), low),
            pltpu.VMEM((2, width, channels), low),
            pltpu.VMEM((2, channels, width), low),
            pltpu.SemaphoreType.DMA((8,)),
            pltpu.SemaphoreType.DMA((4,)),
            pltpu.VMEM((2,) + token_shape, low),
            pltpu.VMEM((2,) + token_shape, low),
            pltpu.VMEM(token_shape, low),
            pltpu.SemaphoreType.DMA((8,)),
        ],
        compiler_params=pltpu.CompilerParams(
            collective_id=0, has_side_effects=True, vmem_limit_bytes=VMEM_LIMIT
        ),
        name="map_mlp_back",
    )(
        grad_low,
        norm_low,
        wide,
        slope,
        w_shrink,
        w_expand,
        unit,
        scale,
        table,
        parts,
        *halving_operands(grads),
    )
    return results[:5], results[5:]


def shift_rows(read_row, shifted, rows, side):
    def body(r, carry):
        line = read_row(r)
        for b in range(7):
            shifted[b, r] = line[b : b + side].reshape(side // 8, 8, 128)
        return carry

    lax.fori_loop(0, rows, body, 0, unroll=2)


def fill_taps(tap_ref, taps, flip):
    for k in range(49):
        tap = tap_ref[48 - k if flip else k].reshape(1, 128)
        taps[k] = jnp.broadcast_to(tap, (8, 128))


def seven_rows(shifted, taps, first, group, side):
    sums = [jnp.zeros((side // 8, 8, 128), jnp.float32) for _ in range(group)]
    for b in range(7):
        for r in range(group + 6):
            line = shifted[b, first + r]
            for k in range(group):
                if 0 <= r - k < 7:
                    sums[k] = sums[k] + taps[(r - k) * 7 + b][None] * line
    return sums


def tap_sums(shifted, read_line, rows, side, group, keep):
    for columns in ((0, 1, 2, 3), (4, 5, 6)):

        def body(g, sums):
            sums = [list(part) for part in sums]
            first = g * group
            lines = [read_line(first + k).reshape(side // 8, 8, 128) for k in range(group)]
            for n, b in enumerate(columns):
                for r in range(group + 6):
                    line = shifted[b, first + r]
                    for k in range(group):
                        if 0 <= r - k < 7:
                            sums[r - k][n] = sums[r - k][n] + jnp.sum(line * lines[k], axis=0)
            return tuple(tuple(part) for part in sums)

        zero = jnp.zeros((8, 128), jnp.float32)
        sums = lax.fori_loop(
            0, rows // group, body, tuple(tuple(zero for _ in columns) for _ in range(7))
        )
        for a in range(7):
            for n, b in enumerate(columns):
                keep(a * 7 + b, jnp.sum(sums[a][n], axis=0, keepdims=True))


class TokenGather:
    def __init__(self, own, everyone, near, held, local_sems, sems):
        self.img = lax.axis_index("img")
        self.tile = lax.axis_index("tile")
        self.own, self.everyone, self.near, self.held = own, everyone, near, held
        self.local_sems, self.sems = local_sems, sems

    def copy(self, k, up, source, target):
        at = 4 * k + 2 * up
        partner = (self.img, self.tile + 1 if up else self.tile - 1)
        return remote(source, target, self.sems.at[at], self.sems.at[at + 1], partner)

    def given(self, k, up):
        if k == 0:
            return self.copy(k, up, self.own, self.near.at[1 - up])
        origin = self.tile - k if up else self.tile + k
        source = self.held.at[1 - up] if k == 1 else self.everyone.at[origin]
        return self.copy(k, up, source, self.everyone.at[origin])

    def gives(self, k, up):
        if up:
            return (self.tile >= k) & (self.tile < 3)
        return (self.tile + k <= 3) & (self.tile > 0)

    def takes(self, k, up):
        return self.tile > k if up else self.tile + k < 3

    def loads(self):
        return (
            pltpu.make_async_copy(self.near, self.held.at[pl.ds(0, 2)], self.local_sems.at[0]),
            pltpu.make_async_copy(self.own, self.held.at[2], self.local_sems.at[1]),
        )

    def local_stores(self, act):
        target = self.everyone.at[self.tile]
        act(pltpu.make_async_copy(self.held.at[2], target, self.local_sems.at[2]))
        for up in (0, 1):

            @pl.when(self.takes(0, up))
            def _():
                target = self.everyone.at[self.tile - 1 if up else self.tile + 1]
                sem = self.local_sems.at[3 + up]
                act(pltpu.make_async_copy(self.held.at[1 - up], target, sem))

    def hand_on(self, k):
        for up in (0, 1):

            @pl.when(self.gives(k, up))
            def _():
                self.given(k, up).start()

    def take(self, k):
        for up in (0, 1):

            @pl.when(self.takes(k, up))
            def _():
                if k == 0:
                    self.copy(k, up, self.own, self.near.at[1 - up]).wait_recv()
                else:
                    origin = self.tile - 1 - k if up else self.tile + 1 + k
                    self.copy(k, up, self.held.at[0], self.everyone.at[origin]).wait_recv()

    def wait_sends(self, steps):
        for k in steps:
            for up in (0, 1):

                @pl.when(self.gives(k, up))
                def _():
                    self.given(k, up).wait_send()


class TokenSum:
    def __init__(self, place, parts, out, scratch):
        self.place, self.parts, self.out = place, parts, out
        self.mine, self.first, self.second, self.sems = scratch

    def copy(self, k):
        place, sems = self.place, self.sems
        if k < 2:
            source, target = self.parts.at[2 * k + 1 - place.low], self.first.at[k]
            partner = place.to_low
        else:
            source, target = self.mine.at[1 - place.high], self.second
            partner = place.to_high
        return remote(source, target, sems.at[2 * k], sems.at[2 * k + 1], partner)

    def load(self, k):
        part = self.parts.at[2 * k + self.place.low]
        return pltpu.make_async_copy(part, self.mine.at[k], self.sems.at[6 + k])

    def step(self, k):
        if k == 0:
            for n in range(2):
                self.copy(n).start()
                self.load(n).start()
        elif k == 1:
            for n in range(2):
                self.copy(n).wait_recv()
                self.load(n).wait()
                for q in range(self.mine.shape[1]):
                    self.mine[n, q] = low_sum(self.mine[n, q], self.first[n, q])
            self.copy(2).start()
        else:
            self.copy(2).wait_recv()
            for q in range(self.out.shape[0]):
                self.out[q] = wide_sum(self.mine[self.place.high, q], self.second[q])

    def wait_sends(self):
        for k in range(3):
            self.copy(k).wait_send()


class SmallSum:
    def __init__(self, place, out, work, inbox, send_sem, recv_sem):
        self.out, self.work, self.inbox = out, work, inbox
        self.send_sem, self.recv_sem = send_sem, recv_sem
        self.total = out.shape[0]
        self.halvings = (
            (place.to_core, place.core),
            (place.to_x, place.x),
            (place.to_y, place.y),
            (place.to_low, place.low),
            (place.to_high, place.high),
        )
        starts, size = [0], self.total
        for _, bit in self.halvings:
            size //= 2
            starts.append(starts[-1] + bit * size)
        self.starts = starts

    def rows(self, start, size):
        return pl.ds(pl.multiple_of(start, 8), size)

    def copy(self, k):
        if k < 5:
            partner, bit = self.halvings[k]
            size = self.total >> (k + 1)
            give = self.rows(self.starts[k] + (1 - bit) * size, size)
            source = self.work.at[give, :]
            target = self.inbox.at[pl.ds(self.total - 2 * size, size), :]
        else:
            partner, _ = self.halvings[9 - k]
            mine = self.rows(self.starts[10 - k], self.total >> (10 - k))
            source = target = self.out.at[mine, :]
        return remote(source, target, self.send_sem.at[k], self.recv_sem.at[k], partner)

    def step(self, k):
        if k > 0:
            self.copy(k - 1).wait_recv()
        if 1 <= k <= 5:
            size = self.total >> k
            at = self.rows(self.starts[k], size)
            summed = self.work[at, :] + self.inbox[pl.ds(self.total - 2 * size, size), :]
            if k < 5:
                self.work[at, :] = summed
            else:
                self.out[at, :] = summed
        if k < 10:
            self.copy(k).start()

    def wait_sends(self):
        for k in range(10):
            self.copy(k).wait_send()


def conv_back_kernel(shapes, pieces, plan, *refs):
    matrices = len(shapes)
    count = len(pieces)
    (dz, pick, place_map, padded, grad_low, tap_ref, sides, one, two, gain) = refs[:10]
    grads = refs[10 : 10 + matrices]
    refs = refs[10 + matrices :]
    map_out, small_out = refs[:2]
    outs = refs[2 : 2 + matrices]
    refs = refs[2 + matrices :]
    halving_refs = refs[: 6 * count + 3]
    refs = refs[6 * count + 3 :]
    field, shifted, taps, tap_out, work, inbox, gathered, small_send, small_recv = refs[:9]
    rim, corner, rim_in, row_in, corner_in, rim_sems = refs[9:]
    place = Place()
    halving = Halving(place, shapes, pieces, grads, outs, halving_refs)
    smalls = SmallSum(place, gathered, work, inbox, small_send, small_recv)
    slots_, cells, channels = dz.shape
    side = padded.shape[1] - 6
    blocks = channels // 128
    j = pl.program_id(0)
    s = j % 2
    c = (j // 2) % blocks
    columns = lanes(c * 128, 128)

    def slot(n):
        for i, k in plan["slots"].get(n, ()):
            if i == "small":
                smalls.step(k)
            else:
                halving.stages[k](i)

    @pl.when(j == 0)
    def _():
        greet(
            (
                place.to_core,
                place.to_x,
                place.to_y,
                place.to_low,
                place.to_high,
                place.to_across,
            )
        )

    rims = rim_copies(place, dz, rim, corner, rim_in, row_in, corner_in, rim_sems)

    for n in range(plan["steps"]):
        if n in plan["slots"] and n != 2 * blocks:
            pl.when(j == n)(partial(slot, n))

    @pl.when(j == 0)
    def _():
        for s in range(slots_):
            both = contract(pick[...], dz[s], 1, 0).astype(jnp.bfloat16)
            rim[s] = both[:RIM_ROWS]
            corner[s] = both[RIM_ROWS:]
        for copy in rims:
            copy.start()

    @pl.when(j < 2 * blocks)
    def _():
        shift_rows(lambda r: padded[0, r].astype(jnp.float32), shifted, side + 6, side)

        @pl.when(s == 0)
        def _():
            tap_out[c] = jnp.zeros(tap_out.shape[1:], jnp.float32)

        def read_line(i):
            line = dz[s, pl.ds(pl.multiple_of(i * side, 8), side), columns]
            return line.astype(jnp.float32)

        def keep(k, value):
            tap_out[c, k : k + 1, :] = tap_out[c, k : k + 1, :] + value

        tap_sums(shifted, read_line, side, side, 4, keep)

    @pl.when(j == 2 * blocks)
    def _():
        for q in range(blocks):
            work[q * 49 : (q + 1) * 49, :] = tap_out[q, :49, :]
        base = blocks * 49
        work[base:, :] = jnp.zeros((SMALL_ROWS - base, 128), jnp.float32)
        for q in range(sides.shape[1] // 128):
            at = slice(q * 128, (q + 1) * 128)
            row = base + q * 16
            work[row : row + 11, :] = sides[:11, at]
            work[row + 11 : row + 12, :] = one[:, at]
            work[row + 12 : row + 13, :] = two[:, at]
        for q in range(blocks):
            row = base + sides.shape[1] // 8 + q
            work[row : row + 1, :] = gain[:, q * 128 : (q + 1) * 128]
        slot(2 * blocks)
        for copy in rims:
            copy.wait()
        for q in range(slots_):
            parts = jnp.concatenate([dz[q], rim_in[q], row_in[q], corner_in[q]], axis=0)
            whole = contract(place_map[...], parts, 1, 0).astype(jnp.bfloat16)
            field[q] = whole.reshape(field.shape[1:])

    @pl.when(j >= 2 * blocks)
    def _():
        fill_taps(tap_ref, taps, True)
        shift_rows(
            lambda r: field[s, r, :, columns].astype(jnp.float32), shifted, side + 6, side
        )

        def body(g, carry):
            for k, line in enumerate(seven_rows(shifted, taps, g * 4, 4, side)):
                at = pl.ds(pl.multiple_of((g * 4 + k) * side, 8), side)
                total = line.reshape(side, 128) + grad_low[0, at, :].astype(jnp.float32)
                map_out[0, at, :] = total.astype(jnp.bfloat16)
            return carry

        lax.fori_loop(0, side // 4, body, 0)

    @pl.when(j == plan["steps"] - 1)
    def _():
        for n in range(plan["steps"], plan["last"] + 1):
            slot(n)
        small_out[...] = gathered[...]
        halving.wait_sends()
        smalls.wait_sends()


def conv_back(
    dz, pick, place_map, padded, grad_low, tap_weights, smalls, grads
):
    slots, cells, channels = grad_low.shape
    rows, cols = padded.shape[1:3]
    side = rows - 6
    blocks = channels // 128
    steps = 4 * blocks
    shapes = [grad.shape for grad in grads]
    pieces = plan_pieces(shapes, 2_100_000)
    plan = spread_plan(len(pieces), steps, (1, 3), (7, 3), (4, 8, 12))
    for k in range(11):
        at = 2 * blocks + 2 * k
        plan["slots"].setdefault(at, []).append(("small", k))
        plan["last"] = max(plan["last"], at)
    any_space = pl.BlockSpec(memory_space=pl.ANY)

    def first_half(j):
        k = jnp.minimum(j, 2 * blocks - 1)
        return (k % 2, 0, 0, k // 2)

    def second_half(j):
        k = jnp.maximum(j - 2 * blocks, 0)
        return (k % 2, 0, k // 2)

    results = pl.pallas_call(
        partial(conv_back_kernel, shapes, pieces, plan),
        grid=(steps,),
        in_specs=[
            fixed_block(dz.shape),
            fixed_block(pick.shape),
            fixed_block(place_map.shape),
            pl.BlockSpec((1, rows, cols, 128), first_half),
            pl.BlockSpec((1, cells, 128), second_half),
            pl.BlockSpec(
                (tap_weights.shape[0], 128), lambda j: (0, jnp.maximum(j - 2 * blocks, 0) // 2)
            ),
        ]
        + [fixed_block(item.shape) for item in smalls]
        + [any_space] * len(grads),
        out_specs=[
            pl.BlockSpec((1, cells, 128), second_half),
            whole_block((SMALL_ROWS, 128)),
        ]
        + [whole_block(item.shape) for item in halving_outputs(shapes)],
        out_shape=[
            jax.ShapeDtypeStruct((slots, cells, channels), jnp.bfloat16),
            jax.ShapeDtypeStruct((SMALL_ROWS, 128), jnp.float32),
        ]
        + halving_outputs(shapes),
        scratch_shapes=halving_scratch(shapes, pieces)
        + [
            pltpu.VMEM((slots, rows, 32, channels), jnp.bfloat16),
            pltpu.VMEM((7, rows, side // 8, 8, 128), jnp.float32),
            pltpu.VMEM((49, 8, 128), jnp.float32),
            pltpu.VMEM((blocks, 56, 128), jnp.float32),
            pltpu.VMEM((SMALL_ROWS, 128), jnp.float32),
            pltpu.VMEM((SMALL_ROWS, 128), jnp.float32),
            pltpu.VMEM((SMALL_ROWS, 128), jnp.float32),
            pltpu.SemaphoreType.DMA((10,)),
            pltpu.SemaphoreType.DMA((10,)),
            pltpu.VMEM((slots, RIM_ROWS, channels), jnp.bfloat16),
            pltpu.VMEM((slots, CORNER_ROWS, channels), jnp.bfloat16),
            pltpu.VMEM((slots, RIM_ROWS, channels), jnp.bfloat16),
            pltpu.VMEM((slots, RIM_ROWS, channels), jnp.bfloat16),
            pltpu.VMEM((slots, CORNER_ROWS, channels), jnp.bfloat16),
            pltpu.SemaphoreType.DMA((6,)),
        ],
        compiler_params=pltpu.CompilerParams(
            collective_id=1, has_side_effects=True, vmem_limit_bytes=VMEM_LIMIT
        ),
        name="conv_back",
    )(
        dz,
        pick,
        place_map,
        padded,
        grad_low,
        tap_weights,
        *smalls,
        *halving_operands(grads),
    )
    return results[0], results[1], results[2:]


def rim_maps(side):
    tile = lax.axis_index("tile")
    low, high = tile % 2, tile // 2
    cells = side * side
    row = jnp.arange(RIM_ROWS + CORNER_ROWS, dtype=jnp.int32)
    edge_col = jnp.where(low == 0, side - 3, 0)
    edge_row = jnp.where(high == 0, side - 3, 0)
    rim_from = (row % side) * side + edge_col + row // side
    k = row - RIM_ROWS
    corner_from = (edge_row + k // 3) * side + edge_col + k % 3
    source = jnp.where(
        row < 3 * side, rim_from, jnp.where((k >= 0) & (k < 9), corner_from, -1)
    )
    pick = (source[:, None] == jnp.arange(cells, dtype=jnp.int32)[None, :]).astype(jnp.bfloat16)
    at = jnp.arange((side + 6) * 32, dtype=jnp.int32)
    i, j = at // 32 - 3, at % 32 - 3
    inside_i, inside_j = (i >= 0) & (i < side), (j >= 0) & (j < side)
    beside_j = ((j < 0) & (low == 1)) | ((j >= side) & (j < side + 3) & (low == 0))
    beside_i = ((i < 0) & (high == 1)) | ((i >= side) & (high == 0))
    q = jnp.where(j < 0, j + 3, j - side)
    p = jnp.where(i < 0, i + 3, i - side)
    skip = jnp.where(high == 1, RIM_ROWS - 3 * side, 0)
    source = jnp.where(
        inside_i & inside_j,
        i * side + j,
        jnp.where(
            inside_i & beside_j,
            cells + q * side + i,
            jnp.where(
                beside_i & inside_j,
                cells + RIM_ROWS + skip + p * side + j,
                jnp.where(beside_i & beside_j, cells + 2 * RIM_ROWS + p * 3 + q, -1),
            ),
        ),
    )
    parts = cells + 2 * RIM_ROWS + CORNER_ROWS
    place_map = (source[:, None] == jnp.arange(parts, dtype=jnp.int32)[None, :]).astype(
        jnp.bfloat16
    )
    return pick, place_map


def slot_rims(place, s, source, rim, corner, rim_in, row_in, corner_in, sems):
    cells = source.shape[1]
    start = pl.multiple_of((1 - place.high) * (cells - RIM_ROWS), 16)
    row = source.at[s, pl.ds(start, RIM_ROWS), :]
    return (
        remote(rim.at[s], rim_in.at[s], sems.at[6 * s], sems.at[6 * s + 1], place.to_low),
        remote(row, row_in.at[s], sems.at[6 * s + 2], sems.at[6 * s + 3], place.to_high),
        remote(
            corner.at[s], corner_in.at[s], sems.at[6 * s + 4], sems.at[6 * s + 5], place.to_across
        ),
    )


def conv_front_kernel(
    source,
    own,
    pick,
    place_map,
    tap_ref,
    table,
    norm_out,
    unit_out,
    scale_out,
    field_out,
    near,
    cells_ref,
    field,
    spread,
    shifted,
    taps,
    rim,
    corner,
    rim_in,
    row_in,
    corner_in,
    sems,
    load_sem,
    store_sem,
    near_sems,
):
    place = Place()
    gather = TokenGather(own, None, near, None, None, near_sems)
    slots, cells, channels = cells_ref.shape
    blocks = channels // 128
    side = field.shape[1] - 6
    j = pl.program_id(0)
    s, c = j // blocks, j % blocks
    columns = lanes(c * 128, 128)
    low = jnp.bfloat16

    def rims(q):
        return slot_rims(place, q, cells_ref, rim, corner, rim_in, row_in, corner_in, sems)

    def select(q):
        both = contract(pick[...], cells_ref[q], 1, 0).astype(low)
        rim[q] = both[:RIM_ROWS]
        corner[q] = both[RIM_ROWS:]
        for copy in rims(q):
            copy.start()

    def store(q):
        return pltpu.make_async_copy(field.at[q], field_out.at[q], store_sem.at[q])

    def build(q):
        for copy in rims(q):
            copy.wait()
        parts = jnp.concatenate([cells_ref[q], rim_in[q], row_in[q], corner_in[q]], axis=0)
        whole = contract(place_map[...], parts, 1, 0).astype(low)
        field[q] = whole.reshape(field.shape[1:])
        store(q).start()

    @pl.when(j == 0)
    def _():
        load = pltpu.make_async_copy(source, cells_ref, load_sem)
        load.start()
        greet((place.to_low, place.to_high, place.to_across))
        load.wait()
        select(0)
        build(0)
        for q in range(1, slots):
            select(q)

    for q in range(1, slots):
        pl.when(j == q * blocks)(partial(build, q))

    @pl.when(j == blocks)
    def _():
        gather.hand_on(0)

    fill_taps(tap_ref, taps, False)
    shift_rows(lambda r: field[s, r, :, columns].astype(jnp.float32), shifted, side + 6, side)

    def body(g, carry):
        for k, line in enumerate(seven_rows(shifted, taps, g * 4, 4, side)):
            at = pl.ds(pl.multiple_of((g * 4 + k) * side, 8), side)
            spread[c, at, :] = line.reshape(side, 128)
        return carry

    lax.fori_loop(0, side // 4, body, 0)

    @pl.when(c == blocks - 1)
    def _():
        gain_row = table[49:50, :]
        chunk = 48

        def norm(n, carry):
            at = pl.ds(pl.multiple_of(n * chunk, 16), chunk)
            values = jnp.concatenate([spread[b, at, :] for b in range(blocks)], axis=1)
            unit, scale = norm_parts(values)
            unit_out[at, :] = unit.astype(low)
            norm_out[at, :] = (unit * gain_row).astype(low)
            scale_out[at, :] = scale
            return carry

        lax.fori_loop(0, cells // chunk, norm, 0)

    @pl.when(j == slots * blocks - 1)
    def _():
        for q in range(slots):
            store(q).wait()
        gather.take(0)
        gather.wait_sends((0,))


def conv_front(source, own, pick, place_map, table):
    slots, cells, channels = source.shape
    side = math.isqrt(cells)
    blocks = channels // 128
    low = jnp.bfloat16
    field_shape = (slots, side + 6, 32, channels)
    any_space = pl.BlockSpec(memory_space=pl.ANY)
    by_slot = lambda j: (j // blocks, 0)
    rows = slots * cells
    return pl.pallas_call(
        conv_front_kernel,
        grid=(slots * blocks,),
        in_specs=[
            any_space,
            any_space,
            fixed_block(pick.shape),
            fixed_block(place_map.shape),
            pl.BlockSpec((table.shape[0], 128), lambda j: (0, j % blocks)),
            fixed_block(table.shape),
        ],
        out_specs=[
            pl.BlockSpec((cells, channels), by_slot),
            pl.BlockSpec((cells, channels), by_slot),
            pl.BlockSpec((cells, 1), by_slot),
            any_space,
            any_space,
        ],
        out_shape=[
            jax.ShapeDtypeStruct((rows, channels), low),
            jax.ShapeDtypeStruct((rows, channels), low),
            jax.ShapeDtypeStruct((rows, 1), jnp.float32),
            jax.ShapeDtypeStruct(field_shape, low),
            jax.ShapeDtypeStruct((2,) + own.shape, low),
        ],
        scratch_shapes=[
            pltpu.VMEM((slots, cells, channels), low),
            pltpu.VMEM(field_shape, low),
            pltpu.VMEM((blocks, cells, 128), jnp.float32),
            pltpu.VMEM((7, side + 6, side // 8, 8, 128), jnp.float32),
            pltpu.VMEM((49, 8, 128), jnp.float32),
            pltpu.VMEM((slots, RIM_ROWS, channels), low),
            pltpu.VMEM((slots, CORNER_ROWS, channels), low),
            pltpu.VMEM((slots, RIM_ROWS, channels), low),
            pltpu.VMEM((slots, RIM_ROWS, channels), low),
            pltpu.VMEM((slots, CORNER_ROWS, channels), low),
            pltpu.SemaphoreType.DMA((6 * slots,)),
            pltpu.SemaphoreType.DMA,
            pltpu.SemaphoreType.DMA((slots,)),
            pltpu.SemaphoreType.DMA((12,)),
        ],
        compiler_params=pltpu.CompilerParams(
            collective_id=2, has_side_effects=True, vmem_limit_bytes=VMEM_LIMIT
        ),
        name="conv_front",
    )(source, own, pick, place_map, table, table)


def map_mlp_kernel(
    norm_low,
    source,
    w_expand,
    w_shrink,
    w_adapt,
    pool,
    live,
    *refs,
):
    gathers = len(refs) > 6
    if gathers:
        own, near, everyone = refs[0], refs[1], refs[7]
        refs, rest = refs[2:7] + refs[8:9], refs[9:]
    wide_out, slope_out, map_out, pooled_out, adapted_out, total = refs
    j = pl.program_id(0)
    low = jnp.bfloat16
    if gathers:
        place = Place()
        gather = TokenGather(own, everyone, near, *rest)

        @pl.when(j == 0)
        def _():
            for copy in gather.loads():
                copy.start()
            greet((place.to_low, place.to_high, place.to_across))
            for copy in gather.loads():
                copy.wait()
            gather.hand_on(1)
            gather.local_stores(lambda copy: copy.start())

        @pl.when(j == 2)
        def _():
            gather.take(1)
            gather.hand_on(2)

    rows, width = norm_low.shape[0], w_expand.shape[1]
    half = rows // 2
    for part in (pl.ds(0, half), pl.ds(half, half)):
        wide, slope = gelu_pair(contract(norm_low[part, :], w_expand[...], 1, 0))
        wide_out[part, :] = wide
        slope_out[part, :] = slope
        term = contract(wide, w_shrink[...], 1, 0)

        @pl.when(j == 0)
        def _():
            total[part, :] = source[part, :].astype(jnp.float32) + term

        @pl.when(j > 0)
        def _():
            total[part, :] = total[part, :] + term

    @pl.when(j == pl.num_programs(0) - 1)
    def _():
        slots, cells, _ = map_out.shape
        for s in range(slots):
            after = total[pl.ds(s * cells, cells), :].astype(low)
            keep = jnp.broadcast_to(live[s], after.shape) > 0
            map_out[s] = jnp.where(keep, after, jnp.zeros_like(after))
            pooled = contract(pool[...], after, 1, 0).astype(low)
            pooled_out[s] = pooled
            adapted_out[s] = contract(pooled, w_adapt[...], 1, 0).astype(low)
        if gathers:
            gather.take(2)
            gather.local_stores(lambda copy: copy.wait())
            gather.wait_sends((1, 2))


def map_mlp(norm_low, source, w_expand, w_shrink, w_adapt, pool, live, own=None, near=None):
    slots, cells, channels = source.shape
    hidden, width = w_expand.shape[1], 1024
    few, model = pool.shape[0], w_adapt.shape[1]
    low = jnp.bfloat16
    extra, extra_space, extra_shape, extra_scratch = [], [], [], []
    params = pltpu.CompilerParams(vmem_limit_bytes=VMEM_LIMIT)
    if own is not None:
        extra, extra_space = [own, near], [pl.BlockSpec(memory_space=pl.ANY)]
        extra_shape = [jax.ShapeDtypeStruct((4,) + own.shape, low)]
        extra_scratch = [
            pltpu.VMEM((3,) + own.shape, low),
            pltpu.SemaphoreType.DMA((5,)),
            pltpu.SemaphoreType.DMA((12,)),
        ]
        params = pltpu.CompilerParams(
            collective_id=4, has_side_effects=True, vmem_limit_bytes=VMEM_LIMIT
        )
    rows = slots * cells
    return pl.pallas_call(
        map_mlp_kernel,
        grid=(hidden // width,),
        in_specs=[
            fixed_block((rows, channels)),
            fixed_block((rows, channels)),
            pl.BlockSpec((channels, width), lambda j: (0, j)),
            pl.BlockSpec((width, channels), lambda j: (j, 0)),
            fixed_block(w_adapt.shape),
            fixed_block(pool.shape),
            fixed_block(live.shape),
        ]
        + extra_space * 2,
        out_specs=[
            pl.BlockSpec((rows, width), lambda j: (0, j)),
            pl.BlockSpec((rows, width), lambda j: (0, j)),
            whole_block((slots, cells, channels)),
            whole_block((slots, few, channels)),
            whole_block((slots, few, model)),
        ]
        + extra_space,
        out_shape=[
            jax.ShapeDtypeStruct((rows, hidden), low),
            jax.ShapeDtypeStruct((rows, hidden), low),
            jax.ShapeDtypeStruct((slots, cells, channels), low),
            jax.ShapeDtypeStruct((slots, few, channels), low),
            jax.ShapeDtypeStruct((slots, few, model), low),
        ]
        + extra_shape,
        scratch_shapes=[pltpu.VMEM((rows, channels), jnp.float32)] + extra_scratch,
        cost_estimate=pl.CostEstimate(
            flops=4 * rows * channels * hidden,
            bytes_accessed=45 * 10**6,
            transcendentals=2 * rows * hidden,
        ),
        compiler_params=params,
        name="map_mlp",
    )(
        norm_low,
        source.reshape(rows, channels),
        w_expand,
        w_shrink,
        w_adapt,
        pool,
        live,
        *extra,
    )


def norm_parts(values):
    centre = values - jnp.mean(values, axis=-1, keepdims=True)
    scale = lax.rsqrt(jnp.mean(centre * centre, axis=-1, keepdims=True) + 1e-06)
    return centre * scale, scale


def norm_back(grad, unit, scale, gain):
    turned = grad * gain
    mean = jnp.mean(turned, axis=-1, keepdims=True)
    mean_unit = jnp.mean(turned * unit, axis=-1, keepdims=True)
    return scale * (turned - mean - unit * mean_unit)


def head_lanes(rows, odd):
    lane = lax.broadcasted_iota(jnp.int32, (rows, 2 * HDIM), 1)
    return (lane >= HDIM) if odd else (lane < HDIM)


def token_front_kernel(*refs):
    (own, everyone, table), refs = refs[:3], refs[3:]
    weights, refs = refs[:6], refs[6:]
    outs, refs = refs[:12], refs[12:]
    buffers, sems, refs = refs[:6], refs[6], refs[7:]
    held, out_sems = refs[:12], refs[12]
    (own_out, all_out, q_out, k_out, v_out, p_out) = held[:6]
    (o_out, x1_out, h_out, g_out, slope_out, x2_out) = held[6:]
    stores = [pltpu.make_async_copy(held[n], outs[n], out_sems.at[n]) for n in range(12)]
    copies = [
        pltpu.make_async_copy(weights[n], buffers[n], sems.at[n]) for n in range(6)
    ]
    for copy in copies:
        copy.start()
    low = jnp.bfloat16
    slots, count, width = own.shape
    gain = table[0:1, :]

    def norm_chunks(source, target, rows):
        def body(n, carry):
            at = pl.ds(pl.multiple_of(n * 48, 16), 48)
            unit, _ = norm_parts(source[at, :].astype(jnp.float32))
            target[at, :] = (unit * gain).astype(low)
            return carry

        lax.fori_loop(0, rows // 48, body, 0)

    for s in range(slots):
        norm_chunks(own.at[s], own_out.at[s], count)
        for t in range(everyone.shape[0]):
            norm_chunks(everyone.at[t, s], all_out.at[s, pl.ds(t * count, count), :], count)
    stores[0].start()
    stores[1].start()
    copies[0].wait()
    for s in range(slots):
        q_out[s] = contract(own_out[s], buffers[0][...], 1, 0).astype(low)
    stores[2].start()
    copies[1].wait()
    copies[2].wait()
    for s in range(slots):
        k_out[s] = contract(all_out[s], buffers[1][...], 1, 0).astype(low)
        v_out[s] = contract(all_out[s], buffers[2][...], 1, 0).astype(low)
    stores[3].start()
    stores[4].start()
    for s in range(slots):
        for pair in range(HEADS // 2):
            at = pl.ds(pair * 2 * HDIM, 2 * HDIM)
            q, k, v = q_out[s, :, at], k_out[s, :, at], v_out[s, :, at]
            q = q * jnp.asarray(HDIM ** (-0.5), low)
            mixed = []
            for odd in range(2):
                part = jnp.where(head_lanes(count, odd), q, jnp.zeros_like(q))
                scores = contract(part, k, 1, 1)
                shifted = jnp.exp(scores - jnp.max(scores, axis=-1, keepdims=True))
                share = 1.0 / jnp.sum(shifted, axis=-1, keepdims=True)
                p = (shifted * share).astype(low)
                p_out[s * HEADS + 2 * pair + odd] = p
                mixed.append(contract(p, v, 1, 0))
            o_out[s, :, at] = jnp.where(head_lanes(count, 0), mixed[0], mixed[1]).astype(low)
    stores[5].start()
    stores[6].start()
    copies[3].wait()
    gain_two = table[1:2, :]
    for s in range(slots):
        x1 = own[s].astype(jnp.float32) + contract(o_out[s], buffers[3][...], 1, 0)
        x1_out[s] = x1
        unit, _ = norm_parts(x1)
        h_out[s] = (unit * gain_two).astype(low)
    stores[7].start()
    stores[8].start()
    copies[4].wait()
    hidden = g_out.shape[2]
    for s in range(slots):
        for c in range(0, hidden, 768):
            at = pl.ds(c, 768)
            g_out[s, :, at], slope_out[s, :, at] = gelu_pair(
                contract(h_out[s], buffers[4][:, at], 1, 0)
            )
    stores[9].start()
    stores[10].start()
    copies[5].wait()
    for s in range(slots):
        x2_out[s] = x1_out[s] + contract(g_out[s], buffers[5][...], 1, 0)
    stores[11].start()
    for copy in stores:
        copy.wait()


def token_front(own, everyone, table, weights):
    slots, count, width = own.shape
    total, hidden = everyone.shape[0] * count, weights[4].shape[1]
    low, wide = jnp.bfloat16, jnp.float32
    shapes = [
        ((slots, count, width), low),
        ((slots, total, width), low),
        ((slots, count, width), low),
        ((slots, total, width), low),
        ((slots, total, width), low),
        ((slots * HEADS, count, total), low),
        ((slots, count, width), low),
        ((slots, count, width), wide),
        ((slots, count, width), low),
        ((slots, count, hidden), low),
        ((slots, count, hidden), low),
        ((slots, count, width), wide),
    ]
    in_vmem = pl.BlockSpec(memory_space=pltpu.VMEM)
    return pl.pallas_call(
        token_front_kernel,
        in_specs=[in_vmem] * 3 + [pl.BlockSpec(memory_space=pl.ANY)] * 6,
        out_specs=[pl.BlockSpec(memory_space=pl.ANY)] * len(shapes),
        out_shape=[jax.ShapeDtypeStruct(shape, dtype) for shape, dtype in shapes],
        scratch_shapes=[pltpu.VMEM(weight.shape, low) for weight in weights]
        + [pltpu.SemaphoreType.DMA((6,))]
        + [pltpu.VMEM(shape, dtype) for shape, dtype in shapes]
        + [pltpu.SemaphoreType.DMA((12,))],
        cost_estimate=pl.CostEstimate(
            flops=9 * 10**9, bytes_accessed=30 * 10**6, transcendentals=3 * 10**6
        ),
        compiler_params=pltpu.CompilerParams(vmem_limit_bytes=VMEM_LIMIT),
        name="token_front",
    )(own, everyone, table, *weights)


def token_back_kernel(*refs):
    (dx2, x1_ref, table), refs = refs[:3], refs[3:]
    saved, refs = refs[:10], refs[10:]
    weights, refs = refs[:6], refs[6:]
    outs, refs = refs[:9], refs[9:]
    gain_out, refs = refs[0], refs[1:]
    kept, refs = refs[:10], refs[10:]
    buffers, refs = refs[:6], refs[6:]
    held, refs = refs[:9], refs[9:]
    du, do, dq, dk, dv, sems, weight_sems, out_sems = refs
    (up_out, down_out, q_out, k_out, v_out, o_out, dx1_out, da_own_out, da_all_out) = held
    stores = [pltpu.make_async_copy(held[n], outs[n], out_sems.at[n]) for n in range(9)]
    (own, everyone, q_all, k_all, v_all, p_all, o_all, h_all, g_all, slope_all) = kept
    order = (8, 9, 7, 6, 4, 5, 3, 2, 0, 1)
    saved_copies = [
        pltpu.make_async_copy(saved[n], kept[n], sems.at[n]) for n in range(10)
    ]
    weight_copies = [
        pltpu.make_async_copy(weights[n], buffers[n], weight_sems.at[n]) for n in range(6)
    ]
    weight_copies[5].start()
    for n in order[:3]:
        saved_copies[n].start()
    weight_copies[4].start()
    weight_copies[3].start()
    for n in order[3:]:
        saved_copies[n].start()
    for n in range(3):
        weight_copies[n].start()
    low = jnp.bfloat16
    slots, count, width = dx2.shape
    hidden = g_all.shape[2]
    gain = table[1:2, :]
    flat = lambda ref: ref[...].reshape(-1, ref.shape[-1])
    grad_low = flat(dx2).astype(low)
    weight_copies[5].wait()
    for n in order[:3]:
        saved_copies[n].wait()
    for c in range(0, hidden, 768):
        at = pl.ds(c, 768)
        grad = contract(grad_low, buffers[5][at, :], 1, 1)
        slope = slope_all[:, :, at].reshape(-1, 768).astype(jnp.float32)
        du[:, at] = (grad * slope).astype(low)
        g = g_all[:, :, at].reshape(-1, 768)
        down_out[at, :] = contract(g, grad_low, 0, 0).astype(low)
        h = flat(h_all)
        up_out[:, at] = contract(h, du[:, at], 0, 0).astype(low)
    stores[0].start()
    stores[1].start()
    weight_copies[4].wait()
    dh = contract(du[...], buffers[4][...], 1, 1)
    unit, scale = norm_parts(flat(x1_ref))
    gain_out[...] = jnp.sum(dh * unit, axis=0, keepdims=True)
    dx1 = flat(dx2) + norm_back(dh, unit, scale, gain)
    dx1_out[...] = dx1.reshape(dx1_out.shape)
    stores[6].start()
    dar = dx1.astype(low)
    weight_copies[3].wait()
    for n in order[3:]:
        saved_copies[n].wait()
    o_out[...] = contract(flat(o_all), dar, 0, 0).astype(low)
    stores[5].start()
    do[...] = contract(dar, buffers[3][...], 1, 1).astype(low).reshape(do.shape)
    for s in range(slots):
        for pair in range(HEADS // 2):
            at = pl.ds(pair * 2 * HDIM, 2 * HDIM)
            q, k, v, grad = q_all[s, :, at], k_all[s, :, at], v_all[s, :, at], do[s, :, at]
            parts = []
            for odd in range(2):
                p = p_all[s * HEADS + 2 * pair + odd]
                mine = jnp.where(head_lanes(count, odd), grad, jnp.zeros_like(grad))
                dp = contract(mine, v, 1, 1)
                wide_p = p.astype(jnp.float32)
                row = jnp.sum(wide_p * dp, axis=-1, keepdims=True)
                ds = (wide_p * (dp - row)).astype(low)
                parts.append(
                    (contract(ds, k, 1, 0), contract(ds, q, 0, 0), contract(p, grad, 0, 0))
                )
            few, many = head_lanes(count, 0), head_lanes(k.shape[0], 0)
            root = HDIM ** (-0.5)
            dq[s, :, at] = (jnp.where(few, parts[0][0], parts[1][0]) * root).astype(low)
            dk[s, :, at] = (jnp.where(many, parts[0][1], parts[1][1]) * root).astype(low)
            dv[s, :, at] = jnp.where(many, parts[0][2], parts[1][2]).astype(low)
    for n in range(3):
        weight_copies[n].wait()
    for s in range(slots):
        da_own_out[s] = contract(dq[s], buffers[0][...], 1, 1)
        both = contract(dk[s], buffers[1][...], 1, 1) + contract(dv[s], buffers[2][...], 1, 1)
        for t in range(da_all_out.shape[0]):
            da_all_out[t, s] = both[t * count : (t + 1) * count].astype(low)
    stores[7].start()
    stores[8].start()
    q_out[...] = contract(flat(own), flat(dq), 0, 0).astype(low)
    stores[2].start()
    k_out[...] = contract(flat(everyone), flat(dk), 0, 0).astype(low)
    stores[3].start()
    v_out[...] = contract(flat(everyone), flat(dv), 0, 0).astype(low)
    stores[4].start()
    for copy in stores:
        copy.wait()


def token_back(dx2, x1, table, saved, weights):
    slots, count, width = dx2.shape
    total, hidden = saved[1].shape[1], weights[4].shape[1]
    low, wide = jnp.bfloat16, jnp.float32
    shapes = [
        ((width, hidden), low),
        ((hidden, width), low),
        ((width, width), low),
        ((width, width), low),
        ((width, width), low),
        ((width, width), low),
        ((slots, count, width), wide),
        ((slots, count, width), wide),
        ((total // count, slots, count, width), low),
        ((1, width), wide),
    ]
    in_vmem = pl.BlockSpec(memory_space=pltpu.VMEM)
    any_space = pl.BlockSpec(memory_space=pl.ANY)
    return pl.pallas_call(
        token_back_kernel,
        in_specs=[in_vmem] * 3 + [any_space] * 16,
        out_specs=[any_space] * 9 + [in_vmem],
        out_shape=[jax.ShapeDtypeStruct(shape, dtype) for shape, dtype in shapes],
        scratch_shapes=[pltpu.VMEM(item.shape, low) for item in saved]
        + [pltpu.VMEM(weight.shape, low) for weight in weights]
        + [pltpu.VMEM(shape, dtype) for shape, dtype in shapes[:9]]
        + [
            pltpu.VMEM((slots * count, hidden), low),
            pltpu.VMEM((slots, count, width), low),
            pltpu.VMEM((slots, count, width), low),
            pltpu.VMEM((slots, total, width), low),
            pltpu.VMEM((slots, total, width), low),
            pltpu.SemaphoreType.DMA((10,)),
            pltpu.SemaphoreType.DMA((6,)),
            pltpu.SemaphoreType.DMA((9,)),
        ],
        cost_estimate=pl.CostEstimate(
            flops=18 * 10**9, bytes_accessed=50 * 10**6, transcendentals=10**6
        ),
        compiler_params=pltpu.CompilerParams(vmem_limit_bytes=VMEM_LIMIT),
        name="token_back",
    )(dx2, x1, table, *saved, *weights)


SMALL_SIDE = 16


def merge_maps(side):
    tile = lax.axis_index("tile")
    low, high = tile % 2, tile // 2
    cells = side * side
    row = jnp.arange(3 * SMALL_SIDE, dtype=jnp.int32)
    edge_col = jnp.where(low == 0, side - 1, 0)
    edge_row = jnp.where(high == 0, side - 1, 0)
    k = row % SMALL_SIDE
    source = jnp.where(
        (row < SMALL_SIDE) & (k < side),
        k * side + edge_col,
        jnp.where(
            (row >= SMALL_SIDE) & (row < 2 * SMALL_SIDE) & (k < side),
            edge_row * side + k,
            jnp.where(row == 2 * SMALL_SIDE, edge_row * side + edge_col, -1),
        ),
    )
    pick = source[:, None] == jnp.arange(cells, dtype=jnp.int32)[None, :]
    at = jnp.arange(9 * cells, dtype=jnp.int32)
    tap, cell = at // cells, at % cells
    i, j = cell // side + tap // 3 - 1, cell % side + tap % 3 - 1
    inside_i, inside_j = (i >= 0) & (i < side), (j >= 0) & (j < side)
    beside_j = ((j < 0) & (low == 1)) | ((j >= side) & (low == 0))
    beside_i = ((i < 0) & (high == 1)) | ((i >= side) & (high == 0))
    source = jnp.where(
        inside_i & inside_j,
        i * side + j,
        jnp.where(
            inside_i & beside_j,
            cells + i,
            jnp.where(
                beside_i & inside_j,
                cells + SMALL_SIDE + j,
                jnp.where(beside_i & beside_j, cells + 2 * SMALL_SIDE, -1),
            ),
        ),
    )
    parts = cells + 3 * SMALL_SIDE
    shifts = source[:, None] == jnp.arange(parts, dtype=jnp.int32)[None, :]
    return pick.astype(jnp.bfloat16), shifts.astype(jnp.bfloat16)


def merge_kernel(
    adapted,
    pooled,
    tokens,
    vit_grad,
    map_grad,
    live,
    table,
    w_adapt,
    pool,
    pick,
    shifts,
    vit_out,
    dx2_out,
    grad_out,
    adapt_out,
    small_out,
    rims,
    inbox,
    moved,
    grads,
    back,
    send_sem,
    recv_sem,
):
    place = Place()
    partners = (place.to_low, place.to_high, place.to_across)
    low = jnp.bfloat16
    slots, cells, width = adapted.shape

    def copies(phase, s):
        made = []
        for n, partner in enumerate(partners):
            at = (phase * slots + s) * 3 + n
            made.append(
                remote(
                    rims.at[phase, s, pl.ds(n * SMALL_SIDE, SMALL_SIDE), :],
                    inbox.at[phase, s, pl.ds(n * SMALL_SIDE, SMALL_SIDE), :],
                    send_sem.at[at],
                    recv_sem.at[at],
                    partner,
                )
            )
        return made

    def give(phase, s, source):
        rims[phase, s] = contract(pick[...], source[s], 1, 0).astype(low)
        for copy in copies(phase, s):
            copy.start()

    def shift(phase, s, source):
        for copy in copies(phase, s):
            copy.wait()
        parts = jnp.concatenate([source[s], inbox[phase, s]], axis=0)
        moved[s] = contract(shifts[...], parts, 1, 0).astype(low).reshape(moved.shape[1:])

    gate_low, gate_high = table[2:3, :], table[3:4, :]
    greet(partners)
    for s in range(slots):
        give(0, s, adapted)
    small_out[...] = jnp.zeros_like(small_out)
    for s in range(slots):
        shift(0, s, adapted)
        f = jnp.zeros((cells, width), jnp.float32)
        for k in range(9):
            f = f + table[4 + k : 5 + k, :] * moved[s, k].astype(jnp.float32)
        x2 = tokens[s]
        alive = live[s]
        logit = jnp.sum(x2 * gate_low, axis=-1, keepdims=True) + jnp.sum(
            f * gate_high, axis=-1, keepdims=True
        )
        gate = 1.0 / (1.0 + jnp.exp(-logit))
        vit_out[s] = ((x2 + gate * f) * alive).astype(low)
        dvo = vit_grad[s].astype(jnp.float32) * alive
        dl = jnp.sum(dvo * f, axis=-1, keepdims=True) * gate * (1.0 - gate)
        dx2_out[s] = dvo + dl * gate_low
        df = gate * dvo + dl * gate_high
        grads[s] = df.astype(low)
        give(1, s, grads)
        for k in range(9):
            part = jnp.sum(df * moved[s, k].astype(jnp.float32), axis=0, keepdims=True)
            small_out[k : k + 1, :] = small_out[k : k + 1, :] + part
        small_out[9:10, :] = small_out[9:10, :] + jnp.sum(dl * x2, axis=0, keepdims=True)
        small_out[10:11, :] = small_out[10:11, :] + jnp.sum(dl * f, axis=0, keepdims=True)
    for s in range(slots):
        shift(1, s, grads)
        total = jnp.zeros((cells, width), jnp.float32)
        for k in range(9):
            total = total + table[12 - k : 13 - k, :] * moved[s, k].astype(jnp.float32)
        back[pl.ds(s * cells, cells), :] = total.astype(low)
    flat = pooled[...].reshape(slots * cells, -1)
    adapt_out[...] = contract(flat, back[...], 0, 0).astype(low)
    for s in range(slots):
        part = contract(back[pl.ds(s * cells, cells), :], w_adapt[...], 1, 1).astype(low)
        spread = contract(pool[...], part, 0, 0)
        grad_out[s] = (map_grad[s].astype(jnp.float32) * live[s] + spread).astype(low)


def merge_step(adapted, pooled, tokens, vit_grad, map_grad, live, table, w_adapt, pool):
    slots, cells, width = adapted.shape
    low = jnp.bfloat16
    pick, shifts = merge_maps(math.isqrt(cells))
    in_vmem = pl.BlockSpec(memory_space=pltpu.VMEM)
    return pl.pallas_call(
        merge_kernel,
        in_specs=[in_vmem] * 11,
        out_specs=[in_vmem] * 5,
        out_shape=[
            jax.ShapeDtypeStruct(adapted.shape, low),
            jax.ShapeDtypeStruct(adapted.shape, jnp.float32),
            jax.ShapeDtypeStruct(map_grad.shape, low),
            jax.ShapeDtypeStruct(w_adapt.shape, low),
            jax.ShapeDtypeStruct((16, width), jnp.float32),
        ],
        scratch_shapes=[
            pltpu.VMEM((2, slots, 3 * SMALL_SIDE, width), low),
            pltpu.VMEM((2, slots, 3 * SMALL_SIDE, width), low),
            pltpu.VMEM((slots, 9, cells, width), low),
            pltpu.VMEM((slots, cells, width), low),
            pltpu.VMEM((slots * cells, width), low),
            pltpu.SemaphoreType.DMA((6 * slots,)),
            pltpu.SemaphoreType.DMA((6 * slots,)),
        ],
        compiler_params=pltpu.CompilerParams(
            collective_id=3, has_side_effects=True, vmem_limit_bytes=VMEM_LIMIT
        ),
        name="merge_step",
    )(
        adapted,
        pooled,
        tokens,
        vit_grad,
        map_grad,
        live,
        table,
        w_adapt,
        pool,
        pick,
        shifts,
    )


def turned(shape):
    return shape[1] % 128 != 0 and shape[0] % 128 == 0


def hand_out_kernel(count, *refs):
    small, refs = refs[0], refs[1:]
    matrices, refs = refs[:count], refs[count:]
    outs, refs = refs[:count], refs[count:]
    large_out, conv_out, small_out, *rows_out = refs
    for n in range(count):
        value = matrices[n][...]
        outs[n][...] = value.T if turned(value.shape) else value
    blocks = large_out.shape[1] // 128
    for b in range(blocks):
        large_out[:, b * 128 : (b + 1) * 128] = small[b * 49 : (b + 1) * 49, :]
        row = 49 * blocks + small_out.shape[1] // 8 + b
        conv_out[pl.ds(b * 128, 128)] = small[row]
    for b in range(small_out.shape[1] // 128):
        row = 49 * blocks + b * 16
        small_out[:, b * 128 : (b + 1) * 128] = small[row : row + 9, :]
        for n, out in enumerate(rows_out):
            out[pl.ds(b * 128, 128)] = small[row + 9 + n]


def hand_out(small, matrices, channels, width):
    in_vmem = pl.BlockSpec(memory_space=pltpu.VMEM)
    count = len(matrices)
    results = pl.pallas_call(
        partial(hand_out_kernel, count),
        in_specs=[in_vmem] * (count + 1),
        out_specs=[in_vmem] * (count + 7),
        out_shape=[
            jax.ShapeDtypeStruct(
                item.shape[::-1] if turned(item.shape) else item.shape, item.dtype
            )
            for item in matrices
        ]
        + [
            jax.ShapeDtypeStruct((49, channels), jnp.float32),
            jax.ShapeDtypeStruct((channels,), jnp.float32),
            jax.ShapeDtypeStruct((9, width), jnp.float32),
        ]
        + [jax.ShapeDtypeStruct((width,), jnp.float32)] * 4,
        name="hand_out",
    )(small, *matrices)
    taps_grad, gain_conv_grad, small_grad, low_grad, high_grad, one_grad, two_grad = results[count:]
    return [
        result.T if turned(item.shape) else result for result, item in zip(results, matrices)
    ] + [one_grad, two_grad, small_grad, low_grad, high_grad, gain_conv_grad, taps_grad]


def chip_layout():
    return lax.axis_size("img") == 8 and lax.axis_size("tile") == 4


def sum_plain(grads, smalls):
    sums = []
    for grad in grads:
        part = lax.psum_scatter(grad, "img", scatter_dimension=0, tiled=True)
        part = lax.psum_scatter(part, "tile", scatter_dimension=1, tiled=True)
        sums.append(part.astype(jnp.float32))
    return sums, lax.psum(tuple(smalls), ("img", "tile"))


def map_back_plain(
    grad_low, norm_low, wide_low, wide_slope, w_shrink, w_expand, unit, scale, gain, padded, taps
):
    slots, cells, channels = grad_low.shape
    side = math.isqrt(cells)
    wide_low = wide_low.reshape(slots, cells, -1)
    wide_slope = wide_slope.reshape(slots, cells, -1)
    w_shrink_grad = outer_sum(wide_low, grad_low)
    grad_wide_low = (project_back(grad_low, w_shrink) * wide_slope).astype(jnp.bfloat16)
    w_expand_grad = outer_sum(norm_low, grad_wide_low)
    back = project_back(grad_wide_low, w_expand)
    gain_conv_grad = jnp.sum(back * unit, axis=(0, 1))
    grad_spread = norm_back(back, unit, scale, gain).reshape(slots, side, side, channels)
    field = padded.astype(jnp.float32)
    taps_grad = jnp.stack(
        [
            jnp.sum(field[:, a : a + side, b : b + side] * grad_spread, axis=(0, 1, 2))
            for a in range(7)
            for b in range(7)
        ]
    )
    padded_grad = add_rims(grad_spread.astype(jnp.bfloat16), 3).astype(jnp.float32)
    moved = depthwise(padded_grad, taps[::-1], 3, 0).reshape(slots, cells, channels)
    map_grad = (grad_low.astype(jnp.float32) + moved).astype(jnp.bfloat16)
    return map_grad, w_expand_grad, w_shrink_grad, gain_conv_grad, taps_grad


def local(
    vit_in,
    map_in,
    group_images,
    vit_grad_out,
    map_grad_out,
    w_query,
    w_key,
    w_value,
    w_out,
    w_up,
    w_down,
    w_expand,
    w_shrink,
    w_adapt,
    gain_attn,
    gain_mlp,
    gain_conv,
    dw_large,
    dw_small,
    gate_low,
    gate_high,
):
    slot_count = vit_in.shape[0]
    tok_side = math.isqrt(vit_in.shape[2])
    pix_side = math.isqrt(map_in.shape[2])
    channels = map_in.shape[3]
    model_width = vit_in.shape[3]
    live_mask = (
        (jnp.arange(slot_count, dtype=jnp.int32) < group_images[0])
        .astype(jnp.float32)
        .reshape(slot_count, 1, 1)
    )
    cells = pix_side * pix_side
    on_chips = chip_layout()
    own = vit_in[:, 0]
    tokens = own.astype(jnp.float32)
    gain_one = gain_attn.astype(jnp.float32)
    conv_gain = gain_conv.astype(jnp.float32)
    large_taps = dw_large.astype(jnp.float32)
    map_table = jnp.concatenate([dw_large, gain_conv[None]]).astype(jnp.float32)
    token_table = jnp.concatenate(
        [gain_attn[None], gain_mlp[None], gate_low[None], gate_high[None], dw_small]
    ).astype(jnp.float32)
    few = jnp.arange(tok_side * tok_side, dtype=jnp.int32)[:, None]
    cell = jnp.arange(cells, dtype=jnp.int32)[None, :]
    holder = cell // pix_side // 2 * tok_side + cell % pix_side // 2
    pool = jnp.where(holder == few, 0.25, 0.0).astype(jnp.bfloat16)
    if on_chips:
        pick, place_map = rim_maps(pix_side)
        conv_norm_low, conv_unit_low, conv_scale, padded_map, near = conv_front(
            map_in[:, 0], own, pick, place_map, map_table
        )
    else:
        near = None
        map_low = map_in[:, 0].reshape(slot_count, pix_side, pix_side, channels)
        padded_map = add_rims(map_low, 3)
        spread_map = depthwise(padded_map.astype(jnp.float32), large_taps, 3, 0)
        conv_unit, conv_scale = norm_parts(spread_map.reshape(slot_count, cells, channels))
        conv_norm_low = (conv_unit * conv_gain).astype(jnp.bfloat16).reshape(-1, channels)
    wide_low, wide_slope, map_result, pooled_low, adapted_low, *gathered = map_mlp(
        conv_norm_low,
        map_in[:, 0],
        w_expand,
        w_shrink,
        w_adapt,
        pool,
        live_mask,
        own if on_chips else None,
        near,
    )
    own_all = gathered[0] if on_chips else lax.all_gather(own, "tile", axis=0, tiled=False)
    token_weights = (w_query, w_key, w_value, w_out, w_up, w_down)
    front = token_front(own, own_all, token_table, token_weights)
    residual_one, residual_two = front[7], front[11]
    saved = front[:7] + front[8:11]
    if on_chips:
        vit_result, grad_residual_two, grad_conv_low, w_adapt_grad, sides = merge_step(
            adapted_low,
            pooled_low,
            residual_two,
            vit_grad_out[:, 0],
            map_grad_out[:, 0],
            live_mask,
            token_table,
            w_adapt,
            pool,
        )
    else:
        adapted_low = adapted_low.reshape(slot_count, tok_side, tok_side, model_width)
        padded_small = add_rims(adapted_low, 1).astype(jnp.float32)
        merged_map, merged_pull = jax.vjp(
            partial(depthwise, radius=1, margin=0), padded_small, dw_small.astype(jnp.float32)
        )
        merged_tokens = merged_map.reshape(slot_count, tok_side * tok_side, model_width)
        vit_after, merging_pull = jax.vjp(
            merging,
            residual_two,
            merged_tokens,
            gate_low.astype(jnp.float32),
            gate_high.astype(jnp.float32),
        )
        vit_result = (vit_after * live_mask).astype(jnp.bfloat16)
        vit_cotangent = vit_grad_out[:, 0].astype(jnp.float32) * live_mask
        map_cotangent = map_grad_out[:, 0].astype(jnp.float32) * live_mask
        grad_residual_two, grad_merged, gate_low_grad, gate_high_grad = merging_pull(vit_cotangent)
        grad_padded_small, dw_small_grad = merged_pull(
            grad_merged.reshape(slot_count, tok_side, tok_side, model_width)
        )
        grad_adapted_low = return_rims(grad_padded_small, 1).astype(jnp.bfloat16)
        grad_adapted_low = grad_adapted_low.reshape(slot_count, tok_side * tok_side, model_width)
        w_adapt_grad = outer_sum(pooled_low, grad_adapted_low)
        grad_pooled = project_back(grad_adapted_low, w_adapt).astype(jnp.bfloat16)
        grad_conv_low = (
            map_cotangent
            + jnp.einsum("pc,spk->sck", pool, grad_pooled, preferred_element_type=jnp.float32)
        ).astype(jnp.bfloat16)
    (
        w_up_grad,
        w_down_grad,
        w_query_grad,
        w_key_grad,
        w_value_grad,
        w_out_grad,
        grad_residual_one,
        grad_own,
        grad_everyone,
        gain_mlp_grad,
    ) = token_back(grad_residual_two, residual_one, token_table, saved, token_weights)
    token_grads = (
        w_up_grad,
        w_down_grad,
        w_adapt_grad,
        w_query_grad,
        w_key_grad,
        w_value_grad,
        w_out_grad,
    )
    if on_chips:
        first, first_sums = map_mlp_back(
            grad_conv_low.reshape(-1, channels),
            conv_norm_low,
            wide_low,
            wide_slope,
            w_shrink,
            w_expand,
            conv_unit_low,
            conv_scale,
            map_table,
            grad_everyone,
            token_grads,
        )
        w_shrink_grad, w_expand_grad, dz, gain_conv_grad, grad_shared = first
    else:
        grad_shared = lax.psum_scatter(
            grad_everyone, "tile", scatter_dimension=0, tiled=False
        ).astype(jnp.float32)
    grad_normed_one = grad_own + grad_shared
    unit_one, scale_one = norm_parts(tokens)
    gain_attn_grad = jnp.sum(grad_normed_one * unit_one, axis=(0, 1)).reshape(1, model_width)
    vit_in_grad = (
        grad_residual_one + norm_back(grad_normed_one, unit_one, scale_one, gain_one)
    ).astype(jnp.bfloat16)
    if on_chips:
        map_in_grad, small, last_sums = conv_back(
            dz.reshape(grad_conv_low.shape),
            pick,
            place_map,
            padded_map,
            grad_conv_low,
            map_table,
            (sides, gain_attn_grad, gain_mlp_grad, gain_conv_grad),
            (w_expand_grad, w_shrink_grad),
        )
        final = hand_out(small, tuple(first_sums) + tuple(last_sums), channels, model_width)
        matrix_sums, small_sums = final[:9], final[9:]
    else:
        map_in_grad, w_expand_grad, w_shrink_grad, gain_conv_grad, taps_grad = map_back_plain(
            grad_conv_low,
            conv_norm_low,
            wide_low,
            wide_slope,
            w_shrink,
            w_expand,
            conv_unit,
            conv_scale,
            conv_gain,
            padded_map,
            large_taps,
        )
        matrix_sums, small_sums = sum_plain(
            token_grads + (w_expand_grad, w_shrink_grad),
            (
                gain_attn_grad.reshape(model_width),
                gain_mlp_grad.reshape(model_width),
                dw_small_grad,
                gate_low_grad,
                gate_high_grad,
                gain_conv_grad,
                taps_grad,
            ),
        )
    return (
        vit_result[:, None],
        map_result[:, None],
        vit_in_grad[:, None],
        map_in_grad[:, None],
        matrix_sums[3],
        matrix_sums[4],
        matrix_sums[5],
        matrix_sums[6],
        matrix_sums[0],
        matrix_sums[1],
        matrix_sums[7],
        matrix_sums[8],
        matrix_sums[2],
        small_sums[0],
        small_sums[1],
        small_sums[5],
        small_sums[6],
        small_sums[2],
        small_sums[3],
        small_sums[4],
    )


def solution(mesh):
    in_specs = (
        P("img", "tile", None, None),
        P("img", "tile", None, None),
        P("img"),
        P("img", "tile", None, None),
        P("img", "tile", None, None),
        P(),
        P(),
        P(),
        P(),
        P(),
        P(),
        P(),
        P(),
        P(),
        P(),
        P(),
        P(),
        P(),
        P(),
        P(),
        P(),
    )
    out_specs = (
        P("img", "tile", None, None),
        P("img", "tile", None, None),
        P("img", "tile", None, None),
        P("img", "tile", None, None),
        P("img", "tile"),
        P("img", "tile"),
        P("img", "tile"),
        P("img", "tile"),
        P("img", "tile"),
        P("img", "tile"),
        P("img", "tile"),
        P("img", "tile"),
        P("img", "tile"),
        P(),
        P(),
        P(),
        P(),
        P(),
        P(),
        P(),
    )
    return jax.shard_map(local, mesh=mesh, in_specs=in_specs, out_specs=out_specs, check_vma=False)
```

```python
from functools import partial
import math

import jax
import jax.numpy as jnp
from jax import lax
from jax.experimental import pallas as pl
from jax.experimental.pallas import tpu as pltpu
from jax.sharding import PartitionSpec as P

HEADS = 12
HDIM = 64


highest = lax.Precision.HIGHEST


def swapped(array, axis, bit):
    return lax.ppermute(array, axis, [(i, i ^ 1 << bit) for i in range(lax.axis_size(axis))])


def gelu_pair(values):
    spread = 0.5 * (1.0 + lax.erf(values * 0.7071067811865476))
    bell = jnp.exp(-0.5 * values * values) * 0.3989422804014327
    return (values * spread).astype(jnp.bfloat16), (spread + values * bell).astype(jnp.bfloat16)


def depthwise(field_map, tap_weights, radius, margin):
    kernel_side = 2 * radius + 1
    channels = tap_weights.shape[1]
    kernel = tap_weights.reshape(kernel_side, kernel_side, 1, channels)
    return lax.conv_general_dilated(
        field_map,
        kernel,
        (1, 1),
        ((margin, margin), (margin, margin)),
        dimension_numbers=("NHWC", "HWIO", "NHWC"),
        feature_group_count=channels,
        precision=highest,
    )


def merging(residual_two, merged_tokens, gate_low, gate_high):
    gate_logit = jnp.sum(residual_two * gate_low, axis=-1, keepdims=True) + jnp.sum(
        merged_tokens * gate_high, axis=-1, keepdims=True
    )
    gate_value = 1.0 / (1.0 + jnp.exp(-gate_logit))
    return residual_two + gate_value * merged_tokens


def project_back(left_side, right_side):
    return jnp.einsum("...j,ij->...i", left_side, right_side, preferred_element_type=jnp.float32)


def outer_sum(left_side, right_side):
    flat_left = left_side.reshape(-1, left_side.shape[-1])
    flat_right = right_side.reshape(-1, right_side.shape[-1])
    return lax.dot_general(
        flat_left, flat_right, (((0,), (0,)), ((), ())), preferred_element_type=jnp.float32
    ).astype(jnp.bfloat16)


def add_rims(tile_field, radius):
    tile_place = lax.axis_index("tile")
    for which_bit in range(2):
        axis_dim = 2 - which_bit
        on_low = tile_place >> which_bit & 1 == 0
        side_len = tile_field.shape[axis_dim]
        upper_rim = lax.slice_in_dim(tile_field, side_len - radius, side_len, axis=axis_dim)
        lower_rim = lax.slice_in_dim(tile_field, 0, radius, axis=axis_dim)
        outgoing = jnp.where(on_low, upper_rim, lower_rim)
        incoming = swapped(outgoing, "tile", which_bit)
        blank_rim = jnp.zeros_like(incoming)
        tile_field = jnp.where(
            on_low,
            jnp.concatenate([blank_rim, tile_field, incoming], axis_dim),
            jnp.concatenate([incoming, tile_field, blank_rim], axis_dim),
        )
    return tile_field


def return_rims(grad_field, radius):
    tile_place = lax.axis_index("tile")
    for which_bit in (1, 0):
        axis_dim = 2 - which_bit
        on_low = tile_place >> which_bit & 1 == 0
        total_len = grad_field.shape[axis_dim]
        side_len = total_len - 2 * radius
        high_rim = lax.slice_in_dim(grad_field, total_len - radius, total_len, axis=axis_dim)
        low_rim = lax.slice_in_dim(grad_field, 0, radius, axis=axis_dim)
        outgoing = jnp.where(on_low, high_rim, low_rim)
        incoming = swapped(outgoing.astype(jnp.bfloat16), "tile", which_bit).astype(outgoing.dtype)
        core_part = lax.slice_in_dim(grad_field, radius, radius + side_len, axis=axis_dim)
        filler_shape = list(incoming.shape)
        filler_shape[axis_dim] = side_len - radius
        filler = jnp.zeros(filler_shape, jnp.float32)
        grad_field = core_part + jnp.where(
            on_low,
            jnp.concatenate([filler, incoming], axis_dim),
            jnp.concatenate([incoming, filler], axis_dim),
        )
    return grad_field


MESH = pl.DeviceIdType.MESH
VMEM_LIMIT = 62 << 20
COPIES = 8
SMALL_ROWS = 512
RIM_ROWS = 80
CORNER_ROWS = 16


def contract(left, right, left_axis, right_axis):
    return lax.dot_general(
        left,
        right,
        (((left_axis,), (right_axis,)), ((), ())),
        preferred_element_type=jnp.float32,
    )


def wide_sum(one, two):
    return one.astype(jnp.float32) + two.astype(jnp.float32)


def low_sum(one, two):
    return wide_sum(one, two).astype(jnp.bfloat16)


def row_loop(first, rows, width, step):
    count = rows // 16
    while count > 1 and (count * 16 * width > 65536 or rows % (count * 16)):
        count -= 1
    chunk = count * 16

    def body(q, carry):
        step(pl.ds(pl.multiple_of(first + q * chunk, 16), chunk))
        return carry

    if rows == chunk:
        body(0, 0)
    else:
        lax.fori_loop(0, rows // chunk, body, 0)


def lanes(start, size):
    return pl.ds(pl.multiple_of(start, 128), size)


class Place:
    def __init__(self):
        img = lax.axis_index("img")
        tile = lax.axis_index("tile")
        self.core, self.x, self.y = img % 2, (img // 2) % 2, img // 4
        self.low, self.high = tile % 2, tile // 2
        self.to_core = (img + 1 - 2 * self.core, tile)
        self.to_x = (img + 2 - 4 * self.x, tile)
        self.to_y = (img + 4 - 8 * self.y, tile)
        self.to_low = (img, tile + 1 - 2 * self.low)
        self.to_high = (img, tile + 2 - 4 * self.high)
        self.to_across = (img, 3 - tile)


def greet(partners):
    barrier = pltpu.get_barrier_semaphore()
    for partner in partners:
        pl.semaphore_signal(barrier, inc=1, device_id=partner, device_id_type=MESH)
    pl.semaphore_wait(barrier, len(partners))


def remote(source, target, send_sem, recv_sem, partner):
    return pltpu.make_async_remote_copy(
        src_ref=source,
        dst_ref=target,
        send_sem=send_sem,
        recv_sem=recv_sem,
        device_id=partner,
        device_id_type=MESH,
    )


def plan_pieces(shapes, piece_bytes):
    pieces = []
    for g, (height, width) in enumerate(shapes):
        rows = height // 8
        count = max(1, round(height * width * 2 / piece_bytes))
        while rows % (count * 32):
            count -= 1
        for p in range(count):
            pieces.append((g, p * (rows // count), rows // count))
    return pieces


def halving_scratch(shapes, pieces):
    count = len(pieces)

    def buffers(shape_of):
        return [
            pltpu.VMEM(shape_of(rows, shapes[g][1]), jnp.bfloat16) for g, _, rows in pieces
        ]

    scratch = buffers(lambda rows, width: (2, 2, rows, width))
    scratch += buffers(lambda rows, width: (2, 2, rows, width))
    scratch += buffers(lambda rows, width: (2, rows, width))
    scratch += buffers(lambda rows, width: (rows, width))
    scratch += buffers(lambda rows, width: (rows, width // 2))
    scratch += buffers(
        lambda rows, width: (rows, width // 4 if width % 512 == 0 else width // 2)
    )
    scratch += [
        pltpu.SemaphoreType.DMA((count * COPIES,)),
        pltpu.SemaphoreType.DMA((count * COPIES,)),
        pltpu.SemaphoreType.DMA((count,)),
    ]
    return scratch


class Halving:
    def __init__(self, place, shapes, pieces, grads, outs, scratch):
        count = len(pieces)
        self.place, self.shapes, self.pieces = place, shapes, pieces
        self.grads, self.outs = grads, outs
        self.own, self.half, self.quarter, self.eighth, self.pair, self.last = (
            scratch[k * count : (k + 1) * count] for k in range(6)
        )
        self.send_sem, self.recv_sem, self.own_sem = scratch[6 * count :]
        self.stages = (
            self.over_core,
            self.over_first,
            self.over_second,
            self.over_third,
            self.over_fourth,
            self.finish,
        )

    def narrow(self, i):
        return self.shapes[self.pieces[i][0]][1] % 512 != 0

    def copy(self, i, k):
        place = self.place
        g, first, rows = self.pieces[i]
        width = self.shapes[g][1] // 4
        half, quarter, eighth = self.half[i], self.quarter[i], self.eighth[i]
        pair, last = self.pair[i], self.last[i]
        part, cut = pl.ds(first, rows), rows // 2
        top, bottom = pl.ds(0, cut), pl.ds(cut, cut)
        if k == 0:
            ends = (self.grads[g].at[:, :, 1 - place.core, part, :], half, place.to_core)
        elif k == 1:
            ends = (half.at[:, 1 - place.x, top, :], quarter.at[:, top, :], place.to_x)
        elif k == 2:
            ends = (half.at[1 - place.y, :, bottom, :], quarter.at[:, bottom, :], place.to_y)
        elif k == 3:
            ends = (quarter.at[1 - place.y, top, :], eighth.at[top, :], place.to_y)
        elif k == 4:
            ends = (quarter.at[1 - place.x, bottom, :], eighth.at[bottom, :], place.to_x)
        elif k < 7 and not self.narrow(i):
            q = k - 5
            side = eighth.at[:, lanes((2 * q + 1 - place.low) * width, width)]
            ends = (side, pair.at[:, pl.ds(q * width, width)], place.to_low)
        elif k == 5:
            side = eighth.at[:, lanes((1 - place.high) * 2 * width, 2 * width)]
            ends = (side, pair, place.to_high)
        elif not self.narrow(i):
            ends = (pair.at[:, lanes((1 - place.high) * width, width)], last, place.to_high)
        else:
            ends = (pair, last, place.to_low)
        at = i * COPIES + k
        return remote(ends[0], ends[1], self.send_sem.at[at], self.recv_sem.at[at], ends[2])

    def own_copy(self, i):
        g, first, rows = self.pieces[i]
        mine = self.grads[g].at[:, :, self.place.core, pl.ds(first, rows), :]
        return pltpu.make_async_copy(mine, self.own[i], self.own_sem.at[i])

    def copies(self, i):
        return (0, 1, 2, 3, 4, 5, 7) if self.narrow(i) else (0, 1, 2, 3, 4, 5, 6, 7)

    def over_core(self, i):
        self.copy(i, 0).start()
        self.own_copy(i).start()

    def over_first(self, i):
        rows = self.pieces[i][2]
        half, own = self.half[i], self.own[i]
        self.copy(i, 0).wait_recv()
        self.own_copy(i).wait()
        for a in range(2):
            for b in range(2):

                def step(s, a=a, b=b):
                    half[a, b, s, :] = low_sum(half[a, b, s, :], own[a, b, s, :])

                row_loop(0, rows, half.shape[-1], step)
        self.copy(i, 1).start()
        self.copy(i, 2).start()

    def over_second(self, i):
        cut = self.pieces[i][2] // 2
        place, half, quarter = self.place, self.half[i], self.quarter[i]
        self.copy(i, 1).wait_recv()
        self.copy(i, 2).wait_recv()
        for a in range(2):

            def step_top(s, a=a):
                quarter[a, s, :] = low_sum(quarter[a, s, :], half[a, place.x, s, :])

            def step_bottom(s, a=a):
                quarter[a, s, :] = low_sum(quarter[a, s, :], half[place.y, a, s, :])

            row_loop(0, cut, quarter.shape[-1], step_top)
            row_loop(cut, cut, quarter.shape[-1], step_bottom)
        self.copy(i, 3).start()
        self.copy(i, 4).start()

    def over_third(self, i):
        cut = self.pieces[i][2] // 2
        place, quarter, eighth = self.place, self.quarter[i], self.eighth[i]
        self.copy(i, 3).wait_recv()
        self.copy(i, 4).wait_recv()

        def step_top(s):
            eighth[s, :] = low_sum(eighth[s, :], quarter[place.y, s, :])

        def step_bottom(s):
            eighth[s, :] = low_sum(eighth[s, :], quarter[place.x, s, :])

        row_loop(0, cut, eighth.shape[-1], step_top)
        row_loop(cut, cut, eighth.shape[-1], step_bottom)
        self.copy(i, 5).start()
        if not self.narrow(i):
            self.copy(i, 6).start()

    def over_fourth(self, i):
        g, _, rows = self.pieces[i]
        width = self.shapes[g][1] // 4
        place, eighth, pair = self.place, self.eighth[i], self.pair[i]
        self.copy(i, 5).wait_recv()
        if self.narrow(i):

            def step(s):
                kept = eighth[s, lanes(place.high * 2 * width, 2 * width)]
                pair[s, :] = low_sum(pair[s, :], kept)

        else:
            self.copy(i, 6).wait_recv()

            def step(s):
                for q in range(2):
                    at = slice(q * width, (q + 1) * width)
                    kept = eighth[s, lanes((2 * q + place.low) * width, width)]
                    pair[s, at] = low_sum(pair[s, at], kept)

        row_loop(0, rows, pair.shape[-1], step)
        self.copy(i, 7).start()

    def finish(self, i):
        g, first, rows = self.pieces[i]
        width = self.shapes[g][1] // 4
        place, pair, last, out = self.place, self.pair[i], self.last[i], self.outs[g]
        self.copy(i, 7).wait_recv()

        def step(s):
            at = pl.ds(pl.multiple_of(s.start + first, 16), s.size)
            if self.narrow(i):
                both = wide_sum(last[s, :], pair[s, :])
                out[at, :] = jnp.where(place.low == 0, both[:, :width], both[:, width:])
            else:
                kept = pair[s, lanes(place.high * width, width)]
                out[at, :] = wide_sum(last[s, :], kept)

        row_loop(0, rows, pair.shape[-1], step)

    def wait_sends(self):
        for i in range(len(self.pieces)):
            for k in self.copies(i):
                self.copy(i, k).wait_send()


def halving_operands(grads):
    return [grad.reshape(2, 2, 2, grad.shape[0] // 8, grad.shape[1]) for grad in grads]


def halving_outputs(shapes):
    return [
        jax.ShapeDtypeStruct((height // 8, width // 4), jnp.float32) for height, width in shapes
    ]


def whole_block(shape):
    return pl.BlockSpec(shape, lambda *_: (0,) * len(shape))


def fixed_block(shape):
    return pl.BlockSpec(shape, lambda *_: (0,) * len(shape), pipeline_mode=pl.Buffered(1))


def rim_copies(place, source, rim, corner, rim_in, row_in, corner_in, sems):
    cells = source.shape[1]
    start = pl.multiple_of((1 - place.high) * (cells - RIM_ROWS), 16)
    return (
        remote(rim, rim_in, sems.at[0], sems.at[1], place.to_low),
        remote(
            source.at[:, pl.ds(start, RIM_ROWS), :], row_in, sems.at[2], sems.at[3], place.to_high
        ),
        remote(corner, corner_in, sems.at[4], sems.at[5], place.to_across),
    )


def mlp_back_kernel(shapes, pieces, plan, *refs):
    matrices = len(shapes)
    count = len(pieces)
    grad_low, norm_low, wide, slope, w_shrink, w_expand, unit, scale, table, parts = refs[:10]
    grads = refs[10 : 10 + matrices]
    refs = refs[10 + matrices :]
    shrink_out, expand_out, dz_out, gain_out, token_out = refs[:5]
    outs = refs[5 : 5 + matrices]
    refs = refs[5 + matrices :]
    halving_refs = refs[: 6 * count + 3]
    refs = refs[6 * count + 3 :]
    norm_turned, back, dz, out_sem, unit_sem = refs[:5]
    buffers, result_buffers, in_sems, result_sems = refs[5:9], refs[9:11], refs[11], refs[12]
    token_refs = refs[13:]
    place = Place()
    halving = Halving(place, shapes, pieces, grads, outs, halving_refs)
    token_sum = TokenSum(place, parts, token_out, token_refs)
    steps = plan["steps"]
    j = pl.program_id(0)

    def slot(n):
        for i, k in plan["slots"].get(n, ()):
            if i == "tokens":
                token_sum.step(k)
            else:
                halving.stages[k](i)

    def slots(odd):
        for n in range(steps):
            if plan["slots"].get(2 * n + odd):
                pl.when(j == n)(partial(slot, 2 * n + odd))

    width = plan["width"]

    unit_load = pltpu.make_async_copy(unit, dz, unit_sem)

    def fetches(n):
        slot_, at = n % 2, lanes(n * width, width)
        parts = (wide.at[:, at], slope.at[:, at], w_shrink.at[at, :], w_expand.at[:, at])
        return [
            pltpu.make_async_copy(part, buffers[k].at[slot_], in_sems.at[slot_ * 4 + k])
            for k, part in enumerate(parts)
        ]

    def stores(n):
        slot_, at = n % 2, lanes(n * width, width)
        targets = (shrink_out.at[at, :], expand_out.at[:, at])
        return [
            pltpu.make_async_copy(
                result_buffers[k].at[slot_], target, result_sems.at[slot_ * 2 + k]
            )
            for k, target in enumerate(targets)
        ]

    @pl.when(j == 0)
    def _():
        for copy in fetches(0):
            copy.start(priority=1)
        unit_load.start()
        greet(
            (
                place.to_core,
                place.to_x,
                place.to_y,
                place.to_low,
                place.to_high,
            )
        )

    @pl.when(j + 1 < steps)
    def _():
        for copy in fetches(j + 1):
            copy.start(priority=1)

    slots(0)

    @pl.when(j == 0)
    def _():
        norm_turned[...] = norm_low[...].T

    for copy in fetches(j):
        copy.wait()

    @pl.when(j >= 2)
    def _():
        for copy in stores(j - 2):
            copy.wait()

    now = j % 2
    grad_wide = contract(grad_low[...], buffers[2][now], 1, 1)
    grad_wide = (grad_wide * buffers[1][now].astype(jnp.float32)).astype(jnp.bfloat16)
    turned = contract(buffers[0][now], grad_low[...], 0, 0)
    result_buffers[0][now] = turned.astype(jnp.bfloat16)
    slots(1)
    turned = contract(norm_turned[...], grad_wide, 1, 0)
    result_buffers[1][now] = turned.astype(jnp.bfloat16)
    term = contract(grad_wide, buffers[3][now], 1, 1)
    for copy in stores(j):
        copy.start(priority=1)

    @pl.when(j == 0)
    def _():
        back[...] = term

    @pl.when(j > 0)
    def _():
        back[...] = back[...] + term

    @pl.when(j == steps - 1)
    def _():
        unit_load.wait()
        gain_row = table[49:50, :]
        chunk = 96

        def body(q, sums):
            at = pl.ds(pl.multiple_of(q * chunk, 16), chunk)
            grad = back[at, :]
            n = dz[at, :].astype(jnp.float32)
            t = grad * gain_row
            mean_t = jnp.mean(t, axis=-1, keepdims=True)
            mean_tn = jnp.mean(t * n, axis=-1, keepdims=True)
            dz[at, :] = (scale[at, :] * (t - mean_t - n * mean_tn)).astype(jnp.bfloat16)
            return sums + jnp.sum((grad * n).reshape(chunk // 8, 8, -1), axis=0)

        sums = jnp.zeros((8, dz.shape[1]), jnp.float32)
        sums = lax.fori_loop(0, dz.shape[0] // chunk, body, sums)
        gain_out[...] = jnp.sum(sums, axis=0, keepdims=True)
        back_copy = pltpu.make_async_copy(dz, dz_out, out_sem)
        back_copy.start()
        for n in range(2 * steps, plan["last"] + 1):
            slot(n)
        back_copy.wait()
        for n in (steps - 2, steps - 1):
            for copy in stores(n):
                copy.wait()
        token_sum.wait_sends()
        halving.wait_sends()


def spread_plan(count, steps, first, second, rest):
    slots = {0: [(i, 0) for i in range(count)]}
    last = 0
    for i in range(count):
        at = [int(first[0] + first[1] * i), int(second[0] + second[1] * i)]
        at += [at[1] + r for r in rest]
        for k, n in enumerate(at):
            slots.setdefault(n, []).append((i, k + 1))
        last = max(last, at[-1])
    for n in slots:
        slots[n].sort(key=lambda item: (-item[1], item[0]))
    return {"slots": slots, "last": last, "steps": steps}


def map_mlp_back(
    grad_low, norm_low, wide, slope, w_shrink, w_expand, unit, scale, table, parts, grads
):
    tokens, channels = grad_low.shape
    hidden = w_shrink.shape[0]
    width = 512
    steps = hidden // width
    shapes = [grad.shape for grad in grads]
    pieces = plan_pieces(shapes, 1_600_000)
    plan = spread_plan(len(pieces), steps, (1, 1.0), (4, 1.0), (2, 4, 6))
    plan["width"] = width
    for k, n in enumerate((0, 5, 11)):
        plan["slots"].setdefault(n, []).append(("tokens", k))
    token_shape = parts.shape[1:]
    low = jnp.bfloat16
    any_space = pl.BlockSpec(memory_space=pl.ANY)
    results = pl.pallas_call(
        partial(mlp_back_kernel, shapes, pieces, plan),
        grid=(steps,),
        in_specs=[
            fixed_block((tokens, channels)),
            fixed_block((tokens, channels)),
            any_space,
            any_space,
            any_space,
            any_space,
            any_space,
            fixed_block((tokens, 1)),
            fixed_block(table.shape),
            any_space,
        ]
        + [any_space] * len(grads),
        out_specs=[
            any_space,
            any_space,
            any_space,
            whole_block((1, channels)),
            whole_block(token_shape),
        ]
        + [whole_block(item.shape) for item in halving_outputs(shapes)],
        out_shape=[
            jax.ShapeDtypeStruct((hidden, channels), low),
            jax.ShapeDtypeStruct((channels, hidden), low),
            jax.ShapeDtypeStruct((tokens, channels), low),
            jax.ShapeDtypeStruct((1, channels), jnp.float32),
            jax.ShapeDtypeStruct(token_shape, jnp.float32),
        ]
        + halving_outputs(shapes),
        scratch_shapes=halving_scratch(shapes, pieces)
        + [
            pltpu.VMEM((channels, tokens), low),
            pltpu.VMEM((tokens, channels), jnp.float32),
            pltpu.VMEM((tokens, channels), low),
            pltpu.SemaphoreType.DMA,
            pltpu.SemaphoreType.DMA,
            pltpu.VMEM((2, tokens, width), low),
            pltpu.VMEM((2, tokens, width), low),
            pltpu.VMEM((2, width, channels), low),
            pltpu.VMEM((2, channels, width), low),
            pltpu.VMEM((2, width, channels), low),
            pltpu.VMEM((2, channels, width), low),
            pltpu.SemaphoreType.DMA((8,)),
            pltpu.SemaphoreType.DMA((4,)),
            pltpu.VMEM((2,) + token_shape, low),
            pltpu.VMEM((2,) + token_shape, low),
            pltpu.VMEM(token_shape, low),
            pltpu.SemaphoreType.DMA((8,)),
        ],
        compiler_params=pltpu.CompilerParams(
            collective_id=0, has_side_effects=True, vmem_limit_bytes=VMEM_LIMIT
        ),
        name="map_mlp_back",
    )(
        grad_low,
        norm_low,
        wide,
        slope,
        w_shrink,
        w_expand,
        unit,
        scale,
        table,
        parts,
        *halving_operands(grads),
    )
    return results[:5], results[5:]


def shift_rows(read_row, shifted, rows, side):
    def body(r, carry):
        line = read_row(r)
        for b in range(7):
            shifted[b, r] = line[b : b + side].reshape(side // 8, 8, 128)
        return carry

    lax.fori_loop(0, rows, body, 0, unroll=6)


def fill_taps(tap_ref, taps, flip):
    for k in range(49):
        tap = tap_ref[48 - k if flip else k].reshape(1, 128)
        taps[k] = jnp.broadcast_to(tap, (8, 128))


def seven_rows(shifted, taps, first, group, side):
    sums = [jnp.zeros((side // 8, 8, 128), jnp.float32) for _ in range(group)]
    for b in range(7):
        for r in range(group + 6):
            line = shifted[b, first + r]
            for k in range(group):
                if 0 <= r - k < 7:
                    sums[k] = sums[k] + taps[(r - k) * 7 + b][None] * line
    return sums


def tap_sums(shifted, read_line, rows, side, group, keep):
    for columns in ((0, 1, 2, 3), (4, 5, 6)):

        def body(g, sums):
            sums = [list(part) for part in sums]
            first = g * group
            lines = [read_line(first + k).reshape(side // 8, 8, 128) for k in range(group)]
            for n, b in enumerate(columns):
                for r in range(group + 6):
                    line = shifted[b, first + r]
                    for k in range(group):
                        if 0 <= r - k < 7:
                            sums[r - k][n] = sums[r - k][n] + jnp.sum(line * lines[k], axis=0)
            return tuple(tuple(part) for part in sums)

        zero = jnp.zeros((8, 128), jnp.float32)
        sums = lax.fori_loop(
            0, rows // group, body, tuple(tuple(zero for _ in columns) for _ in range(7))
        )
        for a in range(7):
            for n, b in enumerate(columns):
                keep(a * 7 + b, jnp.sum(sums[a][n], axis=0, keepdims=True))


class TokenGather:
    def __init__(self, own, everyone, near, held, local_sems, sems):
        self.img = lax.axis_index("img")
        self.tile = lax.axis_index("tile")
        self.own, self.everyone, self.near, self.held = own, everyone, near, held
        self.local_sems, self.sems = local_sems, sems

    def copy(self, k, up, source, target):
        at = 4 * k + 2 * up
        partner = (self.img, self.tile + 1 if up else self.tile - 1)
        return remote(source, target, self.sems.at[at], self.sems.at[at + 1], partner)

    def given(self, k, up):
        if k == 0:
            return self.copy(k, up, self.own, self.near.at[1 - up])
        origin = self.tile - k if up else self.tile + k
        source = self.held.at[1 - up] if k == 1 else self.everyone.at[origin]
        return self.copy(k, up, source, self.everyone.at[origin])

    def gives(self, k, up):
        if up:
            return (self.tile >= k) & (self.tile < 3)
        return (self.tile + k <= 3) & (self.tile > 0)

    def takes(self, k, up):
        return self.tile > k if up else self.tile + k < 3

    def loads(self):
        return (
            pltpu.make_async_copy(self.near, self.held.at[pl.ds(0, 2)], self.local_sems.at[0]),
            pltpu.make_async_copy(self.own, self.held.at[2], self.local_sems.at[1]),
        )

    def local_stores(self, act):
        target = self.everyone.at[self.tile]
        act(pltpu.make_async_copy(self.held.at[2], target, self.local_sems.at[2]))
        for up in (0, 1):

            @pl.when(self.takes(0, up))
            def _():
                target = self.everyone.at[self.tile - 1 if up else self.tile + 1]
                sem = self.local_sems.at[3 + up]
                act(pltpu.make_async_copy(self.held.at[1 - up], target, sem))

    def hand_on(self, k):
        for up in (0, 1):

            @pl.when(self.gives(k, up))
            def _():
                self.given(k, up).start()

    def take(self, k):
        for up in (0, 1):

            @pl.when(self.takes(k, up))
            def _():
                if k == 0:
                    self.copy(k, up, self.own, self.near.at[1 - up]).wait_recv()
                else:
                    origin = self.tile - 1 - k if up else self.tile + 1 + k
                    self.copy(k, up, self.held.at[0], self.everyone.at[origin]).wait_recv()

    def wait_sends(self, steps):
        for k in steps:
            for up in (0, 1):

                @pl.when(self.gives(k, up))
                def _():
                    self.given(k, up).wait_send()


class TokenSum:
    def __init__(self, place, parts, out, scratch):
        self.place, self.parts, self.out = place, parts, out
        self.mine, self.first, self.second, self.sems = scratch

    def copy(self, k):
        place, sems = self.place, self.sems
        if k < 2:
            source, target = self.parts.at[2 * k + 1 - place.low], self.first.at[k]
            partner = place.to_low
        else:
            source, target = self.mine.at[1 - place.high], self.second
            partner = place.to_high
        return remote(source, target, sems.at[2 * k], sems.at[2 * k + 1], partner)

    def load(self, k):
        part = self.parts.at[2 * k + self.place.low]
        return pltpu.make_async_copy(part, self.mine.at[k], self.sems.at[6 + k])

    def step(self, k):
        if k == 0:
            for n in range(2):
                self.copy(n).start()
                self.load(n).start()
        elif k == 1:
            for n in range(2):
                self.copy(n).wait_recv()
                self.load(n).wait()
                for q in range(self.mine.shape[1]):
                    self.mine[n, q] = low_sum(self.mine[n, q], self.first[n, q])
            self.copy(2).start()
        else:
            self.copy(2).wait_recv()
            for q in range(self.out.shape[0]):
                self.out[q] = wide_sum(self.mine[self.place.high, q], self.second[q])

    def wait_sends(self):
        for k in range(3):
            self.copy(k).wait_send()


class SmallSum:
    def __init__(self, place, out, work, inbox, send_sem, recv_sem):
        self.out, self.work, self.inbox = out, work, inbox
        self.send_sem, self.recv_sem = send_sem, recv_sem
        self.total = out.shape[0]
        self.halvings = (
            (place.to_core, place.core),
            (place.to_x, place.x),
            (place.to_y, place.y),
            (place.to_low, place.low),
            (place.to_high, place.high),
        )
        starts, size = [0], self.total
        for _, bit in self.halvings:
            size //= 2
            starts.append(starts[-1] + bit * size)
        self.starts = starts

    def rows(self, start, size):
        return pl.ds(pl.multiple_of(start, 8), size)

    def copy(self, k):
        if k < 5:
            partner, bit = self.halvings[k]
            size = self.total >> (k + 1)
            give = self.rows(self.starts[k] + (1 - bit) * size, size)
            source = self.work.at[give, :]
            target = self.inbox.at[pl.ds(self.total - 2 * size, size), :]
        else:
            partner, _ = self.halvings[9 - k]
            mine = self.rows(self.starts[10 - k], self.total >> (10 - k))
            source = target = self.out.at[mine, :]
        return remote(source, target, self.send_sem.at[k], self.recv_sem.at[k], partner)

    def step(self, k):
        if k > 0:
            self.copy(k - 1).wait_recv()
        if 1 <= k <= 5:
            size = self.total >> k
            at = self.rows(self.starts[k], size)
            summed = self.work[at, :] + self.inbox[pl.ds(self.total - 2 * size, size), :]
            if k < 5:
                self.work[at, :] = summed
            else:
                self.out[at, :] = summed
        if k < 10:
            self.copy(k).start()

    def wait_sends(self):
        for k in range(10):
            self.copy(k).wait_send()


def conv_back_kernel(shapes, pieces, plan, *refs):
    matrices = len(shapes)
    count = len(pieces)
    (dz, pick, place_map, padded, grad_low, tap_ref, sides, one, two, gain) = refs[:10]
    grads = refs[10 : 10 + matrices]
    refs = refs[10 + matrices :]
    map_out, small_out = refs[:2]
    outs = refs[2 : 2 + matrices]
    refs = refs[2 + matrices :]
    halving_refs = refs[: 6 * count + 3]
    refs = refs[6 * count + 3 :]
    field, shifted, taps, tap_out, work, inbox, gathered, small_send, small_recv = refs[:9]
    rim, corner, rim_in, row_in, corner_in, rim_sems = refs[9:]
    place = Place()
    halving = Halving(place, shapes, pieces, grads, outs, halving_refs)
    smalls = SmallSum(place, gathered, work, inbox, small_send, small_recv)
    slots_, cells, channels = dz.shape
    side = padded.shape[1] - 6
    blocks = channels // 128
    j = pl.program_id(0)
    s = j % 2
    c = (j // 2) % blocks
    columns = lanes(c * 128, 128)

    def slot(n):
        for i, k in plan["slots"].get(n, ()):
            if i == "small":
                smalls.step(k)
            else:
                halving.stages[k](i)

    @pl.when(j == 0)
    def _():
        greet(
            (
                place.to_core,
                place.to_x,
                place.to_y,
                place.to_low,
                place.to_high,
                place.to_across,
            )
        )

    rims = rim_copies(place, dz, rim, corner, rim_in, row_in, corner_in, rim_sems)

    for n in range(plan["steps"]):
        if n in plan["slots"] and n != 2 * blocks:
            pl.when(j == n)(partial(slot, n))

    @pl.when(j == 0)
    def _():
        for s in range(slots_):
            both = contract(pick[...], dz[s], 1, 0).astype(jnp.bfloat16)
            rim[s] = both[:RIM_ROWS]
            corner[s] = both[RIM_ROWS:]
        for copy in rims:
            copy.start()

    @pl.when(j < 2 * blocks)
    def _():
        shift_rows(lambda r: padded[0, r].astype(jnp.float32), shifted, side + 6, side)

        @pl.when(s == 0)
        def _():
            tap_out[c] = jnp.zeros(tap_out.shape[1:], jnp.float32)

        def read_line(i):
            line = dz[s, pl.ds(pl.multiple_of(i * side, 8), side), columns]
            return line.astype(jnp.float32)

        def keep(k, value):
            tap_out[c, k : k + 1, :] = tap_out[c, k : k + 1, :] + value

        tap_sums(shifted, read_line, side, side, 4, keep)

    @pl.when(j == 2 * blocks)
    def _():
        for q in range(blocks):
            work[q * 49 : (q + 1) * 49, :] = tap_out[q, :49, :]
        base = blocks * 49
        work[base:, :] = jnp.zeros((SMALL_ROWS - base, 128), jnp.float32)
        for q in range(sides.shape[1] // 128):
            at = slice(q * 128, (q + 1) * 128)
            row = base + q * 16
            work[row : row + 11, :] = sides[:11, at]
            work[row + 11 : row + 12, :] = one[:, at]
            work[row + 12 : row + 13, :] = two[:, at]
        for q in range(blocks):
            row = base + sides.shape[1] // 8 + q
            work[row : row + 1, :] = gain[:, q * 128 : (q + 1) * 128]
        slot(2 * blocks)
        for copy in rims:
            copy.wait()
        for q in range(slots_):
            parts = jnp.concatenate([dz[q], rim_in[q], row_in[q], corner_in[q]], axis=0)
            whole = contract(place_map[...], parts, 1, 0).astype(jnp.bfloat16)
            field[q] = whole.reshape(field.shape[1:])

    @pl.when(j >= 2 * blocks)
    def _():
        fill_taps(tap_ref, taps, True)
        shift_rows(
            lambda r: field[s, r, :, columns].astype(jnp.float32), shifted, side + 6, side
        )

        def body(g, carry):
            for k, line in enumerate(seven_rows(shifted, taps, g * 4, 4, side)):
                at = pl.ds(pl.multiple_of((g * 4 + k) * side, 8), side)
                total = line.reshape(side, 128) + grad_low[0, at, :].astype(jnp.float32)
                map_out[0, at, :] = total.astype(jnp.bfloat16)
            return carry

        lax.fori_loop(0, side // 4, body, 0)

    @pl.when(j == plan["steps"] - 1)
    def _():
        for n in range(plan["steps"], plan["last"] + 1):
            slot(n)
        small_out[...] = gathered[...]
        halving.wait_sends()
        smalls.wait_sends()


def conv_back(
    dz, pick, place_map, padded, grad_low, tap_weights, smalls, grads
):
    slots, cells, channels = grad_low.shape
    rows, cols = padded.shape[1:3]
    side = rows - 6
    blocks = channels // 128
    steps = 4 * blocks
    shapes = [grad.shape for grad in grads]
    pieces = plan_pieces(shapes, 2_100_000)
    plan = spread_plan(len(pieces), steps, (1, 3), (7, 3), (4, 8, 12))
    for k in range(11):
        at = 2 * blocks + 2 * k
        plan["slots"].setdefault(at, []).append(("small", k))
        plan["last"] = max(plan["last"], at)
    any_space = pl.BlockSpec(memory_space=pl.ANY)

    def first_half(j):
        k = jnp.minimum(j, 2 * blocks - 1)
        return (k % 2, 0, 0, k // 2)

    def second_half(j):
        k = jnp.maximum(j - 2 * blocks, 0)
        return (k % 2, 0, k // 2)

    results = pl.pallas_call(
        partial(conv_back_kernel, shapes, pieces, plan),
        grid=(steps,),
        in_specs=[
            fixed_block(dz.shape),
            fixed_block(pick.shape),
            fixed_block(place_map.shape),
            pl.BlockSpec((1, rows, cols, 128), first_half),
            pl.BlockSpec((1, cells, 128), second_half),
            pl.BlockSpec(
                (tap_weights.shape[0], 128), lambda j: (0, jnp.maximum(j - 2 * blocks, 0) // 2)
            ),
        ]
        + [fixed_block(item.shape) for item in smalls]
        + [any_space] * len(grads),
        out_specs=[
            pl.BlockSpec((1, cells, 128), second_half),
            whole_block((SMALL_ROWS, 128)),
        ]
        + [whole_block(item.shape) for item in halving_outputs(shapes)],
        out_shape=[
            jax.ShapeDtypeStruct((slots, cells, channels), jnp.bfloat16),
            jax.ShapeDtypeStruct((SMALL_ROWS, 128), jnp.float32),
        ]
        + halving_outputs(shapes),
        scratch_shapes=halving_scratch(shapes, pieces)
        + [
            pltpu.VMEM((slots, rows, 32, channels), jnp.bfloat16),
            pltpu.VMEM((7, rows, side // 8, 8, 128), jnp.float32),
            pltpu.VMEM((49, 8, 128), jnp.float32),
            pltpu.VMEM((blocks, 56, 128), jnp.float32),
            pltpu.VMEM((SMALL_ROWS, 128), jnp.float32),
            pltpu.VMEM((SMALL_ROWS, 128), jnp.float32),
            pltpu.VMEM((SMALL_ROWS, 128), jnp.float32),
            pltpu.SemaphoreType.DMA((10,)),
            pltpu.SemaphoreType.DMA((10,)),
            pltpu.VMEM((slots, RIM_ROWS, channels), jnp.bfloat16),
            pltpu.VMEM((slots, CORNER_ROWS, channels), jnp.bfloat16),
            pltpu.VMEM((slots, RIM_ROWS, channels), jnp.bfloat16),
            pltpu.VMEM((slots, RIM_ROWS, channels), jnp.bfloat16),
            pltpu.VMEM((slots, CORNER_ROWS, channels), jnp.bfloat16),
            pltpu.SemaphoreType.DMA((6,)),
        ],
        compiler_params=pltpu.CompilerParams(
            collective_id=1, has_side_effects=True, vmem_limit_bytes=VMEM_LIMIT
        ),
        name="conv_back",
    )(
        dz,
        pick,
        place_map,
        padded,
        grad_low,
        tap_weights,
        *smalls,
        *halving_operands(grads),
    )
    return results[0], results[1], results[2:]


def rim_maps(side):
    tile = lax.axis_index("tile")
    low, high = tile % 2, tile // 2
    cells = side * side
    row = jnp.arange(RIM_ROWS + CORNER_ROWS, dtype=jnp.int32)
    edge_col = jnp.where(low == 0, side - 3, 0)
    edge_row = jnp.where(high == 0, side - 3, 0)
    rim_from = (row % side) * side + edge_col + row // side
    k = row - RIM_ROWS
    corner_from = (edge_row + k // 3) * side + edge_col + k % 3
    source = jnp.where(
        row < 3 * side, rim_from, jnp.where((k >= 0) & (k < 9), corner_from, -1)
    )
    pick = (source[:, None] == jnp.arange(cells, dtype=jnp.int32)[None, :]).astype(jnp.bfloat16)
    at = jnp.arange((side + 6) * 32, dtype=jnp.int32)
    i, j = at // 32 - 3, at % 32 - 3
    inside_i, inside_j = (i >= 0) & (i < side), (j >= 0) & (j < side)
    beside_j = ((j < 0) & (low == 1)) | ((j >= side) & (j < side + 3) & (low == 0))
    beside_i = ((i < 0) & (high == 1)) | ((i >= side) & (high == 0))
    q = jnp.where(j < 0, j + 3, j - side)
    p = jnp.where(i < 0, i + 3, i - side)
    skip = jnp.where(high == 1, RIM_ROWS - 3 * side, 0)
    source = jnp.where(
        inside_i & inside_j,
        i * side + j,
        jnp.where(
            inside_i & beside_j,
            cells + q * side + i,
            jnp.where(
                beside_i & inside_j,
                cells + RIM_ROWS + skip + p * side + j,
                jnp.where(beside_i & beside_j, cells + 2 * RIM_ROWS + p * 3 + q, -1),
            ),
        ),
    )
    parts = cells + 2 * RIM_ROWS + CORNER_ROWS
    place_map = (source[:, None] == jnp.arange(parts, dtype=jnp.int32)[None, :]).astype(
        jnp.bfloat16
    )
    return pick, place_map


def slot_rims(place, s, source, rim, corner, rim_in, row_in, corner_in, sems):
    cells = source.shape[1]
    start = pl.multiple_of((1 - place.high) * (cells - RIM_ROWS), 16)
    row = source.at[s, pl.ds(start, RIM_ROWS), :]
    return (
        remote(rim.at[s], rim_in.at[s], sems.at[6 * s], sems.at[6 * s + 1], place.to_low),
        remote(row, row_in.at[s], sems.at[6 * s + 2], sems.at[6 * s + 3], place.to_high),
        remote(
            corner.at[s], corner_in.at[s], sems.at[6 * s + 4], sems.at[6 * s + 5], place.to_across
        ),
    )


def conv_front_kernel(
    source,
    own,
    pick,
    place_map,
    tap_ref,
    table,
    norm_out,
    unit_out,
    scale_out,
    field_out,
    near,
    cells_ref,
    field,
    spread,
    shifted,
    taps,
    rim,
    corner,
    rim_in,
    row_in,
    corner_in,
    sems,
    load_sem,
    store_sem,
    near_sems,
):
    place = Place()
    gather = TokenGather(own, None, near, None, None, near_sems)
    slots, cells, channels = cells_ref.shape
    blocks = channels // 128
    side = field.shape[1] - 6
    j = pl.program_id(0)
    s, c = j // blocks, j % blocks
    columns = lanes(c * 128, 128)
    low = jnp.bfloat16

    def rims(q):
        return slot_rims(place, q, cells_ref, rim, corner, rim_in, row_in, corner_in, sems)

    def select(q):
        both = contract(pick[...], cells_ref[q], 1, 0).astype(low)
        rim[q] = both[:RIM_ROWS]
        corner[q] = both[RIM_ROWS:]
        for copy in rims(q):
            copy.start()

    def store(q):
        return pltpu.make_async_copy(field.at[q], field_out.at[q], store_sem.at[q])

    def build(q):
        for copy in rims(q):
            copy.wait()
        parts = jnp.concatenate([cells_ref[q], rim_in[q], row_in[q], corner_in[q]], axis=0)
        whole = contract(place_map[...], parts, 1, 0).astype(low)
        field[q] = whole.reshape(field.shape[1:])
        store(q).start()

    @pl.when(j == 0)
    def _():
        load = pltpu.make_async_copy(source, cells_ref, load_sem)
        load.start()
        greet((place.to_low, place.to_high, place.to_across))
        load.wait()
        select(0)
        build(0)
        for q in range(1, slots):
            select(q)

    for q in range(1, slots):
        pl.when(j == q * blocks)(partial(build, q))

    @pl.when(j == blocks)
    def _():
        gather.hand_on(0)

    fill_taps(tap_ref, taps, False)
    shift_rows(lambda r: field[s, r, :, columns].astype(jnp.float32), shifted, side + 6, side)

    def body(g, carry):
        for k, line in enumerate(seven_rows(shifted, taps, g * 4, 4, side)):
            at = pl.ds(pl.multiple_of((g * 4 + k) * side, 8), side)
            spread[c, at, :] = line.reshape(side, 128)
        return carry

    lax.fori_loop(0, side // 4, body, 0)

    @pl.when(c == blocks - 1)
    def _():
        gain_row = table[49:50, :]
        chunk = 192

        def norm(n, carry):
            at = pl.ds(pl.multiple_of(n * chunk, 16), chunk)
            values = jnp.concatenate([spread[b, at, :] for b in range(blocks)], axis=1)
            unit, scale = norm_parts(values)
            unit_out[at, :] = unit.astype(low)
            norm_out[at, :] = (unit * gain_row).astype(low)
            scale_out[at, :] = scale
            return carry

        lax.fori_loop(0, cells // chunk, norm, 0)

    @pl.when(j == slots * blocks - 1)
    def _():
        for q in range(slots):
            store(q).wait()
        gather.take(0)
        gather.wait_sends((0,))


def conv_front(source, own, pick, place_map, table):
    slots, cells, channels = source.shape
    side = math.isqrt(cells)
    blocks = channels // 128
    low = jnp.bfloat16
    field_shape = (slots, side + 6, 32, channels)
    any_space = pl.BlockSpec(memory_space=pl.ANY)
    by_slot = lambda j: (j // blocks, 0)
    rows = slots * cells
    return pl.pallas_call(
        conv_front_kernel,
        grid=(slots * blocks,),
        in_specs=[
            any_space,
            any_space,
            fixed_block(pick.shape),
            fixed_block(place_map.shape),
            pl.BlockSpec((table.shape[0], 128), lambda j: (0, j % blocks)),
            fixed_block(table.shape),
        ],
        out_specs=[
            pl.BlockSpec((cells, channels), by_slot),
            pl.BlockSpec((cells, channels), by_slot),
            pl.BlockSpec((cells, 1), by_slot),
            any_space,
            any_space,
        ],
        out_shape=[
            jax.ShapeDtypeStruct((rows, channels), low),
            jax.ShapeDtypeStruct((rows, channels), low),
            jax.ShapeDtypeStruct((rows, 1), jnp.float32),
            jax.ShapeDtypeStruct(field_shape, low),
            jax.ShapeDtypeStruct((2,) + own.shape, low),
        ],
        scratch_shapes=[
            pltpu.VMEM((slots, cells, channels), low),
            pltpu.VMEM(field_shape, low),
            pltpu.VMEM((blocks, cells, 128), jnp.float32),
            pltpu.VMEM((7, side + 6, side // 8, 8, 128), jnp.float32),
            pltpu.VMEM((49, 8, 128), jnp.float32),
            pltpu.VMEM((slots, RIM_ROWS, channels), low),
            pltpu.VMEM((slots, CORNER_ROWS, channels), low),
            pltpu.VMEM((slots, RIM_ROWS, channels), low),
            pltpu.VMEM((slots, RIM_ROWS, channels), low),
            pltpu.VMEM((slots, CORNER_ROWS, channels), low),
            pltpu.SemaphoreType.DMA((6 * slots,)),
            pltpu.SemaphoreType.DMA,
            pltpu.SemaphoreType.DMA((slots,)),
            pltpu.SemaphoreType.DMA((12,)),
        ],
        compiler_params=pltpu.CompilerParams(
            collective_id=2, has_side_effects=True, vmem_limit_bytes=VMEM_LIMIT
        ),
        name="conv_front",
    )(source, own, pick, place_map, table, table)


def map_mlp_kernel(
    norm_low,
    source,
    w_expand,
    w_shrink,
    w_adapt,
    pool,
    live,
    *refs,
):
    gathers = len(refs) > 6
    if gathers:
        own, near, everyone = refs[0], refs[1], refs[7]
        refs, rest = refs[2:7] + refs[8:9], refs[9:]
    wide_out, slope_out, map_out, pooled_out, adapted_out, total = refs
    j = pl.program_id(0)
    low = jnp.bfloat16
    if gathers:
        place = Place()
        gather = TokenGather(own, everyone, near, *rest)

        @pl.when(j == 0)
        def _():
            for copy in gather.loads():
                copy.start()
            greet((place.to_low, place.to_high, place.to_across))
            for copy in gather.loads():
                copy.wait()
            gather.hand_on(1)
            gather.local_stores(lambda copy: copy.start())

        @pl.when(j == 2)
        def _():
            gather.take(1)
            gather.hand_on(2)

    rows, width = norm_low.shape[0], w_expand.shape[1]
    half = rows // 2
    for part in (pl.ds(0, half), pl.ds(half, half)):
        wide, slope = gelu_pair(contract(norm_low[part, :], w_expand[...], 1, 0))
        wide_out[part, :] = wide
        slope_out[part, :] = slope
        term = contract(wide, w_shrink[...], 1, 0)

        @pl.when(j == 0)
        def _():
            total[part, :] = source[part, :].astype(jnp.float32) + term

        @pl.when(j > 0)
        def _():
            total[part, :] = total[part, :] + term

    @pl.when(j == pl.num_programs(0) - 1)
    def _():
        slots, cells, _ = map_out.shape
        for s in range(slots):
            after = total[pl.ds(s * cells, cells), :].astype(low)
            keep = jnp.broadcast_to(live[s], after.shape) > 0
            map_out[s] = jnp.where(keep, after, jnp.zeros_like(after))
            pooled = contract(pool[...], after, 1, 0).astype(low)
            pooled_out[s] = pooled
            adapted_out[s] = contract(pooled, w_adapt[...], 1, 0).astype(low)
        if gathers:
            gather.take(2)
            gather.local_stores(lambda copy: copy.wait())
            gather.wait_sends((1, 2))


def map_mlp(norm_low, source, w_expand, w_shrink, w_adapt, pool, live, own=None, near=None):
    slots, cells, channels = source.shape
    hidden, width = w_expand.shape[1], 1024
    few, model = pool.shape[0], w_adapt.shape[1]
    low = jnp.bfloat16
    extra, extra_space, extra_shape, extra_scratch = [], [], [], []
    params = pltpu.CompilerParams(vmem_limit_bytes=VMEM_LIMIT)
    if own is not None:
        extra, extra_space = [own, near], [pl.BlockSpec(memory_space=pl.ANY)]
        extra_shape = [jax.ShapeDtypeStruct((4,) + own.shape, low)]
        extra_scratch = [
            pltpu.VMEM((3,) + own.shape, low),
            pltpu.SemaphoreType.DMA((5,)),
            pltpu.SemaphoreType.DMA((12,)),
        ]
        params = pltpu.CompilerParams(
            collective_id=4, has_side_effects=True, vmem_limit_bytes=VMEM_LIMIT
        )
    rows = slots * cells
    return pl.pallas_call(
        map_mlp_kernel,
        grid=(hidden // width,),
        in_specs=[
            fixed_block((rows, channels)),
            fixed_block((rows, channels)),
            pl.BlockSpec((channels, width), lambda j: (0, j)),
            pl.BlockSpec((width, channels), lambda j: (j, 0)),
            fixed_block(w_adapt.shape),
            fixed_block(pool.shape),
            fixed_block(live.shape),
        ]
        + extra_space * 2,
        out_specs=[
            pl.BlockSpec((rows, width), lambda j: (0, j)),
            pl.BlockSpec((rows, width), lambda j: (0, j)),
            whole_block((slots, cells, channels)),
            whole_block((slots, few, channels)),
            whole_block((slots, few, model)),
        ]
        + extra_space,
        out_shape=[
            jax.ShapeDtypeStruct((rows, hidden), low),
            jax.ShapeDtypeStruct((rows, hidden), low),
            jax.ShapeDtypeStruct((slots, cells, channels), low),
            jax.ShapeDtypeStruct((slots, few, channels), low),
            jax.ShapeDtypeStruct((slots, few, model), low),
        ]
        + extra_shape,
        scratch_shapes=[pltpu.VMEM((rows, channels), jnp.float32)] + extra_scratch,
        cost_estimate=pl.CostEstimate(
            flops=4 * rows * channels * hidden,
            bytes_accessed=45 * 10**6,
            transcendentals=2 * rows * hidden,
        ),
        compiler_params=params,
        name="map_mlp",
    )(
        norm_low,
        source.reshape(rows, channels),
        w_expand,
        w_shrink,
        w_adapt,
        pool,
        live,
        *extra,
    )


def norm_parts(values):
    centre = values - jnp.mean(values, axis=-1, keepdims=True)
    scale = lax.rsqrt(jnp.mean(centre * centre, axis=-1, keepdims=True) + 1e-06)
    return centre * scale, scale


def norm_back(grad, unit, scale, gain):
    turned = grad * gain
    mean = jnp.mean(turned, axis=-1, keepdims=True)
    mean_unit = jnp.mean(turned * unit, axis=-1, keepdims=True)
    return scale * (turned - mean - unit * mean_unit)


def head_lanes(rows, odd):
    lane = lax.broadcasted_iota(jnp.int32, (rows, 2 * HDIM), 1)
    return (lane >= HDIM) if odd else (lane < HDIM)


def token_front_kernel(*refs):
    (own, everyone, table), refs = refs[:3], refs[3:]
    weights, refs = refs[:6], refs[6:]
    outs, refs = refs[:12], refs[12:]
    buffers, sems, refs = refs[:6], refs[6], refs[7:]
    held, out_sems = refs[:12], refs[12]
    (own_out, all_out, q_out, k_out, v_out, p_out) = held[:6]
    (o_out, x1_out, h_out, g_out, slope_out, x2_out) = held[6:]
    stores = [pltpu.make_async_copy(held[n], outs[n], out_sems.at[n]) for n in range(12)]
    copies = [
        pltpu.make_async_copy(weights[n], buffers[n], sems.at[n]) for n in range(6)
    ]
    for copy in copies:
        copy.start()
    low = jnp.bfloat16
    slots, count, width = own.shape
    gain = table[0:1, :]

    def norm_chunks(source, target, rows):
        def body(n, carry):
            at = pl.ds(pl.multiple_of(n * 144, 16), 144)
            unit, _ = norm_parts(source[at, :].astype(jnp.float32))
            target[at, :] = (unit * gain).astype(low)
            return carry

        lax.fori_loop(0, rows // 144, body, 0)

    for s in range(slots):
        norm_chunks(own.at[s], own_out.at[s], count)
        for t in range(everyone.shape[0]):
            norm_chunks(everyone.at[t, s], all_out.at[s, pl.ds(t * count, count), :], count)
    stores[0].start()
    stores[1].start()
    copies[0].wait()
    for s in range(slots):
        q_out[s] = contract(own_out[s], buffers[0][...], 1, 0).astype(low)
    stores[2].start()
    copies[1].wait()
    copies[2].wait()
    for s in range(slots):
        k_out[s] = contract(all_out[s], buffers[1][...], 1, 0).astype(low)
        v_out[s] = contract(all_out[s], buffers[2][...], 1, 0).astype(low)
    stores[3].start()
    stores[4].start()
    for s in range(slots):
        for pair in range(HEADS // 2):
            at = pl.ds(pair * 2 * HDIM, 2 * HDIM)
            q, k, v = q_out[s, :, at], k_out[s, :, at], v_out[s, :, at]
            q = q * jnp.asarray(HDIM ** (-0.5), low)
            mixed = []
            for odd in range(2):
                part = jnp.where(head_lanes(count, odd), q, jnp.zeros_like(q))
                scores = contract(part, k, 1, 1)
                shifted = jnp.exp(scores - jnp.max(scores, axis=-1, keepdims=True))
                share = 1.0 / jnp.sum(shifted, axis=-1, keepdims=True)
                p = (shifted * share).astype(low)
                p_out[s * HEADS + 2 * pair + odd] = p
                mixed.append(contract(p, v, 1, 0))
            o_out[s, :, at] = jnp.where(head_lanes(count, 0), mixed[0], mixed[1]).astype(low)
    stores[5].start()
    stores[6].start()
    copies[3].wait()
    gain_two = table[1:2, :]
    for s in range(slots):
        x1 = own[s].astype(jnp.float32) + contract(o_out[s], buffers[3][...], 1, 0)
        x1_out[s] = x1
        unit, _ = norm_parts(x1)
        h_out[s] = (unit * gain_two).astype(low)
    stores[7].start()
    stores[8].start()
    copies[4].wait()
    hidden = g_out.shape[2]
    for s in range(slots):
        for c in range(0, hidden, 768):
            at = pl.ds(c, 768)
            g_out[s, :, at], slope_out[s, :, at] = gelu_pair(
                contract(h_out[s], buffers[4][:, at], 1, 0)
            )
    stores[9].start()
    stores[10].start()
    copies[5].wait()
    for s in range(slots):
        x2_out[s] = x1_out[s] + contract(g_out[s], buffers[5][...], 1, 0)
    stores[11].start()
    for copy in stores:
        copy.wait()


def token_front(own, everyone, table, weights):
    slots, count, width = own.shape
    total, hidden = everyone.shape[0] * count, weights[4].shape[1]
    low, wide = jnp.bfloat16, jnp.float32
    shapes = [
        ((slots, count, width), low),
        ((slots, total, width), low),
        ((slots, count, width), low),
        ((slots, total, width), low),
        ((slots, total, width), low),
        ((slots * HEADS, count, total), low),
        ((slots, count, width), low),
        ((slots, count, width), wide),
        ((slots, count, width), low),
        ((slots, count, hidden), low),
        ((slots, count, hidden), low),
        ((slots, count, width), wide),
    ]
    in_vmem = pl.BlockSpec(memory_space=pltpu.VMEM)
    return pl.pallas_call(
        token_front_kernel,
        in_specs=[in_vmem] * 3 + [pl.BlockSpec(memory_space=pl.ANY)] * 6,
        out_specs=[pl.BlockSpec(memory_space=pl.ANY)] * len(shapes),
        out_shape=[jax.ShapeDtypeStruct(shape, dtype) for shape, dtype in shapes],
        scratch_shapes=[pltpu.VMEM(weight.shape, low) for weight in weights]
        + [pltpu.SemaphoreType.DMA((6,))]
        + [pltpu.VMEM(shape, dtype) for shape, dtype in shapes]
        + [pltpu.SemaphoreType.DMA((12,))],
        cost_estimate=pl.CostEstimate(
            flops=9 * 10**9, bytes_accessed=30 * 10**6, transcendentals=3 * 10**6
        ),
        compiler_params=pltpu.CompilerParams(vmem_limit_bytes=VMEM_LIMIT),
        name="token_front",
    )(own, everyone, table, *weights)


def token_back_kernel(*refs):
    (dx2, x1_ref, table), refs = refs[:3], refs[3:]
    saved, refs = refs[:10], refs[10:]
    weights, refs = refs[:6], refs[6:]
    outs, refs = refs[:9], refs[9:]
    gain_out, refs = refs[0], refs[1:]
    kept, refs = refs[:10], refs[10:]
    buffers, refs = refs[:6], refs[6:]
    held, refs = refs[:9], refs[9:]
    du, do, dq, dk, dv, sems, weight_sems, out_sems = refs
    (up_out, down_out, q_out, k_out, v_out, o_out, dx1_out, da_own_out, da_all_out) = held
    stores = [pltpu.make_async_copy(held[n], outs[n], out_sems.at[n]) for n in range(9)]
    (own, everyone, q_all, k_all, v_all, p_all, o_all, h_all, g_all, slope_all) = kept
    order = (8, 9, 7, 6, 4, 5, 3, 2, 0, 1)
    saved_copies = [
        pltpu.make_async_copy(saved[n], kept[n], sems.at[n]) for n in range(10)
    ]
    weight_copies = [
        pltpu.make_async_copy(weights[n], buffers[n], weight_sems.at[n]) for n in range(6)
    ]
    weight_copies[5].start()
    for n in order[:3]:
        saved_copies[n].start()
    weight_copies[4].start()
    weight_copies[3].start()
    for n in order[3:]:
        saved_copies[n].start()
    for n in range(3):
        weight_copies[n].start()
    low = jnp.bfloat16
    slots, count, width = dx2.shape
    hidden = g_all.shape[2]
    gain = table[1:2, :]
    flat = lambda ref: ref[...].reshape(-1, ref.shape[-1])
    grad_low = flat(dx2).astype(low)
    weight_copies[5].wait()
    for n in order[:3]:
        saved_copies[n].wait()
    for c in range(0, hidden, 768):
        at = pl.ds(c, 768)
        grad = contract(grad_low, buffers[5][at, :], 1, 1)
        slope = slope_all[:, :, at].reshape(-1, 768).astype(jnp.float32)
        du[:, at] = (grad * slope).astype(low)
        g = g_all[:, :, at].reshape(-1, 768)
        down_out[at, :] = contract(g, grad_low, 0, 0).astype(low)
        h = flat(h_all)
        up_out[:, at] = contract(h, du[:, at], 0, 0).astype(low)
    stores[0].start()
    stores[1].start()
    weight_copies[4].wait()
    dh = contract(du[...], buffers[4][...], 1, 1)
    unit, scale = norm_parts(flat(x1_ref))
    gain_out[...] = jnp.sum(dh * unit, axis=0, keepdims=True)
    dx1 = flat(dx2) + norm_back(dh, unit, scale, gain)
    dx1_out[...] = dx1.reshape(dx1_out.shape)
    stores[6].start()
    dar = dx1.astype(low)
    weight_copies[3].wait()
    for n in order[3:]:
        saved_copies[n].wait()
    o_out[...] = contract(flat(o_all), dar, 0, 0).astype(low)
    stores[5].start()
    do[...] = contract(dar, buffers[3][...], 1, 1).astype(low).reshape(do.shape)
    for s in range(slots):
        for pair in range(HEADS // 2):
            at = pl.ds(pair * 2 * HDIM, 2 * HDIM)
            q, k, v, grad = q_all[s, :, at], k_all[s, :, at], v_all[s, :, at], do[s, :, at]
            parts = []
            for odd in range(2):
                p = p_all[s * HEADS + 2 * pair + odd]
                mine = jnp.where(head_lanes(count, odd), grad, jnp.zeros_like(grad))
                dp = contract(mine, v, 1, 1)
                wide_p = p.astype(jnp.float32)
                row = jnp.sum(wide_p * dp, axis=-1, keepdims=True)
                ds = (wide_p * (dp - row)).astype(low)
                parts.append(
                    (contract(ds, k, 1, 0), contract(ds, q, 0, 0), contract(p, grad, 0, 0))
                )
            few, many = head_lanes(count, 0), head_lanes(k.shape[0], 0)
            root = HDIM ** (-0.5)
            dq[s, :, at] = (jnp.where(few, parts[0][0], parts[1][0]) * root).astype(low)
            dk[s, :, at] = (jnp.where(many, parts[0][1], parts[1][1]) * root).astype(low)
            dv[s, :, at] = jnp.where(many, parts[0][2], parts[1][2]).astype(low)
    for n in range(3):
        weight_copies[n].wait()
    for s in range(slots):
        da_own_out[s] = contract(dq[s], buffers[0][...], 1, 1)
        both = contract(dk[s], buffers[1][...], 1, 1) + contract(dv[s], buffers[2][...], 1, 1)
        for t in range(da_all_out.shape[0]):
            da_all_out[t, s] = both[t * count : (t + 1) * count].astype(low)
    stores[7].start()
    stores[8].start()
    q_out[...] = contract(flat(own), flat(dq), 0, 0).astype(low)
    stores[2].start()
    k_out[...] = contract(flat(everyone), flat(dk), 0, 0).astype(low)
    stores[3].start()
    v_out[...] = contract(flat(everyone), flat(dv), 0, 0).astype(low)
    stores[4].start()
    for copy in stores:
        copy.wait()


def token_back(dx2, x1, table, saved, weights):
    slots, count, width = dx2.shape
    total, hidden = saved[1].shape[1], weights[4].shape[1]
    low, wide = jnp.bfloat16, jnp.float32
    shapes = [
        ((width, hidden), low),
        ((hidden, width), low),
        ((width, width), low),
        ((width, width), low),
        ((width, width), low),
        ((width, width), low),
        ((slots, count, width), wide),
        ((slots, count, width), wide),
        ((total // count, slots, count, width), low),
        ((1, width), wide),
    ]
    in_vmem = pl.BlockSpec(memory_space=pltpu.VMEM)
    any_space = pl.BlockSpec(memory_space=pl.ANY)
    return pl.pallas_call(
        token_back_kernel,
        in_specs=[in_vmem] * 3 + [any_space] * 16,
        out_specs=[any_space] * 9 + [in_vmem],
        out_shape=[jax.ShapeDtypeStruct(shape, dtype) for shape, dtype in shapes],
        scratch_shapes=[pltpu.VMEM(item.shape, low) for item in saved]
        + [pltpu.VMEM(weight.shape, low) for weight in weights]
        + [pltpu.VMEM(shape, dtype) for shape, dtype in shapes[:9]]
        + [
            pltpu.VMEM((slots * count, hidden), low),
            pltpu.VMEM((slots, count, width), low),
            pltpu.VMEM((slots, count, width), low),
            pltpu.VMEM((slots, total, width), low),
            pltpu.VMEM((slots, total, width), low),
            pltpu.SemaphoreType.DMA((10,)),
            pltpu.SemaphoreType.DMA((6,)),
            pltpu.SemaphoreType.DMA((9,)),
        ],
        cost_estimate=pl.CostEstimate(
            flops=18 * 10**9, bytes_accessed=50 * 10**6, transcendentals=10**6
        ),
        compiler_params=pltpu.CompilerParams(vmem_limit_bytes=VMEM_LIMIT),
        name="token_back",
    )(dx2, x1, table, *saved, *weights)


SMALL_SIDE = 16


def merge_maps(side):
    tile = lax.axis_index("tile")
    low, high = tile % 2, tile // 2
    cells = side * side
    row = jnp.arange(3 * SMALL_SIDE, dtype=jnp.int32)
    edge_col = jnp.where(low == 0, side - 1, 0)
    edge_row = jnp.where(high == 0, side - 1, 0)
    k = row % SMALL_SIDE
    source = jnp.where(
        (row < SMALL_SIDE) & (k < side),
        k * side + edge_col,
        jnp.where(
            (row >= SMALL_SIDE) & (row < 2 * SMALL_SIDE) & (k < side),
            edge_row * side + k,
            jnp.where(row == 2 * SMALL_SIDE, edge_row * side + edge_col, -1),
        ),
    )
    pick = source[:, None] == jnp.arange(cells, dtype=jnp.int32)[None, :]
    at = jnp.arange(9 * cells, dtype=jnp.int32)
    tap, cell = at // cells, at % cells
    i, j = cell // side + tap // 3 - 1, cell % side + tap % 3 - 1
    inside_i, inside_j = (i >= 0) & (i < side), (j >= 0) & (j < side)
    beside_j = ((j < 0) & (low == 1)) | ((j >= side) & (low == 0))
    beside_i = ((i < 0) & (high == 1)) | ((i >= side) & (high == 0))
    source = jnp.where(
        inside_i & inside_j,
        i * side + j,
        jnp.where(
            inside_i & beside_j,
            cells + i,
            jnp.where(
                beside_i & inside_j,
                cells + SMALL_SIDE + j,
                jnp.where(beside_i & beside_j, cells + 2 * SMALL_SIDE, -1),
            ),
        ),
    )
    parts = cells + 3 * SMALL_SIDE
    shifts = source[:, None] == jnp.arange(parts, dtype=jnp.int32)[None, :]
    return pick.astype(jnp.bfloat16), shifts.astype(jnp.bfloat16)


def merge_kernel(
    adapted,
    pooled,
    tokens,
    vit_grad,
    map_grad,
    live,
    table,
    w_adapt,
    pool,
    pick,
    shifts,
    vit_out,
    dx2_out,
    grad_out,
    adapt_out,
    small_out,
    rims,
    inbox,
    moved,
    grads,
    back,
    send_sem,
    recv_sem,
):
    place = Place()
    partners = (place.to_low, place.to_high, place.to_across)
    low = jnp.bfloat16
    slots, cells, width = adapted.shape

    def copies(phase, s):
        made = []
        for n, partner in enumerate(partners):
            at = (phase * slots + s) * 3 + n
            made.append(
                remote(
                    rims.at[phase, s, pl.ds(n * SMALL_SIDE, SMALL_SIDE), :],
                    inbox.at[phase, s, pl.ds(n * SMALL_SIDE, SMALL_SIDE), :],
                    send_sem.at[at],
                    recv_sem.at[at],
                    partner,
                )
            )
        return made

    def give(phase, s, source):
        rims[phase, s] = contract(pick[...], source[s], 1, 0).astype(low)
        for copy in copies(phase, s):
            copy.start()

    def shift(phase, s, source):
        for copy in copies(phase, s):
            copy.wait()
        parts = jnp.concatenate([source[s], inbox[phase, s]], axis=0)
        moved[s] = contract(shifts[...], parts, 1, 0).astype(low).reshape(moved.shape[1:])

    gate_low, gate_high = table[2:3, :], table[3:4, :]
    greet(partners)
    for s in range(slots):
        give(0, s, adapted)
    small_out[...] = jnp.zeros_like(small_out)
    for s in range(slots):
        shift(0, s, adapted)
        f = jnp.zeros((cells, width), jnp.float32)
        for k in range(9):
            f = f + table[4 + k : 5 + k, :] * moved[s, k].astype(jnp.float32)
        x2 = tokens[s]
        alive = live[s]
        logit = jnp.sum(x2 * gate_low, axis=-1, keepdims=True) + jnp.sum(
            f * gate_high, axis=-1, keepdims=True
        )
        gate = 1.0 / (1.0 + jnp.exp(-logit))
        vit_out[s] = ((x2 + gate * f) * alive).astype(low)
        dvo = vit_grad[s].astype(jnp.float32) * alive
        dl = jnp.sum(dvo * f, axis=-1, keepdims=True) * gate * (1.0 - gate)
        dx2_out[s] = dvo + dl * gate_low
        df = gate * dvo + dl * gate_high
        grads[s] = df.astype(low)
        give(1, s, grads)
        for k in range(9):
            part = jnp.sum(df * moved[s, k].astype(jnp.float32), axis=0, keepdims=True)
            small_out[k : k + 1, :] = small_out[k : k + 1, :] + part
        small_out[9:10, :] = small_out[9:10, :] + jnp.sum(dl * x2, axis=0, keepdims=True)
        small_out[10:11, :] = small_out[10:11, :] + jnp.sum(dl * f, axis=0, keepdims=True)
    for s in range(slots):
        shift(1, s, grads)
        total = jnp.zeros((cells, width), jnp.float32)
        for k in range(9):
            total = total + table[12 - k : 13 - k, :] * moved[s, k].astype(jnp.float32)
        back[pl.ds(s * cells, cells), :] = total.astype(low)
    flat = pooled[...].reshape(slots * cells, -1)
    adapt_out[...] = contract(flat, back[...], 0, 0).astype(low)
    for s in range(slots):
        part = contract(back[pl.ds(s * cells, cells), :], w_adapt[...], 1, 1).astype(low)
        spread = contract(pool[...], part, 0, 0)
        grad_out[s] = (map_grad[s].astype(jnp.float32) * live[s] + spread).astype(low)


def merge_step(adapted, pooled, tokens, vit_grad, map_grad, live, table, w_adapt, pool):
    slots, cells, width = adapted.shape
    low = jnp.bfloat16
    pick, shifts = merge_maps(math.isqrt(cells))
    in_vmem = pl.BlockSpec(memory_space=pltpu.VMEM)
    return pl.pallas_call(
        merge_kernel,
        in_specs=[in_vmem] * 11,
        out_specs=[in_vmem] * 5,
        out_shape=[
            jax.ShapeDtypeStruct(adapted.shape, low),
            jax.ShapeDtypeStruct(adapted.shape, jnp.float32),
            jax.ShapeDtypeStruct(map_grad.shape, low),
            jax.ShapeDtypeStruct(w_adapt.shape, low),
            jax.ShapeDtypeStruct((16, width), jnp.float32),
        ],
        scratch_shapes=[
            pltpu.VMEM((2, slots, 3 * SMALL_SIDE, width), low),
            pltpu.VMEM((2, slots, 3 * SMALL_SIDE, width), low),
            pltpu.VMEM((slots, 9, cells, width), low),
            pltpu.VMEM((slots, cells, width), low),
            pltpu.VMEM((slots * cells, width), low),
            pltpu.SemaphoreType.DMA((6 * slots,)),
            pltpu.SemaphoreType.DMA((6 * slots,)),
        ],
        compiler_params=pltpu.CompilerParams(
            collective_id=3, has_side_effects=True, vmem_limit_bytes=VMEM_LIMIT
        ),
        name="merge_step",
    )(
        adapted,
        pooled,
        tokens,
        vit_grad,
        map_grad,
        live,
        table,
        w_adapt,
        pool,
        pick,
        shifts,
    )


def turned(shape):
    return shape[1] % 128 != 0 and shape[0] % 128 == 0


def hand_out_kernel(count, *refs):
    small, refs = refs[0], refs[1:]
    matrices, refs = refs[:count], refs[count:]
    outs, refs = refs[:count], refs[count:]
    large_out, conv_out, small_out, *rows_out = refs
    for n in range(count):
        value = matrices[n][...]
        outs[n][...] = value.T if turned(value.shape) else value
    blocks = large_out.shape[1] // 128
    for b in range(blocks):
        large_out[:, b * 128 : (b + 1) * 128] = small[b * 49 : (b + 1) * 49, :]
        row = 49 * blocks + small_out.shape[1] // 8 + b
        conv_out[pl.ds(b * 128, 128)] = small[row]
    for b in range(small_out.shape[1] // 128):
        row = 49 * blocks + b * 16
        small_out[:, b * 128 : (b + 1) * 128] = small[row : row + 9, :]
        for n, out in enumerate(rows_out):
            out[pl.ds(b * 128, 128)] = small[row + 9 + n]


def hand_out(small, matrices, channels, width):
    in_vmem = pl.BlockSpec(memory_space=pltpu.VMEM)
    count = len(matrices)
    results = pl.pallas_call(
        partial(hand_out_kernel, count),
        in_specs=[in_vmem] * (count + 1),
        out_specs=[in_vmem] * (count + 7),
        out_shape=[
            jax.ShapeDtypeStruct(
                item.shape[::-1] if turned(item.shape) else item.shape, item.dtype
            )
            for item in matrices
        ]
        + [
            jax.ShapeDtypeStruct((49, channels), jnp.float32),
            jax.ShapeDtypeStruct((channels,), jnp.float32),
            jax.ShapeDtypeStruct((9, width), jnp.float32),
        ]
        + [jax.ShapeDtypeStruct((width,), jnp.float32)] * 4,
        name="hand_out",
    )(small, *matrices)
    taps_grad, gain_conv_grad, small_grad, low_grad, high_grad, one_grad, two_grad = results[count:]
    return [
        result.T if turned(item.shape) else result for result, item in zip(results, matrices)
    ] + [one_grad, two_grad, small_grad, low_grad, high_grad, gain_conv_grad, taps_grad]


def chip_layout():
    return lax.axis_size("img") == 8 and lax.axis_size("tile") == 4


def sum_plain(grads, smalls):
    sums = []
    for grad in grads:
        part = lax.psum_scatter(grad, "img", scatter_dimension=0, tiled=True)
        part = lax.psum_scatter(part, "tile", scatter_dimension=1, tiled=True)
        sums.append(part.astype(jnp.float32))
    return sums, lax.psum(tuple(smalls), ("img", "tile"))


def map_back_plain(
    grad_low, norm_low, wide_low, wide_slope, w_shrink, w_expand, unit, scale, gain, padded, taps
):
    slots, cells, channels = grad_low.shape
    side = math.isqrt(cells)
    wide_low = wide_low.reshape(slots, cells, -1)
    wide_slope = wide_slope.reshape(slots, cells, -1)
    w_shrink_grad = outer_sum(wide_low, grad_low)
    grad_wide_low = (project_back(grad_low, w_shrink) * wide_slope).astype(jnp.bfloat16)
    w_expand_grad = outer_sum(norm_low, grad_wide_low)
    back = project_back(grad_wide_low, w_expand)
    gain_conv_grad = jnp.sum(back * unit, axis=(0, 1))
    grad_spread = norm_back(back, unit, scale, gain).reshape(slots, side, side, channels)
    field = padded.astype(jnp.float32)
    taps_grad = jnp.stack(
        [
            jnp.sum(field[:, a : a + side, b : b + side] * grad_spread, axis=(0, 1, 2))
            for a in range(7)
            for b in range(7)
        ]
    )
    padded_grad = add_rims(grad_spread.astype(jnp.bfloat16), 3).astype(jnp.float32)
    moved = depthwise(padded_grad, taps[::-1], 3, 0).reshape(slots, cells, channels)
    map_grad = (grad_low.astype(jnp.float32) + moved).astype(jnp.bfloat16)
    return map_grad, w_expand_grad, w_shrink_grad, gain_conv_grad, taps_grad


def local(
    vit_in,
    map_in,
    group_images,
    vit_grad_out,
    map_grad_out,
    w_query,
    w_key,
    w_value,
    w_out,
    w_up,
    w_down,
    w_expand,
    w_shrink,
    w_adapt,
    gain_attn,
    gain_mlp,
    gain_conv,
    dw_large,
    dw_small,
    gate_low,
    gate_high,
):
    slot_count = vit_in.shape[0]
    tok_side = math.isqrt(vit_in.shape[2])
    pix_side = math.isqrt(map_in.shape[2])
    channels = map_in.shape[3]
    model_width = vit_in.shape[3]
    live_mask = (
        (jnp.arange(slot_count, dtype=jnp.int32) < group_images[0])
        .astype(jnp.float32)
        .reshape(slot_count, 1, 1)
    )
    cells = pix_side * pix_side
    on_chips = chip_layout()
    own = vit_in[:, 0]
    tokens = own.astype(jnp.float32)
    gain_one = gain_attn.astype(jnp.float32)
    conv_gain = gain_conv.astype(jnp.float32)
    large_taps = dw_large.astype(jnp.float32)
    map_table = jnp.concatenate([dw_large, gain_conv[None]]).astype(jnp.float32)
    token_table = jnp.concatenate(
        [gain_attn[None], gain_mlp[None], gate_low[None], gate_high[None], dw_small]
    ).astype(jnp.float32)
    few = jnp.arange(tok_side * tok_side, dtype=jnp.int32)[:, None]
    cell = jnp.arange(cells, dtype=jnp.int32)[None, :]
    holder = cell // pix_side // 2 * tok_side + cell % pix_side // 2
    pool = jnp.where(holder == few, 0.25, 0.0).astype(jnp.bfloat16)
    if on_chips:
        pick, place_map = rim_maps(pix_side)
        conv_norm_low, conv_unit_low, conv_scale, padded_map, near = conv_front(
            map_in[:, 0], own, pick, place_map, map_table
        )
    else:
        near = None
        map_low = map_in[:, 0].reshape(slot_count, pix_side, pix_side, channels)
        padded_map = add_rims(map_low, 3)
        spread_map = depthwise(padded_map.astype(jnp.float32), large_taps, 3, 0)
        conv_unit, conv_scale = norm_parts(spread_map.reshape(slot_count, cells, channels))
        conv_norm_low = (conv_unit * conv_gain).astype(jnp.bfloat16).reshape(-1, channels)
    wide_low, wide_slope, map_result, pooled_low, adapted_low, *gathered = map_mlp(
        conv_norm_low,
        map_in[:, 0],
        w_expand,
        w_shrink,
        w_adapt,
        pool,
        live_mask,
        own if on_chips else None,
        near,
    )
    own_all = gathered[0] if on_chips else lax.all_gather(own, "tile", axis=0, tiled=False)
    token_weights = (w_query, w_key, w_value, w_out, w_up, w_down)
    front = token_front(own, own_all, token_table, token_weights)
    residual_one, residual_two = front[7], front[11]
    saved = front[:7] + front[8:11]
    if on_chips:
        vit_result, grad_residual_two, grad_conv_low, w_adapt_grad, sides = merge_step(
            adapted_low,
            pooled_low,
            residual_two,
            vit_grad_out[:, 0],
            map_grad_out[:, 0],
            live_mask,
            token_table,
            w_adapt,
            pool,
        )
    else:
        adapted_low = adapted_low.reshape(slot_count, tok_side, tok_side, model_width)
        padded_small = add_rims(adapted_low, 1).astype(jnp.float32)
        merged_map, merged_pull = jax.vjp(
            partial(depthwise, radius=1, margin=0), padded_small, dw_small.astype(jnp.float32)
        )
        merged_tokens = merged_map.reshape(slot_count, tok_side * tok_side, model_width)
        vit_after, merging_pull = jax.vjp(
            merging,
            residual_two,
            merged_tokens,
            gate_low.astype(jnp.float32),
            gate_high.astype(jnp.float32),
        )
        vit_result = (vit_after * live_mask).astype(jnp.bfloat16)
        vit_cotangent = vit_grad_out[:, 0].astype(jnp.float32) * live_mask
        map_cotangent = map_grad_out[:, 0].astype(jnp.float32) * live_mask
        grad_residual_two, grad_merged, gate_low_grad, gate_high_grad = merging_pull(vit_cotangent)
        grad_padded_small, dw_small_grad = merged_pull(
            grad_merged.reshape(slot_count, tok_side, tok_side, model_width)
        )
        grad_adapted_low = return_rims(grad_padded_small, 1).astype(jnp.bfloat16)
        grad_adapted_low = grad_adapted_low.reshape(slot_count, tok_side * tok_side, model_width)
        w_adapt_grad = outer_sum(pooled_low, grad_adapted_low)
        grad_pooled = project_back(grad_adapted_low, w_adapt).astype(jnp.bfloat16)
        grad_conv_low = (
            map_cotangent
            + jnp.einsum("pc,spk->sck", pool, grad_pooled, preferred_element_type=jnp.float32)
        ).astype(jnp.bfloat16)
    (
        w_up_grad,
        w_down_grad,
        w_query_grad,
        w_key_grad,
        w_value_grad,
        w_out_grad,
        grad_residual_one,
        grad_own,
        grad_everyone,
        gain_mlp_grad,
    ) = token_back(grad_residual_two, residual_one, token_table, saved, token_weights)
    token_grads = (
        w_up_grad,
        w_down_grad,
        w_adapt_grad,
        w_query_grad,
        w_key_grad,
        w_value_grad,
        w_out_grad,
    )
    if on_chips:
        first, first_sums = map_mlp_back(
            grad_conv_low.reshape(-1, channels),
            conv_norm_low,
            wide_low,
            wide_slope,
            w_shrink,
            w_expand,
            conv_unit_low,
            conv_scale,
            map_table,
            grad_everyone,
            token_grads,
        )
        w_shrink_grad, w_expand_grad, dz, gain_conv_grad, grad_shared = first
    else:
        grad_shared = lax.psum_scatter(
            grad_everyone, "tile", scatter_dimension=0, tiled=False
        ).astype(jnp.float32)
    grad_normed_one = grad_own + grad_shared
    unit_one, scale_one = norm_parts(tokens)
    gain_attn_grad = jnp.sum(grad_normed_one * unit_one, axis=(0, 1)).reshape(1, model_width)
    vit_in_grad = (
        grad_residual_one + norm_back(grad_normed_one, unit_one, scale_one, gain_one)
    ).astype(jnp.bfloat16)
    if on_chips:
        map_in_grad, small, last_sums = conv_back(
            dz.reshape(grad_conv_low.shape),
            pick,
            place_map,
            padded_map,
            grad_conv_low,
            map_table,
            (sides, gain_attn_grad, gain_mlp_grad, gain_conv_grad),
            (w_expand_grad, w_shrink_grad),
        )
        final = hand_out(small, tuple(first_sums) + tuple(last_sums), channels, model_width)
        matrix_sums, small_sums = final[:9], final[9:]
    else:
        map_in_grad, w_expand_grad, w_shrink_grad, gain_conv_grad, taps_grad = map_back_plain(
            grad_conv_low,
            conv_norm_low,
            wide_low,
            wide_slope,
            w_shrink,
            w_expand,
            conv_unit,
            conv_scale,
            conv_gain,
            padded_map,
            large_taps,
        )
        matrix_sums, small_sums = sum_plain(
            token_grads + (w_expand_grad, w_shrink_grad),
            (
                gain_attn_grad.reshape(model_width),
                gain_mlp_grad.reshape(model_width),
                dw_small_grad,
                gate_low_grad,
                gate_high_grad,
                gain_conv_grad,
                taps_grad,
            ),
        )
    return (
        vit_result[:, None],
        map_result[:, None],
        vit_in_grad[:, None],
        map_in_grad[:, None],
        matrix_sums[3],
        matrix_sums[4],
        matrix_sums[5],
        matrix_sums[6],
        matrix_sums[0],
        matrix_sums[1],
        matrix_sums[7],
        matrix_sums[8],
        matrix_sums[2],
        small_sums[0],
        small_sums[1],
        small_sums[5],
        small_sums[6],
        small_sums[2],
        small_sums[3],
        small_sums[4],
    )


def solution(mesh):
    in_specs = (
        P("img", "tile", None, None),
        P("img", "tile", None, None),
        P("img"),
        P("img", "tile", None, None),
        P("img", "tile", None, None),
        P(),
        P(),
        P(),
        P(),
        P(),
        P(),
        P(),
        P(),
        P(),
        P(),
        P(),
        P(),
        P(),
        P(),
        P(),
        P(),
    )
    out_specs = (
        P("img", "tile", None, None),
        P("img", "tile", None, None),
        P("img", "tile", None, None),
        P("img", "tile", None, None),
        P("img", "tile"),
        P("img", "tile"),
        P("img", "tile"),
        P("img", "tile"),
        P("img", "tile"),
        P("img", "tile"),
        P("img", "tile"),
        P("img", "tile"),
        P("img", "tile"),
        P(),
        P(),
        P(),
        P(),
        P(),
        P(),
        P(),
    )
    return jax.shard_map(local, mesh=mesh, in_specs=in_specs, out_specs=out_specs, check_vma=False)
```
